32 devices in a mesh: wide: 8 (over z, x), narrow: 4 (over y, core).
Axes of the slice: x: 2, y: 2, z: 4, core: 2. Of those that a mesh axis runs over, the one named last changes fastest.
Arguments:
- tokens: bfloat16 [32, 1024, 768], P('wide', 'narrow'), may hold values from -6 to 6
- condition: bfloat16 [32, 768], P('wide'), may hold values from -6 to 6
- cotangent: bfloat16 [32, 1024, 768], P('wide', 'narrow'), may hold values from -6 to 6
- counts: int32 [8], P('wide'), may hold values from 1 to 4, as said below
- w_ada: bfloat16 [768, 4608], replicated, may hold values from -0.21875 to 0.21875
- k_attn: bfloat16 [3, 3, 768], replicated, may hold values from -2 to 2
- w_qkv: bfloat16 [768, 3, 768], P(None, None, 'narrow'), may hold values from -0.21875 to 0.21875
- w_out: bfloat16 [768, 768], P('narrow'), may hold values from -1.75 to 1.75
- w_up: bfloat16 [768, 3072], P(None, 'narrow'), may hold values from -0.21875 to 0.21875
- k_ffn: bfloat16 [3, 3, 3072], P(None, None, 'narrow'), may hold values from -2 to 2
- w_down: bfloat16 [3072, 768], P('narrow'), may hold values from -0.109375 to 0.109375
Outputs:
- block: bfloat16 [32, 1024, 768], P('wide', 'narrow')
- grad_tokens: float32 [32, 1024, 768], P('wide', 'narrow')
- grad_condition: float32 [32, 768], P('wide')
- grad_w_ada: float32 [768, 4608], replicated
- grad_k_attn: float32 [3, 3, 768], replicated
- grad_w_qkv: float32 [768, 3, 768], P(None, None, 'narrow')
- grad_w_out: float32 [768, 768], P('narrow')
- grad_w_up: float32 [768, 3072], P(None, 'narrow')
- grad_k_ffn: float32 [3, 3, 3072], P(None, None, 'narrow')
- grad_w_down: float32 [3072, 768], P('narrow')
The draws below stay inside these ranges and needn't reach their ends.
Inputs may be any that keep to these rules, and one draw needn't show every extreme that they name: counts[w] is the number of live latents among the 4 slots of wide index w (slots 0 to counts[w] - 1 are live); some index has all 4 live.
All inputs are finite; a program needn't handle non-finite values.
Results may differ from the reference program's by a relative error of at most 0.015.
The reference program's roundings to bfloat16 on the way count: a program that leaves them out, or rounds other values in their place, can miss the bound.
Values may be sent and summed in bfloat16 or wider, within the bound.
A program may use at most 192 MiB of HBM per device.

```python
import jax
import jax.numpy as jnp
from jax import lax

D = 768
HEADS = 12
FF = 3072
HEAD_DIM = 64
SIDE = 32
TOKENS_LAT = 1024
LAT_DEV = 4
LATENTS = 32
N_WIDE = 8


def drawn_field(key, shape, scale, bound):
    values = jax.random.normal(key, shape, jnp.float32) * scale
    return jnp.clip(values, -bound, bound)


def draw_tokens(key, part):
    return drawn_field(jax.random.fold_in(key, 101), (LATENTS, TOKENS_LAT, D), 1.0, 6.0).astype(jnp.bfloat16)


def draw_condition(key, part):
    return drawn_field(jax.random.fold_in(key, 103), (LATENTS, D), 1.0, 6.0).astype(jnp.bfloat16)


def draw_k_attn(key, part):
    scale = 9.0 ** (-0.5)
    return drawn_field(jax.random.fold_in(key, 109), (3, 3, D), scale, 6.0 * scale).astype(jnp.bfloat16)


def draw_counts(key, part):
    key_one = jax.random.fold_in(key, 11)
    key_two = jax.random.fold_in(key, 23)
    key_three = jax.random.fold_in(key, 37)
    first_draw = jax.random.randint(key_one, (N_WIDE,), 1, LAT_DEV + 1)
    second_draw = jax.random.randint(key_two, (N_WIDE,), 1, LAT_DEV + 1)
    smaller = jnp.minimum(first_draw, second_draw)
    busiest = jax.random.randint(key_three, (), 0, N_WIDE)
    return jnp.where(jnp.arange(N_WIDE) == busiest, LAT_DEV, smaller).astype(jnp.int32)


def steps_of(own_key, shape, shards, smallest, high):
    factor_of, own = 1.0, jax.random.fold_in(own_key, 6)
    for axis_at, shards_of in shards:
        draws = jnp.exp(jax.random.uniform(jax.random.fold_in(own, axis_at), (shards_of,), jnp.float32, smallest / len(shards), high / len(shards)))
        factor_of = factor_of * jnp.repeat(draws, shape[axis_at] // shards_of).reshape([-1 if axis == axis_at else 1 for axis in range(len(shape))])
    return factor_of


def bell_draw(stream_key, shape, spread, limit, shards=(), kind=jnp.bfloat16):
    values = jax.random.normal(stream_key, shape, jnp.float32) * spread
    if len(shards) > 0:
        values = steps_of(stream_key, shape, shards, -0.22, 0.18) * values
    return jnp.clip(values, min=-limit, max=limit).astype(kind)


def setup_inputs(seed: int = 0) -> dict:
    key_of = jax.random.split(jax.random.key(seed), 12)
    tokens = draw_tokens(jax.random.fold_in(key_of[11], 71), 0)
    condition = draw_condition(jax.random.fold_in(key_of[11], 71), 0)
    cotangent = bell_draw(key_of[2], (LATENTS, TOKENS_LAT, D), 1.0, 6.0, ((0, 8), (1, 4)))
    counts = draw_counts(jax.random.fold_in(key_of[11], 71), 0)
    w_ada = bell_draw(key_of[4], (D, 6 * D), D ** -0.5, 0.21875)
    k_attn = draw_k_attn(jax.random.fold_in(key_of[11], 71), 0)
    w_qkv = bell_draw(key_of[6], (D, 3, D), D ** -0.5, 0.21875, ((2, 4),))
    w_out = bell_draw(key_of[7], (D, D), (D // 64) ** -0.5, 1.75, ((0, 4),))
    w_up = bell_draw(key_of[8], (D, FF), D ** -0.5, 0.21875, ((1, 4),))
    k_ffn = bell_draw(key_of[9], (3, 3, FF), 9 ** -0.5, 2.0, ((2, 4),))
    w_down = bell_draw(key_of[10], (FF, D), FF ** -0.5, 0.109375, ((0, 4),))
    return dict(tokens=tokens, condition=condition, cotangent=cotangent, counts=counts, w_ada=w_ada, k_attn=k_attn, w_qkv=w_qkv, w_out=w_out, w_up=w_up, k_ffn=k_ffn, w_down=w_down)


HIGHEST_PREC = lax.Precision.HIGHEST

@jax.custom_vjp
def low(v):
    return lax.optimization_barrier(v.astype(jnp.bfloat16)).astype(jnp.float32)

@jax.custom_vjp
def low_back(v):
    return v

def low_keep(v):
    return (low(v), None)

def low_pass(kept, grad):
    return (grad,)

def back_keep(v):
    return (v, None)

def back_low(kept, grad):
    return (low(grad),)
low.defvjp(low_keep, low_pass)
low_back.defvjp(back_keep, back_low)

def layer_norm(values_in):
    mean_val = lax.optimization_barrier(jnp.mean(values_in, axis=-1, keepdims=True))
    centred = values_in - mean_val
    return centred * lax.rsqrt(lax.optimization_barrier(jnp.mean(centred * centred, axis=-1, keepdims=True)) + 1e-06)

def conv_grid(values_in, kernel):
    channels = values_in.shape[-1]
    shaped = values_in.reshape(SIDE, SIDE, channels)
    padded = jnp.pad(shaped, ((1, 1), (1, 1), (0, 0)))
    summed_taps = jnp.zeros_like(shaped)
    for tap_row in range(3):
        for tap_col in range(3):
            summed_taps = summed_taps + kernel[tap_row, tap_col] * padded[tap_row:tap_row + SIDE, tap_col:tap_col + SIDE]
    return summed_taps.reshape(SIDE * SIDE, channels)

def to_groups(matrix):
    channels = matrix.shape[-1]
    blocks_five = matrix.reshape(SIDE // 2, 2, SIDE // 2, 2, channels)
    return blocks_five.transpose(1, 3, 0, 2, 4).reshape(4, SIDE * SIDE // 4, channels)

def from_groups(groups):
    channels = groups.shape[-1]
    blocks_five = groups.reshape(2, 2, SIDE // 2, SIDE // 2, channels)
    return blocks_five.transpose(2, 0, 3, 1, 4).reshape(SIDE * SIDE, channels)

def latent_forward(params, latent, condition_row):
    w_ada, k_attn, w_qkv, w_out, w_up, k_ffn, w_down = params
    modulation = low_back(jnp.dot(low(jax.nn.silu(condition_row)), w_ada, precision=HIGHEST_PREC))
    shift_one, scale_one, gate_one, shift_two, scale_two, gate_two = jnp.split(modulation, 6)
    h_one = low(layer_norm(latent) * (1.0 + scale_one) + shift_one)
    mixed_in = low(conv_grid(h_one, k_attn))
    projected = low_back(low(jnp.einsum('sd,dte->tse', mixed_in, w_qkv, precision=HIGHEST_PREC)))
    grouped = jax.vmap(to_groups)(projected).reshape(3, 4, TOKENS_LAT // 4, HEADS, HEAD_DIM)
    scores = low_back(jnp.einsum('pqhe,pkhe->phqk', grouped[0], grouped[1], precision=HIGHEST_PREC) * HEAD_DIM ** (-0.5))
    probs_f = jax.nn.softmax(scores, axis=-1)
    context = jnp.einsum('phqk,pkhe->pqhe', low(probs_f), grouped[2], precision=HIGHEST_PREC)
    context = low_back(low(from_groups(context.reshape(4, TOKENS_LAT // 4, D))))
    attended = low_back(jnp.dot(context, w_out, precision=HIGHEST_PREC))
    after_mix = latent + gate_one * attended
    h_two = low(layer_norm(after_mix) * (1.0 + scale_two) + shift_two)
    hidden = low_back(jnp.dot(h_two, w_up, precision=HIGHEST_PREC))
    activated = low(jax.nn.gelu(conv_grid(hidden, k_ffn), approximate=True))
    branch = low_back(jnp.dot(activated, w_down, precision=HIGHEST_PREC))
    return after_mix + gate_two * branch

def reference(tokens, condition, cotangent, counts, w_ada, k_attn, w_qkv, w_out, w_up, k_ffn, w_down):
    params = tuple((weight_arr.astype(jnp.float32) for weight_arr in (w_ada, k_attn, w_qkv, w_out, w_up, k_ffn, w_down)))
    slot_ids = jnp.arange(LATENTS, dtype=jnp.int32)
    live_mask = (slot_ids % LAT_DEV < counts[slot_ids // LAT_DEV]).astype(jnp.float32)

    def process(grad_state, slot_item):
        latent, condition_row, cot_row, live_one = slot_item
        result, pull_back = jax.vjp(latent_forward, params, latent.astype(jnp.float32), condition_row.astype(jnp.float32))
        grad_parts, grad_latent, grad_cond = pull_back(cot_row.astype(jnp.float32) * live_one)
        grad_state = jax.tree.map(jnp.add, grad_state, grad_parts)
        return (grad_state, ((result * live_one).astype(jnp.bfloat16), grad_latent, grad_cond))
    zero_grads = jax.tree.map(jnp.zeros_like, params)
    grad_sums, outputs = lax.scan(process, zero_grads, (tokens, condition, cotangent, live_mask))
    return (outputs[0], outputs[1], outputs[2], grad_sums[0], grad_sums[1], grad_sums[2], grad_sums[3], grad_sums[4], grad_sums[5], grad_sums[6])
```

```python
from functools import partial

import jax
import jax.numpy as jnp
from jax import lax
from jax.experimental import pallas as pl
from jax.experimental.pallas import tpu as pltpu
from jax.sharding import PartitionSpec as P

HEAD_DIM = 64
SIDE = 32
HALF = SIDE // 2
PHASE = HALF * HALF
PAD = PHASE + 2 * HALF
LANES = 128
ROWS = 64
CHUNK = 256
LOG2E = 1.4426950408889634
GELU_C = 0.7978845608028654
GELU_A = 0.044715
MIB = 1 << 20
F32 = jnp.float32
BF16 = jnp.bfloat16

NN = (((1,), (0,)), ((), ()))
NT = (((1,), (1,)), ((), ()))
TN = (((0,), (0,)), ((), ()))


def mm(left, right, dims):
    return lax.dot_general(left, right, dims, preferred_element_type=F32)


def ds(start, size, unit=None):
    return pl.ds(pl.multiple_of(start, unit or size), size)


def tap_source(parity, tap):
    return {-1: (1, -1), 0: (0, 0), 1: (1, 0), 2: (0, 1)}[parity + tap - 1]


def shift_cols(base, shifted, lanes):
    col = lax.broadcasted_iota(jnp.int32, (ROWS, LANES), 0) % HALF

    def rows_step(step, carry):
        for group in range(4):
            rows = ds(HALF + step * ROWS, ROWS, HALF)
            value = base[group, rows, lanes]
            if group % 2:
                moved = jnp.where(col == 0, 0.0, pltpu.roll(value, 1, 0))
            else:
                moved = jnp.where(col == HALF - 1, 0.0, pltpu.roll(value, ROWS - 1, 0))
            shifted[group, rows, lanes] = moved
        return carry

    lax.fori_loop(0, PHASE // ROWS, rows_step, 0)


def clear_edges(ref):
    edge = jnp.zeros((HALF, ref.shape[-1]), ref.dtype)
    for group in range(4):
        ref[group, :HALF, :] = edge
        ref[group, PAD - HALF :, :] = edge


def tap_value(base, shifted, group, tap_row, tap_col, start, lanes):
    src_row, row_move = tap_source(group // 2, tap_row)
    src_col, col_move = tap_source(group % 2, tap_col)
    ref = base if col_move == 0 else shifted
    return ref[2 * src_row + src_col, ds(HALF + row_move * HALF + start, ROWS, HALF), lanes]


def normed(values_in):
    mean_val = jnp.mean(values_in, axis=-1, keepdims=True)
    centred = values_in - mean_val
    inv = lax.rsqrt(jnp.mean(centred * centred, axis=-1, keepdims=True) + 1e-06)
    return centred * inv, inv


def norm_back(unit, inv, grad):
    mean_grad = jnp.mean(grad, axis=-1, keepdims=True)
    mean_dot = jnp.mean(grad * unit, axis=-1, keepdims=True)
    return (grad - mean_grad - unit * mean_dot) * inv


def attn_forward_kernel(
    live_ref, x_ref, cot_ref, mod_ref, taps_ref, wqkv_ref, wout_ref,
    u_ref, qkv_ref, probs_ref, ctx_ref, att_ref, x1_ref, h2_ref, h2t_ref, db_ref,
    base, shifted,
):
    width = x_ref.shape[1]
    rows_all = x_ref.shape[0]
    shift_one, scale_one, gate_one = mod_ref[0:1, :], mod_ref[1:2, :], mod_ref[2:3, :]
    shift_two, scale_two, gate_two = mod_ref[3:4, :], mod_ref[4:5, :], mod_ref[5:6, :]
    clear_edges(base)
    clear_edges(shifted)

    def norm_step(step, carry):
        group, part = step // (PHASE // ROWS), step % (PHASE // ROWS)
        unit, _ = normed(x_ref[ds(step * ROWS, ROWS), :].astype(F32))
        h_one = (unit * (1.0 + scale_one) + shift_one).astype(BF16)
        base[group, ds(HALF + part * ROWS, ROWS, HALF), :] = h_one.astype(F32)
        return carry

    lax.fori_loop(0, rows_all // ROWS, norm_step, 0)

    def conv_step(block, carry):
        lanes = ds(block * LANES, LANES)
        shift_cols(base, shifted, lanes)
        taps = [taps_ref[t : t + 1, lanes] for t in range(9)]

        def rows_step(step, carry):
            for group in range(4):
                total = jnp.zeros((ROWS, LANES), F32)
                for tap in range(9):
                    total += taps[tap] * tap_value(
                        base, shifted, group, tap // 3, tap % 3, step * ROWS, lanes
                    )
                u_ref[ds(group * PHASE + step * ROWS, ROWS), lanes] = total.astype(BF16)
            return carry

        return lax.fori_loop(0, PHASE // ROWS, rows_step, carry)

    lax.fori_loop(0, width // LANES, conv_step, 0)

    def project_step(step, carry):
        rows = ds(step * PHASE, PHASE)
        for part in range(3):
            cols = slice(part * width, (part + 1) * width)
            qkv_ref[rows, cols] = mm(u_ref[rows, :], wqkv_ref[:, cols], NT).astype(BF16)
        return carry

    lax.fori_loop(0, 4, project_step, 0)

    pairs = width // LANES
    first = lax.broadcasted_iota(jnp.int32, (PHASE, LANES), 1) < HEAD_DIM
    zero = jnp.zeros((PHASE, LANES), BF16)

    def attend_step(step, carry):
        group, pair = step // pairs, step % pairs
        rows = ds(group * PHASE, PHASE)
        query = qkv_ref[rows, ds(pair * LANES, LANES)]
        key = qkv_ref[rows, ds(width + pair * LANES, LANES)]
        value = qkv_ref[rows, ds(2 * width + pair * LANES, LANES)]
        found = []
        for head in range(2):
            own = jnp.where(first, query, zero) if head == 0 else jnp.where(first, zero, query)
            scores = mm(key, own, NT)
            top = jnp.max(scores, axis=0, keepdims=True)
            raised = jnp.exp2((scores - top) * (LOG2E * HEAD_DIM**-0.5))
            probs = (raised * (1.0 / jnp.sum(raised, axis=0, keepdims=True))).astype(BF16)
            probs_ref[step, :, head * PHASE : (head + 1) * PHASE] = probs
            found.append(mm(probs, value, TN))
        ctx_ref[rows, ds(pair * LANES, LANES)] = jnp.where(first, found[0], found[1]).astype(BF16)
        return carry

    lax.fori_loop(0, 4 * pairs, attend_step, 0)

    def out_step(step, carry):
        rows = ds(step * PHASE, PHASE)
        att_ref[rows, :] = mm(ctx_ref[rows, :], wout_ref[...], NN)
        return carry

    lax.fori_loop(0, 4, out_step, 0)
    live = live_ref[0, 0]

    def second_step(step, carry):
        rows = ds(step * ROWS, ROWS)
        after = x_ref[rows, :].astype(F32) + gate_one * att_ref[rows, :]
        x1_ref[rows, :] = after
        unit, _ = normed(after)
        h2_ref[rows, :] = (unit * (1.0 + scale_two) + shift_two).astype(BF16)
        db_ref[rows, :] = (cot_ref[rows, :].astype(F32) * live * gate_two).astype(BF16)
        return carry

    lax.fori_loop(0, rows_all // ROWS, second_step, 0)
    for part in range(4):
        h2t_ref[:, part * PHASE : (part + 1) * PHASE] = h2_ref[
            part * PHASE : (part + 1) * PHASE, :
        ].T


def whole(memory=pltpu.VMEM):
    return pl.BlockSpec(memory_space=memory)


def attn_forward(live, x, cot, mod, taps, wqkv, wout):
    rows, width = x.shape
    steps = 4 * (width // LANES)
    shape = jax.ShapeDtypeStruct
    return pl.pallas_call(
        attn_forward_kernel,
        out_shape=(
            shape((rows, width), BF16),
            shape((rows, 3 * width), BF16),
            shape((steps, PHASE, 2 * PHASE), BF16),
            shape((rows, width), BF16),
            shape((rows, width), F32),
            shape((rows, width), F32),
            shape((rows, width), BF16),
            shape((width, rows), BF16),
            shape((rows, width), BF16),
        ),
        in_specs=[whole(pltpu.SMEM)] + [whole()] * 6,
        out_specs=(whole(),) * 9,
        scratch_shapes=[pltpu.VMEM((4, PAD, width), F32), pltpu.VMEM((4, PAD, width), F32)],
        compiler_params=pltpu.CompilerParams(vmem_limit_bytes=56 * MIB),
        name="attn_forward",
    )(live, x, cot, mod, taps, wqkv, wout)


def ffn_kernel(
    h2_ref, h2t_ref, db_ref, wup_ref, wdown_ref, taps_ref,
    branch_ref, dh2_ref, dwup_ref, dwdown_ref, dtaps_ref,
    hid, hid_moved, grad, grad_moved, slope, act, dhid,
):
    rows_all = h2_ref.shape[0]

    @pl.when(pl.program_id(0) == 0)
    def _():
        for ref in (hid, hid_moved, grad, grad_moved):
            clear_edges(ref)
        branch_ref[...] = jnp.zeros_like(branch_ref)
        dh2_ref[...] = jnp.zeros_like(dh2_ref)

    def up_step(group, carry):
        rows = ds(group * PHASE, PHASE)
        hid[group, HALF : HALF + PHASE, :] = mm(h2_ref[rows, :], wup_ref[0], NN)
        return carry

    lax.fori_loop(0, 4, up_step, 0)

    for block in range(CHUNK // LANES):
        lanes = slice(block * LANES, (block + 1) * LANES)
        shift_cols(hid, hid_moved, lanes)
        taps = [taps_ref[0, t : t + 1, lanes] for t in range(9)]

        def act_step(step, carry):
            for group in range(4):
                total = jnp.zeros((ROWS, LANES), F32)
                for tap in range(9):
                    total += taps[tap] * tap_value(
                        hid, hid_moved, group, tap // 3, tap % 3, step * ROWS, lanes
                    )
                square = total * total
                turn = jnp.tanh(total * (square * (GELU_C * GELU_A) + GELU_C))
                half = 0.5 * turn + 0.5
                bend = total * (half - half * half)
                rows = ds(group * PHASE + step * ROWS, ROWS)
                act[rows, lanes] = (total * half).astype(BF16)
                slope[rows, lanes] = half + bend * (
                    square * (6.0 * GELU_C * GELU_A) + 2.0 * GELU_C
                )
            return carry

        lax.fori_loop(0, PHASE // ROWS, act_step, 0)

    def dact_step(group, carry):
        rows = ds(group * PHASE, PHASE)
        dact = mm(db_ref[rows, :], wdown_ref[0], NT)
        grad[group, HALF : HALF + PHASE, :] = dact * slope[rows, :]
        return carry

    lax.fori_loop(0, 4, dact_step, 0)

    for block in range(CHUNK // LANES):
        lanes = slice(block * LANES, (block + 1) * LANES)
        shift_cols(grad, grad_moved, lanes)
        conv_back(grad, grad_moved, hid, lanes, [taps_ref[0, t : t + 1, lanes] for t in range(9)],
                  dtaps_ref.at[0], dhid)

    def final_step(group, carry):
        rows = ds(group * PHASE, PHASE)
        branch_ref[rows, :] += mm(act[rows, :], wdown_ref[0], NN)
        dh2_ref[rows, :] += mm(dhid[rows, :], wup_ref[0], NT)
        return carry

    lax.fori_loop(0, 4, final_step, 0)
    dwup_ref[0] = mm(h2t_ref[...], dhid[...], NN).astype(BF16)
    dwdown_ref[0] = mm(act[...], db_ref[...], TN).astype(BF16)


def conv_back(grad, grad_moved, source, lanes, taps, dtaps_ref, out_ref):
    def rows_step(step, sums):
        sums = list(sums)
        for group in range(4):
            total = jnp.zeros((ROWS, LANES), F32)
            own = source[group, ds(HALF + step * ROWS, ROWS, HALF), lanes]
            for tap in range(9):
                moved = tap_value(
                    grad, grad_moved, group, 2 - tap // 3, 2 - tap % 3, step * ROWS, lanes
                )
                total += taps[tap] * moved
                sums[tap] += (own * moved).reshape(ROWS // 8, 8, LANES).sum(axis=0)
            out_ref[ds(group * PHASE + step * ROWS, ROWS), lanes] = total.astype(out_ref.dtype)
        return tuple(sums)

    start = tuple(jnp.zeros((8, LANES), F32) for _ in range(9))
    sums = lax.fori_loop(0, PHASE // ROWS, rows_step, start)
    for tap in range(9):
        dtaps_ref[tap : tap + 1, lanes] = jnp.sum(sums[tap], axis=0, keepdims=True)


def ffn(h2, h2t, db, wup, wdown, taps):
    rows, width = h2.shape
    shards, _, local = wup.shape
    per = local // CHUNK
    shape = jax.ShapeDtypeStruct
    keep = lambda *block: pl.BlockSpec(block, lambda c: (0,) * len(block))
    return pl.pallas_call(
        ffn_kernel,
        grid=(shards * per,),
        out_shape=(
            shape((rows, width), F32),
            shape((rows, width), F32),
            shape(wup.shape, BF16),
            shape(wdown.shape, BF16),
            shape(taps.shape, F32),
        ),
        in_specs=[
            keep(rows, width),
            keep(width, rows),
            keep(rows, width),
            pl.BlockSpec((1, width, CHUNK), lambda c: (c // per, 0, c % per)),
            pl.BlockSpec((1, CHUNK, width), lambda c: (c // per, c % per, 0)),
            pl.BlockSpec((1, 9, CHUNK), lambda c: (c // per, 0, c % per)),
        ],
        out_specs=(
            keep(rows, width),
            keep(rows, width),
            pl.BlockSpec((1, width, CHUNK), lambda c: (c // per, 0, c % per)),
            pl.BlockSpec((1, CHUNK, width), lambda c: (c // per, c % per, 0)),
            pl.BlockSpec((1, 9, CHUNK), lambda c: (c // per, 0, c % per)),
        ),
        scratch_shapes=[pltpu.VMEM((4, PAD, CHUNK), F32)] * 4
        + [pltpu.VMEM((rows, CHUNK), F32)]
        + [pltpu.VMEM((rows, CHUNK), BF16)] * 2,
        compiler_params=pltpu.CompilerParams(vmem_limit_bytes=56 * MIB),
        name="feed_forward",
    )(h2, h2t, db, wup, wdown, taps)


def mid_kernel(
    live_ref, x1_ref, cot_ref, branch_ref, dh2_ref, att_ref, ctx_ref, mod_ref, wout_ref,
    block_ref, dx1_ref, dctx_ref, dwout_ref, dmod_ref,
    datt,
):
    rows_all, width = x1_ref.shape
    gate_one, scale_two, gate_two = mod_ref[2:3, :], mod_ref[4:5, :], mod_ref[5:6, :]
    live = live_ref[0, 0]

    def fold(value):
        return value.reshape(ROWS // 8, 8, width).sum(axis=0)

    def rows_step(step, sums):
        rows = ds(step * ROWS, ROWS)
        after = x1_ref[rows, :]
        dout = cot_ref[rows, :].astype(F32) * live
        branch = branch_ref[rows, :]
        block_ref[rows, :] = ((after + gate_two * branch) * live).astype(BF16)
        unit, inv = normed(after)
        dh2 = dh2_ref[rows, :]
        dx1 = dout + norm_back(unit, inv, dh2 * (1.0 + scale_two))
        dx1_ref[rows, :] = dx1
        datt[rows, :] = (dx1 * gate_one).astype(BF16)
        found = (dx1 * att_ref[rows, :], dh2, dh2 * unit, dout * branch)
        return tuple(total + fold(one) for total, one in zip(sums, found))

    start = tuple(jnp.zeros((8, width), F32) for _ in range(4))
    sums = lax.fori_loop(0, rows_all // ROWS, rows_step, start)
    for at in range(4):
        dmod_ref[at : at + 1, :] = jnp.sum(sums[at], axis=0, keepdims=True)

    def ctx_step(step, carry):
        rows = ds(step * PHASE, PHASE)
        dctx_ref[rows, :] = mm(datt[rows, :], wout_ref[...], NT).astype(BF16)
        return carry

    lax.fori_loop(0, 4, ctx_step, 0)
    for part in range(3):
        cols = slice(part * PHASE, (part + 1) * PHASE)
        dwout_ref[cols, :] = mm(ctx_ref[:, cols], datt[...], TN).astype(BF16)


def mid(live, x1, cot, branch, dh2, att, ctx, mod, wout):
    rows, width = x1.shape
    shape = jax.ShapeDtypeStruct
    return pl.pallas_call(
        mid_kernel,
        out_shape=(
            shape((rows, width), BF16),
            shape((rows, width), F32),
            shape((rows, width), BF16),
            shape(wout.shape, BF16),
            shape((4, width), F32),
        ),
        in_specs=[whole(pltpu.SMEM)] + [whole()] * 8,
        out_specs=(whole(),) * 5,
        scratch_shapes=[pltpu.VMEM((rows, width), BF16)],
        compiler_params=pltpu.CompilerParams(vmem_limit_bytes=56 * MIB),
        name="residual_backward",
    )(live, x1, cot, branch, dh2, att, ctx, mod, wout)


def attn_backward_kernel(
    u_ref, qkv_ref, probs_ref, dctx_ref, dqkv_ref, dw_ref
):
    rows_all, width = u_ref.shape
    pairs = width // LANES
    first = lax.broadcasted_iota(jnp.int32, (PHASE, LANES), 1) < HEAD_DIM
    zero = jnp.zeros((PHASE, LANES), BF16)
    scale = HEAD_DIM**-0.5

    def attend_step(step, carry):
        group, pair = step // pairs, step % pairs
        rows = ds(group * PHASE, PHASE)
        query = qkv_ref[rows, ds(pair * LANES, LANES)]
        key = qkv_ref[rows, ds(width + pair * LANES, LANES)]
        value = qkv_ref[rows, ds(2 * width + pair * LANES, LANES)]
        dctx = dctx_ref[rows, ds(pair * LANES, LANES)]
        dq, dk, dv = [], None, None
        for head in range(2):
            own = lambda full: jnp.where(first, full, zero) if head == 0 else jnp.where(first, zero, full)
            probs = probs_ref[step, :, head * PHASE : (head + 1) * PHASE]
            probs_f = probs.astype(F32)
            dctx_own, query_own = own(dctx), own(query)
            dprobs = mm(value, dctx_own, NT)
            inner = jnp.sum(dprobs * probs_f, axis=0, keepdims=True)
            dscores = (probs_f * (dprobs - inner)).astype(BF16)
            dv_one = mm(probs, dctx_own, NN)
            dk_one = mm(dscores, query_own, NN)
            dv = dv_one if dv is None else dv + dv_one
            dk = dk_one if dk is None else dk + dk_one
            dq.append(mm(dscores, key, TN))
        dqkv_ref[rows, ds(pair * LANES, LANES)] = (
            jnp.where(first, dq[0], dq[1]) * scale
        ).astype(BF16)
        dqkv_ref[rows, ds(width + pair * LANES, LANES)] = (dk * scale).astype(BF16)
        dqkv_ref[rows, ds(2 * width + pair * LANES, LANES)] = dv.astype(BF16)
        return carry

    lax.fori_loop(0, 4 * pairs, attend_step, 0)
    for part in range(3):
        cols = slice(part * width, (part + 1) * width)

        def weight_step(block, carry, cols=cols, part=part):
            out_rows = ds(block * PHASE, PHASE)
            left = dqkv_ref[:, ds(part * width + block * PHASE, PHASE)]
            dw_ref[out_rows, cols] = mm(left, u_ref[...], TN).astype(BF16)
            return carry

        lax.fori_loop(0, width // PHASE, weight_step, 0)


def attn_backward(u, qkv, probs, dctx):
    rows, width = u.shape
    shape = jax.ShapeDtypeStruct
    return pl.pallas_call(
        attn_backward_kernel,
        out_shape=(shape((rows, 3 * width), BF16), shape((width, 3 * width), BF16)),
        in_specs=[whole()] * 4,
        out_specs=(whole(),) * 2,
        compiler_params=pltpu.CompilerParams(vmem_limit_bytes=56 * MIB),
        name="attn_backward",
    )(u, qkv, probs, dctx)


def input_backward_kernel(
    x_ref, dx1_ref, dqkv_ref, mod_ref, taps_ref, wqkv_ref,
    dx_ref, dmod_ref, dtaps_ref,
    base, shifted, first_in, dh1,
):
    rows_all, width = x_ref.shape
    shift_one, scale_one = mod_ref[0:1, :], mod_ref[1:2, :]
    clear_edges(base)
    clear_edges(shifted)

    def norm_step(step, carry):
        group, part = step // (PHASE // ROWS), step % (PHASE // ROWS)
        unit, _ = normed(x_ref[ds(step * ROWS, ROWS), :].astype(F32))
        h_one = (unit * (1.0 + scale_one) + shift_one).astype(BF16)
        first_in[group, ds(HALF + part * ROWS, ROWS, HALF), :] = h_one.astype(F32)
        return carry

    lax.fori_loop(0, rows_all // ROWS, norm_step, 0)

    def du_step(group, carry):
        rows = ds(group * PHASE, PHASE)
        total = None
        for part in range(3):
            cols = slice(part * width, (part + 1) * width)
            one = mm(dqkv_ref[rows, cols], wqkv_ref[:, cols], NN)
            total = one if total is None else total + one
        base[group, HALF : HALF + PHASE, :] = total
        return carry

    lax.fori_loop(0, 4, du_step, 0)

    def conv_step(block, carry):
        lanes = ds(block * LANES, LANES)
        shift_cols(base, shifted, lanes)
        conv_back(base, shifted, first_in, lanes, [taps_ref[t : t + 1, lanes] for t in range(9)],
                  dtaps_ref, dh1)
        return carry

    lax.fori_loop(0, width // LANES, conv_step, 0)

    def fold(value):
        return value.reshape(ROWS // 8, 8, width).sum(axis=0)

    def rows_step(step, sums):
        rows = ds(step * ROWS, ROWS)
        unit, inv = normed(x_ref[rows, :].astype(F32))
        grad = dh1[rows, :]
        dx = dx1_ref[rows, :] + norm_back(unit, inv, grad * (1.0 + scale_one))
        dx_ref[rows, :] = dx.astype(BF16)
        return tuple(total + fold(one) for total, one in zip(sums, (grad, grad * unit)))

    start = tuple(jnp.zeros((8, width), F32) for _ in range(2))
    sums = lax.fori_loop(0, rows_all // ROWS, rows_step, start)
    for at in range(2):
        dmod_ref[at : at + 1, :] = jnp.sum(sums[at], axis=0, keepdims=True)


def input_backward(x, dx1, dqkv, mod, taps, wqkv):
    rows, width = x.shape
    shape = jax.ShapeDtypeStruct
    return pl.pallas_call(
        input_backward_kernel,
        out_shape=(shape((rows, width), BF16), shape((2, width), F32), shape((9, width), F32)),
        in_specs=[whole()] * 6,
        out_specs=(whole(),) * 3,
        scratch_shapes=[pltpu.VMEM((4, PAD, width), F32)] * 3 + [pltpu.VMEM((rows, width), F32)],
        compiler_params=pltpu.CompilerParams(vmem_limit_bytes=56 * MIB),
        name="input_backward",
    )(x, dx1, dqkv, mod, taps, wqkv)


def to_groups(shard):
    latents, rows, width = shard.shape
    split = shard.reshape(latents, rows // (2 * SIDE), 2, HALF, 2, width)
    return split.transpose(0, 2, 4, 1, 3, 5).reshape(latents, 4, rows // 4, width)


def from_groups(groups):
    latents, _, rows, width = groups.shape
    split = groups.reshape(latents, 2, 2, rows // HALF, HALF, width)
    return split.transpose(0, 3, 1, 4, 2, 5).reshape(latents, 4 * rows, width)


def per_device(
    tokens, condition, cotangent, counts, w_ada, k_attn, w_qkv, w_out, w_up, k_ffn, w_down
):
    lat_dev, shard_rows, width = tokens.shape
    here = lax.axis_index("narrow")
    rows_all = shard_rows * lat_dev
    local = w_up.shape[1]
    gather = partial(lax.all_gather, axis_name="narrow")

    def latent_in(shard):
        return lax.all_to_all(to_groups(shard), "narrow", 0, 2, tiled=True).reshape(rows_all, width)

    def latent_out(latent):
        parts = latent.reshape(1, 4, rows_all // 4, width)
        return from_groups(lax.all_to_all(parts, "narrow", 2, 0, tiled=True))

    x = latent_in(tokens)
    cot = latent_in(cotangent)
    qkv_t = w_qkv.transpose(2, 1, 0).reshape(w_qkv.shape[2], 3 * width)
    wqkv = gather(qkv_t, tiled=True)
    wout = gather(w_out, tiled=True)
    wup = gather(w_up)
    wdown = gather(w_down)
    ffn_taps = gather(k_ffn.reshape(9, local)).astype(F32)
    attn_taps = k_attn.reshape(9, width).astype(F32)

    cond_f = condition.astype(F32)
    silu_low = jax.nn.silu(cond_f).astype(BF16)
    own_silu = lax.dynamic_slice_in_dim(silu_low, here, 1, 0)
    mod = mm(own_silu, w_ada, NN).reshape(6, width)
    live = (here < counts[0]).astype(F32).reshape(1, 1)

    u, qkv, probs, ctx, att, x1, h2, h2t, db = attn_forward(
        live, x, cot, mod, attn_taps, wqkv, wout
    )
    branch, dh2, dwup, dwdown, dffn_taps = ffn(h2, h2t, db, wup, wdown, ffn_taps)
    block_g, dx1, dctx, dwout, dmod_mid = mid(live, x1, cot, branch, dh2, att, ctx, mod, wout)
    dqkv, dwqkv = attn_backward(u, qkv, probs, dctx)
    dx, dmod_first, dattn_taps = input_backward(x, dx1, dqkv, mod, attn_taps, wqkv)

    block = latent_out(block_g)
    grad_tokens = latent_out(dx).astype(F32)

    def reduce(parts):
        return lax.psum(lax.psum_scatter(parts, "narrow", scatter_dimension=0, tiled=True), "wide")

    shared = jnp.concatenate(
        [dwup, dwdown, jnp.pad(dffn_taps, ((0, 0), (0, 7), (0, 0))).astype(BF16)], axis=1
    ).reshape(lat_dev * (2 * width + 16), local)
    late = jnp.concatenate(
        [dwout.reshape(lat_dev, -1, width), dwqkv.reshape(lat_dev, -1, width)], axis=1
    ).reshape(-1, width)
    shared = reduce(shared).astype(F32)
    late = reduce(late).astype(F32)
    grad_w_up, grad_w_down = shared[:width], shared[width : 2 * width]
    grad_k_ffn = shared[2 * width : 2 * width + 9].reshape(3, 3, local)
    heads_width = w_out.shape[0]
    grad_w_out = late[:heads_width]
    grad_w_qkv = late[heads_width:].reshape(heads_width, 3, width).transpose(2, 1, 0)

    dmod = jnp.concatenate([dmod_first, dmod_mid], axis=0)
    small = jnp.concatenate([dmod, dattn_taps, jnp.zeros((1, width), F32)], axis=0).astype(BF16)
    small_all = lax.all_gather(small, ("wide", "narrow"))
    silu_all = lax.all_gather(silu_low, "wide", tiled=True)
    mod_all = small_all[:, :6].reshape(-1, 6 * width)
    grad_k_attn = small_all[:, 6:15].astype(F32).sum(axis=0).reshape(3, 3, width)
    grad_w_ada = mm(silu_all, mod_all, TN)
    mod_low = lax.dynamic_slice_in_dim(mod_all, lax.axis_index("wide") * lat_dev, lat_dev, 0)
    grad_silu = mm(mod_low, w_ada, NT)
    _, pull_silu = jax.vjp(jax.nn.silu, cond_f)
    (grad_condition,) = pull_silu(grad_silu)
    return (
        block,
        grad_tokens,
        grad_condition,
        grad_w_ada,
        grad_k_attn,
        grad_w_qkv,
        grad_w_out,
        grad_w_up,
        grad_k_ffn,
        grad_w_down,
    )


def solution(mesh):
    placed = (
        P("wide", "narrow", None),
        P("wide", None),
        P("wide", "narrow", None),
        P("wide"),
        P(),
        P(),
        P(None, None, "narrow"),
        P("narrow", None),
        P(None, "narrow"),
        P(None, None, "narrow"),
        P("narrow", None),
    )
    return jax.shard_map(
        per_device,
        mesh=mesh,
        in_specs=placed,
        out_specs=(
            P("wide", "narrow", None),
            P("wide", "narrow", None),
            P("wide", None),
            P(),
            P(),
            P(None, None, "narrow"),
            P("narrow", None),
            P(None, "narrow"),
            P(None, None, "narrow"),
            P("narrow", None),
        ),
        check_vma=False,
    )
```

```python
import jax
import jax.numpy as jnp
from jax import lax
from jax.experimental import pallas as pl
from jax.experimental.pallas import tpu as pltpu
from jax.sharding import PartitionSpec as P

HEAD_DIM = 64
SIDE = 32
HALF = SIDE // 2
PHASE = HALF * HALF
PAD = PHASE + 2 * HALF
LANES = 128
ROWS = 64
CHUNK = 256
LOG2E = 1.4426950408889634
GELU_C = 0.7978845608028654
GELU_A = 0.044715
MIB = 1 << 20
F32 = jnp.float32
BF16 = jnp.bfloat16

NN = (((1,), (0,)), ((), ()))
NT = (((1,), (1,)), ((), ()))
TN = (((0,), (0,)), ((), ()))


def mm(left, right, dims):
    return lax.dot_general(left, right, dims, preferred_element_type=F32)


def ds(start, size, unit=None):
    return pl.ds(pl.multiple_of(start, unit or size), size)


def tap_source(parity, tap):
    return {-1: (1, -1), 0: (0, 0), 1: (1, 0), 2: (0, 1)}[parity + tap - 1]


def shift_cols(base, shifted, lanes):
    col = lax.broadcasted_iota(jnp.int32, (ROWS, LANES), 0) % HALF

    def rows_step(step, carry):
        for group in range(4):
            rows = ds(HALF + step * ROWS, ROWS, HALF)
            value = base[group, rows, lanes]
            if group % 2:
                moved = jnp.where(col == 0, 0.0, pltpu.roll(value, 1, 0))
            else:
                moved = jnp.where(col == HALF - 1, 0.0, pltpu.roll(value, ROWS - 1, 0))
            shifted[group, rows, lanes] = moved
        return carry

    lax.fori_loop(0, PHASE // ROWS, rows_step, 0)


def clear_edges(ref):
    edge = jnp.zeros((HALF, ref.shape[-1]), ref.dtype)
    for group in range(4):
        ref[group, :HALF, :] = edge
        ref[group, PAD - HALF :, :] = edge


def tap_value(base, shifted, group, tap_row, tap_col, start, lanes):
    src_row, row_move = tap_source(group // 2, tap_row)
    src_col, col_move = tap_source(group % 2, tap_col)
    ref = base if col_move == 0 else shifted
    return ref[2 * src_row + src_col, ds(HALF + row_move * HALF + start, ROWS, HALF), lanes]


def normed(values_in):
    mean_val = jnp.mean(values_in, axis=-1, keepdims=True)
    centred = values_in - mean_val
    inv = lax.rsqrt(jnp.mean(centred * centred, axis=-1, keepdims=True) + 1e-06)
    return centred * inv, inv


def norm_back(unit, inv, grad):
    mean_grad = jnp.mean(grad, axis=-1, keepdims=True)
    mean_dot = jnp.mean(grad * unit, axis=-1, keepdims=True)
    return (grad - mean_grad - unit * mean_dot) * inv


def narrow_peers(here):
    return [here ^ 2, here ^ 3, here ^ 1]


def remote(src, dst, sems, at, wide, narrow):
    return pltpu.make_async_remote_copy(
        src_ref=src,
        dst_ref=dst,
        send_sem=sems.at[0, at],
        recv_sem=sems.at[1, at],
        device_id=(wide, narrow),
        device_id_type=pl.DeviceIdType.MESH,
    )


class Gather:
    def __init__(self, src, dst, sems, local_sem, first, wide, here):
        half_rows = src.shape[0] // 2
        half = wide % 2
        mine, other = ds(half * half_rows, half_rows), ds((1 - half) * half_rows, half_rows)
        far, near = here ^ 2, here ^ 1
        self.own = pltpu.make_async_copy(src, dst.at[here], local_sem)
        self.near = remote(src, dst.at[here], sems, first, wide, near)
        self.far = remote(src.at[mine], dst.at[here, mine], sems, first + 1, wide, far)
        got, swapped = dst.at[far, mine], dst.at[far, other]
        self.share = remote(got, got, sems, first + 2, wide, near)
        self.swap = remote(got, got, sems, first + 3, wide ^ 1, here)
        self.share_swapped = remote(swapped, swapped, sems, first + 4, wide, near)

    def start_near(self):
        self.own.start()
        self.near.start()

    def start_far(self):
        self.far.start()

    def forward(self):
        self.far.wait_recv()
        self.swap.start()
        self.share.start()

    def forward_swapped(self):
        self.swap.wait_recv()
        self.share_swapped.start()

    def finish(self):
        self.own.wait()
        self.near.wait()
        self.far.wait_send()
        self.swap.wait_send()
        self.share.wait()
        self.share_swapped.wait()


def group_permutation(rows):
    out = lax.broadcasted_iota(jnp.int32, (rows, rows), 0)
    source = lax.broadcasted_iota(jnp.int32, (rows, rows), 1)
    per_group = rows // 4
    group, rest = out // per_group, out % per_group
    line = 2 * (rest // HALF) + group // 2
    wanted = line * SIDE + 2 * (rest % HALF) + group % 2
    return jnp.where(source == wanted, 1.0, 0.0).astype(BF16)


class Exchange:
    def __init__(self, sent, got, sems, local_sem, first, wide, here):
        self.own = pltpu.make_async_copy(sent.at[here], got.at[:, here], local_sem)
        self.copies = [
            remote(sent.at[peer], got.at[:, here], sems, first + at, wide, peer)
            for at, peer in enumerate(narrow_peers(here))
        ]

    def start(self):
        for copy in self.copies:
            copy.start()
        self.own.start()

    def wait(self):
        self.own.wait()
        for copy in self.copies:
            copy.wait()


def front_kernel(
    live_ref, silu_ref, taps_ref, tokens_hbm, cot_hbm, ada_hbm, wqkv_src, wout_src, wup_src, wdown_src, ktaps_src,
    x_ref, cot_ref, mod_ref, u_ref, qkv_ref, probs_ref, ctx_ref, att_ref, x1_ref, h2_ref, h2t_ref, db_ref,
    wqkv_ref, wout_ref, wup_ref, wdown_ref, ktaps_ref,
    base, shifted, shards, sent, sent_cot, got, ada, sems, local_sems, in_sems,
):
    width = u_ref.shape[1]
    rows_all = u_ref.shape[0]
    latents, shard_rows = shards.shape[:2]
    wide, here = lax.axis_index("wide"), lax.axis_index("narrow")
    load_tokens = pltpu.make_async_copy(tokens_hbm, shards, in_sems.at[0])
    load_tokens.start()
    load_ada = pltpu.make_async_copy(ada_hbm, ada, in_sems.at[1])
    load_ada.start()

    barrier = pltpu.get_barrier_semaphore()
    partners = [(wide, peer) for peer in narrow_peers(here)] + [(wide ^ 1, here)]
    for partner in partners:
        pl.semaphore_signal(
            barrier, inc=1, device_id=partner, device_id_type=pl.DeviceIdType.MESH
        )
    permutation = group_permutation(shard_rows)
    load_tokens.wait()

    def permute(to):
        def one(at, carry):
            moved = mm(permutation, shards[at], NN).astype(BF16)
            for group in range(4):
                to[at, group] = moved[group * (shard_rows // 4) : (group + 1) * (shard_rows // 4)]
            return carry

        lax.fori_loop(0, latents, one, 0)

    permute(sent)
    pl.semaphore_wait(barrier, len(partners))
    exchange = Exchange(sent, got, sems, local_sems.at[0], 0, wide, here)
    exchange_cot = Exchange(sent_cot, cot_ref, sems, local_sems.at[1], 3, wide, here)
    gathers = [
        Gather(src, dst, sems, local_sems.at[2 + at], 6 + 5 * at, wide, here)
        for at, (src, dst) in enumerate(
            (
                (wqkv_src, wqkv_ref),
                (wout_src, wout_ref),
                (wup_src, wup_ref),
                (wdown_src, wdown_ref),
                (ktaps_src, ktaps_ref),
            )
        )
    ]
    g_qkv, g_out, g_up, g_down, g_taps = gathers
    exchange.start()
    load_cot = pltpu.make_async_copy(cot_hbm, shards, in_sems.at[0])
    load_cot.start()
    for one in gathers:
        one.start_near()

    load_ada.wait()
    for part in range(6):
        mod_ref[part : part + 1, :] = mm(
            silu_ref[...], ada[:, part * width : (part + 1) * width], NN
        )[0:1, :]
    load_cot.wait()
    permute(sent_cot)
    shift_one, scale_one, gate_one = mod_ref[0:1, :], mod_ref[1:2, :], mod_ref[2:3, :]
    shift_two, scale_two, gate_two = mod_ref[3:4, :], mod_ref[4:5, :], mod_ref[5:6, :]
    clear_edges(base)
    clear_edges(shifted)
    exchange.wait()
    g_qkv.start_far()
    g_out.start_far()
    for group in range(4):
        for source in range(latents):
            start = group * PHASE + source * ROWS
            x_ref[start : start + ROWS, :] = got[group, source]

    def norm_step(step, carry):
        group, part = step // (PHASE // ROWS), step % (PHASE // ROWS)
        unit, _ = normed(x_ref[ds(step * ROWS, ROWS), :].astype(F32))
        h_one = (unit * (1.0 + scale_one) + shift_one).astype(BF16)
        base[group, ds(HALF + part * ROWS, ROWS, HALF), :] = h_one.astype(F32)
        return carry

    lax.fori_loop(0, rows_all // ROWS, norm_step, 0)

    def conv_step(block, carry):
        lanes = ds(block * LANES, LANES)
        shift_cols(base, shifted, lanes)
        taps = [taps_ref[t : t + 1, lanes] for t in range(9)]

        def rows_step(step, carry):
            for group in range(4):
                total = jnp.zeros((ROWS, LANES), F32)
                for tap in range(9):
                    total += taps[tap] * tap_value(
                        base, shifted, group, tap // 3, tap % 3, step * ROWS, lanes
                    )
                u_ref[ds(group * PHASE + step * ROWS, ROWS), lanes] = total.astype(BF16)
            return carry

        return lax.fori_loop(0, PHASE // ROWS, rows_step, carry)

    lax.fori_loop(0, width // LANES, conv_step, 0)
    g_qkv.forward()
    g_out.forward()
    g_up.start_far()
    g_taps.start_far()
    g_qkv.forward_swapped()
    g_out.forward_swapped()
    g_qkv.finish()
    shards_here = wqkv_ref.shape[0]
    slab = wqkv_ref.shape[1]

    def project_step(step, carry):
        rows = ds(step * PHASE, PHASE)
        for part in range(3):
            for shard in range(shards_here):
                weight = wqkv_ref[shard, :, part * width : (part + 1) * width]
                cols = slice(part * width + shard * slab, part * width + (shard + 1) * slab)
                qkv_ref[rows, cols] = mm(u_ref[rows, :], weight, NT).astype(BF16)
        return carry

    lax.fori_loop(0, 4, project_step, 0)

    pairs = width // LANES
    first = lax.broadcasted_iota(jnp.int32, (PHASE, LANES), 1) < HEAD_DIM
    zero = jnp.zeros((PHASE, LANES), BF16)

    def attend_step(step, carry):
        group, pair = step // pairs, step % pairs
        rows = ds(group * PHASE, PHASE)
        query = qkv_ref[rows, ds(pair * LANES, LANES)]
        key = qkv_ref[rows, ds(width + pair * LANES, LANES)]
        value = qkv_ref[rows, ds(2 * width + pair * LANES, LANES)]
        found = []
        for head in range(2):
            own = jnp.where(first, query, zero) if head == 0 else jnp.where(first, zero, query)
            scores = mm(key, own, NT)
            top = jnp.max(scores, axis=0, keepdims=True)
            raised = jnp.exp2((scores - top) * (LOG2E * HEAD_DIM**-0.5))
            probs = (raised * (1.0 / jnp.sum(raised, axis=0, keepdims=True))).astype(BF16)
            probs_ref[step, :, head * PHASE : (head + 1) * PHASE] = probs
            found.append(mm(probs, value, TN))
        ctx_ref[rows, ds(pair * LANES, LANES)] = jnp.where(first, found[0], found[1]).astype(BF16)
        return carry

    lax.fori_loop(0, pairs, attend_step, 0)
    g_up.forward()
    g_taps.forward()
    exchange_cot.start()
    lax.fori_loop(pairs, 3 * pairs, attend_step, 0)
    g_up.forward_swapped()
    g_taps.forward_swapped()
    exchange_cot.wait()
    g_down.start_far()
    lax.fori_loop(3 * pairs, 4 * pairs, attend_step, 0)
    g_out.finish()

    def out_step(step, carry):
        rows = ds(step * PHASE, PHASE)
        total = None
        for shard in range(shards_here):
            one = mm(ctx_ref[rows, shard * slab : (shard + 1) * slab], wout_ref[shard], NN)
            total = one if total is None else total + one
        att_ref[rows, :] = total
        return carry

    lax.fori_loop(0, 4, out_step, 0)
    live = live_ref[0, 0]

    def second_step(step, carry):
        rows = ds(step * ROWS, ROWS)
        after = x_ref[rows, :].astype(F32) + gate_one * att_ref[rows, :]
        x1_ref[rows, :] = after
        unit, _ = normed(after)
        h2_ref[rows, :] = (unit * (1.0 + scale_two) + shift_two).astype(BF16)
        group, source = step // (PHASE // ROWS), step % (PHASE // ROWS)
        db_ref[rows, :] = (cot_ref[group, source].astype(F32) * live * gate_two).astype(BF16)
        return carry

    lax.fori_loop(0, rows_all // ROWS, second_step, 0)
    g_down.forward()
    for part in range(4):
        h2t_ref[:, part * PHASE : (part + 1) * PHASE] = h2_ref[
            part * PHASE : (part + 1) * PHASE, :
        ].T
    g_down.forward_swapped()
    for one in (g_up, g_taps, g_down):
        one.finish()


def whole(memory=pltpu.VMEM):
    return pl.BlockSpec(memory_space=memory)


def front(live, silu_row, taps, tokens, cot, w_ada, wqkv, wout, wup, wdown, ktaps):
    latents, shard_rows, width = tokens.shape
    rows = latents * shard_rows
    steps = 4 * (width // LANES)
    shape = jax.ShapeDtypeStruct
    full = lambda shard: shape((latents,) + shard.shape, BF16)
    moved = (latents, 4, shard_rows // 4, width)
    return pl.pallas_call(
        front_kernel,
        out_shape=(
            shape((rows, width), BF16),
            shape((4, latents, shard_rows // 4, width), BF16),
            shape((6, width), F32),
            shape((rows, width), BF16),
            shape((rows, 3 * width), BF16),
            shape((steps, PHASE, 2 * PHASE), BF16),
            shape((rows, width), BF16),
            shape((rows, width), F32),
            shape((rows, width), F32),
            shape((rows, width), BF16),
            shape((width, rows), BF16),
            shape((rows, width), BF16),
            full(wqkv),
            full(wout),
            full(wup),
            full(wdown),
            full(ktaps),
        ),
        in_specs=[whole(pltpu.SMEM)] + [whole()] * 2 + [whole(pl.ANY)] * 8,
        out_specs=(whole(),) * 14 + (whole(pl.ANY),) * 3,
        scratch_shapes=[
            pltpu.VMEM((4, PAD, width), F32),
            pltpu.VMEM((4, PAD, width), F32),
            pltpu.VMEM((latents, shard_rows, width), BF16),
            pltpu.VMEM(moved, BF16),
            pltpu.VMEM(moved, BF16),
            pltpu.VMEM((4, latents, shard_rows // 4, width), BF16),
            pltpu.VMEM(w_ada.shape, BF16),
            pltpu.SemaphoreType.DMA((2, 6 + 5 * 5)),
            pltpu.SemaphoreType.DMA((7,)),
            pltpu.SemaphoreType.DMA((2,)),
        ],
        compiler_params=pltpu.CompilerParams(
            vmem_limit_bytes=60 * MIB, collective_id=0, has_side_effects=True
        ),
        name="attn_forward",
    )(live, silu_row, taps, tokens, cot, w_ada, wqkv, wout, wup, wdown, ktaps)


def ffn_kernel(
    h2_ref, h2t_ref, db_ref, wup_ref, wdown_ref, taps_ref,
    branch_ref, dh2_ref, dwup_ref, dwdown_ref, dtaps_ref,
    hid, hid_moved, grad, grad_moved, slope, act, dhid,
):
    rows_all = h2_ref.shape[0]

    @pl.when(pl.program_id(0) == 0)
    def _():
        for ref in (hid, hid_moved, grad, grad_moved):
            clear_edges(ref)
        branch_ref[...] = jnp.zeros_like(branch_ref)
        dh2_ref[...] = jnp.zeros_like(dh2_ref)

    def up_step(group, carry):
        rows = ds(group * PHASE, PHASE)
        hid[group, HALF : HALF + PHASE, :] = mm(h2_ref[rows, :], wup_ref[0], NN)
        return carry

    lax.fori_loop(0, 4, up_step, 0)

    for block in range(CHUNK // LANES):
        lanes = slice(block * LANES, (block + 1) * LANES)
        shift_cols(hid, hid_moved, lanes)
        taps = [taps_ref[0, t : t + 1, lanes] for t in range(9)]

        def act_step(step, carry):
            for group in range(4):
                total = jnp.zeros((ROWS, LANES), F32)
                for tap in range(9):
                    total += taps[tap] * tap_value(
                        hid, hid_moved, group, tap // 3, tap % 3, step * ROWS, lanes
                    )
                square = total * total
                turn = jnp.tanh(total * (square * (GELU_C * GELU_A) + GELU_C))
                half = 0.5 * turn + 0.5
                bend = total * (half - half * half)
                rows = ds(group * PHASE + step * ROWS, ROWS)
                act[rows, lanes] = (total * half).astype(BF16)
                slope[rows, lanes] = half + bend * (
                    square * (6.0 * GELU_C * GELU_A) + 2.0 * GELU_C
                )
            return carry

        lax.fori_loop(0, PHASE // ROWS, act_step, 0)

    def dact_step(group, carry):
        rows = ds(group * PHASE, PHASE)
        dact = mm(db_ref[rows, :], wdown_ref[0], NT)
        grad[group, HALF : HALF + PHASE, :] = dact * slope[rows, :]
        return carry

    lax.fori_loop(0, 4, dact_step, 0)

    for block in range(CHUNK // LANES):
        lanes = slice(block * LANES, (block + 1) * LANES)
        shift_cols(grad, grad_moved, lanes)
        conv_back(grad, grad_moved, hid, lanes, [taps_ref[0, t : t + 1, lanes] for t in range(9)],
                  dtaps_ref.at[0], dhid)

    def final_step(group, carry):
        rows = ds(group * PHASE, PHASE)
        branch_ref[rows, :] += mm(act[rows, :], wdown_ref[0], NN)
        dh2_ref[rows, :] += mm(dhid[rows, :], wup_ref[0], NT)
        return carry

    lax.fori_loop(0, 4, final_step, 0)
    dwup_ref[0] = mm(h2t_ref[...], dhid[...], NN).astype(BF16)
    dwdown_ref[0] = mm(act[...], db_ref[...], TN).astype(BF16)


def conv_back(grad, grad_moved, source, lanes, taps, dtaps_ref, out_ref):
    def rows_step(step, sums):
        sums = list(sums)
        for group in range(4):
            total = jnp.zeros((ROWS, LANES), F32)
            own = source[group, ds(HALF + step * ROWS, ROWS, HALF), lanes]
            for tap in range(9):
                moved = tap_value(
                    grad, grad_moved, group, 2 - tap // 3, 2 - tap % 3, step * ROWS, lanes
                )
                total += taps[tap] * moved
                sums[tap] += (own * moved).reshape(ROWS // 8, 8, LANES).sum(axis=0)
            out_ref[ds(group * PHASE + step * ROWS, ROWS), lanes] = total.astype(out_ref.dtype)
        return tuple(sums)

    start = tuple(jnp.zeros((8, LANES), F32) for _ in range(9))
    sums = lax.fori_loop(0, PHASE // ROWS, rows_step, start)
    for tap in range(9):
        dtaps_ref[tap : tap + 1, lanes] = jnp.sum(sums[tap], axis=0, keepdims=True)


def ffn(h2, h2t, db, wup, wdown, taps):
    rows, width = h2.shape
    shards, _, local = wup.shape
    per = local // CHUNK
    shape = jax.ShapeDtypeStruct
    keep = lambda *block: pl.BlockSpec(block, lambda c: (0,) * len(block))
    return pl.pallas_call(
        ffn_kernel,
        grid=(shards * per,),
        out_shape=(
            shape((rows, width), F32),
            shape((rows, width), F32),
            shape(wup.shape, BF16),
            shape(wdown.shape, BF16),
            shape(taps.shape, F32),
        ),
        in_specs=[
            keep(rows, width),
            keep(width, rows),
            keep(rows, width),
            pl.BlockSpec((1, width, CHUNK), lambda c: (c // per, 0, c % per)),
            pl.BlockSpec((1, CHUNK, width), lambda c: (c // per, c % per, 0)),
            pl.BlockSpec((1, 9, CHUNK), lambda c: (c // per, 0, c % per)),
        ],
        out_specs=(
            keep(rows, width),
            keep(rows, width),
            pl.BlockSpec((1, width, CHUNK), lambda c: (c // per, 0, c % per)),
            pl.BlockSpec((1, CHUNK, width), lambda c: (c // per, c % per, 0)),
            pl.BlockSpec((1, 9, CHUNK), lambda c: (c // per, 0, c % per)),
        ),
        scratch_shapes=[pltpu.VMEM((4, PAD, CHUNK), F32)] * 4
        + [pltpu.VMEM((rows, CHUNK), F32)]
        + [pltpu.VMEM((rows, CHUNK), BF16)] * 2,
        compiler_params=pltpu.CompilerParams(vmem_limit_bytes=56 * MIB),
        name="feed_forward",
    )(h2, h2t, db, wup, wdown, taps)


def mid_kernel(
    live_ref, x1_ref, cot_ref, branch_ref, dh2_ref, att_ref, ctx_ref, mod_ref, wout_ref,
    block_ref, dx1_ref, dctx_ref, dwout_ref, dmod_ref,
    datt,
):
    rows_all, width = x1_ref.shape
    gate_one, scale_two, gate_two = mod_ref[2:3, :], mod_ref[4:5, :], mod_ref[5:6, :]
    live = live_ref[0, 0]

    def fold(value):
        return value.reshape(ROWS // 8, 8, width).sum(axis=0)

    def rows_step(step, sums):
        rows = ds(step * ROWS, ROWS)
        after = x1_ref[rows, :]
        dout = cot_ref[rows, :].astype(F32) * live
        branch = branch_ref[rows, :]
        block_ref[rows, :] = ((after + gate_two * branch) * live).astype(BF16)
        unit, inv = normed(after)
        dh2 = dh2_ref[rows, :]
        dx1 = dout + norm_back(unit, inv, dh2 * (1.0 + scale_two))
        dx1_ref[rows, :] = dx1
        datt[rows, :] = (dx1 * gate_one).astype(BF16)
        found = (dx1 * att_ref[rows, :], dh2, dh2 * unit, dout * branch)
        return tuple(total + fold(one) for total, one in zip(sums, found))

    start = tuple(jnp.zeros((8, width), F32) for _ in range(4))
    sums = lax.fori_loop(0, rows_all // ROWS, rows_step, start)
    for at in range(4):
        dmod_ref[at : at + 1, :] = jnp.sum(sums[at], axis=0, keepdims=True)

    def ctx_step(step, carry):
        rows = ds(step * PHASE, PHASE)
        dctx_ref[rows, :] = mm(datt[rows, :], wout_ref[...], NT).astype(BF16)
        return carry

    lax.fori_loop(0, 4, ctx_step, 0)
    for part in range(3):
        cols = slice(part * PHASE, (part + 1) * PHASE)
        dwout_ref[cols, :] = mm(ctx_ref[:, cols], datt[...], TN).astype(BF16)


def mid(live, x1, cot, branch, dh2, att, ctx, mod, wout):
    rows, width = x1.shape
    shape = jax.ShapeDtypeStruct
    return pl.pallas_call(
        mid_kernel,
        out_shape=(
            shape((rows, width), BF16),
            shape((rows, width), F32),
            shape((rows, width), BF16),
            shape(wout.shape, BF16),
            shape((4, width), F32),
        ),
        in_specs=[whole(pltpu.SMEM)] + [whole()] * 8,
        out_specs=(whole(),) * 5,
        scratch_shapes=[pltpu.VMEM((rows, width), BF16)],
        compiler_params=pltpu.CompilerParams(vmem_limit_bytes=56 * MIB),
        name="residual_backward",
    )(live, x1, cot, branch, dh2, att, ctx, mod, wout)


def attn_backward_kernel(
    u_ref, qkv_ref, probs_ref, dctx_ref, dqkv_ref, dw_ref
):
    rows_all, width = u_ref.shape
    pairs = width // LANES
    first = lax.broadcasted_iota(jnp.int32, (PHASE, LANES), 1) < HEAD_DIM
    zero = jnp.zeros((PHASE, LANES), BF16)
    scale = HEAD_DIM**-0.5

    def attend_step(step, carry):
        group, pair = step // pairs, step % pairs
        rows = ds(group * PHASE, PHASE)
        query = qkv_ref[rows, ds(pair * LANES, LANES)]
        key = qkv_ref[rows, ds(width + pair * LANES, LANES)]
        value = qkv_ref[rows, ds(2 * width + pair * LANES, LANES)]
        dctx = dctx_ref[rows, ds(pair * LANES, LANES)]
        dq, dk, dv = [], None, None
        for head in range(2):
            own = lambda full: jnp.where(first, full, zero) if head == 0 else jnp.where(first, zero, full)
            probs = probs_ref[step, :, head * PHASE : (head + 1) * PHASE]
            probs_f = probs.astype(F32)
            dctx_own, query_own = own(dctx), own(query)
            dprobs = mm(value, dctx_own, NT)
            inner = jnp.sum(dprobs * probs_f, axis=0, keepdims=True)
            dscores = (probs_f * (dprobs - inner)).astype(BF16)
            dv_one = mm(probs, dctx_own, NN)
            dk_one = mm(dscores, query_own, NN)
            dv = dv_one if dv is None else dv + dv_one
            dk = dk_one if dk is None else dk + dk_one
            dq.append(mm(dscores, key, TN))
        dqkv_ref[rows, ds(pair * LANES, LANES)] = (
            jnp.where(first, dq[0], dq[1]) * scale
        ).astype(BF16)
        dqkv_ref[rows, ds(width + pair * LANES, LANES)] = (dk * scale).astype(BF16)
        dqkv_ref[rows, ds(2 * width + pair * LANES, LANES)] = dv.astype(BF16)
        return carry

    lax.fori_loop(0, 4 * pairs, attend_step, 0)
    for part in range(3):
        cols = slice(part * width, (part + 1) * width)

        def weight_step(block, carry, cols=cols, part=part):
            out_rows = ds(block * PHASE, PHASE)
            left = dqkv_ref[:, ds(part * width + block * PHASE, PHASE)]
            dw_ref[out_rows, cols] = mm(left, u_ref[...], TN).astype(BF16)
            return carry

        lax.fori_loop(0, width // PHASE, weight_step, 0)


def attn_backward(u, qkv, probs, dctx):
    rows, width = u.shape
    shape = jax.ShapeDtypeStruct
    return pl.pallas_call(
        attn_backward_kernel,
        out_shape=(shape((rows, 3 * width), BF16), shape((width, 3 * width), BF16)),
        in_specs=[whole()] * 4,
        out_specs=(whole(),) * 2,
        compiler_params=pltpu.CompilerParams(vmem_limit_bytes=56 * MIB),
        name="attn_backward",
    )(u, qkv, probs, dctx)


def input_backward_kernel(
    x_ref, dx1_ref, dqkv_ref, mod_ref, taps_ref, wqkv_ref,
    dx_ref, dmod_ref, dtaps_ref,
    base, shifted, first_in, dh1,
):
    rows_all, width = x_ref.shape
    shift_one, scale_one = mod_ref[0:1, :], mod_ref[1:2, :]
    clear_edges(base)
    clear_edges(shifted)

    def norm_step(step, carry):
        group, part = step // (PHASE // ROWS), step % (PHASE // ROWS)
        unit, _ = normed(x_ref[ds(step * ROWS, ROWS), :].astype(F32))
        h_one = (unit * (1.0 + scale_one) + shift_one).astype(BF16)
        first_in[group, ds(HALF + part * ROWS, ROWS, HALF), :] = h_one.astype(F32)
        return carry

    lax.fori_loop(0, rows_all // ROWS, norm_step, 0)

    def du_step(group, carry):
        rows = ds(group * PHASE, PHASE)
        total = None
        for part in range(3):
            cols = slice(part * width, (part + 1) * width)
            one = mm(dqkv_ref[rows, cols], wqkv_ref[:, cols], NN)
            total = one if total is None else total + one
        base[group, HALF : HALF + PHASE, :] = total
        return carry

    lax.fori_loop(0, 4, du_step, 0)

    def conv_step(block, carry):
        lanes = ds(block * LANES, LANES)
        shift_cols(base, shifted, lanes)
        conv_back(base, shifted, first_in, lanes, [taps_ref[t : t + 1, lanes] for t in range(9)],
                  dtaps_ref, dh1)
        return carry

    lax.fori_loop(0, width // LANES, conv_step, 0)

    def fold(value):
        return value.reshape(ROWS // 8, 8, width).sum(axis=0)

    def rows_step(step, sums):
        rows = ds(step * ROWS, ROWS)
        unit, inv = normed(x_ref[rows, :].astype(F32))
        grad = dh1[rows, :]
        dx = dx1_ref[rows, :] + norm_back(unit, inv, grad * (1.0 + scale_one))
        dx_ref[rows, :] = dx.astype(BF16)
        return tuple(total + fold(one) for total, one in zip(sums, (grad, grad * unit)))

    start = tuple(jnp.zeros((8, width), F32) for _ in range(2))
    sums = lax.fori_loop(0, rows_all // ROWS, rows_step, start)
    for at in range(2):
        dmod_ref[at : at + 1, :] = jnp.sum(sums[at], axis=0, keepdims=True)


def input_backward(x, dx1, dqkv, mod, taps, wqkv):
    rows, width = x.shape
    shape = jax.ShapeDtypeStruct
    return pl.pallas_call(
        input_backward_kernel,
        out_shape=(shape((rows, width), BF16), shape((2, width), F32), shape((9, width), F32)),
        in_specs=[whole()] * 6,
        out_specs=(whole(),) * 3,
        scratch_shapes=[pltpu.VMEM((4, PAD, width), F32)] * 3 + [pltpu.VMEM((rows, width), F32)],
        compiler_params=pltpu.CompilerParams(vmem_limit_bytes=56 * MIB),
        name="input_backward",
    )(x, dx1, dqkv, mod, taps, wqkv)


def to_groups(shard):
    latents, rows, width = shard.shape
    split = shard.reshape(latents, rows // (2 * SIDE), 2, HALF, 2, width)
    return split.transpose(0, 2, 4, 1, 3, 5).reshape(latents, 4, rows // 4, width)


def from_groups(groups):
    latents, _, rows, width = groups.shape
    split = groups.reshape(latents, 2, 2, rows // HALF, HALF, width)
    return split.transpose(0, 3, 1, 4, 2, 5).reshape(latents, 4 * rows, width)


def per_device(
    tokens, condition, cotangent, counts, w_ada, k_attn, w_qkv, w_out, w_up, k_ffn, w_down
):
    lat_dev, shard_rows, width = tokens.shape
    here = lax.axis_index("narrow")
    rows_all = shard_rows * lat_dev
    local = w_up.shape[1]

    def latent_out(latent):
        parts = latent.reshape(1, 4, rows_all // 4, width)
        return from_groups(lax.all_to_all(parts, "narrow", 2, 0, tiled=True))

    qkv_t = w_qkv.transpose(2, 1, 0).reshape(w_qkv.shape[2], 3 * width)
    ktaps_own = jnp.pad(k_ffn.reshape(9, local), ((0, 23), (0, 0)))
    attn_taps = k_attn.reshape(9, width).astype(F32)

    cond_f = condition.astype(F32)
    silu_low = jax.nn.silu(cond_f).astype(BF16)
    own_silu = jnp.broadcast_to(lax.dynamic_slice_in_dim(silu_low, here, 1, 0), (16, width))
    live = (here < counts[0]).astype(F32).reshape(1, 1)

    (x, cot, mod, u, qkv, probs, ctx, att, x1, h2, h2t, db, wqkv, wout, wup, wdown, ktaps) = front(
        live, own_silu, attn_taps, tokens, cotangent, w_ada, qkv_t, w_out, w_up, w_down, ktaps_own
    )
    cot = cot.reshape(rows_all, width)
    wqkv = wqkv.reshape(width, 3 * width)
    wout = wout.reshape(width, width)
    ffn_taps = ktaps[:, :9].astype(F32)
    branch, dh2, dwup, dwdown, dffn_taps = ffn(h2, h2t, db, wup, wdown, ffn_taps)
    block_g, dx1, dctx, dwout, dmod_mid = mid(live, x1, cot, branch, dh2, att, ctx, mod, wout)
    dqkv, dwqkv = attn_backward(u, qkv, probs, dctx)
    dx, dmod_first, dattn_taps = input_backward(x, dx1, dqkv, mod, attn_taps, wqkv)

    block = latent_out(block_g)
    grad_tokens = latent_out(dx).astype(F32)

    def reduce(parts):
        return lax.psum(lax.psum_scatter(parts, "narrow", scatter_dimension=0, tiled=True), "wide")

    shared = jnp.concatenate(
        [dwup, dwdown, jnp.pad(dffn_taps, ((0, 0), (0, 7), (0, 0))).astype(BF16)], axis=1
    ).reshape(lat_dev * (2 * width + 16), local)
    late = jnp.concatenate(
        [dwout.reshape(lat_dev, -1, width), dwqkv.reshape(lat_dev, -1, width)], axis=1
    ).reshape(-1, width)
    shared = reduce(shared).astype(F32)
    late = reduce(late).astype(F32)
    grad_w_up, grad_w_down = shared[:width], shared[width : 2 * width]
    grad_k_ffn = shared[2 * width : 2 * width + 9].reshape(3, 3, local)
    heads_width = w_out.shape[0]
    grad_w_out = late[:heads_width]
    grad_w_qkv = late[heads_width:].reshape(heads_width, 3, width).transpose(2, 1, 0)

    dmod = jnp.concatenate([dmod_first, dmod_mid], axis=0)
    small = jnp.concatenate([dmod, dattn_taps, jnp.zeros((1, width), F32)], axis=0).astype(BF16)
    small_all = lax.all_gather(small, ("wide", "narrow"))
    silu_all = lax.all_gather(silu_low, "wide", tiled=True)
    mod_all = small_all[:, :6].reshape(-1, 6 * width)
    grad_k_attn = small_all[:, 6:15].astype(F32).sum(axis=0).reshape(3, 3, width)
    grad_w_ada = mm(silu_all, mod_all, TN)
    mod_low = lax.dynamic_slice_in_dim(mod_all, lax.axis_index("wide") * lat_dev, lat_dev, 0)
    grad_silu = mm(mod_low, w_ada, NT)
    _, pull_silu = jax.vjp(jax.nn.silu, cond_f)
    (grad_condition,) = pull_silu(grad_silu)
    return (
        block,
        grad_tokens,
        grad_condition,
        grad_w_ada,
        grad_k_attn,
        grad_w_qkv,
        grad_w_out,
        grad_w_up,
        grad_k_ffn,
        grad_w_down,
    )


def solution(mesh):
    placed = (
        P("wide", "narrow", None),
        P("wide", None),
        P("wide", "narrow", None),
        P("wide"),
        P(),
        P(),
        P(None, None, "narrow"),
        P("narrow", None),
        P(None, "narrow"),
        P(None, None, "narrow"),
        P("narrow", None),
    )
    return jax.shard_map(
        per_device,
        mesh=mesh,
        in_specs=placed,
        out_specs=(
            P("wide", "narrow", None),
            P("wide", "narrow", None),
            P("wide", None),
            P(),
            P(),
            P(None, None, "narrow"),
            P("narrow", None),
            P(None, "narrow"),
            P(None, None, "narrow"),
            P("narrow", None),
        ),
        check_vma=False,
    )
```

```python
from functools import partial

import jax
import jax.numpy as jnp
from jax import lax
from jax.experimental import pallas as pl
from jax.experimental.pallas import tpu as pltpu
from jax.sharding import PartitionSpec as P

HEAD_DIM = 64
SIDE = 32
HALF = SIDE // 2
PHASE = HALF * HALF
PAD = PHASE + 2 * HALF
LANES = 128
ROWS = 64
CHUNK = 256
LOG2E = 1.4426950408889634
GELU_C = 0.7978845608028654
GELU_A = 0.044715
MIB = 1 << 20
F32 = jnp.float32
BF16 = jnp.bfloat16

NN = (((1,), (0,)), ((), ()))
NT = (((1,), (1,)), ((), ()))
TN = (((0,), (0,)), ((), ()))


def mm(left, right, dims):
    return lax.dot_general(left, right, dims, preferred_element_type=F32)


def ds(start, size, unit=None):
    return pl.ds(pl.multiple_of(start, unit or size), size)


def tap_source(parity, tap):
    return {-1: (1, -1), 0: (0, 0), 1: (1, 0), 2: (0, 1)}[parity + tap - 1]


def shift_cols(base, shifted, lanes):
    col = lax.broadcasted_iota(jnp.int32, (ROWS, LANES), 0) % HALF

    def rows_step(step, carry):
        for group in range(4):
            rows = ds(HALF + step * ROWS, ROWS, HALF)
            value = base[group, rows, lanes]
            if group % 2:
                moved = jnp.where(col == 0, 0.0, pltpu.roll(value, 1, 0))
            else:
                moved = jnp.where(col == HALF - 1, 0.0, pltpu.roll(value, ROWS - 1, 0))
            shifted[group, rows, lanes] = moved
        return carry

    lax.fori_loop(0, PHASE // ROWS, rows_step, 0)


def clear_edges(ref):
    edge = jnp.zeros((HALF, ref.shape[-1]), ref.dtype)
    for group in range(4):
        ref[group, :HALF, :] = edge
        ref[group, PAD - HALF :, :] = edge


def tap_value(base, shifted, group, tap_row, tap_col, start, lanes):
    src_row, row_move = tap_source(group // 2, tap_row)
    src_col, col_move = tap_source(group % 2, tap_col)
    ref = base if col_move == 0 else shifted
    return ref[2 * src_row + src_col, ds(HALF + row_move * HALF + start, ROWS, HALF), lanes]


def normed(values_in):
    mean_val = jnp.mean(values_in, axis=-1, keepdims=True)
    centred = values_in - mean_val
    inv = lax.rsqrt(jnp.mean(centred * centred, axis=-1, keepdims=True) + 1e-06)
    return centred * inv, inv


def norm_back(unit, inv, grad):
    mean_grad = jnp.mean(grad, axis=-1, keepdims=True)
    mean_dot = jnp.mean(grad * unit, axis=-1, keepdims=True)
    return (grad - mean_grad - unit * mean_dot) * inv


def narrow_peers(here):
    return [here ^ 2, here ^ 3, here ^ 1]


def remote(src, dst, sems, at, wide, narrow):
    return pltpu.make_async_remote_copy(
        src_ref=src,
        dst_ref=dst,
        send_sem=sems.at[0, at],
        recv_sem=sems.at[1, at],
        device_id=(wide, narrow),
        device_id_type=pl.DeviceIdType.MESH,
    )


class Gather:
    def __init__(self, src, dst, sems, local_sem, first, wide, here):
        half_rows = src.shape[0] // 2
        half = wide % 2
        mine, other = ds(half * half_rows, half_rows), ds((1 - half) * half_rows, half_rows)
        far, near = here ^ 2, here ^ 1
        self.own = pltpu.make_async_copy(src, dst.at[0], local_sem)
        self.near = remote(src, dst.at[1], sems, first, wide, near)
        self.far = remote(src.at[mine], dst.at[2, mine], sems, first + 1, wide, far)
        self.share = remote(dst.at[2, mine], dst.at[3, mine], sems, first + 2, wide, near)
        self.swap = remote(dst.at[2, mine], dst.at[2, mine], sems, first + 3, wide ^ 1, here)
        self.share_swapped = remote(dst.at[2, other], dst.at[3, other], sems, first + 4, wide, near)

    def start_near(self):
        self.own.start()
        self.near.start()

    def start_far(self):
        self.far.start()

    def forward(self):
        self.far.wait_recv()
        self.swap.start()
        self.share.start()

    def forward_swapped(self):
        self.swap.wait_recv()
        self.share_swapped.start()

    def finish(self):
        self.own.wait()
        self.near.wait()
        self.far.wait_send()
        self.swap.wait_send()
        self.share.wait()
        self.share_swapped.wait()


def group_permutation(rows):
    out = lax.broadcasted_iota(jnp.int32, (rows, rows), 0)
    source = lax.broadcasted_iota(jnp.int32, (rows, rows), 1)
    per_group = rows // 4
    group, rest = out // per_group, out % per_group
    line = 2 * (rest // HALF) + group // 2
    wanted = line * SIDE + 2 * (rest % HALF) + group % 2
    return jnp.where(source == wanted, 1.0, 0.0).astype(BF16)


class Exchange:
    def __init__(self, sent, got, sems, local_sem, first, wide, here):
        self.own = pltpu.make_async_copy(sent.at[here], got.at[:, here], local_sem)
        self.copies = [
            remote(sent.at[peer], got.at[:, here], sems, first + at, wide, peer)
            for at, peer in enumerate(narrow_peers(here))
        ]

    def start(self):
        for copy in self.copies:
            copy.start()
        self.own.start()

    def wait(self):
        self.own.wait()
        for copy in self.copies:
            copy.wait()


class Return:
    def __init__(self, sent, got, sems, local_sem, first, wide, here):
        self.own = pltpu.make_async_copy(sent.at[:, here], got.at[here], local_sem)
        self.copies = [
            remote(sent.at[:, peer], got.at[here], sems, first + at, wide, peer)
            for at, peer in enumerate(narrow_peers(here))
        ]

    start = Exchange.start
    wait = Exchange.wait


HALVINGS = 3


class WideSum:
    def __init__(self, source, work, full, got, sems, first, wide, here, n_wide, done=0):
        self.source, self.work, self.full, self.got = source, work, full, got
        self.rows = work.shape[0]
        self.levels = min(HALVINGS, n_wide.bit_length() - 1)
        self.extra = n_wide.bit_length() - 1 - self.levels
        self.done = done
        self.wide, self.here, self.sems, self.first = wide, here, sems, first
        self.offsets = [0]
        for level in range(self.levels):
            bit = (wide // 2**level) % 2
            self.offsets.append(self.offsets[-1] + bit * (self.rows >> (level + 1)))
        self.waiting = []

    def size(self, level):
        return self.rows >> level

    def at(self, ref, offset, size):
        return ref.at[ds(offset, size, 16)]

    def half_copy(self, level):
        size, base = self.size(level + 1), self.offsets[level]
        send = base + size - (self.offsets[level + 1] - base)
        source = self.source if level == self.done else self.work
        landing = self.rows - self.size(level)
        return remote(
            self.at(source, send, size), self.got.at[landing : landing + size],
            self.sems, self.first + level, self.wide ^ (1 << level), self.here,
        )

    def start_half(self, level):
        self.half_copy(level).start()

    def finish_half(self, level):
        self.half_copy(level).wait_recv()
        size, landing = self.size(level + 1), self.rows - self.size(level)
        rows = ds(self.offsets[level + 1], size, 16)
        source = self.source if level == self.done else self.work
        self.work[rows, :] = (
            source[rows, :].astype(F32) + self.got[landing : landing + size, :].astype(F32)
        ).astype(BF16)

    def extras(self):
        size = self.size(self.levels)
        rows = ds(self.offsets[self.levels], size, 16)
        source = self.source if self.done == self.levels else self.work
        self.full[rows, :] = source[rows, :]
        for at in range(self.extra):
            landing = self.rows - size + at * size
            copy = remote(
                self.full.at[rows], self.got.at[landing : landing + size],
                self.sems, self.first + 2 * self.levels + at,
                self.wide ^ (1 << (self.levels + at)), self.here,
            )
            copy.start()
            copy.wait()
            self.full[rows, :] = (
                self.full[rows, :].astype(F32) + self.got[landing : landing + size, :].astype(F32)
            ).astype(BF16)

    def spread_copy(self, level):
        part = self.at(self.full, self.offsets[level + 1], self.size(level + 1))
        return remote(
            part, part, self.sems, self.first + self.levels + level, self.wide ^ (1 << level), self.here
        )

    def actions(self):
        acts = []
        for level in range(self.done, self.levels):
            acts.append([partial(self.start_half, level)])
            if level > self.done:
                acts[-1].insert(0, partial(self.finish_half, level - 1))
        tail = [self.extras]
        if self.done < self.levels:
            tail.insert(0, partial(self.finish_half, self.levels - 1))
        for level in reversed(range(self.levels)):
            acts.append(tail + [lambda level=level: self.spread_copy(level).start()])
            tail = [lambda level=level: self.spread_copy(level).wait_recv()]
        acts.append(tail)
        return acts

    def wait_sends(self):
        for level in range(self.done, self.levels):
            self.half_copy(level).wait_send()
        for level in range(self.levels):
            self.spread_copy(level).wait_send()


def greet(partners):
    barrier = pltpu.get_barrier_semaphore()
    for partner in partners:
        pl.semaphore_signal(
            barrier, inc=1, device_id=partner, device_id_type=pl.DeviceIdType.MESH
        )
    pl.semaphore_wait(barrier, len(partners))


def wide_partners(wide, here, n_wide):
    return [(wide ^ (1 << level), here) for level in range(n_wide.bit_length() - 1)]


def sum_semaphores(n_wide):
    levels = n_wide.bit_length() - 1
    return levels + min(levels, HALVINGS)


def sum_landing(rows, n_wide):
    levels = n_wide.bit_length() - 1
    last = rows >> min(levels, HALVINGS)
    return rows - last + max(levels - HALVINGS, 0) * last


def front_kernel(
    live_ref, silu_ref, taps_ref, tokens_hbm, cot_hbm, ada_hbm, wqkv_src, wout_src, wup_src, wdown_src, ktaps_src,
    x_ref, cot_ref, mod_ref, u_ref, qkv_ref, probs_ref, ctx_ref, att_ref, x1_ref, h2_ref, h2t_ref, db_ref,
    wqkv_ref, wout_ref, wup_ref, wdown_ref, ktaps_ref,
    base, shifted, shards, sent, sent_cot, got, ada, sems, local_sems, in_sems,
):
    width = u_ref.shape[1]
    rows_all = u_ref.shape[0]
    latents, shard_rows = shards.shape[:2]
    wide, here = lax.axis_index("wide"), lax.axis_index("narrow")
    load_tokens = pltpu.make_async_copy(tokens_hbm, shards, in_sems.at[0])
    load_tokens.start()
    load_ada = pltpu.make_async_copy(ada_hbm, ada, in_sems.at[1])
    load_ada.start()

    barrier = pltpu.get_barrier_semaphore()
    partners = [(wide, peer) for peer in narrow_peers(here)] + [(wide ^ 1, here)]
    for partner in partners:
        pl.semaphore_signal(
            barrier, inc=1, device_id=partner, device_id_type=pl.DeviceIdType.MESH
        )
    permutation = group_permutation(shard_rows)
    load_tokens.wait()

    def permute(to):
        def one(at, carry):
            moved = mm(permutation, shards[at], NN).astype(BF16)
            for group in range(4):
                to[at, group] = moved[group * (shard_rows // 4) : (group + 1) * (shard_rows // 4)]
            return carry

        lax.fori_loop(0, latents, one, 0)

    permute(sent)
    pl.semaphore_wait(barrier, len(partners))
    exchange = Exchange(sent, got, sems, local_sems.at[0], 0, wide, here)
    exchange_cot = Exchange(sent_cot, cot_ref, sems, local_sems.at[1], 3, wide, here)
    gathers = [
        Gather(src, dst, sems, local_sems.at[2 + at], 6 + 5 * at, wide, here)
        for at, (src, dst) in enumerate(
            (
                (wqkv_src, wqkv_ref),
                (wout_src, wout_ref),
                (wup_src, wup_ref),
                (wdown_src, wdown_ref),
                (ktaps_src, ktaps_ref),
            )
        )
    ]
    g_qkv, g_out, g_up, g_down, g_taps = gathers
    exchange.start()
    load_cot = pltpu.make_async_copy(cot_hbm, shards, in_sems.at[0])
    load_cot.start()
    for one in gathers:
        one.start_near()

    load_ada.wait()
    for part in range(6):
        mod_ref[part : part + 1, :] = mm(
            silu_ref[...], ada[:, part * width : (part + 1) * width], NN
        )[0:1, :]
    load_cot.wait()
    permute(sent_cot)
    shift_one, scale_one, gate_one = mod_ref[0:1, :], mod_ref[1:2, :], mod_ref[2:3, :]
    shift_two, scale_two, gate_two = mod_ref[3:4, :], mod_ref[4:5, :], mod_ref[5:6, :]
    clear_edges(base)
    clear_edges(shifted)
    exchange.wait()
    g_qkv.start_far()
    g_out.start_far()
    for group in range(4):
        for source in range(latents):
            start = group * PHASE + source * ROWS
            x_ref[start : start + ROWS, :] = got[group, source]

    def norm_step(step, carry):
        group, part = step // (PHASE // ROWS), step % (PHASE // ROWS)
        unit, _ = normed(x_ref[ds(step * ROWS, ROWS), :].astype(F32))
        h_one = (unit * (1.0 + scale_one) + shift_one).astype(BF16)
        base[group, ds(HALF + part * ROWS, ROWS, HALF), :] = h_one.astype(F32)
        return carry

    lax.fori_loop(0, rows_all // ROWS, norm_step, 0)

    def conv_step(block, carry):
        lanes = ds(block * LANES, LANES)
        shift_cols(base, shifted, lanes)
        taps = [taps_ref[t : t + 1, lanes] for t in range(9)]

        def rows_step(step, carry):
            for group in range(4):
                total = jnp.zeros((ROWS, LANES), F32)
                for tap in range(9):
                    total += taps[tap] * tap_value(
                        base, shifted, group, tap // 3, tap % 3, step * ROWS, lanes
                    )
                u_ref[ds(group * PHASE + step * ROWS, ROWS), lanes] = total.astype(BF16)
            return carry

        return lax.fori_loop(0, PHASE // ROWS, rows_step, carry)

    lax.fori_loop(0, width // LANES, conv_step, 0)
    g_qkv.forward()
    g_out.forward()
    g_up.start_far()
    g_taps.start_far()
    g_qkv.forward_swapped()
    g_out.forward_swapped()
    g_qkv.finish()
    shards_here = wqkv_ref.shape[0]
    slab = wqkv_ref.shape[1]

    def project_step(step, carry):
        rows = ds(step * PHASE, PHASE)
        for part in range(3):
            for shard in range(shards_here):
                weight = wqkv_ref[shard, :, part * width : (part + 1) * width]
                cols = slice(part * width + shard * slab, part * width + (shard + 1) * slab)
                qkv_ref[rows, cols] = mm(u_ref[rows, :], weight, NT).astype(BF16)
        return carry

    lax.fori_loop(0, 4, project_step, 0)

    pairs = width // LANES
    first = lax.broadcasted_iota(jnp.int32, (PHASE, LANES), 1) < HEAD_DIM
    zero = jnp.zeros((PHASE, LANES), BF16)

    def attend_step(step, carry):
        group, pair = step // pairs, step % pairs
        rows = ds(group * PHASE, PHASE)
        query = qkv_ref[rows, ds(pair * LANES, LANES)]
        key = qkv_ref[rows, ds(width + pair * LANES, LANES)]
        value = qkv_ref[rows, ds(2 * width + pair * LANES, LANES)]
        found = []
        for head in range(2):
            own = jnp.where(first, query, zero) if head == 0 else jnp.where(first, zero, query)
            scores = mm(key, own, NT)
            top = jnp.max(scores, axis=0, keepdims=True)
            raised = jnp.exp2((scores - top) * (LOG2E * HEAD_DIM**-0.5))
            probs = (raised * (1.0 / jnp.sum(raised, axis=0, keepdims=True))).astype(BF16)
            probs_ref[step, :, head * PHASE : (head + 1) * PHASE] = probs
            found.append(mm(probs, value, TN))
        ctx_ref[rows, ds(pair * LANES, LANES)] = jnp.where(first, found[0], found[1]).astype(BF16)
        return carry

    lax.fori_loop(0, pairs, attend_step, 0)
    g_up.forward()
    g_taps.forward()
    exchange_cot.start()
    lax.fori_loop(pairs, 3 * pairs, attend_step, 0)
    g_up.forward_swapped()
    g_taps.forward_swapped()
    exchange_cot.wait()
    g_down.start_far()
    lax.fori_loop(3 * pairs, 4 * pairs, attend_step, 0)
    g_out.finish()

    def out_step(step, carry):
        rows = ds(step * PHASE, PHASE)
        total = None
        for shard in range(shards_here):
            one = mm(ctx_ref[rows, shard * slab : (shard + 1) * slab], wout_ref[shard], NN)
            total = one if total is None else total + one
        att_ref[rows, :] = total.astype(BF16)
        x1_ref[rows, :] = x_ref[rows, :].astype(F32) + gate_one * total
        return carry

    lax.fori_loop(0, 4, out_step, 0)
    live = live_ref[0, 0]

    def second_step(step, carry):
        rows = ds(step * ROWS, ROWS)
        unit, _ = normed(x1_ref[rows, :])
        h2_ref[rows, :] = (unit * (1.0 + scale_two) + shift_two).astype(BF16)
        group, source = step // (PHASE // ROWS), step % (PHASE // ROWS)
        db_ref[rows, :] = (cot_ref[group, source].astype(F32) * live * gate_two).astype(BF16)
        return carry

    lax.fori_loop(0, rows_all // ROWS, second_step, 0)
    g_down.forward()
    for part in range(4):
        h2t_ref[:, part * PHASE : (part + 1) * PHASE] = h2_ref[
            part * PHASE : (part + 1) * PHASE, :
        ].T
    g_down.forward_swapped()
    for one in (g_up, g_taps, g_down):
        one.finish()


def whole(memory=pltpu.VMEM):
    return pl.BlockSpec(memory_space=memory)


def front(live, silu_row, taps, tokens, cot, w_ada, wqkv, wout, wup, wdown, ktaps):
    latents, shard_rows, width = tokens.shape
    rows = latents * shard_rows
    steps = 4 * (width // LANES)
    shape = jax.ShapeDtypeStruct
    full = lambda shard: shape((latents,) + shard.shape, BF16)
    moved = (latents, 4, shard_rows // 4, width)
    return pl.pallas_call(
        front_kernel,
        out_shape=(
            shape((rows, width), BF16),
            shape((4, latents, shard_rows // 4, width), BF16),
            shape((6, width), F32),
            shape((rows, width), BF16),
            shape((rows, 3 * width), BF16),
            shape((steps, PHASE, 2 * PHASE), BF16),
            shape((rows, width), BF16),
            shape((rows, width), BF16),
            shape((rows, width), F32),
            shape((rows, width), BF16),
            shape((width, rows), BF16),
            shape((rows, width), BF16),
            full(wqkv),
            full(wout),
            full(wup),
            full(wdown),
            full(ktaps),
        ),
        in_specs=[whole(pltpu.SMEM)] + [whole()] * 2 + [whole(pl.ANY)] * 8,
        out_specs=(whole(),) * 14 + (whole(pl.ANY),) * 3,
        scratch_shapes=[
            pltpu.VMEM((4, PAD, width), F32),
            pltpu.VMEM((4, PAD, width), F32),
            pltpu.VMEM((latents, shard_rows, width), BF16),
            pltpu.VMEM(moved, BF16),
            pltpu.VMEM(moved, BF16),
            pltpu.VMEM((4, latents, shard_rows // 4, width), BF16),
            pltpu.VMEM(w_ada.shape, BF16),
            pltpu.SemaphoreType.DMA((2, 6 + 5 * 5)),
            pltpu.SemaphoreType.DMA((7,)),
            pltpu.SemaphoreType.DMA((2,)),
        ],
        compiler_params=pltpu.CompilerParams(
            vmem_limit_bytes=60 * MIB, collective_id=0, has_side_effects=True
        ),
        name="attn_forward",
    )(live, silu_row, taps, tokens, cot, w_ada, wqkv, wout, wup, wdown, ktaps)


def ffn_kernel(
    live_ref, h2_ref, h2t_ref, db_ref, x1_ref, cot_ref, att_ref, mod_ref, wup_ref, wdown_ref, taps_ref,
    block_ref, dx1_ref, datt_ref, dmod_ref, sums_ref,
    hid, hid_moved, grad, grad_moved, slope, act, dhid, branch, dh2, dtaps, work, chip_sum, got_near, got_far,
    sems,
):
    rows_all, width = h2_ref.shape
    wide, here = lax.axis_index("wide"), lax.axis_index("narrow")
    step, steps = pl.program_id(0), pl.num_programs(0)
    part, turn, odd = (step // 2) % (steps // 4), step // 2, step % 2
    early = step < steps // 2

    def to_near(at):
        return remote(work.at[at % 2], got_near.at[at], sems, at, wide, here ^ 1)

    def to_far(at):
        return remote(chip_sum.at[at], got_far.at[at], sems, steps // 2 + at, wide, here ^ 2)

    @pl.when(step == 0)
    def _():
        barrier = pltpu.get_barrier_semaphore()
        for partner in (here ^ 1, here ^ 2):
            pl.semaphore_signal(
                barrier, inc=1, device_id=(wide, partner), device_id_type=pl.DeviceIdType.MESH
            )
        for ref in (hid, hid_moved, grad, grad_moved):
            clear_edges(ref)
        branch[...] = jnp.zeros_like(branch)
        dh2[...] = jnp.zeros_like(dh2)
        dtaps[...] = jnp.zeros_like(dtaps)
        pl.semaphore_wait(barrier, 2)

    def up_step(group, carry):
        rows = ds(group * PHASE, PHASE)
        hid[group, HALF : HALF + PHASE, :] = mm(h2_ref[rows, :], wup_ref[0], NN)
        return carry

    lax.fori_loop(0, 4, up_step, 0)

    for block in range(CHUNK // LANES):
        lanes = slice(block * LANES, (block + 1) * LANES)
        shift_cols(hid, hid_moved, lanes)
        taps = [taps_ref[0, t : t + 1, lanes] for t in range(9)]

        def act_step(at, carry):
            for group in range(4):
                total = jnp.zeros((ROWS, LANES), F32)
                for tap in range(9):
                    total += taps[tap] * tap_value(
                        hid, hid_moved, group, tap // 3, tap % 3, at * ROWS, lanes
                    )
                square = total * total
                turned = jnp.tanh(total * (square * (GELU_C * GELU_A) + GELU_C))
                half = 0.5 * turned + 0.5
                bend = total * (half - half * half)
                rows = ds(group * PHASE + at * ROWS, ROWS)
                act[rows, lanes] = (total * half).astype(BF16)
                slope[rows, lanes] = half + bend * (
                    square * (6.0 * GELU_C * GELU_A) + 2.0 * GELU_C
                )
            return carry

        lax.fori_loop(0, PHASE // ROWS, act_step, 0)

    def dact_step(group, carry):
        rows = ds(group * PHASE, PHASE)
        dact = mm(db_ref[rows, :], wdown_ref[0], NT)
        grad[group, HALF : HALF + PHASE, :] = dact * slope[rows, :]
        return carry

    lax.fori_loop(0, 4, dact_step, 0)

    for block in range(CHUNK // LANES):
        lanes = slice(block * LANES, (block + 1) * LANES)
        shift_cols(grad, grad_moved, lanes)
        conv_back(grad, grad_moved, hid, lanes, [taps_ref[0, t : t + 1, lanes] for t in range(9)],
                  dtaps, dhid)

    def final_step(group, carry):
        rows = ds(group * PHASE, PHASE)
        branch[rows, :] += mm(act[rows, :], wdown_ref[0], NN)
        dh2[rows, :] += mm(dhid[rows, :], wup_ref[0], NT)
        return carry

    lax.fori_loop(0, 4, final_step, 0)

    @pl.when(jnp.logical_and(odd == 0, turn >= 2))
    def _():
        to_near(turn - 2).wait_send()

    slot = work.at[jnp.where(odd == 0, turn % 2, 2)]
    slot[:width, :] = mm(h2t_ref[...], dhid[...], NN).astype(BF16)
    down = mm(act[...], db_ref[...], TN).astype(BF16)
    for block in range(width // CHUNK):
        rows = slice(width + block * CHUNK, width + (block + 1) * CHUNK)
        slot[rows, :] = down[:, block * CHUNK : (block + 1) * CHUNK]
    slot[2 * width :, :] = dtaps[...].astype(BF16)

    @pl.when(odd == 0)
    def _():
        to_near(turn).start()

    @pl.when(odd == 1)
    def _():
        to_near(turn).wait_recv()

    @pl.when(jnp.logical_and(odd == 1, early))
    def _():
        chip_sum[part] = (work[2].astype(F32) + got_near[turn].astype(F32)).astype(BF16)
        to_far(part).start()

    @pl.when(jnp.logical_and(odd == 1, jnp.logical_not(early)))
    def _():
        to_far(part).wait_recv()
        sums_ref[part] = (
            work[2].astype(F32) + got_near[turn].astype(F32) + got_far[part].astype(F32)
        ).astype(BF16)

    @pl.when(step == steps - 1)
    def _():
        gate_one, scale_two, gate_two = mod_ref[2:3, :], mod_ref[4:5, :], mod_ref[5:6, :]
        live = live_ref[0, 0]

        def fold(value):
            return value.reshape(ROWS // 8, 8, width).sum(axis=0)

        def rows_step(at, sums):
            rows = ds(at * ROWS, ROWS)
            after = x1_ref[rows, :]
            dout = cot_ref[rows, :].astype(F32) * live
            branch_rows = branch[rows, :]
            block_ref[rows, :] = ((after + gate_two * branch_rows) * live).astype(BF16)
            unit, inv = normed(after)
            dh2_rows = dh2[rows, :]
            dx1 = dout + norm_back(unit, inv, dh2_rows * (1.0 + scale_two))
            dx1_ref[rows, :] = dx1
            datt_ref[rows, :] = (dx1 * gate_one).astype(BF16)
            found = (dx1 * att_ref[rows, :].astype(F32), dh2_rows, dh2_rows * unit, dout * branch_rows)
            return tuple(total + fold(one) for total, one in zip(sums, found))

        start = tuple(jnp.zeros((8, width), F32) for _ in range(4))
        sums = lax.fori_loop(0, rows_all // ROWS, rows_step, start)
        for at in range(4):
            dmod_ref[at : at + 1, :] = jnp.sum(sums[at], axis=0, keepdims=True)
        for at in (steps // 2 - 2, steps // 2 - 1):
            to_near(at).wait_send()
        for at in range(steps // 4):
            to_far(at).wait_send()


def conv_back(grad, grad_moved, source, lanes, taps, dtaps_ref, out_ref):
    def rows_step(step, sums):
        sums = list(sums)
        for group in range(4):
            total = jnp.zeros((ROWS, LANES), F32)
            own = source[group, ds(HALF + step * ROWS, ROWS, HALF), lanes]
            for tap in range(9):
                moved = tap_value(
                    grad, grad_moved, group, 2 - tap // 3, 2 - tap % 3, step * ROWS, lanes
                )
                total += taps[tap] * moved
                sums[tap] += (own * moved).reshape(ROWS // 8, 8, LANES).sum(axis=0)
            out_ref[ds(group * PHASE + step * ROWS, ROWS), lanes] = total.astype(out_ref.dtype)
        return tuple(sums)

    start = tuple(jnp.zeros((8, LANES), F32) for _ in range(9))
    sums = lax.fori_loop(0, PHASE // ROWS, rows_step, start)
    for tap in range(9):
        dtaps_ref[tap : tap + 1, lanes] = jnp.sum(sums[tap], axis=0, keepdims=True)


def ffn(live, h2, h2t, db, x1, cot, att, mod, wup, wdown, taps):
    rows, width = h2.shape
    shards, _, local = wup.shape
    per = local // CHUNK
    parcel = (2 * width + 16, CHUNK)
    shape = jax.ShapeDtypeStruct
    keep = lambda *block: pl.BlockSpec(
        block, lambda c: (0,) * len(block), pipeline_mode=pl.Buffered(1)
    )
    slot_of = lambda c: jnp.where(c < 2 * per, 3, 1) - c % 2
    part_of = lambda c: (c // 2) % per
    return pl.pallas_call(
        ffn_kernel,
        grid=(shards * per,),
        out_shape=(
            shape((rows, width), BF16),
            shape((rows, width), F32),
            shape((rows, width), BF16),
            shape((4, width), F32),
            shape((per,) + parcel, BF16),
        ),
        in_specs=[
            whole(pltpu.SMEM),
            keep(rows, width),
            keep(width, rows),
            keep(rows, width),
            keep(rows, width),
            keep(rows, width),
            keep(rows, width),
            keep(6, width),
            pl.BlockSpec((1, width, CHUNK), lambda c: (slot_of(c), 0, part_of(c))),
            pl.BlockSpec((1, CHUNK, width), lambda c: (slot_of(c), part_of(c), 0)),
            pl.BlockSpec((1, 9, CHUNK), lambda c: (slot_of(c), 0, part_of(c))),
        ],
        out_specs=(
            keep(rows, width),
            keep(rows, width),
            keep(rows, width),
            keep(4, width),
            keep(per, *parcel),
        ),
        scratch_shapes=[pltpu.VMEM((4, PAD, CHUNK), F32)] * 4
        + [pltpu.VMEM((rows, CHUNK), F32)]
        + [pltpu.VMEM((rows, CHUNK), BF16)] * 2
        + [pltpu.VMEM((rows, width), F32)] * 2
        + [
            pltpu.VMEM((16, CHUNK), F32),
            pltpu.VMEM((3,) + parcel, BF16),
            pltpu.VMEM((per,) + parcel, BF16),
            pltpu.VMEM((2 * per,) + parcel, BF16),
            pltpu.VMEM((per,) + parcel, BF16),
            pltpu.SemaphoreType.DMA((2, 3 * per)),
        ],
        compiler_params=pltpu.CompilerParams(
            vmem_limit_bytes=60 * MIB, collective_id=1, has_side_effects=True
        ),
        name="feed_forward",
    )(live, h2, h2t, db, x1, cot, att, mod, wup, wdown, taps)


def attn_backward_kernel(
    n_wide, datt_ref, ctx_ref, u_ref, wout_ref, block_in, parcels, qkv_hbm, probs_hbm,
    dqkv_ref, block_ref, own_ref, gup_ref, gdown_ref, gtaps_ref,
    dctx, probs_buf, weights, got_near, chip_sum, got_far, got_block, work, full, got_sums, taps_sum, taps_got,
    sems, local_sems, in_sems, sum_sems,
):
    rows_all, width = u_ref.shape
    wide, here = lax.axis_index("wide"), lax.axis_index("narrow")
    pairs = width // LANES
    half_pairs = pairs // 2
    steps = 4 * pairs
    load_qkv = pltpu.make_async_copy(qkv_hbm, dqkv_ref, in_sems.at[2])
    load_qkv.start()

    def pair_of(step):
        return (half_pairs + step // 4) % pairs

    def load_probs(step):
        return pltpu.make_async_copy(
            probs_hbm.at[(step % 4) * pairs + pair_of(step)], probs_buf.at[step % 2], in_sems.at[step % 2]
        )

    load_probs(0).start()
    greet([(wide, peer) for peer in narrow_peers(here)] + wide_partners(wide, here, n_wide))
    back = Return(block_in, got_block, sems, local_sems.at[0], 0, wide, here)
    back.start()
    pieces = full.shape[0]
    rows = full.shape[1]
    per_sum = sum_semaphores(n_wide)
    sums = [
        WideSum(parcels.at[at, :rows], work.at[at], full.at[at], got_sums.at[at], sum_sems, at * per_sum,
                wide, here, n_wide)
        for at in range(pieces)
    ]
    levels = n_wide.bit_length() - 1

    def taps_copy(level):
        return remote(taps_sum.at[level], taps_got.at[level], sems, 6 + level, wide ^ (1 << level), here)

    def taps_add(level):
        taps_copy(level).wait_recv()
        taps_sum[level + 1] = taps_sum[level] + taps_got[level]
        if level + 1 < levels:
            taps_copy(level + 1).start()

    for at in range(pieces):
        taps_sum[0, :, at * CHUNK : (at + 1) * CHUNK] = parcels[at, rows:, :].astype(F32)
    acts = [one.actions() for one in sums]
    for act in acts[0][0]:
        act()
    taps_copy(0).start()

    def ctx_step(step, carry):
        span = ds(step * PHASE, PHASE)
        slab = wout_ref.shape[1]
        for slot in range(4):
            dctx[span, slot * slab : (slot + 1) * slab] = mm(
                datt_ref[span, :], wout_ref[slot], NT
            ).astype(BF16)
        return carry

    lax.fori_loop(0, 4, ctx_step, 0)
    load_qkv.wait()

    first = lax.broadcasted_iota(jnp.int32, (PHASE, LANES), 1) < HEAD_DIM
    zero = jnp.zeros((PHASE, LANES), BF16)
    scale = HEAD_DIM**-0.5

    def attend_step(step, carry):
        group, pair = step % 4, pair_of(step)
        load_probs(step).wait()

        @pl.when(step + 1 < steps)
        def _():
            load_probs(step + 1).start()

        span = ds(group * PHASE, PHASE)
        query = dqkv_ref[span, ds(pair * LANES, LANES)]
        key = dqkv_ref[span, ds(width + pair * LANES, LANES)]
        value = dqkv_ref[span, ds(2 * width + pair * LANES, LANES)]
        dctx_pair = dctx[span, ds(pair * LANES, LANES)]
        dq, dk, dv = [], None, None
        for head in range(2):
            own = lambda both: jnp.where(first, both, zero) if head == 0 else jnp.where(first, zero, both)
            probs = probs_buf[step % 2, :, head * PHASE : (head + 1) * PHASE]
            probs_f = probs.astype(F32)
            dctx_own, query_own = own(dctx_pair), own(query)
            dprobs = mm(value, dctx_own, NT)
            inner = jnp.sum(dprobs * probs_f, axis=0, keepdims=True)
            dscores = (probs_f * (dprobs - inner)).astype(BF16)
            dv_one = mm(probs, dctx_own, NN)
            dk_one = mm(dscores, query_own, NN)
            dv = dv_one if dv is None else dv + dv_one
            dk = dk_one if dk is None else dk + dk_one
            dq.append(mm(dscores, key, TN))
        dqkv_ref[span, ds(pair * LANES, LANES)] = (
            jnp.where(first, dq[0], dq[1]) * scale
        ).astype(BF16)
        dqkv_ref[span, ds(width + pair * LANES, LANES)] = (dk * scale).astype(BF16)
        dqkv_ref[span, ds(2 * width + pair * LANES, LANES)] = dv.astype(BF16)
        return carry

    def run(acts_now):
        for act in acts_now:
            act()

    def weight_grads(half):
        span = width // 2
        slab = span // 2
        for part in range(4):
            cols = slice(half * span, (half + 1) * span)
            if part < 3:
                left = dqkv_ref[:, part * width + half * span : part * width + (half + 1) * span]
                found = mm(left, u_ref[...], TN).astype(BF16)
            else:
                found = mm(ctx_ref[:, cols], datt_ref[...], TN).astype(BF16)
            for one in range(2):
                weights[2 * half + one, part * slab : (part + 1) * slab, :] = found[
                    one * slab : (one + 1) * slab
                ]

    near_early = remote(weights.at[3], got_near.at[0], sems, 3, wide, here ^ 1)
    near_late = remote(weights.at[1], got_near.at[1], sems, 4, wide, here ^ 1)
    far = remote(chip_sum, got_far, sems, 5, wide, here ^ 2)

    third = steps // 6
    lax.fori_loop(0, third, attend_step, 0)
    run(acts[0][1] + acts[1][0])
    taps_add(0)
    lax.fori_loop(third, 2 * third, attend_step, 0)
    run(acts[0][2])
    taps_add(1)
    lax.fori_loop(2 * third, 3 * third, attend_step, 0)
    run(acts[0][3] + acts[1][1] + acts[2][0])
    weight_grads(1)
    near_early.start()
    run(acts[0][4] + acts[1][2])
    near_early.wait_recv()
    chip_sum[...] = (weights[2].astype(F32) + got_near[0].astype(F32)).astype(BF16)
    far.start()
    lax.fori_loop(3 * third, 4 * third, attend_step, 0)
    run(acts[0][5] + acts[1][3] + acts[2][1])
    back.wait()
    permutation = group_permutation(got_block.shape[1] * got_block.shape[2])

    def unpermute(at, carry):
        groups = jnp.concatenate([got_block[at, group] for group in range(4)], axis=0)
        block_ref[at] = mm(permutation, groups, TN).astype(BF16)
        return carry

    lax.fori_loop(0, got_block.shape[0], unpermute, 0)
    lax.fori_loop(4 * third, 5 * third, attend_step, 0)
    run(acts[1][4] + acts[2][2])
    lax.fori_loop(5 * third, 6 * third, attend_step, 0)
    run(acts[0][6] + acts[1][5] + acts[2][3])
    weight_grads(0)
    near_late.start()
    for level in range(2, levels):
        taps_add(level)
    gtaps_ref[...] = taps_sum[levels]

    def put(at):
        cols = slice(at * CHUNK, (at + 1) * CHUNK)
        gup_ref[:, cols] = full[at, :width, :].astype(F32)
        for block in range(width // CHUNK):
            span = slice(width + block * CHUNK, width + (block + 1) * CHUNK)
            gdown_ref[cols, block * CHUNK : (block + 1) * CHUNK] = full[at, span, :].astype(F32)

    run(acts[2][4])
    put(0)
    near_late.wait_recv()
    run(acts[1][6] + acts[2][5])
    put(1)
    far.wait_recv()
    own_ref[...] = (
        weights[0].astype(F32) + got_near[1].astype(F32) + got_far[...].astype(F32)
    ).astype(BF16)
    run(acts[2][6])
    put(2)
    for one in sums:
        one.wait_sends()
    for level in range(levels):
        taps_copy(level).wait_send()
    near_early.wait_send()
    near_late.wait_send()
    far.wait_send()


def attn_backward(n_wide, datt, ctx, u, wout, block, parcels, qkv, probs):
    rows, width = u.shape
    slots, slab, _ = wout.shape
    pieces, parcel_rows, _ = parcels.shape
    sum_rows = parcel_rows - 16
    shape = jax.ShapeDtypeStruct
    levels = n_wide.bit_length() - 1
    per_sum = sum_semaphores(n_wide)
    return pl.pallas_call(
        partial(attn_backward_kernel, n_wide),
        out_shape=(
            shape((rows, 3 * width), BF16),
            shape((slots, rows // slots, width), BF16),
            shape((4 * slab, width), BF16),
            shape((width, pieces * CHUNK), F32),
            shape((pieces * CHUNK, width), F32),
            shape((16, pieces * CHUNK), F32),
        ),
        in_specs=[whole()] * 6 + [whole(pl.ANY)] * 2,
        out_specs=(whole(),) * 6,
        scratch_shapes=[
            pltpu.VMEM((rows, width), BF16),
            pltpu.VMEM((2, PHASE, 2 * PHASE), BF16),
            pltpu.VMEM((slots, 4 * slab, width), BF16),
            pltpu.VMEM((2, 4 * slab, width), BF16),
            pltpu.VMEM((4 * slab, width), BF16),
            pltpu.VMEM((4 * slab, width), BF16),
            pltpu.VMEM((slots, 4, rows // (4 * slots), width), BF16),
            pltpu.VMEM((pieces, sum_rows, CHUNK), BF16),
            pltpu.VMEM((pieces, sum_rows, CHUNK), BF16),
            pltpu.VMEM((pieces, sum_landing(sum_rows, n_wide), CHUNK), BF16),
            pltpu.VMEM((levels + 1, 16, pieces * CHUNK), F32),
            pltpu.VMEM((levels, 16, pieces * CHUNK), F32),
            pltpu.SemaphoreType.DMA((2, 6 + levels)),
            pltpu.SemaphoreType.DMA((1,)),
            pltpu.SemaphoreType.DMA((3,)),
            pltpu.SemaphoreType.DMA((2, pieces * per_sum)),
        ],
        compiler_params=pltpu.CompilerParams(
            vmem_limit_bytes=60 * MIB, collective_id=2, has_side_effects=True
        ),
        name="attn_backward",
    )(datt, ctx, u, wout, block, parcels, qkv, probs)


def input_backward_kernel(
    n_wide, x_ref, dx1_ref, dqkv_ref, mod_ref, taps_ref, wqkv_ref, own_ref,
    dx_ref, dmod_ref, dtaps_ref, gattn_ref,
    base, shifted, first_in, dh1, dx, got_dx, work, full, got_sums, sems, local_sems, sum_sems,
):
    rows_all, width = x_ref.shape
    wide, here = lax.axis_index("wide"), lax.axis_index("narrow")
    shift_one, scale_one = mod_ref[0:1, :], mod_ref[1:2, :]
    greet([(wide, peer) for peer in narrow_peers(here)] + wide_partners(wide, here, n_wide))
    pieces = full.shape[0]
    rows = full.shape[1]
    per_sum = sum_semaphores(n_wide)
    sums = [
        WideSum(own_ref.at[at * rows : (at + 1) * rows], work.at[at], full.at[at], got_sums.at[at], sum_sems,
                at * per_sum, wide, here, n_wide)
        for at in range(pieces)
    ]
    acts = [one.actions() for one in sums]

    def run(*some):
        for act in some:
            for one in act:
                one()

    run(acts[0][0])
    clear_edges(base)
    clear_edges(shifted)

    def norm_step(step, carry):
        group, part = step // (PHASE // ROWS), step % (PHASE // ROWS)
        unit, _ = normed(x_ref[ds(step * ROWS, ROWS), :].astype(F32))
        h_one = (unit * (1.0 + scale_one) + shift_one).astype(BF16)
        first_in[group, ds(HALF + part * ROWS, ROWS, HALF), :] = h_one.astype(F32)
        return carry

    lax.fori_loop(0, rows_all // ROWS, norm_step, 0)
    slab = wqkv_ref.shape[1]

    def du_step(group, carry):
        span = ds(group * PHASE, PHASE)
        total = None
        for part in range(3):
            for slot in range(4):
                cols = slice(part * width + slot * slab, part * width + (slot + 1) * slab)
                weight = wqkv_ref[slot, :, part * width : (part + 1) * width]
                one = mm(dqkv_ref[span, cols], weight, NN)
                total = one if total is None else total + one
        base[group, HALF : HALF + PHASE, :] = total
        return carry

    run(acts[0][1], acts[1][0])
    lax.fori_loop(0, 4, du_step, 0)
    run(acts[0][2], acts[1][1])

    def conv_step(block, carry):
        lanes = ds(block * LANES, LANES)
        shift_cols(base, shifted, lanes)
        conv_back(base, shifted, first_in, lanes, [taps_ref[t : t + 1, lanes] for t in range(9)],
                  dtaps_ref, dh1)
        return carry

    lax.fori_loop(0, width // (2 * LANES), conv_step, 0)
    run(acts[0][3], acts[1][2])
    lax.fori_loop(width // (2 * LANES), width // LANES, conv_step, 0)
    run(acts[0][4], acts[1][3])

    def fold(value):
        return value.reshape(ROWS // 8, 8, width).sum(axis=0)

    def rows_step(step, sums):
        span = ds(step * ROWS, ROWS)
        group, source = step // (PHASE // ROWS), step % (PHASE // ROWS)
        unit, inv = normed(x_ref[span, :].astype(F32))
        grad = dh1[span, :]
        dx[group, source] = (
            dx1_ref[span, :] + norm_back(unit, inv, grad * (1.0 + scale_one))
        ).astype(BF16)
        return tuple(total + fold(one) for total, one in zip(sums, (grad, grad * unit)))

    start = tuple(jnp.zeros((8, width), F32) for _ in range(2))
    found = lax.fori_loop(0, rows_all // ROWS, rows_step, start)
    for at in range(2):
        dmod_ref[at : at + 1, :] = jnp.sum(found[at], axis=0, keepdims=True)
    back = Return(dx, got_dx, sems, local_sems.at[0], 0, wide, here)
    back.start()
    run(acts[0][5], acts[1][4])
    run(acts[0][6], acts[1][5])
    gattn_ref[:rows, :] = full[0].astype(F32)
    permutation = group_permutation(got_dx.shape[1] * got_dx.shape[2])
    back.wait()

    def unpermute(at, carry):
        groups = jnp.concatenate([got_dx[at, group] for group in range(4)], axis=0)
        dx_ref[at] = mm(permutation, groups, TN)
        return carry

    lax.fori_loop(0, got_dx.shape[0], unpermute, 0)
    run(acts[1][6])
    gattn_ref[rows:, :] = full[1].astype(F32)
    for one in sums:
        one.wait_sends()


def input_backward(n_wide, x, dx1, dqkv, mod, taps, wqkv, own):
    rows, width = x.shape
    slots = wqkv.shape[0]
    pieces = 2
    sum_rows = own.shape[0] // pieces
    shape = jax.ShapeDtypeStruct
    per_sum = sum_semaphores(n_wide)
    return pl.pallas_call(
        partial(input_backward_kernel, n_wide),
        out_shape=(
            shape((slots, rows // slots, width), F32),
            shape((2, width), F32),
            shape((16, width), F32),
            shape(own.shape, F32),
        ),
        in_specs=[whole()] * 7,
        out_specs=(whole(),) * 4,
        scratch_shapes=[pltpu.VMEM((4, PAD, width), F32)] * 3
        + [
            pltpu.VMEM((rows, width), F32),
            pltpu.VMEM((4, slots, rows // (4 * slots), width), BF16),
            pltpu.VMEM((slots, 4, rows // (4 * slots), width), BF16),
            pltpu.VMEM((pieces, sum_rows, width), BF16),
            pltpu.VMEM((pieces, sum_rows, width), BF16),
            pltpu.VMEM((pieces, sum_landing(sum_rows, n_wide), width), BF16),
            pltpu.SemaphoreType.DMA((2, 3)),
            pltpu.SemaphoreType.DMA((1,)),
            pltpu.SemaphoreType.DMA((2, pieces * per_sum)),
        ],
        compiler_params=pltpu.CompilerParams(
            vmem_limit_bytes=60 * MIB, collective_id=3, has_side_effects=True
        ),
        name="input_backward",
    )(x, dx1, dqkv, mod, taps, wqkv, own)


def per_device(
    tokens, condition, cotangent, counts, w_ada, k_attn, w_qkv, w_out, w_up, k_ffn, w_down
):
    lat_dev, shard_rows, width = tokens.shape
    here = lax.axis_index("narrow")
    rows_all = shard_rows * lat_dev
    local = w_up.shape[1]

    n_wide = lax.axis_size("wide")
    qkv_t = w_qkv.transpose(2, 1, 0).reshape(w_qkv.shape[2], 3 * width)
    ktaps_own = jnp.pad(k_ffn.reshape(9, local), ((0, 23), (0, 0)))
    attn_taps = k_attn.reshape(9, width).astype(F32)

    cond_f = condition.astype(F32)
    silu_low = jax.nn.silu(cond_f).astype(BF16)
    own_silu = jnp.broadcast_to(lax.dynamic_slice_in_dim(silu_low, here, 1, 0), (16, width))
    live = (here < counts[0]).astype(F32).reshape(1, 1)

    (x, cot, mod, u, qkv, probs, ctx, att, x1, h2, h2t, db, wqkv, wout, wup, wdown, ktaps) = front(
        live, own_silu, attn_taps, tokens, cotangent, w_ada, qkv_t, w_out, w_up, w_down, ktaps_own
    )
    cot = cot.reshape(rows_all, width)
    ffn_taps = ktaps[:, :9].astype(F32)
    block_g, dx1, datt, dmod_mid, parcels = ffn(
        live, h2, h2t, db, x1, cot, att, mod, wup, wdown, ffn_taps
    )
    block_g = block_g.reshape(4, lat_dev, shard_rows // 4, width)
    dqkv, block, own, grad_w_up, grad_w_down, gtaps = attn_backward(
        n_wide, datt, ctx, u, wout, block_g, parcels, qkv, probs
    )
    grad_tokens, dmod_first, dattn_taps, gattn = input_backward(
        n_wide, x, dx1, dqkv, mod, attn_taps, wqkv, own
    )
    grad_k_ffn = gtaps[:9].reshape(3, 3, local)
    heads_width = w_out.shape[0]
    gattn = gattn.reshape(4, heads_width, width)
    grad_w_qkv = gattn[:3].transpose(2, 0, 1)
    grad_w_out = gattn[3]

    dmod = jnp.concatenate([dmod_first, dmod_mid], axis=0)
    small = jnp.concatenate([dmod, dattn_taps[:9], jnp.zeros((1, width), F32)], axis=0).astype(BF16)
    small_all = lax.all_gather(small, ("wide", "narrow"))
    silu_all = lax.all_gather(silu_low, "wide", tiled=True)
    mod_all = small_all[:, :6].reshape(-1, 6 * width)
    grad_k_attn = small_all[:, 6:15].astype(F32).sum(axis=0).reshape(3, 3, width)
    grad_w_ada = mm(silu_all, mod_all, TN)
    mod_low = lax.dynamic_slice_in_dim(mod_all, lax.axis_index("wide") * lat_dev, lat_dev, 0)
    grad_silu = mm(mod_low, w_ada, NT)
    _, pull_silu = jax.vjp(jax.nn.silu, cond_f)
    (grad_condition,) = pull_silu(grad_silu)
    return (
        block,
        grad_tokens,
        grad_condition,
        grad_w_ada,
        grad_k_attn,
        grad_w_qkv,
        grad_w_out,
        grad_w_up,
        grad_k_ffn,
        grad_w_down,
    )


def solution(mesh):
    placed = (
        P("wide", "narrow", None),
        P("wide", None),
        P("wide", "narrow", None),
        P("wide"),
        P(),
        P(),
        P(None, None, "narrow"),
        P("narrow", None),
        P(None, "narrow"),
        P(None, None, "narrow"),
        P("narrow", None),
    )
    return jax.shard_map(
        per_device,
        mesh=mesh,
        in_specs=placed,
        out_specs=(
            P("wide", "narrow", None),
            P("wide", "narrow", None),
            P("wide", None),
            P(),
            P(),
            P(None, None, "narrow"),
            P("narrow", None),
            P(None, "narrow"),
            P(None, None, "narrow"),
            P("narrow", None),
        ),
        check_vma=False,
    )
```

```python
from functools import partial

import jax
import jax.numpy as jnp
from jax import lax
from jax.experimental import pallas as pl
from jax.experimental.pallas import tpu as pltpu
from jax.sharding import PartitionSpec as P

HEAD_DIM = 64
SIDE = 32
HALF = SIDE // 2
PHASE = HALF * HALF
PAD = PHASE + 2 * HALF
LANES = 128
ROWS = 64
CHUNK = 256
LOG2E = 1.4426950408889634
GELU_C = 0.7978845608028654
GELU_A = 0.044715
MIB = 1 << 20
F32 = jnp.float32
BF16 = jnp.bfloat16

NN = (((1,), (0,)), ((), ()))
NT = (((1,), (1,)), ((), ()))
TN = (((0,), (0,)), ((), ()))


def mm(left, right, dims):
    return lax.dot_general(left, right, dims, preferred_element_type=F32)


def ds(start, size, unit=None):
    return pl.ds(pl.multiple_of(start, unit or size), size)


def tap_source(parity, tap):
    return {-1: (1, -1), 0: (0, 0), 1: (1, 0), 2: (0, 1)}[parity + tap - 1]


def shift_cols(base, shifted, lanes):
    col = lax.broadcasted_iota(jnp.int32, (ROWS, LANES), 0) % HALF

    def rows_step(step, carry):
        for group in range(4):
            rows = ds(HALF + step * ROWS, ROWS, HALF)
            value = base[group, rows, lanes]
            if group % 2:
                moved = jnp.where(col == 0, 0.0, pltpu.roll(value, 1, 0))
            else:
                moved = jnp.where(col == HALF - 1, 0.0, pltpu.roll(value, ROWS - 1, 0))
            shifted[group, rows, lanes] = moved
        return carry

    lax.fori_loop(0, PHASE // ROWS, rows_step, 0)


def clear_edges(ref):
    edge = jnp.zeros((HALF, ref.shape[-1]), ref.dtype)
    for group in range(4):
        ref[group, :HALF, :] = edge
        ref[group, PAD - HALF :, :] = edge


def tap_value(base, shifted, group, tap_row, tap_col, start, lanes):
    src_row, row_move = tap_source(group // 2, tap_row)
    src_col, col_move = tap_source(group % 2, tap_col)
    ref = base if col_move == 0 else shifted
    return ref[2 * src_row + src_col, ds(HALF + row_move * HALF + start, ROWS, HALF), lanes]


def normed(values_in):
    mean_val = jnp.mean(values_in, axis=-1, keepdims=True)
    centred = values_in - mean_val
    inv = lax.rsqrt(jnp.mean(centred * centred, axis=-1, keepdims=True) + 1e-06)
    return centred * inv, inv


def norm_back(unit, inv, grad):
    mean_grad = jnp.mean(grad, axis=-1, keepdims=True)
    mean_dot = jnp.mean(grad * unit, axis=-1, keepdims=True)
    return (grad - mean_grad - unit * mean_dot) * inv


def narrow_peers(here):
    return [here ^ 2, here ^ 3, here ^ 1]


def remote(src, dst, sems, at, wide, narrow):
    return pltpu.make_async_remote_copy(
        src_ref=src,
        dst_ref=dst,
        send_sem=sems.at[0, at],
        recv_sem=sems.at[1, at],
        device_id=(wide, narrow),
        device_id_type=pl.DeviceIdType.MESH,
    )


class Gather:
    def __init__(self, src, dst, sems, local_sem, first, wide, here):
        count = src.shape[0]
        half_rows = count // 2
        half = wide % 2
        far, near = here ^ 2, here ^ 1

        def at(slot, which=None):
            if which is None:
                return dst.at[slot * count : (slot + 1) * count]
            return dst.at[ds(slot * count + which * half_rows, half_rows, 16)]

        self.own = pltpu.make_async_copy(src, at(0), local_sem)
        self.near = remote(src, at(1), sems, first, wide, near)
        self.far = remote(src.at[ds(half * half_rows, half_rows, 16)], at(2, half), sems, first + 1, wide, far)
        self.share = remote(at(2, half), at(3, half), sems, first + 2, wide, near)
        self.swap = remote(at(2, half), at(2, half), sems, first + 3, wide ^ 1, here)
        self.share_swapped = remote(at(2, 1 - half), at(3, 1 - half), sems, first + 4, wide, near)

    def start_near(self):
        self.own.start()
        self.near.start()

    def start_far(self):
        self.far.start()

    def forward(self):
        self.far.wait_recv()
        self.swap.start()
        self.share.start()

    def forward_swapped(self):
        self.swap.wait_recv()
        self.share_swapped.start()

    def finish(self):
        self.own.wait()
        self.near.wait()
        self.far.wait_send()
        self.swap.wait_send()
        self.share.wait()
        self.share_swapped.wait()


def group_permutation(rows):
    out = lax.broadcasted_iota(jnp.int32, (rows, rows), 0)
    source = lax.broadcasted_iota(jnp.int32, (rows, rows), 1)
    per_group = rows // 4
    group, rest = out // per_group, out % per_group
    line = 2 * (rest // HALF) + group // 2
    wanted = line * SIDE + 2 * (rest % HALF) + group % 2
    return jnp.where(source == wanted, 1.0, 0.0).astype(BF16)


class Exchange:
    def __init__(self, sent, got, sems, local_sem, first, wide, here):
        self.own = pltpu.make_async_copy(sent.at[here], got.at[:, here], local_sem)
        self.copies = [
            remote(sent.at[peer], got.at[:, here], sems, first + at, wide, peer)
            for at, peer in enumerate(narrow_peers(here))
        ]

    def start(self):
        for copy in self.copies:
            copy.start()
        self.own.start()

    def wait(self):
        self.own.wait()
        for copy in self.copies:
            copy.wait()


class Return:
    def __init__(self, sent, got, sems, local_sem, first, wide, here):
        self.own = pltpu.make_async_copy(sent.at[:, here], got.at[here], local_sem)
        self.copies = [
            remote(sent.at[:, peer], got.at[here], sems, first + at, wide, peer)
            for at, peer in enumerate(narrow_peers(here))
        ]

    start = Exchange.start
    wait = Exchange.wait


HALVINGS = 3


class WideSum:
    def __init__(self, source, work, full, got, sems, first, wide, here, n_wide, done=0):
        self.source, self.work, self.full, self.got = source, work, full, got
        self.rows = work.shape[0]
        self.levels = min(HALVINGS, n_wide.bit_length() - 1)
        self.extra = n_wide.bit_length() - 1 - self.levels
        self.done = done
        self.wide, self.here, self.sems, self.first = wide, here, sems, first
        self.offsets = [0]
        for level in range(self.levels):
            bit = (wide // 2**level) % 2
            self.offsets.append(self.offsets[-1] + bit * (self.rows >> (level + 1)))
        self.waiting = []

    def size(self, level):
        return self.rows >> level

    def at(self, ref, offset, size):
        return ref.at[ds(offset, size, 16)]

    def half_copy(self, level):
        size, base = self.size(level + 1), self.offsets[level]
        send = base + size - (self.offsets[level + 1] - base)
        source = self.source if level == self.done else self.work
        landing = self.rows - self.size(level)
        return remote(
            self.at(source, send, size), self.got.at[landing : landing + size],
            self.sems, self.first + level, self.wide ^ (1 << level), self.here,
        )

    def start_half(self, level):
        self.half_copy(level).start()

    def finish_half(self, level):
        self.half_copy(level).wait_recv()
        size, landing = self.size(level + 1), self.rows - self.size(level)
        rows = ds(self.offsets[level + 1], size, 16)
        source = self.source if level == self.done else self.work
        self.work[rows, :] = (
            source[rows, :].astype(F32) + self.got[landing : landing + size, :].astype(F32)
        ).astype(BF16)

    def extras(self):
        size = self.size(self.levels)
        rows = ds(self.offsets[self.levels], size, 16)
        source = self.source if self.done == self.levels else self.work
        self.full[rows, :] = source[rows, :]
        for at in range(self.extra):
            landing = self.rows - size + at * size
            copy = remote(
                self.full.at[rows], self.got.at[landing : landing + size],
                self.sems, self.first + 2 * self.levels + at,
                self.wide ^ (1 << (self.levels + at)), self.here,
            )
            copy.start()
            copy.wait()
            self.full[rows, :] = (
                self.full[rows, :].astype(F32) + self.got[landing : landing + size, :].astype(F32)
            ).astype(BF16)

    def spread_copy(self, level):
        part = self.at(self.full, self.offsets[level + 1], self.size(level + 1))
        return remote(
            part, part, self.sems, self.first + self.levels + level, self.wide ^ (1 << level), self.here
        )

    def actions(self):
        acts = []
        for level in range(self.done, self.levels):
            acts.append([partial(self.start_half, level)])
            if level > self.done:
                acts[-1].insert(0, partial(self.finish_half, level - 1))
        tail = [self.extras]
        if self.done < self.levels:
            tail.insert(0, partial(self.finish_half, self.levels - 1))
        for level in reversed(range(self.levels)):
            acts.append(tail + [lambda level=level: self.spread_copy(level).start()])
            tail = [lambda level=level: self.spread_copy(level).wait_recv()]
        acts.append(tail)
        return acts

    def wait_sends(self):
        for level in range(self.done, self.levels):
            self.half_copy(level).wait_send()
        for level in range(self.levels):
            self.spread_copy(level).wait_send()


def halvings_ahead(pieces, levels):
    return [min(levels, pieces - at) for at in range(pieces)]


def greet(partners):
    barrier = pltpu.get_barrier_semaphore()
    for partner in partners:
        pl.semaphore_signal(
            barrier, inc=1, device_id=partner, device_id_type=pl.DeviceIdType.MESH
        )
    pl.semaphore_wait(barrier, len(partners))


def wide_partners(wide, here, n_wide):
    return [(wide ^ (1 << level), here) for level in range(n_wide.bit_length() - 1)]


def sum_semaphores(n_wide):
    levels = n_wide.bit_length() - 1
    return levels + min(levels, HALVINGS)


def sum_landing(rows, n_wide):
    levels = n_wide.bit_length() - 1
    last = rows >> min(levels, HALVINGS)
    return rows - last + max(levels - HALVINGS, 0) * last


def front_kernel(
    live_ref, silu_ref, taps_ref, tokens_hbm, cot_hbm, ada_hbm, wqkv_src, wout_src, wup_src, wdown_src, ktaps_src,
    x_ref, cot_ref, mod_ref, u_ref, qkv_ref, probs_ref, ctx_ref, att_ref, x1_ref, h2_ref, h2t_ref, db_ref,
    wqkv_ref, wout_ref, wup_ref, wdown_ref, ktaps_ref,
    base, shifted, shards, sent, sent_cot, got, ada, sems, local_sems, in_sems,
):
    width = u_ref.shape[1]
    rows_all = u_ref.shape[0]
    latents, shard_rows = shards.shape[:2]
    wide, here = lax.axis_index("wide"), lax.axis_index("narrow")
    load_tokens = pltpu.make_async_copy(tokens_hbm, shards, in_sems.at[0])
    load_tokens.start()
    load_ada = pltpu.make_async_copy(ada_hbm, ada, in_sems.at[1])
    load_ada.start()

    barrier = pltpu.get_barrier_semaphore()
    partners = [(wide, peer) for peer in narrow_peers(here)] + [(wide ^ 1, here)]
    for partner in partners:
        pl.semaphore_signal(
            barrier, inc=1, device_id=partner, device_id_type=pl.DeviceIdType.MESH
        )
    permutation = group_permutation(shard_rows)
    load_tokens.wait()

    def permute(to):
        def one(at, carry):
            moved = mm(permutation, shards[at], NN).astype(BF16)
            for group in range(4):
                to[at, group] = moved[group * (shard_rows // 4) : (group + 1) * (shard_rows // 4)]
            return carry

        lax.fori_loop(0, latents, one, 0)

    permute(sent)
    pl.semaphore_wait(barrier, len(partners))
    exchange = Exchange(sent, got, sems, local_sems.at[0], 0, wide, here)
    exchange_cot = Exchange(sent_cot, cot_ref, sems, local_sems.at[1], 3, wide, here)
    gathers = [
        Gather(src, dst, sems, local_sems.at[2 + at], 6 + 5 * at, wide, here)
        for at, (src, dst) in enumerate(
            (
                (wqkv_src, wqkv_ref),
                (wout_src, wout_ref),
                (wup_src, wup_ref),
                (wdown_src, wdown_ref),
                (ktaps_src, ktaps_ref),
            )
        )
    ]
    g_qkv, g_out, g_up, g_down, g_taps = gathers
    exchange.start()
    load_cot = pltpu.make_async_copy(cot_hbm, shards, in_sems.at[0])
    load_cot.start()
    for one in gathers:
        one.start_near()

    load_ada.wait()
    for part in range(6):
        mod_ref[part : part + 1, :] = mm(
            silu_ref[...], ada[:, part * width : (part + 1) * width], NN
        )[0:1, :]
    load_cot.wait()
    permute(sent_cot)
    shift_one, scale_one, gate_one = mod_ref[0:1, :], mod_ref[1:2, :], mod_ref[2:3, :]
    shift_two, scale_two, gate_two = mod_ref[3:4, :], mod_ref[4:5, :], mod_ref[5:6, :]
    clear_edges(base)
    clear_edges(shifted)
    exchange.wait()
    g_qkv.start_far()
    g_out.start_far()
    for group in range(4):
        for source in range(latents):
            start = group * PHASE + source * ROWS
            x_ref[start : start + ROWS, :] = got[group, source]

    def norm_step(step, carry):
        group, part = step // (PHASE // ROWS), step % (PHASE // ROWS)
        unit, _ = normed(x_ref[ds(step * ROWS, ROWS), :].astype(F32))
        h_one = (unit * (1.0 + scale_one) + shift_one).astype(BF16)
        base[group, ds(HALF + part * ROWS, ROWS, HALF), :] = h_one.astype(F32)
        return carry

    lax.fori_loop(0, rows_all // ROWS, norm_step, 0)

    def conv_step(block, carry):
        lanes = ds(block * LANES, LANES)
        shift_cols(base, shifted, lanes)
        taps = [taps_ref[t : t + 1, lanes] for t in range(9)]

        def rows_step(step, carry):
            for group in range(4):
                total = jnp.zeros((ROWS, LANES), F32)
                for tap in range(9):
                    total += taps[tap] * tap_value(
                        base, shifted, group, tap // 3, tap % 3, step * ROWS, lanes
                    )
                u_ref[ds(group * PHASE + step * ROWS, ROWS), lanes] = total.astype(BF16)
            return carry

        return lax.fori_loop(0, PHASE // ROWS, rows_step, carry)

    lax.fori_loop(0, width // LANES, conv_step, 0)
    g_qkv.forward()
    g_out.forward()
    g_up.start_far()
    g_taps.start_far()
    g_qkv.forward_swapped()
    g_out.forward_swapped()
    g_qkv.finish()

    def project_step(step, carry):
        rows = ds(step * PHASE, PHASE)
        for part in range(3):
            cols = slice(part * width, (part + 1) * width)
            qkv_ref[rows, cols] = mm(u_ref[rows, :], wqkv_ref[:, cols], NT).astype(BF16)
        return carry

    lax.fori_loop(0, 4, project_step, 0)

    pairs = width // LANES
    first = lax.broadcasted_iota(jnp.int32, (PHASE, LANES), 1) < HEAD_DIM
    zero = jnp.zeros((PHASE, LANES), BF16)

    def attend_step(step, carry):
        group, pair = step // pairs, step % pairs
        rows = ds(group * PHASE, PHASE)
        query = qkv_ref[rows, ds(pair * LANES, LANES)]
        key = qkv_ref[rows, ds(width + pair * LANES, LANES)]
        value = qkv_ref[rows, ds(2 * width + pair * LANES, LANES)]
        found = []
        for head in range(2):
            own = jnp.where(first, query, zero) if head == 0 else jnp.where(first, zero, query)
            scores = mm(key, own, NT)
            top = jnp.max(scores, axis=0, keepdims=True)
            raised = jnp.exp2((scores - top) * (LOG2E * HEAD_DIM**-0.5))
            probs = (raised * (1.0 / jnp.sum(raised, axis=0, keepdims=True))).astype(BF16)
            probs_ref[step, :, head * PHASE : (head + 1) * PHASE] = probs
            found.append(mm(probs, value, TN))
        ctx_ref[rows, ds(pair * LANES, LANES)] = jnp.where(first, found[0], found[1]).astype(BF16)
        return carry

    lax.fori_loop(0, pairs, attend_step, 0)
    g_up.forward()
    g_taps.forward()
    exchange_cot.start()
    lax.fori_loop(pairs, 3 * pairs, attend_step, 0)
    g_up.forward_swapped()
    g_taps.forward_swapped()
    exchange_cot.wait()
    g_down.start_far()
    lax.fori_loop(3 * pairs, 4 * pairs, attend_step, 0)
    g_out.finish()

    def out_step(step, carry):
        rows = ds(step * PHASE, PHASE)
        total = mm(ctx_ref[rows, :], wout_ref[...], NN)
        att_ref[rows, :] = total.astype(BF16)
        x1_ref[rows, :] = x_ref[rows, :].astype(F32) + gate_one * total
        return carry

    lax.fori_loop(0, 4, out_step, 0)
    live = live_ref[0, 0]

    def second_step(step, carry):
        rows = ds(step * ROWS, ROWS)
        unit, _ = normed(x1_ref[rows, :])
        h2_ref[rows, :] = (unit * (1.0 + scale_two) + shift_two).astype(BF16)
        group, source = step // (PHASE // ROWS), step % (PHASE // ROWS)
        db_ref[rows, :] = (cot_ref[group, source].astype(F32) * live * gate_two).astype(BF16)
        return carry

    lax.fori_loop(0, rows_all // ROWS, second_step, 0)
    g_down.forward()
    for part in range(4):
        h2t_ref[:, part * PHASE : (part + 1) * PHASE] = h2_ref[
            part * PHASE : (part + 1) * PHASE, :
        ].T
    g_down.forward_swapped()
    for one in (g_up, g_taps, g_down):
        one.finish()


def whole(memory=pltpu.VMEM):
    return pl.BlockSpec(memory_space=memory)


def front(live, silu_row, taps, tokens, cot, w_ada, wqkv, wout, wup, wdown, ktaps):
    latents, shard_rows, width = tokens.shape
    rows = latents * shard_rows
    steps = 4 * (width // LANES)
    shape = jax.ShapeDtypeStruct
    full = lambda shard: shape((latents * shard.shape[0],) + shard.shape[1:], BF16)
    moved = (latents, 4, shard_rows // 4, width)
    return pl.pallas_call(
        front_kernel,
        out_shape=(
            shape((rows, width), BF16),
            shape((4, latents, shard_rows // 4, width), BF16),
            shape((6, width), F32),
            shape((rows, width), BF16),
            shape((rows, 3 * width), BF16),
            shape((steps, PHASE, 2 * PHASE), BF16),
            shape((rows, width), BF16),
            shape((rows, width), BF16),
            shape((rows, width), F32),
            shape((rows, width), BF16),
            shape((width, rows), BF16),
            shape((rows, width), BF16),
            full(wqkv),
            full(wout),
            full(wup),
            full(wdown),
            full(ktaps),
        ),
        in_specs=[whole(pltpu.SMEM)] + [whole()] * 2 + [whole(pl.ANY)] * 8,
        out_specs=(whole(),) * 14 + (whole(pl.ANY),) * 3,
        scratch_shapes=[
            pltpu.VMEM((4, PAD, width), F32),
            pltpu.VMEM((4, PAD, width), F32),
            pltpu.VMEM((latents, shard_rows, width), BF16),
            pltpu.VMEM(moved, BF16),
            pltpu.VMEM(moved, BF16),
            pltpu.VMEM((4, latents, shard_rows // 4, width), BF16),
            pltpu.VMEM(w_ada.shape, BF16),
            pltpu.SemaphoreType.DMA((2, 6 + 5 * 5)),
            pltpu.SemaphoreType.DMA((7,)),
            pltpu.SemaphoreType.DMA((2,)),
        ],
        compiler_params=pltpu.CompilerParams(
            vmem_limit_bytes=60 * MIB, collective_id=0, has_side_effects=True
        ),
        name="attn_forward",
    )(live, silu_row, taps, tokens, cot, w_ada, wqkv, wout, wup, wdown, ktaps)


def ffn_kernel(
    n_wide, live_ref, h2_ref, h2t_ref, db_ref, x1_ref, cot_ref, att_ref, mod_ref,
    wup_before, wup_even, wup_odd, wup_after, wdown_even, wdown_odd, taps_even, taps_odd,
    block_ref, dx1_ref, datt_ref, dmod_ref, sums_ref,
    hid_even, hid_odd, hid_moved, grad, grad_moved, slope, act, act_t, dhid, branch, dtaps,
    work, chip_sum, got_near, got_far, got_sums, sems, sum_sems,
):
    rows_all, width = h2_ref.shape
    dh2 = dx1_ref
    wide, here = lax.axis_index("wide"), lax.axis_index("narrow")
    step, steps = pl.program_id(0), pl.num_programs(0)
    quarters = [slice(q * PHASE, (q + 1) * PHASE) for q in range(4)]
    inside = slice(HALF, HALF + PHASE)
    lane_blocks = [slice(at * LANES, (at + 1) * LANES) for at in range(CHUNK // LANES)]
    col = lax.broadcasted_iota(jnp.int32, (ROWS, LANES), 0) % HALF

    partners = [(wide, here ^ 1), (wide, here ^ 2)] + wide_partners(wide, here, n_wide)[:HALVINGS]
    pieces, sum_rows = got_sums.shape[0], got_sums.shape[1]
    sums = [
        WideSum(sums_ref.at[at, : 2 * width], sums_ref.at[at, : 2 * width], None, got_sums.at[at], sum_sems,
                at * HALVINGS, wide, here, n_wide)
        for at in range(pieces)
    ]
    schedule = halvings_ahead(pieces, sums[0].levels)

    def to_near(at):
        return remote(work.at[at % 2], got_near.at[at], sems, at, wide, here ^ 1)

    def to_far(at):
        return remote(chip_sum.at[at], got_far.at[at], sems, steps + at, wide, here ^ 2)

    @pl.when(step == 0)
    def _():
        barrier = pltpu.get_barrier_semaphore()
        for partner in partners:
            pl.semaphore_signal(
                barrier, inc=1, device_id=partner, device_id_type=pl.DeviceIdType.MESH
            )
        for ref in (hid_even, hid_odd, hid_moved, grad, grad_moved):
            clear_edges(ref)
        branch[...] = jnp.zeros_like(branch)
        dh2[...] = jnp.zeros_like(dh2)
        dtaps[...] = jnp.zeros_like(dtaps)
        dhid[...] = jnp.zeros_like(dhid)
        full = mm(h2_ref[...], wup_even[...], NN)
        for q in range(4):
            hid_even[q, inside, :] = full[quarters[q]]
        pl.semaphore_wait(barrier, len(partners))

    def moved_cols(group, value):
        if group % 2:
            return jnp.where(col == 0, 0.0, pltpu.roll(value, 1, 0))
        return jnp.where(col == HALF - 1, 0.0, pltpu.roll(value, ROWS - 1, 0))

    def static_tap(base, shifted, group, tap_row, tap_col, start, lanes):
        src_row, row_move = tap_source(group // 2, tap_row)
        src_col, col_move = tap_source(group % 2, tap_col)
        ref = base if col_move == 0 else shifted
        first = HALF + row_move * HALF + start
        return ref[2 * src_row + src_col, first : first + ROWS, lanes]

    def weights_back(q, wup_last, slot):
        dh2[quarters[q], :] += mm(dhid[quarters[q], :], wup_last[...], NT)
        if q < width // PHASE:
            slot[quarters[q], :] = mm(h2t_ref[quarters[q], :], dhid[...], NN).astype(BF16)

    def forward(hid, wdown, taps_ref, wup_last, slot):
        taps = [[taps_ref[0, t : t + 1, lanes] for t in range(9)] for lanes in lane_blocks]
        for part in range(PHASE // ROWS):
            rows = slice(HALF + part * ROWS, HALF + (part + 1) * ROWS)
            for group in range(4):
                for lanes in lane_blocks:
                    hid_moved[group, rows, lanes] = moved_cols(group, hid[group, rows, lanes])
        for part in range(PHASE // ROWS):
            grad[part, inside, :] = mm(db_ref[quarters[part], :], wdown[...], NT)
            weights_back(part, wup_last, slot)
            for group in range(4):
                for at, lanes in enumerate(lane_blocks):
                    total = jnp.zeros((ROWS, LANES), F32)
                    for tap in range(9):
                        total += taps[at][tap] * static_tap(
                            hid, hid_moved, group, tap // 3, tap % 3, part * ROWS, lanes
                        )
                    square = total * total
                    turned = jnp.tanh(total * (square * (GELU_C * GELU_A) + GELU_C))
                    half = 0.5 * turned + 0.5
                    bend = total * (half - half * half)
                    start = group * PHASE + part * ROWS
                    act[start : start + ROWS, lanes] = (total * half).astype(BF16)
                    slope[start : start + ROWS, lanes] = half + bend * (
                        square * (6.0 * GELU_C * GELU_A) + 2.0 * GELU_C
                    )

    def backward(hid, hid_next, wdown, wup_next, taps_ref, slot):
        taps = [[taps_ref[0, t : t + 1, lanes] for t in range(9)] for lanes in lane_blocks]
        act_t[...] = act[...].T
        for part in range(PHASE // ROWS):
            rows = slice(HALF + part * ROWS, HALF + (part + 1) * ROWS)
            for group in range(4):
                start = group * PHASE + part * ROWS
                for lanes in lane_blocks:
                    value = grad[group, rows, lanes] * slope[start : start + ROWS, lanes]
                    grad[group, rows, lanes] = value
                    grad_moved[group, rows, lanes] = moved_cols(group, value)
        sums = [[jnp.zeros((8, LANES), F32) for _ in range(9)] for _ in lane_blocks]
        for part in range(PHASE // ROWS):
            hid_next[part, inside, :] = mm(h2_ref[quarters[part], :], wup_next[...], NN)
            branch[quarters[part], :] += mm(act[quarters[part], :], wdown[...], NN)
            if part < width // CHUNK:
                block = slice(part * CHUNK, (part + 1) * CHUNK)
                slot[width + part * CHUNK : width + (part + 1) * CHUNK, :] = mm(
                    act_t[...], db_ref[:, block], NN
                ).astype(BF16)
            for group in range(4):
                start = group * PHASE + part * ROWS
                for at, lanes in enumerate(lane_blocks):
                    own = hid[group, HALF + part * ROWS : HALF + (part + 1) * ROWS, lanes]
                    total = jnp.zeros((ROWS, LANES), F32)
                    for tap in range(9):
                        moved = static_tap(
                            grad, grad_moved, group, 2 - tap // 3, 2 - tap % 3, part * ROWS, lanes
                        )
                        total += taps[at][tap] * moved
                        sums[at][tap] += (own * moved).reshape(ROWS // 8, 8, LANES).sum(axis=0)
                    dhid[start : start + ROWS, lanes] = total.astype(BF16)
        for at, lanes in enumerate(lane_blocks):
            for tap in range(9):
                dtaps[tap : tap + 1, lanes] = jnp.sum(sums[at][tap], axis=0, keepdims=True)
        slot[2 * width :, :] = dtaps[...].astype(BF16)

    def settle(pair):
        to_near(pair).wait_recv()

        @pl.when(pair < steps // 2)
        def _():
            chip_sum[pair] = (work[2].astype(F32) + got_near[pair].astype(F32)).astype(BF16)
            to_far(pair).start()

        @pl.when(pair >= steps // 2)
        def _():
            part = pair - steps // 2
            to_far(part).wait_recv()
            sums_ref[part] = (
                work[2].astype(F32) + got_near[pair].astype(F32) + got_far[part].astype(F32)
            ).astype(BF16)

        for part in range(pieces):

            @pl.when(pair == steps // 2 + part)
            def _():
                for at in range(part):
                    sums[at].finish_half(part - at - 1)
                for at in range(part + 1):
                    if part - at < schedule[at]:
                        sums[at].start_half(part - at)

    forward(hid_even, wdown_even, taps_even, wup_before, work.at[2])

    @pl.when(step >= 1)
    def _():
        settle(step - 1)

    @pl.when(step >= 2)
    def _():
        to_near(step - 2).wait_send()

    even_slot = work.at[step % 2]
    backward(hid_even, hid_odd, wdown_even, wup_odd, taps_even, even_slot)
    forward(hid_odd, wdown_odd, taps_odd, wup_even, even_slot)
    to_near(step).start()
    backward(hid_odd, hid_even, wdown_odd, wup_after, taps_odd, work.at[2])

    @pl.when(step == steps - 1)
    def _():
        for q in range(4):
            weights_back(q, wup_odd, work.at[2])
        settle(step)
        gate_one, scale_two, gate_two = mod_ref[2:3, :], mod_ref[4:5, :], mod_ref[5:6, :]
        live = live_ref[0, 0]

        def fold(value):
            return value.reshape(ROWS // 8, 8, width).sum(axis=0)

        def rows_step(at, sums):
            rows = ds(at * ROWS, ROWS)
            after = x1_ref[rows, :]
            dout = cot_ref[rows, :].astype(F32) * live
            branch_rows = branch[rows, :]
            block_ref[rows, :] = ((after + gate_two * branch_rows) * live).astype(BF16)
            unit, inv = normed(after)
            dh2_rows = dh2[rows, :]
            dx1 = dout + norm_back(unit, inv, dh2_rows * (1.0 + scale_two))
            dx1_ref[rows, :] = dx1
            datt_ref[rows, :] = (dx1 * gate_one).astype(BF16)
            found = (dx1 * att_ref[rows, :].astype(F32), dh2_rows, dh2_rows * unit, dout * branch_rows)
            return tuple(total + fold(one) for total, one in zip(sums, found))

        start = tuple(jnp.zeros((8, width), F32) for _ in range(4))
        totals = lax.fori_loop(0, rows_all // ROWS, rows_step, start)
        for at in range(4):
            dmod_ref[at : at + 1, :] = jnp.sum(totals[at], axis=0, keepdims=True)
        for at in (steps - 2, steps - 1):
            to_near(at).wait_send()
        for at in range(steps // 2):
            to_far(at).wait_send()
        for at in range(pieces):
            sums[at].finish_half(schedule[at] - 1)
            for level in range(schedule[at]):
                sums[at].half_copy(level).wait_send()


def conv_back(grad, grad_moved, source, lanes, taps, dtaps_ref, out_ref):
    def rows_step(step, sums):
        sums = list(sums)
        for group in range(4):
            total = jnp.zeros((ROWS, LANES), F32)
            own = source[group, ds(HALF + step * ROWS, ROWS, HALF), lanes]
            for tap in range(9):
                moved = tap_value(
                    grad, grad_moved, group, 2 - tap // 3, 2 - tap % 3, step * ROWS, lanes
                )
                total += taps[tap] * moved
                sums[tap] += (own * moved).reshape(ROWS // 8, 8, LANES).sum(axis=0)
            out_ref[ds(group * PHASE + step * ROWS, ROWS), lanes] = total.astype(out_ref.dtype)
        return tuple(sums)

    start = tuple(jnp.zeros((8, LANES), F32) for _ in range(9))
    sums = lax.fori_loop(0, PHASE // ROWS, rows_step, start)
    for tap in range(9):
        dtaps_ref[tap : tap + 1, lanes] = jnp.sum(sums[tap], axis=0, keepdims=True)


def ffn(n_wide, live, h2, h2t, db, x1, cot, att, mod, wup, wdown, taps):
    rows, width = h2.shape
    shards, _, local = taps.shape
    per = local // CHUNK
    steps = shards * per // 2
    parcel = (2 * width + 16, CHUNK)
    shape = jax.ShapeDtypeStruct
    keep = lambda *block: pl.BlockSpec(
        block, lambda c: (0,) * len(block), pipeline_mode=pl.Buffered(1)
    )

    def slot_and_part(step, odd):
        return jnp.where(step < per, 3, 1) - odd, step % per

    def up_block(move, odd):
        def index(step):
            return slot_and_part(jnp.clip(step + move, 0, steps - 1), odd)

        return pl.BlockSpec((width, CHUNK), index)

    def down_block(odd):
        def index(step):
            slot, part = slot_and_part(step, odd)
            return slot * per + part, 0

        return pl.BlockSpec((CHUNK, width), index)

    def taps_block(odd):
        def index(step):
            slot, part = slot_and_part(step, odd)
            return slot, 0, part

        return pl.BlockSpec((1, 9, CHUNK), index)

    return pl.pallas_call(
        partial(ffn_kernel, n_wide),
        grid=(steps,),
        out_shape=(
            shape((rows, width), BF16),
            shape((rows, width), F32),
            shape((rows, width), BF16),
            shape((4, width), F32),
            shape((per,) + parcel, BF16),
        ),
        in_specs=[
            whole(pltpu.SMEM),
            keep(rows, width),
            keep(width, rows),
            keep(rows, width),
            keep(rows, width),
            keep(rows, width),
            keep(rows, width),
            keep(6, width),
            up_block(-1, 1),
            up_block(0, 0),
            up_block(0, 1),
            up_block(1, 0),
            down_block(0),
            down_block(1),
            taps_block(0),
            taps_block(1),
        ],
        out_specs=(
            keep(rows, width),
            keep(rows, width),
            keep(rows, width),
            keep(4, width),
            keep(per, *parcel),
        ),
        scratch_shapes=[pltpu.VMEM((4, PAD, CHUNK), F32)] * 5
        + [
            pltpu.VMEM((rows, CHUNK), F32),
            pltpu.VMEM((rows, CHUNK), BF16),
            pltpu.VMEM((CHUNK, rows), BF16),
            pltpu.VMEM((rows, CHUNK), BF16),
            pltpu.VMEM((rows, width), F32),
            pltpu.VMEM((16, CHUNK), F32),
            pltpu.VMEM((3,) + parcel, BF16),
            pltpu.VMEM((per,) + parcel, BF16),
            pltpu.VMEM((steps,) + parcel, BF16),
            pltpu.VMEM((per,) + parcel, BF16),
            pltpu.VMEM((per, sum_landing(2 * width, n_wide), CHUNK), BF16),
            pltpu.SemaphoreType.DMA((2, steps + per)),
            pltpu.SemaphoreType.DMA((2, per * HALVINGS)),
        ],
        compiler_params=pltpu.CompilerParams(
            vmem_limit_bytes=62 * MIB, collective_id=1, has_side_effects=True
        ),
        name="feed_forward",
    )(live, h2, h2t, db, x1, cot, att, mod, wup, wup, wup, wup, wdown, wdown, taps, taps)


def attn_backward_kernel(
    n_wide, datt_ref, ctx_ref, u_ref, wout_ref, parcels, qkv_hbm, probs_hbm,
    dqkv_ref, own_ref, full, gtaps_ref,
    dctx, probs_buf, weights, got_near, chip_sum, got_far, work, got_sums, taps_sum, taps_got,
    sems, in_sems, sum_sems,
):
    rows_all, width = u_ref.shape
    wide, here = lax.axis_index("wide"), lax.axis_index("narrow")
    pairs = width // LANES
    half_pairs = pairs // 2
    steps = 4 * pairs
    load_qkv = pltpu.make_async_copy(qkv_hbm, dqkv_ref, in_sems.at[2])
    load_qkv.start()

    def pair_of(step):
        return (half_pairs + step // 4) % pairs

    def load_probs(step):
        return pltpu.make_async_copy(
            probs_hbm.at[(step % 4) * pairs + pair_of(step)], probs_buf.at[step % 2], in_sems.at[step % 2]
        )

    load_probs(0).start()
    greet([(wide, here ^ 2), (wide, here ^ 1)] + wide_partners(wide, here, n_wide))
    pieces = full.shape[0]
    rows = full.shape[1]
    per_sum = sum_semaphores(n_wide)
    ahead = halvings_ahead(pieces, min(HALVINGS, n_wide.bit_length() - 1))
    sums = [
        WideSum(parcels.at[at, :rows], work.at[at], full.at[at], got_sums.at[at], sum_sems, at * per_sum,
                wide, here, n_wide, done=ahead[at])
        for at in range(pieces)
    ]
    levels = n_wide.bit_length() - 1
    queues = [one.actions() for one in sums]

    def advance(*which):
        for at in which:
            if queues[at]:
                for act in queues[at].pop(0):
                    act()

    def taps_copy(level):
        return remote(taps_sum.at[level], taps_got.at[level], sems, 3 + level, wide ^ (1 << level), here)

    def taps_add(level):
        taps_copy(level).wait_recv()
        taps_sum[level + 1] = taps_sum[level] + taps_got[level]
        if level + 1 < levels:
            taps_copy(level + 1).start()

    for at in range(pieces):
        taps_sum[0, :, at * CHUNK : (at + 1) * CHUNK] = parcels[at, rows:, :].astype(F32)
    taps_copy(0).start()
    advance(2, 0, 1)

    def ctx_step(step, carry):
        span = ds(step * PHASE, PHASE)
        dctx[span, :] = mm(datt_ref[span, :], wout_ref[...], NT).astype(BF16)
        return carry

    lax.fori_loop(0, 4, ctx_step, 0)
    load_qkv.wait()

    first = lax.broadcasted_iota(jnp.int32, (PHASE, LANES), 1) < HEAD_DIM
    zero = jnp.zeros((PHASE, LANES), BF16)
    scale = HEAD_DIM**-0.5

    def attend(step):
        group, pair = step % 4, pair_of(step)
        load_probs(step).wait()

        @pl.when(step + 1 < steps)
        def _():
            load_probs(step + 1).start()

        span = ds(group * PHASE, PHASE)
        query = dqkv_ref[span, ds(pair * LANES, LANES)]
        key = dqkv_ref[span, ds(width + pair * LANES, LANES)]
        value = dqkv_ref[span, ds(2 * width + pair * LANES, LANES)]
        dctx_pair = dctx[span, ds(pair * LANES, LANES)]
        dq, dk, dv = [], None, None
        for head in range(2):
            own = lambda both: jnp.where(first, both, zero) if head == 0 else jnp.where(first, zero, both)
            probs = probs_buf[step % 2, :, head * PHASE : (head + 1) * PHASE]
            probs_f = probs.astype(F32)
            dctx_own, query_own = own(dctx_pair), own(query)
            dprobs = mm(value, dctx_own, NT)
            inner = jnp.sum(dprobs * probs_f, axis=0, keepdims=True)
            dscores = (probs_f * (dprobs - inner)).astype(BF16)
            dv_one = mm(probs, dctx_own, NN)
            dk_one = mm(dscores, query_own, NN)
            dv = dv_one if dv is None else dv + dv_one
            dk = dk_one if dk is None else dk + dk_one
            dq.append(mm(dscores, key, TN))
        dqkv_ref[span, ds(pair * LANES, LANES)] = (
            jnp.where(first, dq[0], dq[1]) * scale
        ).astype(BF16)
        dqkv_ref[span, ds(width + pair * LANES, LANES)] = (dk * scale).astype(BF16)
        dqkv_ref[span, ds(2 * width + pair * LANES, LANES)] = dv.astype(BF16)

    def attend_loop(begin, end, plan):
        def body(step, carry):
            for at, what in plan:
                pl.when(step == at)(what)
            attend(step)
            return carry

        lax.fori_loop(begin, end, body, 0)

    def weight_grads(half):
        span = width // 2
        slab = span // 2
        for part in range(4):
            cols = slice(half * span, (half + 1) * span)
            if part < 3:
                left = dqkv_ref[:, part * width + half * span : part * width + (half + 1) * span]
                found = mm(left, u_ref[...], TN).astype(BF16)
            else:
                found = mm(ctx_ref[:, cols], datt_ref[...], TN).astype(BF16)
            for one in range(2):
                weights[2 * half + one, part * slab : (part + 1) * slab, :] = found[
                    one * slab : (one + 1) * slab
                ]

    near_early = remote(weights.at[3], got_near.at[0], sems, 0, wide, here ^ 1)
    near_late = remote(weights.at[1], got_near.at[1], sems, 1, wide, here ^ 1)
    far = remote(chip_sum, got_far, sems, 2, wide, here ^ 2)

    later = lambda *which: partial(advance, *which)
    attend_loop(
        0, steps // 2,
        [(2, later(2, 0)), (5, later(1)), (7, partial(taps_add, 0)), (8, later(2, 0)), (11, later(1))],
    )
    weight_grads(1)
    near_early.start()
    advance(2)
    near_early.wait_recv()
    chip_sum[...] = (weights[2].astype(F32) + got_near[0].astype(F32)).astype(BF16)
    far.start()
    attend_loop(
        steps // 2, steps,
        [(13, later(1, 0)), (14, partial(taps_add, 1)), (16, later(2))],
    )
    weight_grads(0)
    near_late.start()
    for level in range(2, levels):
        taps_add(level)
    gtaps_ref[...] = taps_sum[levels]
    near_late.wait_recv()
    while any(queues):
        advance(0, 1, 2)
    far.wait_recv()
    own_ref[...] = (
        weights[0].astype(F32) + got_near[1].astype(F32) + got_far[...].astype(F32)
    ).astype(BF16)
    for one in sums:
        one.wait_sends()
    for level in range(levels):
        taps_copy(level).wait_send()
    near_early.wait_send()
    near_late.wait_send()
    far.wait_send()


def attn_backward(n_wide, datt, ctx, u, wout, parcels, qkv, probs):
    rows, width = u.shape
    slots = lax.axis_size("narrow")
    slab = wout.shape[0] // slots
    pieces, parcel_rows, _ = parcels.shape
    sum_rows = parcel_rows - 16
    shape = jax.ShapeDtypeStruct
    levels = n_wide.bit_length() - 1
    per_sum = sum_semaphores(n_wide)
    return pl.pallas_call(
        partial(attn_backward_kernel, n_wide),
        out_shape=(
            shape((rows, 3 * width), BF16),
            shape((4 * slab, width), BF16),
            shape((pieces, sum_rows, CHUNK), BF16),
            shape((16, pieces * CHUNK), F32),
        ),
        in_specs=[whole()] * 5 + [whole(pl.ANY)] * 2,
        out_specs=(whole(),) * 4,
        scratch_shapes=[
            pltpu.VMEM((rows, width), BF16),
            pltpu.VMEM((2, PHASE, 2 * PHASE), BF16),
            pltpu.VMEM((slots, 4 * slab, width), BF16),
            pltpu.VMEM((2, 4 * slab, width), BF16),
            pltpu.VMEM((4 * slab, width), BF16),
            pltpu.VMEM((4 * slab, width), BF16),
            pltpu.VMEM((pieces, sum_rows, CHUNK), BF16),
            pltpu.VMEM((pieces, sum_landing(sum_rows, n_wide), CHUNK), BF16),
            pltpu.VMEM((levels + 1, 16, pieces * CHUNK), F32),
            pltpu.VMEM((levels, 16, pieces * CHUNK), F32),
            pltpu.SemaphoreType.DMA((2, 3 + levels)),
            pltpu.SemaphoreType.DMA((3,)),
            pltpu.SemaphoreType.DMA((2, pieces * per_sum)),
        ],
        compiler_params=pltpu.CompilerParams(
            vmem_limit_bytes=56 * MIB, collective_id=2, has_side_effects=True
        ),
        name="attn_backward",
    )(datt, ctx, u, wout, parcels, qkv, probs)


def one_hot(rows, columns, wanted):
    row = lax.broadcasted_iota(jnp.int32, (rows, columns), 0)
    column = lax.broadcasted_iota(jnp.int32, (rows, columns), 1)
    return jnp.where(column == wanted(row), 1.0, 0.0).astype(BF16)


SMALL = 16


def input_backward_kernel(
    n_wide, x_ref, dx1_ref, dqkv_ref, mod_ref, taps_ref, wqkv_ref, own_ref, silu_ref, dmod_ref, block_in,
    got_dx, got_block, full, small, dtaps_ref,
    base, shifted, first_in, dh1, dx, work, got_sums, tap_sums, tap_got, sems, local_sems, sum_sems, small_sems,
):
    rows_all, width = x_ref.shape
    wide, here = lax.axis_index("wide"), lax.axis_index("narrow")
    shift_one, scale_one = mod_ref[0:1, :], mod_ref[1:2, :]
    greet([(wide, peer) for peer in narrow_peers(here)] + wide_partners(wide, here, n_wide))
    pieces = full.shape[0]
    rows = full.shape[1]
    per_sum = sum_semaphores(n_wide)
    sums = [
        WideSum(own_ref.at[at * rows : (at + 1) * rows], work.at[at], full.at[at], got_sums.at[at], sum_sems,
                at * per_sum, wide, here, n_wide)
        for at in range(pieces)
    ]
    queues = [one.actions() for one in sums]

    def advance(*which):
        for at in which:
            if queues[at]:
                for act in queues[at].pop(0):
                    act()

    advance(0, 1)
    block_back = Return(block_in, got_block, sems, local_sems.at[1], 3, wide, here)
    block_back.start()
    clear_edges(base)
    clear_edges(shifted)

    def norm_step(step, carry):
        group, part = step // (PHASE // ROWS), step % (PHASE // ROWS)
        unit, _ = normed(x_ref[ds(step * ROWS, ROWS), :].astype(F32))
        h_one = (unit * (1.0 + scale_one) + shift_one).astype(BF16)
        first_in[group, ds(HALF + part * ROWS, ROWS, HALF), :] = h_one.astype(F32)
        return carry

    lax.fori_loop(0, rows_all // ROWS, norm_step, 0)

    def du_step(group, carry):
        span = ds(group * PHASE, PHASE)
        total = None
        for part in range(3):
            cols = slice(part * width, (part + 1) * width)
            one = mm(dqkv_ref[span, cols], wqkv_ref[:, cols], NN)
            total = one if total is None else total + one
        base[group, HALF : HALF + PHASE, :] = total
        return carry

    lax.fori_loop(0, 3, du_step, 0)
    advance(0)
    lax.fori_loop(3, 4, du_step, 0)

    def conv_step(block, carry):
        lanes = ds(block * LANES, LANES)
        shift_cols(base, shifted, lanes)
        conv_back(base, shifted, first_in, lanes, [taps_ref[t : t + 1, lanes] for t in range(9)],
                  dtaps_ref, dh1)
        return carry

    for block in range(width // LANES):
        if block % 2:
            advance(0)
        else:
            advance(1)
        lax.fori_loop(block, block + 1, conv_step, 0)

    def fold(value):
        return value.reshape(ROWS // 8, 8, width).sum(axis=0)

    back = Return(dx, got_dx, sems, local_sems.at[0], 0, wide, here)

    def rows_step(at, sums):
        source = (at // 4 + 2) % 4 ^ here
        group = at % 4
        span = ds(group * PHASE + source * ROWS, ROWS)
        unit, inv = normed(x_ref[span, :].astype(F32))
        grad = dh1[span, :]
        dx[group, source] = (
            dx1_ref[span, :] + norm_back(unit, inv, grad * (1.0 + scale_one))
        ).astype(BF16)
        return tuple(total + fold(one) for total, one in zip(sums, (grad, grad * unit)))

    found = tuple(jnp.zeros((8, width), F32) for _ in range(2))
    for at in range(4):
        found = lax.fori_loop(4 * at, 4 * at + 4, rows_step, found)
        if at < 2:
            back.copies[at].start()
        elif at == 3:
            back.copies[2].start()
    back.own.start()
    dmod = [jnp.sum(one, axis=0, keepdims=True) for one in found]
    dmod += [dmod_ref[at : at + 1, :] for at in range(4)]

    partners = wide_partners(wide, here, n_wide)[::-1] + [(wide, here ^ 2), (wide, here ^ 1)]
    levels = len(partners)
    stack = jnp.concatenate([silu_ref[0:1, :].astype(F32)] + dmod + [jnp.zeros((SMALL - 7, width), F32)])
    small[0] = stack.astype(BF16)
    tap_sums[0, :9, :] = dtaps_ref[:9, :]
    tap_sums[0, 9:, :] = jnp.zeros((7, width), F32)

    def small_copies(level):
        have = 1 << level
        return (
            remote(small.at[:have], small.at[have : 2 * have], small_sems, 2 * level, *partners[level]),
            remote(tap_sums.at[level], tap_got.at[level], small_sems, 2 * level + 1, *partners[level]),
        )

    def small_start(level):
        for copy in small_copies(level):
            copy.start()

    def small_finish(level):
        for copy in small_copies(level):
            copy.wait_recv()
        tap_sums[level + 1] = tap_sums[level] + tap_got[level]

    small_start(0)
    advance(0, 1)
    for level in range(levels):
        small_finish(level)
        if level + 1 < levels:
            small_start(level + 1)
        if level == 1:
            advance(0, 1)
    dtaps_ref[...] = tap_sums[levels]
    while any(queues):
        advance(0, 1)
    block_back.wait()
    back.wait()
    for level in range(levels):
        for copy in small_copies(level):
            copy.wait_send()
    for one in sums:
        one.wait_sends()


def input_backward(n_wide, x, dx1, dqkv, mod, taps, wqkv, own, silu_row, dmod, block):
    rows, width = x.shape
    slots = lax.axis_size("narrow")
    pieces = 2
    sum_rows = own.shape[0] // pieces
    shape = jax.ShapeDtypeStruct
    per_sum = sum_semaphores(n_wide)
    levels = (n_wide * slots).bit_length() - 1
    back = shape((slots, 4, rows // (4 * slots), width), BF16)
    return pl.pallas_call(
        partial(input_backward_kernel, n_wide),
        out_shape=(
            back,
            back,
            shape((pieces, sum_rows, width), BF16),
            shape((1 << levels, SMALL, width), BF16),
            shape((SMALL, width), F32),
        ),
        in_specs=[whole()] * 10,
        out_specs=(whole(),) * 5,
        scratch_shapes=[pltpu.VMEM((4, PAD, width), F32)] * 3
        + [
            pltpu.VMEM((rows, width), F32),
            pltpu.VMEM((4, slots, rows // (4 * slots), width), BF16),
            pltpu.VMEM((pieces, sum_rows, width), BF16),
            pltpu.VMEM((pieces, sum_landing(sum_rows, n_wide), width), BF16),
            pltpu.VMEM((levels + 1, SMALL, width), F32),
            pltpu.VMEM((levels, SMALL, width), F32),
            pltpu.SemaphoreType.DMA((2, 6)),
            pltpu.SemaphoreType.DMA((2,)),
            pltpu.SemaphoreType.DMA((2, pieces * per_sum)),
            pltpu.SemaphoreType.DMA((2, 2 * levels)),
        ],
        compiler_params=pltpu.CompilerParams(
            vmem_limit_bytes=56 * MIB, collective_id=3, has_side_effects=True
        ),
        name="input_backward",
    )(x, dx1, dqkv, mod, taps, wqkv, own, silu_row, dmod, block)


def outputs_kernel(
    dx_in, block_in, attn_sum, ffn_sum, small, cond_ref, ada_hbm,
    gada_hbm, dx_hbm, block_hbm, gqkv_hbm, gout_hbm, gup_hbm, gdown_hbm, gcond_ref,
    ada, gada, dx, block, gqkv, gout, gup, gdown, sems, in_sem,
):
    width = small.shape[-1]
    here = lax.axis_index("narrow")
    load_ada = pltpu.make_async_copy(ada_hbm, ada, in_sem.at[0])
    load_ada.start()
    started = []

    def put(src, dst):
        copy = pltpu.make_async_copy(src, dst, sems.at[len(started)])
        copy.start()
        started.append(copy)

    devices = small.shape[0]
    shares = small[...].reshape(devices * SMALL, width)
    pick = lambda row: mm(
        one_hot(devices, devices * SMALL, lambda at: at * SMALL + row), shares, NN
    ).astype(BF16)
    silu_all = pick(0)
    for part in range(6):
        gada[part] = mm(silu_all, pick(1 + part), TN)
        put(gada.at[part], gada_hbm.at[:, part * width : (part + 1) * width])
    slab = attn_sum.shape[1] // 2
    for part in range(3):
        gqkv[part] = attn_sum[part // 2, (part % 2) * slab : (part % 2 + 1) * slab, :].astype(F32).T
        put(gqkv.at[part], gqkv_hbm.at[part])
    gout[...] = attn_sum[1, slab:, :].astype(F32)
    put(gout, gout_hbm)
    permutation = group_permutation(dx_in.shape[1] * dx_in.shape[2])
    for at in range(dx_in.shape[0]):
        for source, held, out in ((dx_in, dx, dx_hbm), (block_in, block, block_hbm)):
            groups = jnp.concatenate([source[at, group] for group in range(4)], axis=0)
            held[at] = mm(permutation, groups, TN).astype(held.dtype)
            put(held.at[at], out.at[at])
    for at in range(ffn_sum.shape[0]):
        cols = slice(at * CHUNK, (at + 1) * CHUNK)
        gup[:, cols] = ffn_sum[at, :width, :].astype(F32)
        for part in range(width // CHUNK):
            span = slice(width + part * CHUNK, width + (part + 1) * CHUNK)
            gdown[cols, part * CHUNK : (part + 1) * CHUNK] = ffn_sum[at, span, :].astype(F32)
        put(gdown.at[cols], gdown_hbm.at[cols])
    put(gup, gup_hbm)

    def own_column(row, part):
        away = row ^ here
        place = ((away // 2) % 2) * (devices // 4) + (away % 2) * (devices // 2)
        return jnp.where(row < cond_ref.shape[0], place * SMALL + 1 + part, -1)

    load_ada.wait()
    grad_silu = jnp.zeros((16, width), F32)
    for part in range(6):
        own = mm(
            one_hot(16, devices * SMALL, lambda row, part=part: own_column(row, part)), shares, NN
        ).astype(BF16)
        grad_silu += mm(own, ada[:, part * width : (part + 1) * width], NT)
    cond = cond_ref[...].astype(F32)
    gate = 1.0 / (1.0 + jnp.exp(-cond))
    gcond_ref[...] = grad_silu[: cond_ref.shape[0]] * (gate * (1.0 + cond * (1.0 - gate)))
    for copy in started:
        copy.wait()


def outputs(dx, block, attn_sum, ffn_sum, small, cond, w_ada):
    slots, _, quarter, width = dx.shape
    slab = attn_sum.shape[1] // 2
    pieces = ffn_sum.shape[0]
    local = pieces * CHUNK
    shape = jax.ShapeDtypeStruct
    tokens = (slots, 4 * quarter, width)
    return pl.pallas_call(
        outputs_kernel,
        out_shape=(
            shape(w_ada.shape, F32),
            shape(tokens, F32),
            shape(tokens, BF16),
            shape((3, width, slab), F32),
            shape((slab, width), F32),
            shape((width, local), F32),
            shape((local, width), F32),
            shape(cond.shape, F32),
        ),
        in_specs=[whole()] * 6 + [whole(pl.ANY)],
        out_specs=(whole(pl.ANY),) * 7 + (whole(),),
        scratch_shapes=[
            pltpu.VMEM(w_ada.shape, BF16),
            pltpu.VMEM((6, width, width), F32),
            pltpu.VMEM(tokens, F32),
            pltpu.VMEM(tokens, BF16),
            pltpu.VMEM((3, width, slab), F32),
            pltpu.VMEM((slab, width), F32),
            pltpu.VMEM((width, local), F32),
            pltpu.VMEM((local, width), F32),
            pltpu.SemaphoreType.DMA((6 + 3 + 1 + 2 * slots + pieces + 1,)),
            pltpu.SemaphoreType.DMA((1,)),
        ],
        compiler_params=pltpu.CompilerParams(vmem_limit_bytes=56 * MIB),
        name="outputs",
    )(dx, block, attn_sum, ffn_sum, small, cond, w_ada)


def per_device(
    tokens, condition, cotangent, counts, w_ada, k_attn, w_qkv, w_out, w_up, k_ffn, w_down
):
    lat_dev, shard_rows, width = tokens.shape
    here = lax.axis_index("narrow")
    rows_all = shard_rows * lat_dev
    local = w_up.shape[1]

    n_wide = lax.axis_size("wide")
    qkv_t = w_qkv.transpose(2, 1, 0).reshape(w_qkv.shape[2], 3 * width)
    ktaps_own = jnp.pad(k_ffn.reshape(9, local), ((0, 23), (0, 0)))
    attn_taps = k_attn.reshape(9, width).astype(F32)

    cond_f = condition.astype(F32)
    silu_low = jax.nn.silu(cond_f).astype(BF16)
    own_silu = jnp.broadcast_to(lax.dynamic_slice_in_dim(silu_low, here, 1, 0), (16, width))
    live = (here < counts[0]).astype(F32).reshape(1, 1)

    (x, cot, mod, u, qkv, probs, ctx, att, x1, h2, h2t, db, wqkv, wout, wup, wdown, ktaps) = front(
        live, own_silu, attn_taps, tokens, cotangent, w_ada, qkv_t, w_out, w_up, w_down, ktaps_own
    )
    cot = cot.reshape(rows_all, width)
    ffn_taps = ktaps.reshape(lat_dev, -1, local)[:, :9].astype(F32)
    block_g, dx1, datt, dmod_mid, parcels = ffn(
        n_wide, live, h2, h2t, db, x1, cot, att, mod, wup, wdown, ffn_taps
    )
    block_g = block_g.reshape(4, lat_dev, shard_rows // 4, width)
    dqkv, own, ffn_sum, gtaps = attn_backward(n_wide, datt, ctx, u, wout, parcels, qkv, probs)
    got_dx, got_block, attn_sum, small, dattn_taps = input_backward(
        n_wide, x, dx1, dqkv, mod, attn_taps, wqkv, own, own_silu, dmod_mid, block_g
    )
    grad_w_ada, grad_tokens, block, gqkv, grad_w_out, grad_w_up, grad_w_down, grad_condition = outputs(
        got_dx, got_block, attn_sum, ffn_sum, small, condition, w_ada
    )
    grad_k_ffn = gtaps[:9].reshape(3, 3, local)
    grad_k_attn = dattn_taps[:9].reshape(3, 3, width)
    grad_w_qkv = gqkv.transpose(1, 0, 2)
    return (
        block,
        grad_tokens,
        grad_condition,
        grad_w_ada,
        grad_k_attn,
        grad_w_qkv,
        grad_w_out,
        grad_w_up,
        grad_k_ffn,
        grad_w_down,
    )


def solution(mesh):
    placed = (
        P("wide", "narrow", None),
        P("wide", None),
        P("wide", "narrow", None),
        P("wide"),
        P(),
        P(),
        P(None, None, "narrow"),
        P("narrow", None),
        P(None, "narrow"),
        P(None, None, "narrow"),
        P("narrow", None),
    )
    return jax.shard_map(
        per_device,
        mesh=mesh,
        in_specs=placed,
        out_specs=(
            P("wide", "narrow", None),
            P("wide", "narrow", None),
            P("wide", None),
            P(),
            P(),
            P(None, None, "narrow"),
            P("narrow", None),
            P(None, "narrow"),
            P(None, None, "narrow"),
            P("narrow", None),
        ),
        check_vma=False,
    )
```

```python
from functools import partial

import jax
import jax.numpy as jnp
from jax import lax
from jax.experimental import pallas as pl
from jax.experimental.pallas import tpu as pltpu
from jax.sharding import PartitionSpec as P

HEAD_DIM = 64
SIDE = 32
HALF = SIDE // 2
PHASE = HALF * HALF
PAD = PHASE + 2 * HALF
LANES = 128
ROWS = 64
CHUNK = 256
LOG2E = 1.4426950408889634
GELU_C = 0.7978845608028654
GELU_A = 0.044715
MIB = 1 << 20
F32 = jnp.float32
BF16 = jnp.bfloat16

NN = (((1,), (0,)), ((), ()))
NT = (((1,), (1,)), ((), ()))
TN = (((0,), (0,)), ((), ()))


def mm(left, right, dims):
    return lax.dot_general(left, right, dims, preferred_element_type=F32)


def ds(start, size, unit=None):
    return pl.ds(pl.multiple_of(start, unit or size), size)


def tap_source(parity, tap):
    return {-1: (1, -1), 0: (0, 0), 1: (1, 0), 2: (0, 1)}[parity + tap - 1]


def shift_cols(base, shifted, lanes):
    col = lax.broadcasted_iota(jnp.int32, (ROWS, LANES), 0) % HALF

    def rows_step(step, carry):
        for group in range(4):
            rows = ds(HALF + step * ROWS, ROWS, HALF)
            value = base[group, rows, lanes]
            if group % 2:
                moved = jnp.where(col == 0, 0.0, pltpu.roll(value, 1, 0))
            else:
                moved = jnp.where(col == HALF - 1, 0.0, pltpu.roll(value, ROWS - 1, 0))
            shifted[group, rows, lanes] = moved
        return carry

    lax.fori_loop(0, PHASE // ROWS, rows_step, 0)


def clear_edges(ref):
    edge = jnp.zeros((HALF, ref.shape[-1]), ref.dtype)
    for group in range(4):
        ref[group, :HALF, :] = edge
        ref[group, PAD - HALF :, :] = edge


def tap_value(base, shifted, group, tap_row, tap_col, start, lanes):
    src_row, row_move = tap_source(group // 2, tap_row)
    src_col, col_move = tap_source(group % 2, tap_col)
    ref = base if col_move == 0 else shifted
    return ref[2 * src_row + src_col, ds(HALF + row_move * HALF + start, ROWS, HALF), lanes]


def normed(values_in):
    mean_val = jnp.mean(values_in, axis=-1, keepdims=True)
    centred = values_in - mean_val
    inv = lax.rsqrt(jnp.mean(centred * centred, axis=-1, keepdims=True) + 1e-06)
    return centred * inv, inv


def norm_back(unit, inv, grad):
    mean_grad = jnp.mean(grad, axis=-1, keepdims=True)
    mean_dot = jnp.mean(grad * unit, axis=-1, keepdims=True)
    return (grad - mean_grad - unit * mean_dot) * inv


def narrow_peers(here):
    return [here ^ 2, here ^ 3, here ^ 1]


def remote(src, dst, sems, at, wide, narrow):
    return pltpu.make_async_remote_copy(
        src_ref=src,
        dst_ref=dst,
        send_sem=sems.at[0, at],
        recv_sem=sems.at[1, at],
        device_id=(wide, narrow),
        device_id_type=pl.DeviceIdType.MESH,
    )


class Gather:
    COPIES = 11

    def __init__(self, src, dst, sems, local_sem, first, wide, here):
        count = src.shape[0]
        quarter = count // 4
        front = -(-quarter // 32) * 16
        mine = wide % 4
        far, near = here ^ 2, here ^ 1

        def slot(k):
            return dst.at[k * count : (k + 1) * count]

        def at(k, which, start=0, size=quarter):
            return dst.at[ds(k * count + which * quarter + start, size, 16)]

        def send(number, source, target, wide_to, narrow_to):
            return remote(source, target, sems, first + number, wide_to, narrow_to)

        def same(number, which, wide_to, start=0, size=quarter):
            return send(number, at(2, which, start, size), at(2, which, start, size), wide_to, here)

        def share(number, which, start=0, size=quarter):
            return send(number, at(2, which, start, size), at(3, which, start, size), wide, near)

        own_part = src.at[ds(mine * quarter, quarter, 16)]
        rest = quarter - front
        self.own = pltpu.make_async_copy(src, slot(0), local_sem)
        self.near = send(0, src, slot(1), wide, near)
        self.far = send(1, own_part, at(2, mine), wide, far)
        self.swaps = [same(2, mine, wide ^ 1), same(3, mine, wide ^ 2)]
        self.corners = [same(4, mine ^ 1, wide ^ 2, 0, front), same(5, mine ^ 2, wide ^ 1, front, rest)]
        self.shares = [
            share(6, mine),
            share(7, mine ^ 1),
            share(8, mine ^ 2),
            share(9, mine ^ 3, 0, front),
            share(10, mine ^ 3, front, rest),
        ]

    def start_near(self):
        self.own.start()
        self.near.start()

    def start_far(self):
        self.far.start()

    def swap(self):
        self.far.wait_recv()
        self.swaps[0].start()
        self.swaps[1].start()
        self.shares[0].start()

    def corner(self):
        for which in range(2):
            self.swaps[which].wait_recv()
            self.corners[which].start()
            self.shares[1 + which].start()

    def share_corner(self):
        for which in range(2):
            self.corners[which].wait_recv()
            self.shares[3 + which].start()

    def finish(self):
        self.own.wait()
        self.near.wait()
        self.far.wait_send()
        for copy in self.swaps + self.corners:
            copy.wait_send()
        for copy in self.shares:
            copy.wait()


def group_permutation(rows):
    out = lax.broadcasted_iota(jnp.int32, (rows, rows), 0)
    source = lax.broadcasted_iota(jnp.int32, (rows, rows), 1)
    per_group = rows // 4
    group, rest = out // per_group, out % per_group
    line = 2 * (rest // HALF) + group // 2
    wanted = line * SIDE + 2 * (rest % HALF) + group % 2
    return jnp.where(source == wanted, 1.0, 0.0).astype(BF16)


class Exchange:
    def __init__(self, sent, got, sems, local_sem, first, wide, here):
        self.own = pltpu.make_async_copy(sent.at[here], got.at[:, here], local_sem)
        self.copies = [
            remote(sent.at[peer], got.at[:, here], sems, first + at, wide, peer)
            for at, peer in enumerate(narrow_peers(here))
        ]

    def start(self):
        for copy in self.copies:
            copy.start()
        self.own.start()

    def wait(self):
        self.own.wait()
        for copy in self.copies:
            copy.wait()


class Return:
    def __init__(self, sent, got, sems, local_sem, first, wide, here):
        self.own = pltpu.make_async_copy(sent.at[:, here], got.at[here], local_sem)
        self.copies = [
            remote(sent.at[:, peer], got.at[here], sems, first + at, wide, peer)
            for at, peer in enumerate(narrow_peers(here))
        ]

    start = Exchange.start
    wait = Exchange.wait


HALVINGS = 3


class WideSum:
    def __init__(self, source, work, full, got, sems, first, wide, here, n_wide, done=0):
        self.source, self.work, self.full, self.got = source, work, full, got
        self.rows = work.shape[0]
        self.levels = min(HALVINGS, n_wide.bit_length() - 1)
        self.extra = n_wide.bit_length() - 1 - self.levels
        self.done = done
        self.wide, self.here, self.sems, self.first = wide, here, sems, first
        self.offsets = [0]
        for level in range(self.levels):
            bit = (wide // 2**level) % 2
            self.offsets.append(self.offsets[-1] + bit * (self.rows >> (level + 1)))
        self.waiting = []

    def size(self, level):
        return self.rows >> level

    def at(self, ref, offset, size):
        return ref.at[ds(offset, size, 16)]

    def half_copy(self, level):
        size, base = self.size(level + 1), self.offsets[level]
        send = base + size - (self.offsets[level + 1] - base)
        source = self.source if level == self.done else self.work
        landing = self.rows - self.size(level)
        return remote(
            self.at(source, send, size), self.got.at[landing : landing + size],
            self.sems, self.first + level, self.wide ^ (1 << level), self.here,
        )

    def start_half(self, level):
        self.half_copy(level).start()

    def finish_half(self, level):
        self.half_copy(level).wait_recv()
        size, landing = self.size(level + 1), self.rows - self.size(level)
        rows = ds(self.offsets[level + 1], size, 16)
        source = self.source if level == self.done else self.work
        self.work[rows, :] = (
            source[rows, :].astype(F32) + self.got[landing : landing + size, :].astype(F32)
        ).astype(BF16)

    def extras(self):
        size = self.size(self.levels)
        rows = ds(self.offsets[self.levels], size, 16)
        source = self.source if self.done == self.levels else self.work
        self.full[rows, :] = source[rows, :]
        for at in range(self.extra):
            landing = self.rows - size + at * size
            copy = remote(
                self.full.at[rows], self.got.at[landing : landing + size],
                self.sems, self.first + 2 * self.levels + at,
                self.wide ^ (1 << (self.levels + at)), self.here,
            )
            copy.start()
            copy.wait()
            self.full[rows, :] = (
                self.full[rows, :].astype(F32) + self.got[landing : landing + size, :].astype(F32)
            ).astype(BF16)

    def spread_copy(self, level):
        part = self.at(self.full, self.offsets[level + 1], self.size(level + 1))
        return remote(
            part, part, self.sems, self.first + self.levels + level, self.wide ^ (1 << level), self.here
        )

    def actions(self):
        acts = []
        for level in range(self.done, self.levels):
            acts.append([partial(self.start_half, level)])
            if level > self.done:
                acts[-1].insert(0, partial(self.finish_half, level - 1))
        tail = [self.extras]
        if self.done < self.levels:
            tail.insert(0, partial(self.finish_half, self.levels - 1))
        for level in reversed(range(self.levels)):
            acts.append(tail + [lambda level=level: self.spread_copy(level).start()])
            tail = [lambda level=level: self.spread_copy(level).wait_recv()]
        acts.append(tail)
        return acts

    def wait_sends(self):
        for level in range(self.done, self.levels):
            self.half_copy(level).wait_send()
        for level in range(self.levels):
            self.spread_copy(level).wait_send()


def halvings_ahead(pieces, levels):
    return [min(levels, pieces - at) for at in range(pieces)]


def greet(partners):
    barrier = pltpu.get_barrier_semaphore()
    for partner in partners:
        pl.semaphore_signal(
            barrier, inc=1, device_id=partner, device_id_type=pl.DeviceIdType.MESH
        )
    pl.semaphore_wait(barrier, len(partners))


def wide_partners(wide, here, n_wide):
    return [(wide ^ (1 << level), here) for level in range(n_wide.bit_length() - 1)]


def sum_semaphores(n_wide):
    levels = n_wide.bit_length() - 1
    return levels + min(levels, HALVINGS)


def sum_landing(rows, n_wide):
    levels = n_wide.bit_length() - 1
    last = rows >> min(levels, HALVINGS)
    return rows - last + max(levels - HALVINGS, 0) * last


def front_kernel(
    live_ref, silu_ref, taps_ref, tokens_hbm, cot_hbm, ada_hbm, wqkv_src, wout_src, wup_src, wdown_src, ktaps_src,
    x_ref, cot_ref, mod_ref, u_ref, qkv_ref, probs_ref, ctx_ref, att_ref, x1_ref, h2_ref, h2t_ref, db_ref,
    wqkv_ref, wout_ref, wup_ref, wdown_ref, ktaps_ref,
    base, shifted, shards, sent, sent_cot, got, ada, up_own, down_own, sems, local_sems, in_sems,
):
    width = u_ref.shape[1]
    rows_all = u_ref.shape[0]
    latents, shard_rows = shards.shape[:2]
    wide, here = lax.axis_index("wide"), lax.axis_index("narrow")
    load_tokens = pltpu.make_async_copy(tokens_hbm, shards, in_sems.at[0])
    load_tokens.start()
    load_ada = pltpu.make_async_copy(ada_hbm, ada, in_sems.at[1])
    load_ada.start()
    load_up = pltpu.make_async_copy(wup_src, up_own, in_sems.at[2])
    load_up.start()
    load_down = pltpu.make_async_copy(wdown_src, down_own, in_sems.at[3])
    load_down.start()

    barrier = pltpu.get_barrier_semaphore()
    partners = [(wide, peer) for peer in narrow_peers(here)] + [(wide ^ 1, here), (wide ^ 2, here)]
    for partner in partners:
        pl.semaphore_signal(
            barrier, inc=1, device_id=partner, device_id_type=pl.DeviceIdType.MESH
        )
    permutation = group_permutation(shard_rows)
    load_tokens.wait()

    def permute(to):
        def one(at, carry):
            moved = mm(permutation, shards[at], NN).astype(BF16)
            for group in range(4):
                to[at, group] = moved[group * (shard_rows // 4) : (group + 1) * (shard_rows // 4)]
            return carry

        lax.fori_loop(0, latents, one, 0)

    permute(sent)
    pl.semaphore_wait(barrier, len(partners))
    exchange = Exchange(sent, got, sems, local_sems.at[0], 0, wide, here)
    exchange_cot = Exchange(sent_cot, cot_ref, sems, local_sems.at[1], 3, wide, here)
    gathers = [
        Gather(src, dst, sems, local_sems.at[2 + at], 9 + Gather.COPIES * at, wide, here)
        for at, (src, dst) in enumerate(
            (
                (wqkv_src, wqkv_ref),
                (wout_src, wout_ref),
                (up_own, wup_ref),
                (down_own, wdown_ref),
            )
        )
    ]
    g_qkv, g_out, g_up, g_down = gathers
    taps_own = pltpu.make_async_copy(ktaps_src, ktaps_ref.at[0], local_sems.at[6])
    taps_sends = [
        remote(ktaps_src, ktaps_ref.at[peer ^ here], sems, 6 + at, wide, peer)
        for at, peer in enumerate(narrow_peers(here))
    ]
    exchange.start()
    load_cot = pltpu.make_async_copy(cot_hbm, shards, in_sems.at[0])
    load_cot.start()
    load_up.wait()
    load_down.wait()
    for one in gathers:
        one.start_near()
    taps_own.start()
    for one in taps_sends:
        one.start()

    load_ada.wait()
    for part in range(6):
        mod_ref[part : part + 1, :] = mm(
            silu_ref[...], ada[:, part * width : (part + 1) * width], NN
        )[0:1, :]
    load_cot.wait()
    permute(sent_cot)
    shift_one, scale_one, gate_one = mod_ref[0:1, :], mod_ref[1:2, :], mod_ref[2:3, :]
    shift_two, scale_two, gate_two = mod_ref[3:4, :], mod_ref[4:5, :], mod_ref[5:6, :]
    clear_edges(base)
    clear_edges(shifted)
    exchange.wait()
    g_qkv.start_far()
    g_out.start_far()
    for group in range(4):
        for source in range(latents):
            start = group * PHASE + source * ROWS
            x_ref[start : start + ROWS, :] = got[group, source]

    def norm_step(step, carry):
        group, part = step // (PHASE // ROWS), step % (PHASE // ROWS)
        unit, _ = normed(x_ref[ds(step * ROWS, ROWS), :].astype(F32))
        h_one = (unit * (1.0 + scale_one) + shift_one).astype(BF16)
        base[group, ds(HALF + part * ROWS, ROWS, HALF), :] = h_one.astype(F32)
        return carry

    lax.fori_loop(0, rows_all // ROWS, norm_step, 0)
    g_qkv.swap()
    g_out.swap()
    g_up.start_far()

    def conv_step(block, carry):
        lanes = ds(block * LANES, LANES)
        shift_cols(base, shifted, lanes)
        taps = [taps_ref[t : t + 1, lanes] for t in range(9)]

        def rows_step(step, carry):
            for group in range(4):
                total = jnp.zeros((ROWS, LANES), F32)
                for tap in range(9):
                    total += taps[tap] * tap_value(
                        base, shifted, group, tap // 3, tap % 3, step * ROWS, lanes
                    )
                u_ref[ds(group * PHASE + step * ROWS, ROWS), lanes] = total.astype(BF16)
            return carry

        return lax.fori_loop(0, PHASE // ROWS, rows_step, carry)

    blocks = width // LANES
    lax.fori_loop(0, 2 * blocks // 3, conv_step, 0)
    g_qkv.corner()
    g_out.corner()
    g_up.swap()
    exchange_cot.start()
    lax.fori_loop(2 * blocks // 3, blocks, conv_step, 0)
    g_qkv.share_corner()
    g_qkv.finish()

    def project_step(step, carry):
        rows = ds(step * PHASE, PHASE)
        for part in range(3):
            cols = slice(part * width, (part + 1) * width)
            qkv_ref[rows, cols] = mm(u_ref[rows, :], wqkv_ref[:, cols], NT).astype(BF16)
        return carry

    lax.fori_loop(0, 4, project_step, 0)

    pairs = width // LANES
    first = lax.broadcasted_iota(jnp.int32, (PHASE, LANES), 1) < HEAD_DIM
    zero = jnp.zeros((PHASE, LANES), BF16)

    def attend_step(step, carry):
        group, pair = step // pairs, step % pairs
        rows = ds(group * PHASE, PHASE)
        query = qkv_ref[rows, ds(pair * LANES, LANES)]
        key = qkv_ref[rows, ds(width + pair * LANES, LANES)]
        value = qkv_ref[rows, ds(2 * width + pair * LANES, LANES)]
        found = []
        for head in range(2):
            own = jnp.where(first, query, zero) if head == 0 else jnp.where(first, zero, query)
            scores = mm(key, own, NT)
            top = jnp.max(scores, axis=0, keepdims=True)
            raised = jnp.exp2((scores - top) * (LOG2E * HEAD_DIM**-0.5))
            probs = (raised * (1.0 / jnp.sum(raised, axis=0, keepdims=True))).astype(BF16)
            probs_ref[step, :, head * PHASE : (head + 1) * PHASE] = probs
            found.append(mm(probs, value, TN))
        ctx_ref[rows, ds(pair * LANES, LANES)] = jnp.where(first, found[0], found[1]).astype(BF16)
        return carry

    g_up.corner()
    g_out.share_corner()
    lax.fori_loop(0, pairs, attend_step, 0)
    g_up.share_corner()
    exchange_cot.wait()
    g_down.start_far()
    lax.fori_loop(pairs, 3 * pairs, attend_step, 0)
    g_down.swap()
    lax.fori_loop(3 * pairs, 4 * pairs, attend_step, 0)
    g_out.finish()

    def out_step(step, carry):
        rows = ds(step * PHASE, PHASE)
        total = mm(ctx_ref[rows, :], wout_ref[...], NN)
        att_ref[rows, :] = total.astype(BF16)
        x1_ref[rows, :] = x_ref[rows, :].astype(F32) + gate_one * total
        return carry

    lax.fori_loop(0, 4, out_step, 0)
    live = live_ref[0, 0]

    def second_step(step, carry):
        rows = ds(step * ROWS, ROWS)
        unit, _ = normed(x1_ref[rows, :])
        h2_ref[rows, :] = (unit * (1.0 + scale_two) + shift_two).astype(BF16)
        group, source = step // (PHASE // ROWS), step % (PHASE // ROWS)
        db_ref[rows, :] = (cot_ref[group, source].astype(F32) * live * gate_two).astype(BF16)
        return carry

    g_down.corner()
    lax.fori_loop(0, rows_all // ROWS, second_step, 0)
    g_down.share_corner()
    for part in range(4):
        h2t_ref[:, part * PHASE : (part + 1) * PHASE] = h2_ref[
            part * PHASE : (part + 1) * PHASE, :
        ].T
    g_up.finish()
    g_down.finish()
    taps_own.wait()
    for one in taps_sends:
        one.wait()


def whole(memory=pltpu.VMEM):
    return pl.BlockSpec(memory_space=memory)


def front(live, silu_row, taps, tokens, cot, w_ada, wqkv, wout, wup, wdown, ktaps):
    latents, shard_rows, width = tokens.shape
    rows = latents * shard_rows
    steps = 4 * (width // LANES)
    shape = jax.ShapeDtypeStruct
    full = lambda shard: shape((latents * shard.shape[0],) + shard.shape[1:], BF16)
    moved = (latents, 4, shard_rows // 4, width)
    return pl.pallas_call(
        front_kernel,
        out_shape=(
            shape((rows, width), BF16),
            shape((4, latents, shard_rows // 4, width), BF16),
            shape((6, width), F32),
            shape((rows, width), BF16),
            shape((rows, 3 * width), BF16),
            shape((steps, PHASE, 2 * PHASE), BF16),
            shape((rows, width), BF16),
            shape((rows, width), BF16),
            shape((rows, width), F32),
            shape((rows, width), BF16),
            shape((width, rows), BF16),
            shape((rows, width), BF16),
            full(wqkv),
            full(wout),
            full(wup),
            full(wdown),
            shape((latents,) + ktaps.shape, BF16),
        ),
        in_specs=[whole(pltpu.SMEM)] + [whole()] * 2 + [whole(pl.ANY)] * 3 + [whole()] * 2 + [whole(pl.ANY)] * 2 + [whole()],
        out_specs=(whole(),) * 14 + (whole(pl.ANY),) * 2 + (whole(),),
        scratch_shapes=[
            pltpu.VMEM((4, PAD, width), F32),
            pltpu.VMEM((4, PAD, width), F32),
            pltpu.VMEM((latents, shard_rows, width), BF16),
            pltpu.VMEM(moved, BF16),
            pltpu.VMEM(moved, BF16),
            pltpu.VMEM((4, latents, shard_rows // 4, width), BF16),
            pltpu.VMEM(w_ada.shape, BF16),
            pltpu.VMEM(wup.shape, BF16),
            pltpu.VMEM(wdown.shape, BF16),
            pltpu.SemaphoreType.DMA((2, 9 + 4 * Gather.COPIES)),
            pltpu.SemaphoreType.DMA((7,)),
            pltpu.SemaphoreType.DMA((4,)),
        ],
        compiler_params=pltpu.CompilerParams(
            vmem_limit_bytes=60 * MIB, collective_id=0, has_side_effects=True
        ),
        name="attn_forward",
    )(live, silu_row, taps, tokens, cot, w_ada, wqkv, wout, wup, wdown, ktaps)


def ffn_kernel(
    n_wide, live_ref, h2_ref, h2t_ref, db_ref, x1_ref, cot_ref, att_ref, mod_ref,
    wup_before, wup_even, wup_odd, wup_after, wdown_even, wdown_odd, taps_even, taps_odd,
    block_ref, dx1_ref, datt_ref, dmod_ref, sums_ref,
    hid_even, hid_odd, hid_moved, grad, grad_moved, slope, act, act_t, dhid, branch, dtaps,
    work, chip_sum, got_near, got_far, got_sums, sems, sum_sems,
):
    rows_all, width = h2_ref.shape
    dh2 = dx1_ref
    wide, here = lax.axis_index("wide"), lax.axis_index("narrow")
    step, steps = pl.program_id(0), pl.num_programs(0)
    quarters = [slice(q * PHASE, (q + 1) * PHASE) for q in range(4)]
    inside = slice(HALF, HALF + PHASE)
    lane_blocks = [slice(at * LANES, (at + 1) * LANES) for at in range(CHUNK // LANES)]
    col = lax.broadcasted_iota(jnp.int32, (ROWS, LANES), 0) % HALF

    partners = [(wide, here ^ 1), (wide, here ^ 2)] + wide_partners(wide, here, n_wide)[:HALVINGS]
    pieces, sum_rows = got_sums.shape[0], got_sums.shape[1]
    sums = [
        WideSum(sums_ref.at[at, : 2 * width], sums_ref.at[at, : 2 * width], None, got_sums.at[at], sum_sems,
                at * HALVINGS, wide, here, n_wide)
        for at in range(pieces)
    ]
    schedule = halvings_ahead(pieces, sums[0].levels)

    def to_near(at):
        return remote(work.at[at % 2], got_near.at[at], sems, at, wide, here ^ 1)

    def to_far(at):
        return remote(chip_sum.at[at], got_far.at[at], sems, steps + at, wide, here ^ 2)

    @pl.when(step == 0)
    def _():
        barrier = pltpu.get_barrier_semaphore()
        for partner in partners:
            pl.semaphore_signal(
                barrier, inc=1, device_id=partner, device_id_type=pl.DeviceIdType.MESH
            )
        for ref in (hid_even, hid_odd, hid_moved, grad, grad_moved):
            clear_edges(ref)
        branch[...] = jnp.zeros_like(branch)
        dh2[...] = jnp.zeros_like(dh2)
        dtaps[...] = jnp.zeros_like(dtaps)
        dhid[...] = jnp.zeros_like(dhid)
        full = mm(h2_ref[...], wup_even[...], NN)
        for q in range(4):
            hid_even[q, inside, :] = full[quarters[q]]
        pl.semaphore_wait(barrier, len(partners))

    def moved_cols(group, value):
        if group % 2:
            return jnp.where(col == 0, 0.0, pltpu.roll(value, 1, 0))
        return jnp.where(col == HALF - 1, 0.0, pltpu.roll(value, ROWS - 1, 0))

    def static_tap(base, shifted, group, tap_row, tap_col, start, lanes):
        src_row, row_move = tap_source(group // 2, tap_row)
        src_col, col_move = tap_source(group % 2, tap_col)
        ref = base if col_move == 0 else shifted
        first = HALF + row_move * HALF + start
        return ref[2 * src_row + src_col, first : first + ROWS, lanes]

    def weights_back(q, wup_last, slot):
        dh2[quarters[q], :] += mm(dhid[quarters[q], :], wup_last[...], NT)
        if q < width // PHASE:
            slot[quarters[q], :] = mm(h2t_ref[quarters[q], :], dhid[...], NN).astype(BF16)

    def forward(hid, wdown, taps_ref, wup_last, slot):
        taps = [[taps_ref[0, t : t + 1, lanes] for t in range(9)] for lanes in lane_blocks]
        for part in range(PHASE // ROWS):
            rows = slice(HALF + part * ROWS, HALF + (part + 1) * ROWS)
            for group in range(4):
                for lanes in lane_blocks:
                    hid_moved[group, rows, lanes] = moved_cols(group, hid[group, rows, lanes])
        for part in range(PHASE // ROWS):
            grad[part, inside, :] = mm(db_ref[quarters[part], :], wdown[...], NT)
            weights_back(part, wup_last, slot)
            for group in range(4):
                for at, lanes in enumerate(lane_blocks):
                    total = jnp.zeros((ROWS, LANES), F32)
                    for tap in range(9):
                        total += taps[at][tap] * static_tap(
                            hid, hid_moved, group, tap // 3, tap % 3, part * ROWS, lanes
                        )
                    square = total * total
                    turned = jnp.tanh(total * (square * (GELU_C * GELU_A) + GELU_C))
                    half = 0.5 * turned + 0.5
                    bend = total * (half - half * half)
                    start = group * PHASE + part * ROWS
                    act[start : start + ROWS, lanes] = (total * half).astype(BF16)
                    slope[start : start + ROWS, lanes] = half + bend * (
                        square * (6.0 * GELU_C * GELU_A) + 2.0 * GELU_C
                    )

    def backward(hid, hid_next, wdown, wup_next, taps_ref, slot):
        taps = [[taps_ref[0, t : t + 1, lanes] for t in range(9)] for lanes in lane_blocks]
        act_t[...] = act[...].T
        for part in range(PHASE // ROWS):
            rows = slice(HALF + part * ROWS, HALF + (part + 1) * ROWS)
            for group in range(4):
                start = group * PHASE + part * ROWS
                for lanes in lane_blocks:
                    value = grad[group, rows, lanes] * slope[start : start + ROWS, lanes]
                    grad[group, rows, lanes] = value
                    grad_moved[group, rows, lanes] = moved_cols(group, value)
        sums = [[jnp.zeros((8, LANES), F32) for _ in range(9)] for _ in lane_blocks]
        for part in range(PHASE // ROWS):
            hid_next[part, inside, :] = mm(h2_ref[quarters[part], :], wup_next[...], NN)
            branch[quarters[part], :] += mm(act[quarters[part], :], wdown[...], NN)
            if part < width // CHUNK:
                block = slice(part * CHUNK, (part + 1) * CHUNK)
                slot[width + part * CHUNK : width + (part + 1) * CHUNK, :] = mm(
                    act_t[...], db_ref[:, block], NN
                ).astype(BF16)
            for group in range(4):
                start = group * PHASE + part * ROWS
                for at, lanes in enumerate(lane_blocks):
                    own = hid[group, HALF + part * ROWS : HALF + (part + 1) * ROWS, lanes]
                    total = jnp.zeros((ROWS, LANES), F32)
                    for tap in range(9):
                        moved = static_tap(
                            grad, grad_moved, group, 2 - tap // 3, 2 - tap % 3, part * ROWS, lanes
                        )
                        total += taps[at][tap] * moved
                        sums[at][tap] += (own * moved).reshape(ROWS // 8, 8, LANES).sum(axis=0)
                    dhid[start : start + ROWS, lanes] = total.astype(BF16)
        for at, lanes in enumerate(lane_blocks):
            for tap in range(9):
                dtaps[tap : tap + 1, lanes] = jnp.sum(sums[at][tap], axis=0, keepdims=True)
        slot[2 * width :, :] = dtaps[...].astype(BF16)

    def settle(pair):
        to_near(pair).wait_recv()

        @pl.when(pair < steps // 2)
        def _():
            chip_sum[pair] = (work[2].astype(F32) + got_near[pair].astype(F32)).astype(BF16)
            to_far(pair).start()

        @pl.when(pair >= steps // 2)
        def _():
            part = pair - steps // 2
            to_far(part).wait_recv()
            sums_ref[part] = (
                work[2].astype(F32) + got_near[pair].astype(F32) + got_far[part].astype(F32)
            ).astype(BF16)

        for part in range(pieces):

            @pl.when(pair == steps // 2 + part)
            def _():
                for at in range(part):
                    sums[at].finish_half(part - at - 1)
                for at in range(part + 1):
                    if part - at < schedule[at]:
                        sums[at].start_half(part - at)

    forward(hid_even, wdown_even, taps_even, wup_before, work.at[2])

    @pl.when(step >= 1)
    def _():
        settle(step - 1)

    @pl.when(step >= 2)
    def _():
        to_near(step - 2).wait_send()

    even_slot = work.at[step % 2]
    backward(hid_even, hid_odd, wdown_even, wup_odd, taps_even, even_slot)
    forward(hid_odd, wdown_odd, taps_odd, wup_even, even_slot)
    to_near(step).start()
    backward(hid_odd, hid_even, wdown_odd, wup_after, taps_odd, work.at[2])

    @pl.when(step == steps - 1)
    def _():
        for q in range(4):
            weights_back(q, wup_odd, work.at[2])
        settle(step)
        gate_one, scale_two, gate_two = mod_ref[2:3, :], mod_ref[4:5, :], mod_ref[5:6, :]
        live = live_ref[0, 0]

        def fold(value):
            return value.reshape(ROWS // 8, 8, width).sum(axis=0)

        def rows_step(at, sums):
            rows = ds(at * ROWS, ROWS)
            after = x1_ref[rows, :]
            dout = cot_ref[rows, :].astype(F32) * live
            branch_rows = branch[rows, :]
            block_ref[rows, :] = ((after + gate_two * branch_rows) * live).astype(BF16)
            unit, inv = normed(after)
            dh2_rows = dh2[rows, :]
            dx1 = dout + norm_back(unit, inv, dh2_rows * (1.0 + scale_two))
            dx1_ref[rows, :] = dx1
            datt_ref[rows, :] = (dx1 * gate_one).astype(BF16)
            found = (dx1 * att_ref[rows, :].astype(F32), dh2_rows, dh2_rows * unit, dout * branch_rows)
            return tuple(total + fold(one) for total, one in zip(sums, found))

        start = tuple(jnp.zeros((8, width), F32) for _ in range(4))
        totals = lax.fori_loop(0, rows_all // ROWS, rows_step, start)
        for at in range(4):
            dmod_ref[at : at + 1, :] = jnp.sum(totals[at], axis=0, keepdims=True)
        for at in (steps - 2, steps - 1):
            to_near(at).wait_send()
        for at in range(steps // 2):
            to_far(at).wait_send()
        for at in range(pieces):
            sums[at].finish_half(schedule[at] - 1)
            for level in range(schedule[at]):
                sums[at].half_copy(level).wait_send()


def conv_back(grad, grad_moved, source, lanes, taps, dtaps_ref, out_ref):
    def rows_step(step, sums):
        sums = list(sums)
        for group in range(4):
            total = jnp.zeros((ROWS, LANES), F32)
            own = source[group, ds(HALF + step * ROWS, ROWS, HALF), lanes]
            for tap in range(9):
                moved = tap_value(
                    grad, grad_moved, group, 2 - tap // 3, 2 - tap % 3, step * ROWS, lanes
                )
                total += taps[tap] * moved
                sums[tap] += (own * moved).reshape(ROWS // 8, 8, LANES).sum(axis=0)
            out_ref[ds(group * PHASE + step * ROWS, ROWS), lanes] = total.astype(out_ref.dtype)
        return tuple(sums)

    start = tuple(jnp.zeros((8, LANES), F32) for _ in range(9))
    sums = lax.fori_loop(0, PHASE // ROWS, rows_step, start)
    for tap in range(9):
        dtaps_ref[tap : tap + 1, lanes] = jnp.sum(sums[tap], axis=0, keepdims=True)


def ffn(n_wide, live, h2, h2t, db, x1, cot, att, mod, wup, wdown, taps):
    rows, width = h2.shape
    shards, _, local = taps.shape
    per = local // CHUNK
    steps = shards * per // 2
    parcel = (2 * width + 16, CHUNK)
    shape = jax.ShapeDtypeStruct
    keep = lambda *block: pl.BlockSpec(
        block, lambda c: (0,) * len(block), pipeline_mode=pl.Buffered(1)
    )

    def slot_and_part(step, odd):
        return jnp.where(step < per, 3, 1) - odd, step % per

    def up_block(move, odd):
        def index(step):
            return slot_and_part(jnp.clip(step + move, 0, steps - 1), odd)

        return pl.BlockSpec((width, CHUNK), index)

    def down_block(odd):
        def index(step):
            slot, part = slot_and_part(step, odd)
            return slot * per + part, 0

        return pl.BlockSpec((CHUNK, width), index)

    def taps_block(odd):
        def index(step):
            slot, part = slot_and_part(step, odd)
            return slot, 0, part

        return pl.BlockSpec((1, 9, CHUNK), index)

    return pl.pallas_call(
        partial(ffn_kernel, n_wide),
        grid=(steps,),
        out_shape=(
            shape((rows, width), BF16),
            shape((rows, width), F32),
            shape((rows, width), BF16),
            shape((4, width), F32),
            shape((per,) + parcel, BF16),
        ),
        in_specs=[
            whole(pltpu.SMEM),
            keep(rows, width),
            keep(width, rows),
            keep(rows, width),
            keep(rows, width),
            keep(rows, width),
            keep(rows, width),
            keep(6, width),
            up_block(-1, 1),
            up_block(0, 0),
            up_block(0, 1),
            up_block(1, 0),
            down_block(0),
            down_block(1),
            taps_block(0),
            taps_block(1),
        ],
        out_specs=(
            keep(rows, width),
            keep(rows, width),
            keep(rows, width),
            keep(4, width),
            keep(per, *parcel),
        ),
        scratch_shapes=[pltpu.VMEM((4, PAD, CHUNK), F32)] * 5
        + [
            pltpu.VMEM((rows, CHUNK), F32),
            pltpu.VMEM((rows, CHUNK), BF16),
            pltpu.VMEM((CHUNK, rows), BF16),
            pltpu.VMEM((rows, CHUNK), BF16),
            pltpu.VMEM((rows, width), F32),
            pltpu.VMEM((16, CHUNK), F32),
            pltpu.VMEM((3,) + parcel, BF16),
            pltpu.VMEM((per,) + parcel, BF16),
            pltpu.VMEM((steps,) + parcel, BF16),
            pltpu.VMEM((per,) + parcel, BF16),
            pltpu.VMEM((per, sum_landing(2 * width, n_wide), CHUNK), BF16),
            pltpu.SemaphoreType.DMA((2, steps + per)),
            pltpu.SemaphoreType.DMA((2, per * HALVINGS)),
        ],
        compiler_params=pltpu.CompilerParams(
            vmem_limit_bytes=62 * MIB, collective_id=1, has_side_effects=True
        ),
        name="feed_forward",
    )(live, h2, h2t, db, x1, cot, att, mod, wup, wup, wup, wup, wdown, wdown, taps, taps)


def attn_backward_kernel(
    n_wide, datt_ref, ctx_ref, u_ref, wout_ref, parcels, qkv_hbm, probs_hbm,
    dqkv_ref, own_ref, full, gtaps_ref,
    dctx, probs_buf, weights, got_near, chip_sum, got_far, work, got_sums, taps_sum, taps_got,
    sems, in_sems, sum_sems,
):
    rows_all, width = u_ref.shape
    wide, here = lax.axis_index("wide"), lax.axis_index("narrow")
    pairs = width // LANES
    half_pairs = pairs // 2
    steps = 4 * pairs
    slots = weights.shape[0]
    load_qkv = pltpu.make_async_copy(qkv_hbm, dqkv_ref, in_sems.at[2])
    load_qkv.start()

    def pair_of(step):
        return (half_pairs + step // 4) % pairs

    def load_probs(step):
        return pltpu.make_async_copy(
            probs_hbm.at[(step % 4) * pairs + pair_of(step)], probs_buf.at[step % 2], in_sems.at[step % 2]
        )

    load_probs(0).start()
    greet([(wide, here ^ 2), (wide, here ^ 1)] + wide_partners(wide, here, n_wide))
    pieces = full.shape[0]
    rows = full.shape[1]
    per_sum = sum_semaphores(n_wide)
    ahead = halvings_ahead(pieces, min(HALVINGS, n_wide.bit_length() - 1))
    sums = [
        WideSum(parcels.at[at, :rows], work.at[at], full.at[at], got_sums.at[at], sum_sems, at * per_sum,
                wide, here, n_wide, done=ahead[at])
        for at in range(pieces)
    ]
    levels = n_wide.bit_length() - 1
    queues = [one.actions() for one in sums]

    def advance(*which):
        for at in which:
            if queues[at]:
                for act in queues[at].pop(0):
                    act()

    def taps_copy(level):
        return remote(taps_sum.at[level], taps_got.at[level], sems, 6 + level, wide ^ (1 << level), here)

    def taps_add(level):
        taps_copy(level).wait_recv()
        taps_sum[level + 1] = taps_sum[level] + taps_got[level]
        if level + 1 < levels:
            taps_copy(level + 1).start()

    for at in range(pieces):
        taps_sum[0, :, at * CHUNK : (at + 1) * CHUNK] = parcels[at, rows:, :].astype(F32)
    taps_copy(0).start()
    advance(2, 0, 1)

    def ctx_step(step, carry):
        span = ds(step * PHASE, PHASE)
        dctx[span, :] = mm(datt_ref[span, :], wout_ref[...], NT).astype(BF16)
        return carry

    lax.fori_loop(0, 4, ctx_step, 0)
    load_qkv.wait()

    first = lax.broadcasted_iota(jnp.int32, (PHASE, LANES), 1) < HEAD_DIM
    zero = jnp.zeros((PHASE, LANES), BF16)
    scale = HEAD_DIM**-0.5

    def attend(step):
        group, pair = step % 4, pair_of(step)
        load_probs(step).wait()

        @pl.when(step + 1 < steps)
        def _():
            load_probs(step + 1).start()

        span = ds(group * PHASE, PHASE)
        query = dqkv_ref[span, ds(pair * LANES, LANES)]
        key = dqkv_ref[span, ds(width + pair * LANES, LANES)]
        value = dqkv_ref[span, ds(2 * width + pair * LANES, LANES)]
        dctx_pair = dctx[span, ds(pair * LANES, LANES)]
        dq, dk, dv = [], None, None
        for head in range(2):
            own = lambda both: jnp.where(first, both, zero) if head == 0 else jnp.where(first, zero, both)
            probs = probs_buf[step % 2, :, head * PHASE : (head + 1) * PHASE]
            probs_f = probs.astype(F32)
            dctx_own, query_own = own(dctx_pair), own(query)
            dprobs = mm(value, dctx_own, NT)
            inner = jnp.sum(dprobs * probs_f, axis=0, keepdims=True)
            dscores = (probs_f * (dprobs - inner)).astype(BF16)
            dv_one = mm(probs, dctx_own, NN)
            dk_one = mm(dscores, query_own, NN)
            dv = dv_one if dv is None else dv + dv_one
            dk = dk_one if dk is None else dk + dk_one
            dq.append(mm(dscores, key, TN))
        dqkv_ref[span, ds(pair * LANES, LANES)] = (
            jnp.where(first, dq[0], dq[1]) * scale
        ).astype(BF16)
        dqkv_ref[span, ds(width + pair * LANES, LANES)] = (dk * scale).astype(BF16)
        dqkv_ref[span, ds(2 * width + pair * LANES, LANES)] = dv.astype(BF16)

    def attend_loop(begin, end, plan):
        def body(step, carry):
            for at, what in plan:
                pl.when(step == at)(what)
            attend(step)
            return carry

        lax.fori_loop(begin, end, body, 0)

    slab = width // slots

    def weight_grads(half):
        span = width // 2
        for part in range(3):
            left = dqkv_ref[:, part * width + half * span : part * width + (half + 1) * span]
            found = mm(left, u_ref[...], TN).astype(BF16)
            for one in range(2):
                weights[2 * half + one, part * slab : (part + 1) * slab, :] = found[
                    one * slab : (one + 1) * slab
                ]

    head, tail = slice(3 * slab), slice(3 * slab, 4 * slab)

    def near_copy(early, rows, at):
        return remote(
            weights.at[3 if early else 1, rows], got_near.at[0 if early else 1, rows], sems, at, wide, here ^ 1
        )

    def far_copy(rows, at):
        return remote(chip_sum.at[rows], got_far.at[rows], sems, at, wide, here ^ 2)

    def add_chip(rows):
        chip_sum[rows, :] = (weights[2, rows, :].astype(F32) + got_near[0, rows, :].astype(F32)).astype(BF16)

    near_out, near_early = near_copy(True, tail, 0), near_copy(True, head, 1)
    late_out, near_late = near_copy(False, tail, 2), near_copy(False, head, 3)
    far_out, far = far_copy(tail, 4), far_copy(head, 5)

    for part in range(width // PHASE):
        cols = slice(part * PHASE, (part + 1) * PHASE)
        found = mm(ctx_ref[:, cols], datt_ref[...], TN).astype(BF16)
        for slot in range(slots):
            low, high = max(part * PHASE, slot * slab), min((part + 1) * PHASE, (slot + 1) * slab)
            if low < high:
                weights[slot, 3 * slab + low - slot * slab : 3 * slab + high - slot * slab, :] = found[
                    low - part * PHASE : high - part * PHASE
                ]
    near_out.start()
    late_out.start()

    def send_out():
        near_out.wait_recv()
        add_chip(tail)
        far_out.start()

    later = lambda *which: partial(advance, *which)
    attend_loop(
        0, steps // 2,
        [(1, send_out), (2, later(2, 0)), (5, later(1)), (7, partial(taps_add, 0)), (8, later(2, 0)), (11, later(1))],
    )
    weight_grads(1)
    near_early.start()
    advance(2)
    near_early.wait_recv()
    add_chip(head)
    far.start()
    attend_loop(
        steps // 2, steps,
        [(13, later(1, 0)), (14, partial(taps_add, 1)), (16, later(2))],
    )
    weight_grads(0)
    near_late.start()
    for level in range(2, levels):
        taps_add(level)
    gtaps_ref[...] = taps_sum[levels]
    near_late.wait_recv()
    late_out.wait_recv()
    while any(queues):
        advance(0, 1, 2)
    far_out.wait_recv()
    far.wait_recv()
    own_ref[...] = (
        weights[0].astype(F32) + got_near[1].astype(F32) + got_far[...].astype(F32)
    ).astype(BF16)
    for one in sums:
        one.wait_sends()
    for level in range(levels):
        taps_copy(level).wait_send()
    for copy in (near_out, near_early, late_out, near_late, far_out, far):
        copy.wait_send()


def attn_backward(n_wide, datt, ctx, u, wout, parcels, qkv, probs):
    rows, width = u.shape
    slots = lax.axis_size("narrow")
    slab = wout.shape[0] // slots
    pieces, parcel_rows, _ = parcels.shape
    sum_rows = parcel_rows - 16
    shape = jax.ShapeDtypeStruct
    levels = n_wide.bit_length() - 1
    per_sum = sum_semaphores(n_wide)
    return pl.pallas_call(
        partial(attn_backward_kernel, n_wide),
        out_shape=(
            shape((rows, 3 * width), BF16),
            shape((4 * slab, width), BF16),
            shape((pieces, sum_rows, CHUNK), BF16),
            shape((16, pieces * CHUNK), F32),
        ),
        in_specs=[whole()] * 5 + [whole(pl.ANY)] * 2,
        out_specs=(whole(),) * 4,
        scratch_shapes=[
            pltpu.VMEM((rows, width), BF16),
            pltpu.VMEM((2, PHASE, 2 * PHASE), BF16),
            pltpu.VMEM((slots, 4 * slab, width), BF16),
            pltpu.VMEM((2, 4 * slab, width), BF16),
            pltpu.VMEM((4 * slab, width), BF16),
            pltpu.VMEM((4 * slab, width), BF16),
            pltpu.VMEM((pieces, sum_rows, CHUNK), BF16),
            pltpu.VMEM((pieces, sum_landing(sum_rows, n_wide), CHUNK), BF16),
            pltpu.VMEM((levels + 1, 16, pieces * CHUNK), F32),
            pltpu.VMEM((levels, 16, pieces * CHUNK), F32),
            pltpu.SemaphoreType.DMA((2, 6 + levels)),
            pltpu.SemaphoreType.DMA((3,)),
            pltpu.SemaphoreType.DMA((2, pieces * per_sum)),
        ],
        compiler_params=pltpu.CompilerParams(
            vmem_limit_bytes=56 * MIB, collective_id=2, has_side_effects=True
        ),
        name="attn_backward",
    )(datt, ctx, u, wout, parcels, qkv, probs)


def one_hot(rows, columns, wanted):
    row = lax.broadcasted_iota(jnp.int32, (rows, columns), 0)
    column = lax.broadcasted_iota(jnp.int32, (rows, columns), 1)
    return jnp.where(column == wanted(row), 1.0, 0.0).astype(BF16)


SMALL = 16


def input_backward_kernel(
    n_wide, x_ref, dx1_ref, dqkv_ref, mod_ref, taps_ref, wqkv_ref, own_ref, silu_ref, dmod_ref, block_in,
    got_dx, got_block, full, small, dtaps_ref,
    base, shifted, first_in, dh1, dx, work, got_sums, tap_sums, tap_got, sems, local_sems, sum_sems, small_sems,
):
    rows_all, width = x_ref.shape
    wide, here = lax.axis_index("wide"), lax.axis_index("narrow")
    shift_one, scale_one = mod_ref[0:1, :], mod_ref[1:2, :]
    greet([(wide, peer) for peer in narrow_peers(here)] + wide_partners(wide, here, n_wide))
    pieces = full.shape[0]
    rows = full.shape[1]
    per_sum = sum_semaphores(n_wide)
    sums = [
        WideSum(own_ref.at[at * rows : (at + 1) * rows], work.at[at], full.at[at], got_sums.at[at], sum_sems,
                at * per_sum, wide, here, n_wide)
        for at in range(pieces)
    ]
    queues = [one.actions() for one in sums]

    def advance(*which):
        for at in which:
            if queues[at]:
                for act in queues[at].pop(0):
                    act()

    advance(0, 1)
    block_back = Return(block_in, got_block, sems, local_sems.at[1], 3, wide, here)
    block_back.start()
    clear_edges(base)
    clear_edges(shifted)

    def norm_step(step, carry):
        group, part = step // (PHASE // ROWS), step % (PHASE // ROWS)
        unit, _ = normed(x_ref[ds(step * ROWS, ROWS), :].astype(F32))
        h_one = (unit * (1.0 + scale_one) + shift_one).astype(BF16)
        first_in[group, ds(HALF + part * ROWS, ROWS, HALF), :] = h_one.astype(F32)
        return carry

    lax.fori_loop(0, rows_all // ROWS, norm_step, 0)

    def du_step(group, carry):
        span = ds(group * PHASE, PHASE)
        total = None
        for part in range(3):
            cols = slice(part * width, (part + 1) * width)
            one = mm(dqkv_ref[span, cols], wqkv_ref[:, cols], NN)
            total = one if total is None else total + one
        base[group, HALF : HALF + PHASE, :] = total
        return carry

    lax.fori_loop(0, 3, du_step, 0)
    advance(0)
    lax.fori_loop(3, 4, du_step, 0)

    def conv_step(block, carry):
        lanes = ds(block * LANES, LANES)
        shift_cols(base, shifted, lanes)
        conv_back(base, shifted, first_in, lanes, [taps_ref[t : t + 1, lanes] for t in range(9)],
                  dtaps_ref, dh1)
        return carry

    for block in range(width // LANES):
        if block % 2:
            advance(0)
        else:
            advance(1)
        lax.fori_loop(block, block + 1, conv_step, 0)

    def fold(value):
        return value.reshape(ROWS // 8, 8, width).sum(axis=0)

    back = Return(dx, got_dx, sems, local_sems.at[0], 0, wide, here)

    def rows_step(at, sums):
        group, source = at // 4, at % 4
        span = ds(at * ROWS, ROWS)
        unit, inv = normed(x_ref[span, :].astype(F32))
        grad = dh1[span, :]
        dx[group, source] = (
            dx1_ref[span, :] + norm_back(unit, inv, grad * (1.0 + scale_one))
        ).astype(BF16)
        return tuple(total + fold(one) for total, one in zip(sums, (grad, grad * unit)))

    partners = [(wide, here ^ 2)] + wide_partners(wide, here, n_wide)[::-1] + [(wide, here ^ 1)]
    levels = len(partners)
    tap_sums[0, :9, :] = dtaps_ref[:9, :]
    tap_sums[0, 9:, :] = jnp.zeros((7, width), F32)

    def taps_copy(level):
        return remote(tap_sums.at[level], tap_got.at[level], small_sems, 2 * level + 1, *partners[level])

    def taps_step(level):
        taps_copy(level).wait_recv()
        tap_sums[level + 1] = tap_sums[level] + tap_got[level]
        if level + 1 < levels:
            taps_copy(level + 1).start()

    taps_copy(0).start()
    found = tuple(jnp.zeros((8, width), F32) for _ in range(2))
    for at in range(2):
        found = lax.fori_loop(8 * at, 8 * at + 8, rows_step, found)
        taps_step(at)
    dmod = [jnp.sum(one, axis=0, keepdims=True) for one in found]
    dmod += [dmod_ref[at : at + 1, :] for at in range(4)]

    stack = jnp.concatenate([silu_ref[0:1, :].astype(F32)] + dmod + [jnp.zeros((SMALL - 7, width), F32)])
    small[0] = stack.astype(BF16)

    def small_copy(level):
        have = 1 << level
        return remote(small.at[:have], small.at[have : 2 * have], small_sems, 2 * level, *partners[level])

    small_copy(0).start()
    for copy in back.copies:
        copy.start()
    back.own.start()
    advance(0, 1)
    for level in range(levels):
        small_copy(level).wait_recv()
        if level + 1 < levels:
            small_copy(level + 1).start()
        if level >= 2:
            taps_step(level)
        advance(0, 1)
    dtaps_ref[...] = tap_sums[levels]
    while any(queues):
        advance(0, 1)
    block_back.wait()
    back.wait()
    for level in range(levels):
        small_copy(level).wait_send()
        taps_copy(level).wait_send()
    for one in sums:
        one.wait_sends()


def input_backward(n_wide, x, dx1, dqkv, mod, taps, wqkv, own, silu_row, dmod, block):
    rows, width = x.shape
    slots = lax.axis_size("narrow")
    pieces = 2
    sum_rows = own.shape[0] // pieces
    shape = jax.ShapeDtypeStruct
    per_sum = sum_semaphores(n_wide)
    levels = (n_wide * slots).bit_length() - 1
    back = shape((slots, 4, rows // (4 * slots), width), BF16)
    return pl.pallas_call(
        partial(input_backward_kernel, n_wide),
        out_shape=(
            back,
            back,
            shape((pieces, sum_rows, width), BF16),
            shape((1 << levels, SMALL, width), BF16),
            shape((SMALL, width), F32),
        ),
        in_specs=[whole()] * 10,
        out_specs=(whole(),) * 5,
        scratch_shapes=[pltpu.VMEM((4, PAD, width), F32)] * 3
        + [
            pltpu.VMEM((rows, width), F32),
            pltpu.VMEM((4, slots, rows // (4 * slots), width), BF16),
            pltpu.VMEM((pieces, sum_rows, width), BF16),
            pltpu.VMEM((pieces, sum_landing(sum_rows, n_wide), width), BF16),
            pltpu.VMEM((levels + 1, SMALL, width), F32),
            pltpu.VMEM((levels, SMALL, width), F32),
            pltpu.SemaphoreType.DMA((2, 6)),
            pltpu.SemaphoreType.DMA((2,)),
            pltpu.SemaphoreType.DMA((2, pieces * per_sum)),
            pltpu.SemaphoreType.DMA((2, 2 * levels)),
        ],
        compiler_params=pltpu.CompilerParams(
            vmem_limit_bytes=56 * MIB, collective_id=3, has_side_effects=True
        ),
        name="input_backward",
    )(x, dx1, dqkv, mod, taps, wqkv, own, silu_row, dmod, block)


def outputs_kernel(
    dx_in, block_in, attn_sum, ffn_sum, small, cond_ref, ada_hbm,
    gada_hbm, dx_hbm, block_hbm, gqkv_hbm, gout_hbm, gup_hbm, gdown_hbm, gcond_ref,
    ada, gada, dx, block, gqkv, gout, gup, gdown, sems, in_sem,
):
    width = small.shape[-1]
    here = lax.axis_index("narrow")
    load_ada = pltpu.make_async_copy(ada_hbm, ada, in_sem.at[0])
    load_ada.start()
    started = []

    def put(src, dst):
        copy = pltpu.make_async_copy(src, dst, sems.at[len(started)])
        copy.start()
        started.append(copy)

    devices = small.shape[0]
    shares = small[...].reshape(devices * SMALL, width)
    pick = lambda row: mm(
        one_hot(devices, devices * SMALL, lambda at: at * SMALL + row), shares, NN
    ).astype(BF16)
    silu_all = pick(0)
    for part in range(6):
        gada[part] = mm(silu_all, pick(1 + part), TN)
        put(gada.at[part], gada_hbm.at[:, part * width : (part + 1) * width])
    slab = attn_sum.shape[1] // 2
    for part in range(3):
        gqkv[part] = attn_sum[part // 2, (part % 2) * slab : (part % 2 + 1) * slab, :].astype(F32).T
        put(gqkv.at[part], gqkv_hbm.at[part])
    gout[...] = attn_sum[1, slab:, :].astype(F32)
    put(gout, gout_hbm)
    permutation = group_permutation(dx_in.shape[1] * dx_in.shape[2])
    for at in range(dx_in.shape[0]):
        for source, held, out in ((dx_in, dx, dx_hbm), (block_in, block, block_hbm)):
            groups = jnp.concatenate([source[at, group] for group in range(4)], axis=0)
            held[at] = mm(permutation, groups, TN).astype(held.dtype)
            put(held.at[at], out.at[at])
    for at in range(ffn_sum.shape[0]):
        cols = slice(at * CHUNK, (at + 1) * CHUNK)
        gup[:, cols] = ffn_sum[at, :width, :].astype(F32)
        for part in range(width // CHUNK):
            span = slice(width + part * CHUNK, width + (part + 1) * CHUNK)
            gdown[cols, part * CHUNK : (part + 1) * CHUNK] = ffn_sum[at, span, :].astype(F32)
        put(gdown.at[cols], gdown_hbm.at[cols])
    put(gup, gup_hbm)

    def own_column(row, part):
        away = row ^ here
        place = ((away // 2) % 2) + (away % 2) * (devices // 2)
        return jnp.where(row < cond_ref.shape[0], place * SMALL + 1 + part, -1)

    load_ada.wait()
    grad_silu = jnp.zeros((16, width), F32)
    for part in range(6):
        own = mm(
            one_hot(16, devices * SMALL, lambda row, part=part: own_column(row, part)), shares, NN
        ).astype(BF16)
        grad_silu += mm(own, ada[:, part * width : (part + 1) * width], NT)
    cond = cond_ref[...].astype(F32)
    gate = 1.0 / (1.0 + jnp.exp(-cond))
    gcond_ref[...] = grad_silu[: cond_ref.shape[0]] * (gate * (1.0 + cond * (1.0 - gate)))
    for copy in started:
        copy.wait()


def outputs(dx, block, attn_sum, ffn_sum, small, cond, w_ada):
    slots, _, quarter, width = dx.shape
    slab = attn_sum.shape[1] // 2
    pieces = ffn_sum.shape[0]
    local = pieces * CHUNK
    shape = jax.ShapeDtypeStruct
    tokens = (slots, 4 * quarter, width)
    return pl.pallas_call(
        outputs_kernel,
        out_shape=(
            shape(w_ada.shape, F32),
            shape(tokens, F32),
            shape(tokens, BF16),
            shape((3, width, slab), F32),
            shape((slab, width), F32),
            shape((width, local), F32),
            shape((local, width), F32),
            shape(cond.shape, F32),
        ),
        in_specs=[whole()] * 6 + [whole(pl.ANY)],
        out_specs=(whole(pl.ANY),) * 7 + (whole(),),
        scratch_shapes=[
            pltpu.VMEM(w_ada.shape, BF16),
            pltpu.VMEM((6, width, width), F32),
            pltpu.VMEM(tokens, F32),
            pltpu.VMEM(tokens, BF16),
            pltpu.VMEM((3, width, slab), F32),
            pltpu.VMEM((slab, width), F32),
            pltpu.VMEM((width, local), F32),
            pltpu.VMEM((local, width), F32),
            pltpu.SemaphoreType.DMA((6 + 3 + 1 + 2 * slots + pieces + 1,)),
            pltpu.SemaphoreType.DMA((1,)),
        ],
        compiler_params=pltpu.CompilerParams(vmem_limit_bytes=56 * MIB),
        name="outputs",
    )(dx, block, attn_sum, ffn_sum, small, cond, w_ada)


def per_device(
    tokens, condition, cotangent, counts, w_ada, k_attn, w_qkv, w_out, w_up, k_ffn, w_down
):
    lat_dev, shard_rows, width = tokens.shape
    here = lax.axis_index("narrow")
    rows_all = shard_rows * lat_dev
    local = w_up.shape[1]

    n_wide = lax.axis_size("wide")
    qkv_t = w_qkv.transpose(2, 1, 0).reshape(w_qkv.shape[2], 3 * width)
    ktaps_own = jnp.pad(k_ffn.reshape(9, local), ((0, 7), (0, 0)))
    attn_taps = k_attn.reshape(9, width).astype(F32)

    cond_f = condition.astype(F32)
    silu_low = jax.nn.silu(cond_f).astype(BF16)
    own_silu = jnp.broadcast_to(lax.dynamic_slice_in_dim(silu_low, here, 1, 0), (16, width))
    live = (here < counts[0]).astype(F32).reshape(1, 1)

    (x, cot, mod, u, qkv, probs, ctx, att, x1, h2, h2t, db, wqkv, wout, wup, wdown, ktaps) = front(
        live, own_silu, attn_taps, tokens, cotangent, w_ada, qkv_t, w_out, w_up, w_down, ktaps_own
    )
    cot = cot.reshape(rows_all, width)
    ffn_taps = ktaps[:, :9].astype(F32)
    block_g, dx1, datt, dmod_mid, parcels = ffn(
        n_wide, live, h2, h2t, db, x1, cot, att, mod, wup, wdown, ffn_taps
    )
    block_g = block_g.reshape(4, lat_dev, shard_rows // 4, width)
    dqkv, own, ffn_sum, gtaps = attn_backward(n_wide, datt, ctx, u, wout, parcels, qkv, probs)
    got_dx, got_block, attn_sum, small, dattn_taps = input_backward(
        n_wide, x, dx1, dqkv, mod, attn_taps, wqkv, own, own_silu, dmod_mid, block_g
    )
    grad_w_ada, grad_tokens, block, gqkv, grad_w_out, grad_w_up, grad_w_down, grad_condition = outputs(
        got_dx, got_block, attn_sum, ffn_sum, small, condition, w_ada
    )
    grad_k_ffn = gtaps[:9].reshape(3, 3, local)
    grad_k_attn = dattn_taps[:9].reshape(3, 3, width)
    grad_w_qkv = gqkv.transpose(1, 0, 2)
    return (
        block,
        grad_tokens,
        grad_condition,
        grad_w_ada,
        grad_k_attn,
        grad_w_qkv,
        grad_w_out,
        grad_w_up,
        grad_k_ffn,
        grad_w_down,
    )


def solution(mesh):
    placed = (
        P("wide", "narrow", None),
        P("wide", None),
        P("wide", "narrow", None),
        P("wide"),
        P(),
        P(),
        P(None, None, "narrow"),
        P("narrow", None),
        P(None, "narrow"),
        P(None, None, "narrow"),
        P("narrow", None),
    )
    return jax.shard_map(
        per_device,
        mesh=mesh,
        in_specs=placed,
        out_specs=(
            P("wide", "narrow", None),
            P("wide", "narrow", None),
            P("wide", None),
            P(),
            P(),
            P(None, None, "narrow"),
            P("narrow", None),
            P(None, "narrow"),
            P(None, None, "narrow"),
            P("narrow", None),
        ),
        check_vma=False,
    )
```

```python
from functools import partial

import jax
import jax.numpy as jnp
from jax import lax
from jax.experimental import pallas as pl
from jax.experimental.pallas import tpu as pltpu
from jax.sharding import PartitionSpec as P

HEAD_DIM = 64
SIDE = 32
HALF = SIDE // 2
PHASE = HALF * HALF
PAD = PHASE + 2 * HALF
LANES = 128
ROWS = 64
CHUNK = 256
LOG2E = 1.4426950408889634
GELU_C = 0.7978845608028654
GELU_A = 0.044715
MIB = 1 << 20
F32 = jnp.float32
BF16 = jnp.bfloat16

NN = (((1,), (0,)), ((), ()))
NT = (((1,), (1,)), ((), ()))
TN = (((0,), (0,)), ((), ()))


def mm(left, right, dims):
    return lax.dot_general(left, right, dims, preferred_element_type=F32)


def ds(start, size, unit=None):
    return pl.ds(pl.multiple_of(start, unit or size), size)


def tap_source(parity, tap):
    return {-1: (1, -1), 0: (0, 0), 1: (1, 0), 2: (0, 1)}[parity + tap - 1]


def shift_cols(base, shifted, lanes):
    col = lax.broadcasted_iota(jnp.int32, (ROWS, LANES), 0) % HALF

    def rows_step(step, carry):
        for group in range(4):
            rows = ds(HALF + step * ROWS, ROWS, HALF)
            value = base[group, rows, lanes]
            if group % 2:
                moved = jnp.where(col == 0, 0.0, pltpu.roll(value, 1, 0))
            else:
                moved = jnp.where(col == HALF - 1, 0.0, pltpu.roll(value, ROWS - 1, 0))
            shifted[group, rows, lanes] = moved
        return carry

    lax.fori_loop(0, PHASE // ROWS, rows_step, 0)


def clear_edges(ref):
    edge = jnp.zeros((HALF, ref.shape[-1]), ref.dtype)
    for group in range(4):
        ref[group, :HALF, :] = edge
        ref[group, PAD - HALF :, :] = edge


def tap_value(base, shifted, group, tap_row, tap_col, start, lanes):
    src_row, row_move = tap_source(group // 2, tap_row)
    src_col, col_move = tap_source(group % 2, tap_col)
    ref = base if col_move == 0 else shifted
    return ref[2 * src_row + src_col, ds(HALF + row_move * HALF + start, ROWS, HALF), lanes]


def normed(values_in):
    mean_val = jnp.mean(values_in, axis=-1, keepdims=True)
    centred = values_in - mean_val
    inv = lax.rsqrt(jnp.mean(centred * centred, axis=-1, keepdims=True) + 1e-06)
    return centred * inv, inv


def norm_back(unit, inv, grad):
    mean_grad = jnp.mean(grad, axis=-1, keepdims=True)
    mean_dot = jnp.mean(grad * unit, axis=-1, keepdims=True)
    return (grad - mean_grad - unit * mean_dot) * inv


def narrow_peers(here):
    return [here ^ 2, here ^ 3, here ^ 1]


def remote(src, dst, sems, at, wide, narrow):
    return pltpu.make_async_remote_copy(
        src_ref=src,
        dst_ref=dst,
        send_sem=sems.at[0, at],
        recv_sem=sems.at[1, at],
        device_id=(wide, narrow),
        device_id_type=pl.DeviceIdType.MESH,
    )


class Gather:
    COPIES = 11

    def __init__(self, src, dst, sems, local_sem, first, wide, here):
        count = src.shape[0]
        quarter = count // 4
        front = -(-quarter // 32) * 16
        mine = wide % 4
        far, near = here ^ 2, here ^ 1

        def slot(k):
            return dst.at[k * count : (k + 1) * count]

        def at(k, which, start=0, size=quarter):
            return dst.at[ds(k * count + which * quarter + start, size, 16)]

        def send(number, source, target, wide_to, narrow_to):
            return remote(source, target, sems, first + number, wide_to, narrow_to)

        def same(number, which, wide_to, start=0, size=quarter):
            return send(number, at(2, which, start, size), at(2, which, start, size), wide_to, here)

        def share(number, which, start=0, size=quarter):
            return send(number, at(2, which, start, size), at(3, which, start, size), wide, near)

        own_part = src.at[ds(mine * quarter, quarter, 16)]
        rest = quarter - front
        self.own = pltpu.make_async_copy(src, slot(0), local_sem)
        self.near = send(0, src, slot(1), wide, near)
        self.far = send(1, own_part, at(2, mine), wide, far)
        self.swaps = [same(2, mine, wide ^ 1), same(3, mine, wide ^ 2)]
        self.corners = [same(4, mine ^ 1, wide ^ 2, 0, front), same(5, mine ^ 2, wide ^ 1, front, rest)]
        self.shares = [
            share(6, mine),
            share(7, mine ^ 1),
            share(8, mine ^ 2),
            share(9, mine ^ 3, 0, front),
            share(10, mine ^ 3, front, rest),
        ]

    def start_near(self):
        self.own.start()
        self.near.start()

    def start_far(self):
        self.far.start()

    def swap(self):
        self.far.wait_recv()
        self.swaps[0].start()
        self.swaps[1].start()
        self.shares[0].start()

    def corner(self):
        for which in range(2):
            self.swaps[which].wait_recv()
            self.corners[which].start()
            self.shares[1 + which].start()

    def share_corner(self):
        for which in range(2):
            self.corners[which].wait_recv()
            self.shares[3 + which].start()

    def finish(self):
        self.own.wait()
        self.near.wait()
        self.far.wait_send()
        for copy in self.swaps + self.corners:
            copy.wait_send()
        for copy in self.shares:
            copy.wait()


def group_permutation(rows):
    out = lax.broadcasted_iota(jnp.int32, (rows, rows), 0)
    source = lax.broadcasted_iota(jnp.int32, (rows, rows), 1)
    per_group = rows // 4
    group, rest = out // per_group, out % per_group
    line = 2 * (rest // HALF) + group // 2
    wanted = line * SIDE + 2 * (rest % HALF) + group % 2
    return jnp.where(source == wanted, 1.0, 0.0).astype(BF16)


class Exchange:
    def __init__(self, sent, got, sems, local_sem, first, wide, here):
        self.own = pltpu.make_async_copy(sent.at[here], got.at[:, here], local_sem)
        self.copies = [
            remote(sent.at[peer], got.at[:, here], sems, first + at, wide, peer)
            for at, peer in enumerate(narrow_peers(here))
        ]

    def start(self):
        for copy in self.copies:
            copy.start()
        self.own.start()

    def wait(self):
        self.own.wait()
        for copy in self.copies:
            copy.wait()


class Return:
    def __init__(self, sent, got, sems, local_sem, first, wide, here):
        self.own = pltpu.make_async_copy(sent.at[:, here], got.at[here], local_sem)
        self.copies = [
            remote(sent.at[:, peer], got.at[here], sems, first + at, wide, peer)
            for at, peer in enumerate(narrow_peers(here))
        ]

    start = Exchange.start
    wait = Exchange.wait


HALVINGS = 3


class WideSum:
    def __init__(self, source, work, full, got, sems, first, wide, here, n_wide, done=0, order=None):
        self.source, self.work, self.full, self.got = source, work, full, got
        self.rows = work.shape[0]
        self.levels = min(HALVINGS, n_wide.bit_length() - 1)
        self.extra = n_wide.bit_length() - 1 - self.levels
        self.done = done
        self.wide, self.here, self.sems, self.first = wide, here, sems, first
        self.offsets = [0]
        self.masks = [1 << at for at in (order or range(HALVINGS)) if at < self.levels]
        for level in range(self.levels):
            bit = (wide // self.masks[level]) % 2
            self.offsets.append(self.offsets[-1] + bit * (self.rows >> (level + 1)))
        self.waiting = []

    def size(self, level):
        return self.rows >> level

    def at(self, ref, offset, size):
        return ref.at[ds(offset, size, 16)]

    def half_copy(self, level):
        size, base = self.size(level + 1), self.offsets[level]
        send = base + size - (self.offsets[level + 1] - base)
        source = self.source if level == self.done else self.work
        landing = self.rows - self.size(level)
        return remote(
            self.at(source, send, size), self.got.at[landing : landing + size],
            self.sems, self.first + level, self.wide ^ self.masks[level], self.here,
        )

    def start_half(self, level):
        self.half_copy(level).start()

    def finish_half(self, level):
        self.half_copy(level).wait_recv()
        size, landing = self.size(level + 1), self.rows - self.size(level)
        rows = ds(self.offsets[level + 1], size, 16)
        source = self.source if level == self.done else self.work
        self.work[rows, :] = (
            source[rows, :].astype(F32) + self.got[landing : landing + size, :].astype(F32)
        ).astype(BF16)

    def extras(self):
        size = self.size(self.levels)
        rows = ds(self.offsets[self.levels], size, 16)
        source = self.source if self.done == self.levels else self.work
        self.full[rows, :] = source[rows, :]
        for at in range(self.extra):
            landing = self.rows - size + at * size
            copy = remote(
                self.full.at[rows], self.got.at[landing : landing + size],
                self.sems, self.first + 2 * self.levels + at,
                self.wide ^ (1 << (self.levels + at)), self.here,
            )
            copy.start()
            copy.wait()
            self.full[rows, :] = (
                self.full[rows, :].astype(F32) + self.got[landing : landing + size, :].astype(F32)
            ).astype(BF16)

    def spread_copy(self, level):
        part = self.at(self.full, self.offsets[level + 1], self.size(level + 1))
        return remote(
            part, part, self.sems, self.first + self.levels + level, self.wide ^ self.masks[level], self.here
        )

    def actions(self):
        acts = []
        for level in range(self.done, self.levels):
            acts.append([partial(self.start_half, level)])
            if level > self.done:
                acts[-1].insert(0, partial(self.finish_half, level - 1))
        tail = [self.extras]
        if self.done < self.levels:
            tail.insert(0, partial(self.finish_half, self.levels - 1))
        for level in reversed(range(self.levels)):
            acts.append(tail + [lambda level=level: self.spread_copy(level).start()])
            tail = [lambda level=level: self.spread_copy(level).wait_recv()]
        acts.append(tail)
        return acts

    def wait_sends(self):
        for level in range(self.done, self.levels):
            self.half_copy(level).wait_send()
        for level in range(self.levels):
            self.spread_copy(level).wait_send()


def halvings_ahead(pieces, levels):
    return [min(levels, pieces - at) for at in range(pieces)]


def greet(partners):
    barrier = pltpu.get_barrier_semaphore()
    for partner in partners:
        pl.semaphore_signal(
            barrier, inc=1, device_id=partner, device_id_type=pl.DeviceIdType.MESH
        )
    pl.semaphore_wait(barrier, len(partners))


def wide_partners(wide, here, n_wide):
    return [(wide ^ (1 << level), here) for level in range(n_wide.bit_length() - 1)]


def sum_semaphores(n_wide):
    levels = n_wide.bit_length() - 1
    return levels + min(levels, HALVINGS)


def sum_landing(rows, n_wide):
    levels = n_wide.bit_length() - 1
    last = rows >> min(levels, HALVINGS)
    return rows - last + max(levels - HALVINGS, 0) * last


def front_kernel(
    live_ref, silu_ref, taps_ref, tokens_hbm, cot_hbm, ada_hbm, wqkv_src, wout_src, wup_src, wdown_src, ktaps_src,
    x_hbm, cot_hbm_out, u_hbm, qkv_hbm, probs_hbm, ctx_hbm, wqkv_hbm, wout_hbm,
    mod_ref, att_ref, x1_ref, h2_ref, h2t_ref, db_ref, wup_ref, wdown_ref, ktaps_ref,
    x_ref, cot_ref, u_ref, qkv_ref, probs_ref, ctx_ref, wqkv_ref, wout_ref,
    base, shifted, shards, sent, sent_cot, got, ada, up_own, down_own, sems, local_sems, in_sems, out_sems,
):
    width = u_ref.shape[1]
    flushed = []

    def flush(src, dst):
        copy = pltpu.make_async_copy(src, dst, out_sems.at[len(flushed)])
        copy.start()
        flushed.append(copy)

    rows_all = u_ref.shape[0]
    latents, shard_rows = shards.shape[:2]
    wide, here = lax.axis_index("wide"), lax.axis_index("narrow")
    load_tokens = pltpu.make_async_copy(tokens_hbm, shards, in_sems.at[0])
    load_tokens.start()
    load_ada = pltpu.make_async_copy(ada_hbm, ada, in_sems.at[1])
    load_ada.start()
    load_up = pltpu.make_async_copy(wup_src, up_own, in_sems.at[2])
    load_up.start()
    load_down = pltpu.make_async_copy(wdown_src, down_own, in_sems.at[3])
    load_down.start()

    barrier = pltpu.get_barrier_semaphore()
    partners = [(wide, peer) for peer in narrow_peers(here)] + [(wide ^ 1, here), (wide ^ 2, here)]
    for partner in partners:
        pl.semaphore_signal(
            barrier, inc=1, device_id=partner, device_id_type=pl.DeviceIdType.MESH
        )
    permutation = group_permutation(shard_rows)
    load_tokens.wait()

    def permute(to):
        def one(at, carry):
            moved = mm(permutation, shards[at], NN).astype(BF16)
            for group in range(4):
                to[at, group] = moved[group * (shard_rows // 4) : (group + 1) * (shard_rows // 4)]
            return carry

        lax.fori_loop(0, latents, one, 0)

    permute(sent)
    pl.semaphore_wait(barrier, len(partners))
    exchange = Exchange(sent, got, sems, local_sems.at[0], 0, wide, here)
    exchange_cot = Exchange(sent_cot, cot_ref, sems, local_sems.at[1], 3, wide, here)
    gathers = [
        Gather(src, dst, sems, local_sems.at[2 + at], 9 + Gather.COPIES * at, wide, here)
        for at, (src, dst) in enumerate(
            (
                (wqkv_src, wqkv_ref),
                (wout_src, wout_ref),
                (up_own, wup_ref),
                (down_own, wdown_ref),
            )
        )
    ]
    g_qkv, g_out, g_up, g_down = gathers
    taps_own = pltpu.make_async_copy(ktaps_src, ktaps_ref.at[0], local_sems.at[6])
    taps_sends = [
        remote(ktaps_src, ktaps_ref.at[peer ^ here], sems, 6 + at, wide, peer)
        for at, peer in enumerate(narrow_peers(here))
    ]
    exchange.start()
    load_cot = pltpu.make_async_copy(cot_hbm, shards, in_sems.at[0])
    load_cot.start()
    load_up.wait()
    load_down.wait()
    for one in gathers:
        one.start_near()
    taps_own.start()
    for one in taps_sends:
        one.start()

    load_ada.wait()
    for part in range(6):
        mod_ref[part : part + 1, :] = mm(
            silu_ref[...], ada[:, part * width : (part + 1) * width], NN
        )[0:1, :]
    load_cot.wait()
    permute(sent_cot)
    shift_one, scale_one, gate_one = mod_ref[0:1, :], mod_ref[1:2, :], mod_ref[2:3, :]
    shift_two, scale_two, gate_two = mod_ref[3:4, :], mod_ref[4:5, :], mod_ref[5:6, :]
    clear_edges(base)
    clear_edges(shifted)
    exchange.wait()
    g_qkv.start_far()
    g_out.start_far()
    for group in range(4):
        for source in range(latents):
            start = group * PHASE + source * ROWS
            x_ref[start : start + ROWS, :] = got[group, source]
    flush(x_ref, x_hbm)

    def norm_step(step, carry):
        group, part = step // (PHASE // ROWS), step % (PHASE // ROWS)
        unit, _ = normed(x_ref[ds(step * ROWS, ROWS), :].astype(F32))
        h_one = (unit * (1.0 + scale_one) + shift_one).astype(BF16)
        base[group, ds(HALF + part * ROWS, ROWS, HALF), :] = h_one.astype(F32)
        return carry

    lax.fori_loop(0, rows_all // ROWS, norm_step, 0)
    g_qkv.swap()
    g_out.swap()
    g_up.start_far()

    def conv_step(block, carry):
        lanes = ds(block * LANES, LANES)
        shift_cols(base, shifted, lanes)
        taps = [taps_ref[t : t + 1, lanes] for t in range(9)]

        def rows_step(step, carry):
            for group in range(4):
                total = jnp.zeros((ROWS, LANES), F32)
                for tap in range(9):
                    total += taps[tap] * tap_value(
                        base, shifted, group, tap // 3, tap % 3, step * ROWS, lanes
                    )
                u_ref[ds(group * PHASE + step * ROWS, ROWS), lanes] = total.astype(BF16)
            return carry

        return lax.fori_loop(0, PHASE // ROWS, rows_step, carry)

    blocks = width // LANES
    lax.fori_loop(0, 2 * blocks // 3, conv_step, 0)
    g_qkv.corner()
    g_out.corner()
    g_up.swap()
    exchange_cot.start()
    lax.fori_loop(2 * blocks // 3, blocks, conv_step, 0)
    flush(u_ref, u_hbm)
    g_qkv.share_corner()
    g_qkv.finish()
    flush(wqkv_ref, wqkv_hbm)

    def project_step(step, carry):
        rows = ds(step * PHASE, PHASE)
        for part in range(3):
            cols = slice(part * width, (part + 1) * width)
            qkv_ref[rows, cols] = mm(u_ref[rows, :], wqkv_ref[:, cols], NT).astype(BF16)
        return carry

    lax.fori_loop(0, 4, project_step, 0)

    pairs = width // LANES
    first = lax.broadcasted_iota(jnp.int32, (PHASE, LANES), 1) < HEAD_DIM
    zero = jnp.zeros((PHASE, LANES), BF16)

    def attend_step(step, carry):
        group, pair = step // pairs, step % pairs
        rows = ds(group * PHASE, PHASE)
        query = qkv_ref[rows, ds(pair * LANES, LANES)]
        key = qkv_ref[rows, ds(width + pair * LANES, LANES)]
        value = qkv_ref[rows, ds(2 * width + pair * LANES, LANES)]
        found = []
        for head in range(2):
            own = jnp.where(first, query, zero) if head == 0 else jnp.where(first, zero, query)
            scores = mm(key, own, NT)
            top = jnp.max(scores, axis=0, keepdims=True)
            raised = jnp.exp2((scores - top) * (LOG2E * HEAD_DIM**-0.5))
            probs = (raised * (1.0 / jnp.sum(raised, axis=0, keepdims=True))).astype(BF16)
            probs_ref[step, :, head * PHASE : (head + 1) * PHASE] = probs
            found.append(mm(probs, value, TN))
        ctx_ref[rows, ds(pair * LANES, LANES)] = jnp.where(first, found[0], found[1]).astype(BF16)
        return carry

    flush(qkv_ref, qkv_hbm)
    g_up.corner()
    g_out.share_corner()

    def attend_group(group):
        lax.fori_loop(group * pairs, (group + 1) * pairs, attend_step, 0)
        done = slice(group * pairs, (group + 1) * pairs)
        flush(probs_ref.at[done], probs_hbm.at[done])

    attend_group(0)
    g_up.share_corner()
    exchange_cot.wait()
    flush(cot_ref, cot_hbm_out)
    g_down.start_far()
    attend_group(1)
    attend_group(2)
    g_down.swap()
    attend_group(3)
    flush(ctx_ref, ctx_hbm)
    g_out.finish()
    flush(wout_ref, wout_hbm)

    def out_step(step, carry):
        rows = ds(step * PHASE, PHASE)
        total = mm(ctx_ref[rows, :], wout_ref[...], NN)
        att_ref[rows, :] = total.astype(BF16)
        x1_ref[rows, :] = x_ref[rows, :].astype(F32) + gate_one * total
        return carry

    lax.fori_loop(0, 4, out_step, 0)
    live = live_ref[0, 0]

    def second_step(step, carry):
        rows = ds(step * ROWS, ROWS)
        unit, _ = normed(x1_ref[rows, :])
        h2_ref[rows, :] = (unit * (1.0 + scale_two) + shift_two).astype(BF16)
        group, source = step // (PHASE // ROWS), step % (PHASE // ROWS)
        db_ref[rows, :] = (cot_ref[group, source].astype(F32) * live * gate_two).astype(BF16)
        return carry

    g_down.corner()
    lax.fori_loop(0, rows_all // ROWS, second_step, 0)
    g_down.share_corner()
    for part in range(4):
        h2t_ref[:, part * PHASE : (part + 1) * PHASE] = h2_ref[
            part * PHASE : (part + 1) * PHASE, :
        ].T
    g_up.finish()
    g_down.finish()
    for copy in flushed:
        copy.wait()
    taps_own.wait()
    for one in taps_sends:
        one.wait()


def whole(memory=pltpu.VMEM):
    return pl.BlockSpec(memory_space=memory)


def front(live, silu_row, taps, tokens, cot, w_ada, wqkv, wout, wup, wdown, ktaps):
    latents, shard_rows, width = tokens.shape
    rows = latents * shard_rows
    steps = 4 * (width // LANES)
    shape = jax.ShapeDtypeStruct
    full = lambda shard: shape((latents * shard.shape[0],) + shard.shape[1:], BF16)
    moved = (latents, 4, shard_rows // 4, width)
    streamed = (
        shape((rows, width), BF16),
        shape((4, latents, shard_rows // 4, width), BF16),
        shape((rows, width), BF16),
        shape((rows, 3 * width), BF16),
        shape((steps, PHASE, 2 * PHASE), BF16),
        shape((rows, width), BF16),
        full(wqkv),
        full(wout),
    )
    return pl.pallas_call(
        front_kernel,
        out_shape=streamed
        + (
            shape((6, width), F32),
            shape((rows, width), BF16),
            shape((rows, width), F32),
            shape((rows, width), BF16),
            shape((width, rows), BF16),
            shape((rows, width), BF16),
            full(wup),
            full(wdown),
            shape((latents,) + ktaps.shape, BF16),
        ),
        in_specs=[whole(pltpu.SMEM)] + [whole()] * 2 + [whole(pl.ANY)] * 3 + [whole()] * 2 + [whole(pl.ANY)] * 2 + [whole()],
        out_specs=(whole(pl.ANY),) * 8 + (whole(),) * 6 + (whole(pl.ANY),) * 2 + (whole(),),
        scratch_shapes=[pltpu.VMEM(one.shape, one.dtype) for one in streamed]
        + [
            pltpu.VMEM((4, PAD, width), F32),
            pltpu.VMEM((4, PAD, width), F32),
            pltpu.VMEM((latents, shard_rows, width), BF16),
            pltpu.VMEM(moved, BF16),
            pltpu.VMEM(moved, BF16),
            pltpu.VMEM((4, latents, shard_rows // 4, width), BF16),
            pltpu.VMEM(w_ada.shape, BF16),
            pltpu.VMEM(wup.shape, BF16),
            pltpu.VMEM(wdown.shape, BF16),
            pltpu.SemaphoreType.DMA((2, 9 + 4 * Gather.COPIES)),
            pltpu.SemaphoreType.DMA((7,)),
            pltpu.SemaphoreType.DMA((4,)),
            pltpu.SemaphoreType.DMA((len(streamed) + 3,)),
        ],
        compiler_params=pltpu.CompilerParams(
            vmem_limit_bytes=60 * MIB, collective_id=0, has_side_effects=True
        ),
        name="attn_forward",
    )(live, silu_row, taps, tokens, cot, w_ada, wqkv, wout, wup, wdown, ktaps)


def ffn_kernel(
    n_wide, live_ref, h2_ref, h2t_ref, db_ref, x1_hbm, cot_hbm, att_hbm, mod_ref,
    wup_before, wup_even, wup_odd, wup_after, wdown_even, wdown_odd, taps_even, taps_odd,
    block_ref, dx1_ref, datt_ref, dmod_ref, sums_ref,
    hid_even, hid_odd, hid_moved, grad, grad_moved, slope, act, act_t, dhid, branch, dtaps,
    work, chip_sum, got_near, got_far, got_sums, x1_ref, cot_ref, att_ref, sems, sum_sems, in_sems,
):
    rows_all, width = h2_ref.shape
    loads = [
        pltpu.make_async_copy(src, dst, in_sems.at[at])
        for at, (src, dst) in enumerate(((x1_hbm, x1_ref), (cot_hbm, cot_ref), (att_hbm, att_ref)))
    ]
    dh2 = dx1_ref
    wide, here = lax.axis_index("wide"), lax.axis_index("narrow")
    step, steps = pl.program_id(0), pl.num_programs(0)
    quarters = [slice(q * PHASE, (q + 1) * PHASE) for q in range(4)]
    inside = slice(HALF, HALF + PHASE)
    lane_blocks = [slice(at * LANES, (at + 1) * LANES) for at in range(CHUNK // LANES)]
    col = lax.broadcasted_iota(jnp.int32, (ROWS, LANES), 0) % HALF

    partners = [(wide, here ^ 1), (wide, here ^ 2)] + wide_partners(wide, here, n_wide)[:HALVINGS]
    pieces, sum_rows = got_sums.shape[0], got_sums.shape[1]
    sums = [
        WideSum(sums_ref.at[at, : 2 * width], sums_ref.at[at, : 2 * width], None, got_sums.at[at], sum_sems,
                at * HALVINGS, wide, here, n_wide)
        for at in range(pieces)
    ]
    schedule = halvings_ahead(pieces, sums[0].levels)

    def to_near(at):
        return remote(work.at[at % 2], got_near.at[at], sems, at, wide, here ^ 1)

    def to_far(at):
        return remote(chip_sum.at[at], got_far.at[at], sems, steps + at, wide, here ^ 2)

    @pl.when(step == 0)
    def _():
        for load in loads:
            load.start()
        barrier = pltpu.get_barrier_semaphore()
        for partner in partners:
            pl.semaphore_signal(
                barrier, inc=1, device_id=partner, device_id_type=pl.DeviceIdType.MESH
            )
        for ref in (hid_even, hid_odd, hid_moved, grad, grad_moved):
            clear_edges(ref)
        branch[...] = jnp.zeros_like(branch)
        dh2[...] = jnp.zeros_like(dh2)
        dtaps[...] = jnp.zeros_like(dtaps)
        dhid[...] = jnp.zeros_like(dhid)
        full = mm(h2_ref[...], wup_even[...], NN)
        for q in range(4):
            hid_even[q, inside, :] = full[quarters[q]]
        pl.semaphore_wait(barrier, len(partners))

    def moved_cols(group, value):
        if group % 2:
            return jnp.where(col == 0, 0.0, pltpu.roll(value, 1, 0))
        return jnp.where(col == HALF - 1, 0.0, pltpu.roll(value, ROWS - 1, 0))

    def static_tap(base, shifted, group, tap_row, tap_col, start, lanes):
        src_row, row_move = tap_source(group // 2, tap_row)
        src_col, col_move = tap_source(group % 2, tap_col)
        ref = base if col_move == 0 else shifted
        first = HALF + row_move * HALF + start
        return ref[2 * src_row + src_col, first : first + ROWS, lanes]

    def weights_back(q, wup_last, slot):
        dh2[quarters[q], :] += mm(dhid[quarters[q], :], wup_last[...], NT)
        if q < width // PHASE:
            slot[quarters[q], :] = mm(h2t_ref[quarters[q], :], dhid[...], NN).astype(BF16)

    def forward_products(part, wdown, wup_last, slot):
        grad[part, inside, :] = mm(db_ref[quarters[part], :], wdown[...], NT)
        yield
        for cols in quarters[: width // PHASE]:
            dh2[quarters[part], cols] += mm(dhid[quarters[part], :], wup_last[cols, :], NT)
            yield
        if part < width // PHASE:
            slot[quarters[part], :] = mm(h2t_ref[quarters[part], :], dhid[...], NN).astype(BF16)
        yield

    def backward_products(part, hid_next, wdown, wup_next, slot):
        hid_next[part, inside, :] = mm(h2_ref[quarters[part], :], wup_next[...], NN)
        yield
        for cols in quarters[: width // PHASE]:
            branch[quarters[part], cols] += mm(act[quarters[part], :], wdown[:, cols], NN)
            yield
        if part < width // CHUNK:
            block = slice(part * CHUNK, (part + 1) * CHUNK)
            slot[width + part * CHUNK : width + (part + 1) * CHUNK, :] = mm(
                act_t[...], db_ref[:, block], NN
            ).astype(BF16)
        yield

    def forward(hid, wdown, taps_ref, wup_last, slot):
        taps = [[taps_ref[0, t : t + 1, lanes] for t in range(9)] for lanes in lane_blocks]
        for part in range(PHASE // ROWS):
            rows = slice(HALF + part * ROWS, HALF + (part + 1) * ROWS)
            for group in range(4):
                for lanes in lane_blocks:
                    hid_moved[group, rows, lanes] = moved_cols(group, hid[group, rows, lanes])
        for part in range(PHASE // ROWS):
            products = forward_products(part, wdown, wup_last, slot)
            for group in range(4):
                for at, lanes in enumerate(lane_blocks):
                    next(products, None)
                    total = jnp.zeros((ROWS, LANES), F32)
                    for tap in range(9):
                        total += taps[at][tap] * static_tap(
                            hid, hid_moved, group, tap // 3, tap % 3, part * ROWS, lanes
                        )
                    square = total * total
                    turned = jnp.tanh(total * (square * (GELU_C * GELU_A) + GELU_C))
                    half = 0.5 * turned + 0.5
                    bend = total * (half - half * half)
                    start = group * PHASE + part * ROWS
                    act[start : start + ROWS, lanes] = (total * half).astype(BF16)
                    slope[start : start + ROWS, lanes] = half + bend * (
                        square * (6.0 * GELU_C * GELU_A) + 2.0 * GELU_C
                    )

    def backward(hid, hid_next, wdown, wup_next, taps_ref, slot):
        taps = [[taps_ref[0, t : t + 1, lanes] for t in range(9)] for lanes in lane_blocks]
        act_t[...] = act[...].T
        for part in range(PHASE // ROWS):
            rows = slice(HALF + part * ROWS, HALF + (part + 1) * ROWS)
            for group in range(4):
                start = group * PHASE + part * ROWS
                for lanes in lane_blocks:
                    value = grad[group, rows, lanes] * slope[start : start + ROWS, lanes]
                    grad[group, rows, lanes] = value
                    grad_moved[group, rows, lanes] = moved_cols(group, value)
        sums = [[jnp.zeros((8, LANES), F32) for _ in range(9)] for _ in lane_blocks]
        for part in range(PHASE // ROWS):
            products = backward_products(part, hid_next, wdown, wup_next, slot)
            for group in range(4):
                start = group * PHASE + part * ROWS
                for at, lanes in enumerate(lane_blocks):
                    next(products, None)
                    own = hid[group, HALF + part * ROWS : HALF + (part + 1) * ROWS, lanes]
                    total = jnp.zeros((ROWS, LANES), F32)
                    for tap in range(9):
                        moved = static_tap(
                            grad, grad_moved, group, 2 - tap // 3, 2 - tap % 3, part * ROWS, lanes
                        )
                        total += taps[at][tap] * moved
                        sums[at][tap] += (own * moved).reshape(ROWS // 8, 8, LANES).sum(axis=0)
                    dhid[start : start + ROWS, lanes] = total.astype(BF16)
        for at, lanes in enumerate(lane_blocks):
            for tap in range(9):
                dtaps[tap : tap + 1, lanes] = jnp.sum(sums[at][tap], axis=0, keepdims=True)
        slot[2 * width :, :] = dtaps[...].astype(BF16)

    def settle(pair):
        to_near(pair).wait_recv()

        @pl.when(pair < steps // 2)
        def _():
            chip_sum[pair] = (work[2].astype(F32) + got_near[pair].astype(F32)).astype(BF16)
            to_far(pair).start()

        @pl.when(pair >= steps // 2)
        def _():
            part = pair - steps // 2
            to_far(part).wait_recv()
            sums_ref[part] = (
                work[2].astype(F32) + got_near[pair].astype(F32) + got_far[part].astype(F32)
            ).astype(BF16)

        for part in range(pieces):

            @pl.when(pair == steps // 2 + part)
            def _():
                for at in range(part):
                    sums[at].finish_half(part - at - 1)
                for at in range(part + 1):
                    if part - at < schedule[at]:
                        sums[at].start_half(part - at)

    forward(hid_even, wdown_even, taps_even, wup_before, work.at[2])

    @pl.when(step >= 1)
    def _():
        settle(step - 1)

    @pl.when(step >= 2)
    def _():
        to_near(step - 2).wait_send()

    even_slot = work.at[step % 2]
    backward(hid_even, hid_odd, wdown_even, wup_odd, taps_even, even_slot)
    forward(hid_odd, wdown_odd, taps_odd, wup_even, even_slot)
    to_near(step).start()
    backward(hid_odd, hid_even, wdown_odd, wup_after, taps_odd, work.at[2])

    @pl.when(step == steps - 1)
    def _():
        for q in range(4):
            weights_back(q, wup_odd, work.at[2])
        settle(step)
        for load in loads:
            load.wait()
        gate_one, scale_two, gate_two = mod_ref[2:3, :], mod_ref[4:5, :], mod_ref[5:6, :]
        live = live_ref[0, 0]

        def fold(value):
            return value.reshape(ROWS // 8, 8, width).sum(axis=0)

        def rows_step(at, sums):
            rows = ds(at * ROWS, ROWS)
            after = x1_ref[rows, :]
            dout = cot_ref[rows, :].astype(F32) * live
            branch_rows = branch[rows, :]
            block_ref[rows, :] = ((after + gate_two * branch_rows) * live).astype(BF16)
            unit, inv = normed(after)
            dh2_rows = dh2[rows, :]
            dx1 = dout + norm_back(unit, inv, dh2_rows * (1.0 + scale_two))
            dx1_ref[rows, :] = dx1
            datt_ref[rows, :] = (dx1 * gate_one).astype(BF16)
            found = (dx1 * att_ref[rows, :].astype(F32), dh2_rows, dh2_rows * unit, dout * branch_rows)
            return tuple(total + fold(one) for total, one in zip(sums, found))

        start = tuple(jnp.zeros((8, width), F32) for _ in range(4))
        totals = lax.fori_loop(0, rows_all // ROWS, rows_step, start)
        for at in range(4):
            dmod_ref[at : at + 1, :] = jnp.sum(totals[at], axis=0, keepdims=True)
        for at in (steps - 2, steps - 1):
            to_near(at).wait_send()
        for at in range(steps // 2):
            to_far(at).wait_send()
        for at in range(pieces):
            sums[at].finish_half(schedule[at] - 1)
            for level in range(schedule[at]):
                sums[at].half_copy(level).wait_send()


def conv_back(grad, grad_moved, source, lanes, taps, dtaps_ref, out_ref):
    def rows_step(step, sums):
        sums = list(sums)
        for group in range(4):
            total = jnp.zeros((ROWS, LANES), F32)
            own = source[group, ds(HALF + step * ROWS, ROWS, HALF), lanes]
            for tap in range(9):
                moved = tap_value(
                    grad, grad_moved, group, 2 - tap // 3, 2 - tap % 3, step * ROWS, lanes
                )
                total += taps[tap] * moved
                sums[tap] += (own * moved).reshape(ROWS // 8, 8, LANES).sum(axis=0)
            out_ref[ds(group * PHASE + step * ROWS, ROWS), lanes] = total.astype(out_ref.dtype)
        return tuple(sums)

    start = tuple(jnp.zeros((8, LANES), F32) for _ in range(9))
    sums = lax.fori_loop(0, PHASE // ROWS, rows_step, start)
    for tap in range(9):
        dtaps_ref[tap : tap + 1, lanes] = jnp.sum(sums[tap], axis=0, keepdims=True)


def ffn(n_wide, live, h2, h2t, db, x1, cot, att, mod, wup, wdown, taps):
    rows, width = h2.shape
    shards, _, local = taps.shape
    per = local // CHUNK
    steps = shards * per // 2
    parcel = (2 * width + 16, CHUNK)
    shape = jax.ShapeDtypeStruct
    keep = lambda *block: pl.BlockSpec(
        block, lambda c: (0,) * len(block), pipeline_mode=pl.Buffered(1)
    )

    def slot_and_part(step, odd):
        return jnp.where(step < per, 3, 1) - odd, step % per

    def up_block(move, odd):
        def index(step):
            return slot_and_part(jnp.clip(step + move, 0, steps - 1), odd)

        return pl.BlockSpec((width, CHUNK), index)

    def down_block(odd):
        def index(step):
            slot, part = slot_and_part(step, odd)
            return slot * per + part, 0

        return pl.BlockSpec((CHUNK, width), index)

    def taps_block(odd):
        def index(step):
            slot, part = slot_and_part(step, odd)
            return slot, 0, part

        return pl.BlockSpec((1, 9, CHUNK), index)

    return pl.pallas_call(
        partial(ffn_kernel, n_wide),
        grid=(steps,),
        out_shape=(
            shape((rows, width), BF16),
            shape((rows, width), F32),
            shape((rows, width), BF16),
            shape((4, width), F32),
            shape((per,) + parcel, BF16),
        ),
        in_specs=[
            whole(pltpu.SMEM),
            keep(rows, width),
            keep(width, rows),
            keep(rows, width),
            whole(pl.ANY),
            whole(pl.ANY),
            whole(pl.ANY),
            keep(6, width),
            up_block(-1, 1),
            up_block(0, 0),
            up_block(0, 1),
            up_block(1, 0),
            down_block(0),
            down_block(1),
            taps_block(0),
            taps_block(1),
        ],
        out_specs=(
            keep(rows, width),
            keep(rows, width),
            keep(rows, width),
            keep(4, width),
            keep(per, *parcel),
        ),
        scratch_shapes=[pltpu.VMEM((4, PAD, CHUNK), F32)] * 5
        + [
            pltpu.VMEM((rows, CHUNK), F32),
            pltpu.VMEM((rows, CHUNK), BF16),
            pltpu.VMEM((CHUNK, rows), BF16),
            pltpu.VMEM((rows, CHUNK), BF16),
            pltpu.VMEM((rows, width), F32),
            pltpu.VMEM((16, CHUNK), F32),
            pltpu.VMEM((3,) + parcel, BF16),
            pltpu.VMEM((per,) + parcel, BF16),
            pltpu.VMEM((steps,) + parcel, BF16),
            pltpu.VMEM((per,) + parcel, BF16),
            pltpu.VMEM((per, sum_landing(2 * width, n_wide), CHUNK), BF16),
            pltpu.VMEM((rows, width), F32),
            pltpu.VMEM((rows, width), BF16),
            pltpu.VMEM((rows, width), BF16),
            pltpu.SemaphoreType.DMA((2, steps + per)),
            pltpu.SemaphoreType.DMA((2, per * HALVINGS)),
            pltpu.SemaphoreType.DMA((3,)),
        ],
        compiler_params=pltpu.CompilerParams(
            vmem_limit_bytes=62 * MIB, collective_id=1, has_side_effects=True
        ),
        name="feed_forward",
    )(live, h2, h2t, db, x1, cot, att, mod, wup, wup, wup, wup, wdown, wdown, taps, taps)


def attn_backward_kernel(
    n_wide, datt_ref, ctx_ref, u_ref, wout_ref, parcels, qkv_hbm, probs_hbm,
    dqkv_ref, own_ref, full, gtaps_ref,
    dctx, probs_buf, weights, got_near, chip_sum, got_far, work, got_sums, taps_sum, taps_got,
    sems, in_sems, sum_sems,
):
    rows_all, width = u_ref.shape
    wide, here = lax.axis_index("wide"), lax.axis_index("narrow")
    pairs = width // LANES
    half_pairs = pairs // 2
    steps = 4 * pairs
    slots = weights.shape[0]
    load_qkv = pltpu.make_async_copy(qkv_hbm, dqkv_ref, in_sems.at[2])
    load_qkv.start()

    def pair_of(step):
        return (half_pairs + step // 4) % pairs

    def load_probs(step):
        return pltpu.make_async_copy(
            probs_hbm.at[(step % 4) * pairs + pair_of(step)], probs_buf.at[step % 2], in_sems.at[step % 2]
        )

    load_probs(0).start()
    greet([(wide, here ^ 2), (wide, here ^ 1)] + wide_partners(wide, here, n_wide))
    pieces = full.shape[0]
    rows = full.shape[1]
    per_sum = sum_semaphores(n_wide)
    ahead = halvings_ahead(pieces, min(HALVINGS, n_wide.bit_length() - 1))
    sums = [
        WideSum(parcels.at[at, :rows], work.at[at], full.at[at], got_sums.at[at], sum_sems, at * per_sum,
                wide, here, n_wide, done=ahead[at])
        for at in range(pieces)
    ]
    levels = n_wide.bit_length() - 1
    queues = [one.actions() for one in sums]

    def advance(*which):
        for at in which:
            if queues[at]:
                for act in queues[at].pop(0):
                    act()

    def taps_copy(level):
        return remote(taps_sum.at[level], taps_got.at[level], sems, 6 + level, wide ^ (1 << level), here)

    def taps_add(level):
        taps_copy(level).wait_recv()
        taps_sum[level + 1] = taps_sum[level] + taps_got[level]
        if level + 1 < levels:
            taps_copy(level + 1).start()

    for at in range(pieces):
        taps_sum[0, :, at * CHUNK : (at + 1) * CHUNK] = parcels[at, rows:, :].astype(F32)
    taps_copy(0).start()
    advance(2, 0, 1)

    def ctx_step(step, carry):
        span = ds(step * PHASE, PHASE)
        dctx[span, :] = mm(datt_ref[span, :], wout_ref[...], NT).astype(BF16)
        return carry

    lax.fori_loop(0, 4, ctx_step, 0)
    load_qkv.wait()

    first = lax.broadcasted_iota(jnp.int32, (PHASE, LANES), 1) < HEAD_DIM
    zero = jnp.zeros((PHASE, LANES), BF16)
    scale = HEAD_DIM**-0.5

    def attend(step):
        group, pair = step % 4, pair_of(step)
        load_probs(step).wait()

        @pl.when(step + 1 < steps)
        def _():
            load_probs(step + 1).start()

        span = ds(group * PHASE, PHASE)
        query = dqkv_ref[span, ds(pair * LANES, LANES)]
        key = dqkv_ref[span, ds(width + pair * LANES, LANES)]
        value = dqkv_ref[span, ds(2 * width + pair * LANES, LANES)]
        dctx_pair = dctx[span, ds(pair * LANES, LANES)]
        dq, dk, dv = [], None, None
        for head in range(2):
            own = lambda both: jnp.where(first, both, zero) if head == 0 else jnp.where(first, zero, both)
            probs = probs_buf[step % 2, :, head * PHASE : (head + 1) * PHASE]
            probs_f = probs.astype(F32)
            dctx_own, query_own = own(dctx_pair), own(query)
            dprobs = mm(value, dctx_own, NT)
            inner = jnp.sum(dprobs * probs_f, axis=0, keepdims=True)
            dscores = (probs_f * (dprobs - inner)).astype(BF16)
            dv_one = mm(probs, dctx_own, NN)
            dk_one = mm(dscores, query_own, NN)
            dv = dv_one if dv is None else dv + dv_one
            dk = dk_one if dk is None else dk + dk_one
            dq.append(mm(dscores, key, TN))
        dqkv_ref[span, ds(pair * LANES, LANES)] = (
            jnp.where(first, dq[0], dq[1]) * scale
        ).astype(BF16)
        dqkv_ref[span, ds(width + pair * LANES, LANES)] = (dk * scale).astype(BF16)
        dqkv_ref[span, ds(2 * width + pair * LANES, LANES)] = dv.astype(BF16)

    def attend_loop(begin, end, plan):
        def body(step, carry):
            for at, what in plan:
                pl.when(step == at)(what)
            attend(step)
            return carry

        lax.fori_loop(begin, end, body, 0)

    slab = width // slots

    def weight_grads(half):
        span = width // 2
        for part in range(3):
            left = dqkv_ref[:, part * width + half * span : part * width + (half + 1) * span]
            found = mm(left, u_ref[...], TN).astype(BF16)
            for one in range(2):
                weights[2 * half + one, part * slab : (part + 1) * slab, :] = found[
                    one * slab : (one + 1) * slab
                ]

    head, tail = slice(3 * slab), slice(3 * slab, 4 * slab)

    def near_copy(early, rows, at):
        return remote(
            weights.at[3 if early else 1, rows], got_near.at[0 if early else 1, rows], sems, at, wide, here ^ 1
        )

    def far_copy(rows, at):
        return remote(chip_sum.at[rows], got_far.at[rows], sems, at, wide, here ^ 2)

    def add_chip(rows):
        chip_sum[rows, :] = (weights[2, rows, :].astype(F32) + got_near[0, rows, :].astype(F32)).astype(BF16)

    near_out, near_early = near_copy(True, tail, 0), near_copy(True, head, 1)
    late_out, near_late = near_copy(False, tail, 2), near_copy(False, head, 3)
    far_out, far = far_copy(tail, 4), far_copy(head, 5)

    for part in range(width // PHASE):
        cols = slice(part * PHASE, (part + 1) * PHASE)
        found = mm(ctx_ref[:, cols], datt_ref[...], TN).astype(BF16)
        for slot in range(slots):
            low, high = max(part * PHASE, slot * slab), min((part + 1) * PHASE, (slot + 1) * slab)
            if low < high:
                weights[slot, 3 * slab + low - slot * slab : 3 * slab + high - slot * slab, :] = found[
                    low - part * PHASE : high - part * PHASE
                ]
    near_out.start()
    late_out.start()

    def send_out():
        near_out.wait_recv()
        add_chip(tail)
        far_out.start()

    later = lambda *which: partial(advance, *which)
    attend_loop(
        0, steps // 2,
        [(1, send_out), (2, later(2, 0)), (5, later(1)), (7, partial(taps_add, 0)), (8, later(2, 0)), (11, later(1))],
    )
    weight_grads(1)
    near_early.start()
    advance(2)
    near_early.wait_recv()
    add_chip(head)
    far.start()
    attend_loop(
        steps // 2, steps,
        [(13, later(1, 0)), (14, partial(taps_add, 1)), (16, later(2))],
    )
    weight_grads(0)
    near_late.start()
    for level in range(2, levels):
        taps_add(level)
    gtaps_ref[...] = taps_sum[levels]
    near_late.wait_recv()
    late_out.wait_recv()
    while any(queues):
        advance(0, 1, 2)
    far_out.wait_recv()
    far.wait_recv()
    own_ref[...] = (
        weights[0].astype(F32) + got_near[1].astype(F32) + got_far[...].astype(F32)
    ).astype(BF16)
    for one in sums:
        one.wait_sends()
    for level in range(levels):
        taps_copy(level).wait_send()
    for copy in (near_out, near_early, late_out, near_late, far_out, far):
        copy.wait_send()


def attn_backward(n_wide, datt, ctx, u, wout, parcels, qkv, probs):
    rows, width = u.shape
    slots = lax.axis_size("narrow")
    slab = wout.shape[0] // slots
    pieces, parcel_rows, _ = parcels.shape
    sum_rows = parcel_rows - 16
    shape = jax.ShapeDtypeStruct
    levels = n_wide.bit_length() - 1
    per_sum = sum_semaphores(n_wide)
    return pl.pallas_call(
        partial(attn_backward_kernel, n_wide),
        out_shape=(
            shape((rows, 3 * width), BF16),
            shape((4 * slab, width), BF16),
            shape((pieces, sum_rows, CHUNK), BF16),
            shape((16, pieces * CHUNK), F32),
        ),
        in_specs=[whole()] * 5 + [whole(pl.ANY)] * 2,
        out_specs=(whole(),) * 4,
        scratch_shapes=[
            pltpu.VMEM((rows, width), BF16),
            pltpu.VMEM((2, PHASE, 2 * PHASE), BF16),
            pltpu.VMEM((slots, 4 * slab, width), BF16),
            pltpu.VMEM((2, 4 * slab, width), BF16),
            pltpu.VMEM((4 * slab, width), BF16),
            pltpu.VMEM((4 * slab, width), BF16),
            pltpu.VMEM((pieces, sum_rows, CHUNK), BF16),
            pltpu.VMEM((pieces, sum_landing(sum_rows, n_wide), CHUNK), BF16),
            pltpu.VMEM((levels + 1, 16, pieces * CHUNK), F32),
            pltpu.VMEM((levels, 16, pieces * CHUNK), F32),
            pltpu.SemaphoreType.DMA((2, 6 + levels)),
            pltpu.SemaphoreType.DMA((3,)),
            pltpu.SemaphoreType.DMA((2, pieces * per_sum)),
        ],
        compiler_params=pltpu.CompilerParams(
            vmem_limit_bytes=56 * MIB, collective_id=2, has_side_effects=True
        ),
        name="attn_backward",
    )(datt, ctx, u, wout, parcels, qkv, probs)


def one_hot(rows, columns, wanted):
    row = lax.broadcasted_iota(jnp.int32, (rows, columns), 0)
    column = lax.broadcasted_iota(jnp.int32, (rows, columns), 1)
    return jnp.where(column == wanted(row), 1.0, 0.0).astype(BF16)


SMALL = 16


def input_backward_kernel(
    n_wide, x_ref, mod_ref, taps_ref, own_ref, silu_ref, dmod_ref, dx1_hbm, dqkv_hbm, wqkv_hbm, block_in,
    got_dx, got_block, full, small, late, dtaps_ref,
    base, shifted, first_in, dh1, dx1_ref, dqkv_ref, wqkv_ref, dx, work, got_sums, tap_sums, tap_got,
    sems, local_sems, sum_sems, small_sems, late_sems,
):
    rows_all, width = x_ref.shape
    wide, here = lax.axis_index("wide"), lax.axis_index("narrow")
    loads = [
        pltpu.make_async_copy(src, dst, local_sems.at[2 + at])
        for at, (src, dst) in enumerate(
            ((dqkv_hbm, dqkv_ref), (wqkv_hbm, wqkv_ref), (dx1_hbm, dx1_ref))
        )
    ]
    for load in loads:
        load.start()
    shift_one, scale_one = mod_ref[0:1, :], mod_ref[1:2, :]
    greet([(wide, peer) for peer in narrow_peers(here)] + wide_partners(wide, here, n_wide))
    pieces = full.shape[0]
    rows = full.shape[1]
    per_sum = sum_semaphores(n_wide)
    sums = [
        WideSum(own_ref.at[at * rows : (at + 1) * rows], work.at[at], full.at[at], got_sums.at[at], sum_sems,
                at * per_sum, wide, here, n_wide, order=((0, 1, 2), (1, 2, 0))[at])
        for at in range(pieces)
    ]
    queues = [one.actions() for one in sums]

    def advance(*which):
        for at in which:
            if queues[at]:
                for act in queues[at].pop(0):
                    act()

    partners = [(wide, here ^ 2)] + wide_partners(wide, here, n_wide)[::-1] + [(wide, here ^ 1)]
    levels = len(partners)

    def small_copy(level):
        have = 1 << level
        return remote(small.at[:have], small.at[have : 2 * have], small_sems, 2 * level, *partners[level])

    def late_copy(level):
        have = 1 << level
        return remote(late.at[:have], late.at[have : 2 * have], late_sems, level, *partners[level])

    def small_step(level):
        small_copy(level).wait_recv()
        if level + 1 < levels:
            small_copy(level + 1).start()

    early = [silu_ref[0:1, :].astype(F32)] + [dmod_ref[at : at + 1, :] for at in range(4)]
    small[0] = jnp.concatenate(early + [jnp.zeros((SMALL - 5, width), F32)]).astype(BF16)
    small_copy(0).start()
    advance(0, 1)
    block_back = Return(block_in, got_block, sems, local_sems.at[1], 3, wide, here)
    block_back.start()
    clear_edges(base)
    clear_edges(shifted)

    def norm_step(step, carry):
        group, part = step // (PHASE // ROWS), step % (PHASE // ROWS)
        unit, _ = normed(x_ref[ds(step * ROWS, ROWS), :].astype(F32))
        h_one = (unit * (1.0 + scale_one) + shift_one).astype(BF16)
        first_in[group, ds(HALF + part * ROWS, ROWS, HALF), :] = h_one.astype(F32)
        return carry

    lax.fori_loop(0, rows_all // ROWS, norm_step, 0)

    def du_step(group, carry):
        span = ds(group * PHASE, PHASE)
        total = None
        for part in range(3):
            cols = slice(part * width, (part + 1) * width)
            one = mm(dqkv_ref[span, cols], wqkv_ref[:, cols], NN)
            total = one if total is None else total + one
        base[group, HALF : HALF + PHASE, :] = total
        return carry

    loads[0].wait()
    loads[1].wait()
    small_step(0)
    lax.fori_loop(0, 2, du_step, 0)
    advance(0, 1)
    lax.fori_loop(2, 4, du_step, 0)

    def conv_step(block, carry):
        lanes = ds(block * LANES, LANES)
        shift_cols(base, shifted, lanes)
        conv_back(base, shifted, first_in, lanes, [taps_ref[t : t + 1, lanes] for t in range(9)],
                  dtaps_ref, dh1)
        return carry

    for block in range(width // LANES):
        if block % 2:
            advance(0, 1)
        if 1 <= block < levels:
            small_step(block)
        lax.fori_loop(block, block + 1, conv_step, 0)
    for level in range(max(1, width // LANES), levels):
        small_step(level)
    loads[2].wait()

    def fold(value):
        return value.reshape(ROWS // 8, 8, width).sum(axis=0)

    back = Return(dx, got_dx, sems, local_sems.at[0], 0, wide, here)

    def rows_step(at, sums):
        group, source = at // 4, at % 4
        span = ds(at * ROWS, ROWS)
        unit, inv = normed(x_ref[span, :].astype(F32))
        grad = dh1[span, :]
        dx[group, source] = (
            dx1_ref[span, :] + norm_back(unit, inv, grad * (1.0 + scale_one))
        ).astype(BF16)
        return tuple(total + fold(one) for total, one in zip(sums, (grad, grad * unit)))

    tap_sums[0, :9, :] = dtaps_ref[:9, :]
    tap_sums[0, 9:, :] = jnp.zeros((7, width), F32)

    def taps_copy(level):
        return remote(tap_sums.at[level], tap_got.at[level], small_sems, 2 * level + 1, *partners[level])

    def taps_step(level):
        taps_copy(level).wait_recv()
        tap_sums[level + 1] = tap_sums[level] + tap_got[level]
        if level + 1 < levels:
            taps_copy(level + 1).start()

    taps_copy(0).start()
    found = tuple(jnp.zeros((8, width), F32) for _ in range(2))
    for at in range(2):
        found = lax.fori_loop(8 * at, 8 * at + 8, rows_step, found)
        taps_step(at)
    chunks = [
        jnp.sum(one, axis=0, keepdims=True)[:, at * LANES : (at + 1) * LANES]
        for one in found
        for at in range(width // LANES)
    ]
    late[0] = jnp.concatenate(chunks + [jnp.zeros((SMALL - len(chunks), LANES), F32)]).astype(BF16)
    late_copy(0).start()
    for copy in back.copies:
        copy.start()
    back.own.start()
    advance(0, 1)
    for level in range(levels):
        late_copy(level).wait_recv()
        if level + 1 < levels:
            late_copy(level + 1).start()
        if level >= 2:
            taps_step(level)
        if level % 2:
            advance(0, 1)
    dtaps_ref[...] = tap_sums[levels]
    while any(queues):
        advance(0, 1)
    block_back.wait()
    back.wait()
    for level in range(levels):
        small_copy(level).wait_send()
        late_copy(level).wait_send()
        taps_copy(level).wait_send()
    for one in sums:
        one.wait_sends()


def input_backward(n_wide, x, dx1, dqkv, mod, taps, wqkv, own, silu_row, dmod, block):
    rows, width = x.shape
    slots = lax.axis_size("narrow")
    pieces = 2
    sum_rows = own.shape[0] // pieces
    shape = jax.ShapeDtypeStruct
    per_sum = sum_semaphores(n_wide)
    levels = (n_wide * slots).bit_length() - 1
    back = shape((slots, 4, rows // (4 * slots), width), BF16)
    return pl.pallas_call(
        partial(input_backward_kernel, n_wide),
        out_shape=(
            back,
            back,
            shape((pieces, sum_rows, width), BF16),
            shape((1 << levels, SMALL, width), BF16),
            shape((1 << levels, SMALL, LANES), BF16),
            shape((SMALL, width), F32),
        ),
        in_specs=[whole()] * 6 + [whole(pl.ANY)] * 4,
        out_specs=(whole(),) * 6,
        scratch_shapes=[pltpu.VMEM((4, PAD, width), F32)] * 3
        + [
            pltpu.VMEM((rows, width), F32),
            pltpu.VMEM((rows, width), F32),
            pltpu.VMEM((rows, 3 * width), BF16),
            pltpu.VMEM(wqkv.shape, BF16),
            pltpu.VMEM((4, slots, rows // (4 * slots), width), BF16),
            pltpu.VMEM((pieces, sum_rows, width), BF16),
            pltpu.VMEM((pieces, sum_landing(sum_rows, n_wide), width), BF16),
            pltpu.VMEM((levels + 1, SMALL, width), F32),
            pltpu.VMEM((levels, SMALL, width), F32),
            pltpu.SemaphoreType.DMA((2, 6)),
            pltpu.SemaphoreType.DMA((5,)),
            pltpu.SemaphoreType.DMA((2, pieces * per_sum)),
            pltpu.SemaphoreType.DMA((2, 2 * levels)),
            pltpu.SemaphoreType.DMA((2, levels)),
        ],
        compiler_params=pltpu.CompilerParams(
            vmem_limit_bytes=56 * MIB, collective_id=3, has_side_effects=True
        ),
        name="input_backward",
    )(x, mod, taps, own, silu_row, dmod, dx1, dqkv, wqkv, block)


def outputs_kernel(
    dx_in, block_in, attn_sum, ffn_sum, small, late, cond_ref, ada_hbm,
    gada_hbm, dx_hbm, block_hbm, gqkv_hbm, gout_hbm, gup_hbm, gdown_hbm, gcond_ref,
    ada, gada, dx, block, gqkv, gout, gup, gdown, sems, in_sem,
):
    width = small.shape[-1]
    here = lax.axis_index("narrow")
    load_ada = pltpu.make_async_copy(ada_hbm, ada, in_sem.at[0])
    load_ada.start()
    started = []

    def put(src, dst):
        copy = pltpu.make_async_copy(src, dst, sems.at[len(started)])
        copy.start()
        started.append(copy)

    devices = small.shape[0]
    shares = small[...].reshape(devices * SMALL, width)
    pick = lambda row: mm(
        one_hot(devices, devices * SMALL, lambda at: at * SMALL + row), shares, NN
    ).astype(BF16)
    late_shares = late[...].reshape(devices * SMALL, LANES)
    blocks = width // LANES

    def pick_late(part):
        return jnp.concatenate(
            [
                mm(
                    one_hot(devices, devices * SMALL, lambda at, at_row=part * blocks + at_block: at * SMALL + at_row),
                    late_shares, NN,
                )
                for at_block in range(blocks)
            ],
            axis=1,
        ).astype(BF16)

    silu_all = pick(0)
    dmods = [pick_late(part) if part < 2 else pick(part - 1) for part in range(6)]
    for part in range(6):
        gada[part] = mm(silu_all, dmods[part], TN)
        put(gada.at[part], gada_hbm.at[:, part * width : (part + 1) * width])
    slab = attn_sum.shape[1] // 2
    for part in range(3):
        gqkv[part] = attn_sum[part // 2, (part % 2) * slab : (part % 2 + 1) * slab, :].astype(F32).T
        put(gqkv.at[part], gqkv_hbm.at[part])
    gout[...] = attn_sum[1, slab:, :].astype(F32)
    put(gout, gout_hbm)
    permutation = group_permutation(dx_in.shape[1] * dx_in.shape[2])
    for at in range(dx_in.shape[0]):
        for source, held, out in ((dx_in, dx, dx_hbm), (block_in, block, block_hbm)):
            groups = jnp.concatenate([source[at, group] for group in range(4)], axis=0)
            held[at] = mm(permutation, groups, TN).astype(held.dtype)
            put(held.at[at], out.at[at])
    for at in range(ffn_sum.shape[0]):
        cols = slice(at * CHUNK, (at + 1) * CHUNK)
        gup[:, cols] = ffn_sum[at, :width, :].astype(F32)
        for part in range(width // CHUNK):
            span = slice(width + part * CHUNK, width + (part + 1) * CHUNK)
            gdown[cols, part * CHUNK : (part + 1) * CHUNK] = ffn_sum[at, span, :].astype(F32)
        put(gdown.at[cols], gdown_hbm.at[cols])
    put(gup, gup_hbm)

    def own_place(row):
        away = row ^ here
        place = ((away // 2) % 2) + (away % 2) * (devices // 2)
        return jnp.where(row < cond_ref.shape[0], place, -1)

    load_ada.wait()
    choose = one_hot(16, devices, own_place)
    grad_silu = jnp.zeros((16, width), F32)
    for part in range(6):
        own = mm(choose, dmods[part], NN).astype(BF16)
        grad_silu += mm(own, ada[:, part * width : (part + 1) * width], NT)
    cond = cond_ref[...].astype(F32)
    gate = 1.0 / (1.0 + jnp.exp(-cond))
    gcond_ref[...] = grad_silu[: cond_ref.shape[0]] * (gate * (1.0 + cond * (1.0 - gate)))
    for copy in started:
        copy.wait()


def outputs(dx, block, attn_sum, ffn_sum, small, late, cond, w_ada):
    slots, _, quarter, width = dx.shape
    slab = attn_sum.shape[1] // 2
    pieces = ffn_sum.shape[0]
    local = pieces * CHUNK
    shape = jax.ShapeDtypeStruct
    tokens = (slots, 4 * quarter, width)
    return pl.pallas_call(
        outputs_kernel,
        out_shape=(
            shape(w_ada.shape, F32),
            shape(tokens, F32),
            shape(tokens, BF16),
            shape((3, width, slab), F32),
            shape((slab, width), F32),
            shape((width, local), F32),
            shape((local, width), F32),
            shape(cond.shape, F32),
        ),
        in_specs=[whole()] * 7 + [whole(pl.ANY)],
        out_specs=(whole(pl.ANY),) * 7 + (whole(),),
        scratch_shapes=[
            pltpu.VMEM(w_ada.shape, BF16),
            pltpu.VMEM((6, width, width), F32),
            pltpu.VMEM(tokens, F32),
            pltpu.VMEM(tokens, BF16),
            pltpu.VMEM((3, width, slab), F32),
            pltpu.VMEM((slab, width), F32),
            pltpu.VMEM((width, local), F32),
            pltpu.VMEM((local, width), F32),
            pltpu.SemaphoreType.DMA((6 + 3 + 1 + 2 * slots + pieces + 1,)),
            pltpu.SemaphoreType.DMA((1,)),
        ],
        compiler_params=pltpu.CompilerParams(vmem_limit_bytes=56 * MIB),
        name="outputs",
    )(dx, block, attn_sum, ffn_sum, small, late, cond, w_ada)


def per_device(
    tokens, condition, cotangent, counts, w_ada, k_attn, w_qkv, w_out, w_up, k_ffn, w_down
):
    lat_dev, shard_rows, width = tokens.shape
    here = lax.axis_index("narrow")
    rows_all = shard_rows * lat_dev
    local = w_up.shape[1]

    n_wide = lax.axis_size("wide")
    qkv_t = w_qkv.transpose(2, 1, 0).reshape(w_qkv.shape[2], 3 * width)
    ktaps_own = jnp.pad(k_ffn.reshape(9, local), ((0, 7), (0, 0)))
    attn_taps = k_attn.reshape(9, width).astype(F32)

    cond_f = condition.astype(F32)
    silu_low = jax.nn.silu(cond_f).astype(BF16)
    own_silu = jnp.broadcast_to(lax.dynamic_slice_in_dim(silu_low, here, 1, 0), (16, width))
    live = (here < counts[0]).astype(F32).reshape(1, 1)

    (x, cot, u, qkv, probs, ctx, wqkv, wout, mod, att, x1, h2, h2t, db, wup, wdown, ktaps) = front(
        live, own_silu, attn_taps, tokens, cotangent, w_ada, qkv_t, w_out, w_up, w_down, ktaps_own
    )
    cot = cot.reshape(rows_all, width)
    ffn_taps = ktaps[:, :9].astype(F32)
    block_g, dx1, datt, dmod_mid, parcels = ffn(
        n_wide, live, h2, h2t, db, x1, cot, att, mod, wup, wdown, ffn_taps
    )
    block_g = block_g.reshape(4, lat_dev, shard_rows // 4, width)
    dqkv, own, ffn_sum, gtaps = attn_backward(n_wide, datt, ctx, u, wout, parcels, qkv, probs)
    got_dx, got_block, attn_sum, small, late, dattn_taps = input_backward(
        n_wide, x, dx1, dqkv, mod, attn_taps, wqkv, own, own_silu, dmod_mid, block_g
    )
    grad_w_ada, grad_tokens, block, gqkv, grad_w_out, grad_w_up, grad_w_down, grad_condition = outputs(
        got_dx, got_block, attn_sum, ffn_sum, small, late, condition, w_ada
    )
    grad_k_ffn = gtaps[:9].reshape(3, 3, local)
    grad_k_attn = dattn_taps[:9].reshape(3, 3, width)
    grad_w_qkv = gqkv.transpose(1, 0, 2)
    return (
        block,
        grad_tokens,
        grad_condition,
        grad_w_ada,
        grad_k_attn,
        grad_w_qkv,
        grad_w_out,
        grad_w_up,
        grad_k_ffn,
        grad_w_down,
    )


def solution(mesh):
    placed = (
        P("wide", "narrow", None),
        P("wide", None),
        P("wide", "narrow", None),
        P("wide"),
        P(),
        P(),
        P(None, None, "narrow"),
        P("narrow", None),
        P(None, "narrow"),
        P(None, None, "narrow"),
        P("narrow", None),
    )
    return jax.shard_map(
        per_device,
        mesh=mesh,
        in_specs=placed,
        out_specs=(
            P("wide", "narrow", None),
            P("wide", "narrow", None),
            P("wide", None),
            P(),
            P(),
            P(None, None, "narrow"),
            P("narrow", None),
            P(None, "narrow"),
            P(None, None, "narrow"),
            P("narrow", None),
        ),
        check_vma=False,
    )
```

```python
from functools import partial

import jax
import jax.numpy as jnp
from jax import lax
from jax.experimental import pallas as pl
from jax.experimental.pallas import tpu as pltpu
from jax.sharding import PartitionSpec as P

HEAD_DIM = 64
SIDE = 32
HALF = SIDE // 2
PHASE = HALF * HALF
PAD = PHASE + 2 * HALF
LANES = 128
ROWS = 64
CHUNK = 256
LOG2E = 1.4426950408889634
GELU_C = 0.7978845608028654
GELU_A = 0.044715
MIB = 1 << 20
F32 = jnp.float32
BF16 = jnp.bfloat16

NN = (((1,), (0,)), ((), ()))
NT = (((1,), (1,)), ((), ()))
TN = (((0,), (0,)), ((), ()))


def mm(left, right, dims):
    return lax.dot_general(left, right, dims, preferred_element_type=F32)


def ds(start, size, unit=None):
    return pl.ds(pl.multiple_of(start, unit or size), size)


def tap_source(parity, tap):
    return {-1: (1, -1), 0: (0, 0), 1: (1, 0), 2: (0, 1)}[parity + tap - 1]


def shift_cols(base, shifted, lanes):
    col = lax.broadcasted_iota(jnp.int32, (ROWS, LANES), 0) % HALF

    def rows_step(step, carry):
        for group in range(4):
            rows = ds(HALF + step * ROWS, ROWS, HALF)
            value = base[group, rows, lanes]
            if group % 2:
                moved = jnp.where(col == 0, 0.0, pltpu.roll(value, 1, 0))
            else:
                moved = jnp.where(col == HALF - 1, 0.0, pltpu.roll(value, ROWS - 1, 0))
            shifted[group, rows, lanes] = moved
        return carry

    lax.fori_loop(0, PHASE // ROWS, rows_step, 0)


def clear_edges(ref):
    edge = jnp.zeros((HALF, ref.shape[-1]), ref.dtype)
    for group in range(4):
        ref[group, :HALF, :] = edge
        ref[group, PAD - HALF :, :] = edge


def tap_value(base, shifted, group, tap_row, tap_col, start, lanes):
    src_row, row_move = tap_source(group // 2, tap_row)
    src_col, col_move = tap_source(group % 2, tap_col)
    ref = base if col_move == 0 else shifted
    return ref[2 * src_row + src_col, ds(HALF + row_move * HALF + start, ROWS, HALF), lanes]


def normed(values_in):
    mean_val = jnp.mean(values_in, axis=-1, keepdims=True)
    centred = values_in - mean_val
    inv = lax.rsqrt(jnp.mean(centred * centred, axis=-1, keepdims=True) + 1e-06)
    return centred * inv, inv


def norm_back(unit, inv, grad):
    mean_grad = jnp.mean(grad, axis=-1, keepdims=True)
    mean_dot = jnp.mean(grad * unit, axis=-1, keepdims=True)
    return (grad - mean_grad - unit * mean_dot) * inv


def narrow_peers(here):
    return [here ^ 2, here ^ 3, here ^ 1]


def remote(src, dst, sems, at, wide, narrow):
    return pltpu.make_async_remote_copy(
        src_ref=src,
        dst_ref=dst,
        send_sem=sems.at[0, at],
        recv_sem=sems.at[1, at],
        device_id=(wide, narrow),
        device_id_type=pl.DeviceIdType.MESH,
    )


class Gather:
    COPIES = 11

    def __init__(self, src, dst, sems, local_sem, first, wide, here):
        count = src.shape[0]
        quarter = count // 4
        front = -(-quarter // 32) * 16
        mine = wide % 4
        far, near = here ^ 2, here ^ 1

        def slot(k):
            return dst.at[k * count : (k + 1) * count]

        def at(k, which, start=0, size=quarter):
            return dst.at[ds(k * count + which * quarter + start, size, 16)]

        def send(number, source, target, wide_to, narrow_to):
            return remote(source, target, sems, first + number, wide_to, narrow_to)

        def same(number, which, wide_to, start=0, size=quarter):
            return send(number, at(2, which, start, size), at(2, which, start, size), wide_to, here)

        def share(number, which, start=0, size=quarter):
            return send(number, at(2, which, start, size), at(3, which, start, size), wide, near)

        own_part = src.at[ds(mine * quarter, quarter, 16)]
        rest = quarter - front
        self.own = pltpu.make_async_copy(src, slot(0), local_sem)
        self.near = send(0, src, slot(1), wide, near)
        self.far = send(1, own_part, at(2, mine), wide, far)
        self.swaps = [same(2, mine, wide ^ 1), same(3, mine, wide ^ 2)]
        self.corners = [same(4, mine ^ 1, wide ^ 2, 0, front), same(5, mine ^ 2, wide ^ 1, front, rest)]
        self.shares = [
            share(6, mine),
            share(7, mine ^ 1),
            share(8, mine ^ 2),
            share(9, mine ^ 3, 0, front),
            share(10, mine ^ 3, front, rest),
        ]

    def start_near(self):
        self.own.start()
        self.near.start()

    def start_far(self):
        self.far.start()

    def swap(self):
        self.far.wait_recv()
        self.swaps[0].start()
        self.swaps[1].start()
        self.shares[0].start()

    def corner(self):
        for which in range(2):
            self.swaps[which].wait_recv()
            self.corners[which].start()
            self.shares[1 + which].start()

    def share_corner(self):
        for which in range(2):
            self.corners[which].wait_recv()
            self.shares[3 + which].start()

    def finish(self):
        self.own.wait()
        self.near.wait()
        self.far.wait_send()
        for copy in self.swaps + self.corners:
            copy.wait_send()
        for copy in self.shares:
            copy.wait()


def group_permutation(rows):
    out = lax.broadcasted_iota(jnp.int32, (rows, rows), 0)
    source = lax.broadcasted_iota(jnp.int32, (rows, rows), 1)
    per_group = rows // 4
    group, rest = out // per_group, out % per_group
    line = 2 * (rest // HALF) + group // 2
    wanted = line * SIDE + 2 * (rest % HALF) + group % 2
    return jnp.where(source == wanted, 1.0, 0.0).astype(BF16)


class Exchange:
    def __init__(self, sent, got, sems, local_sem, first, wide, here):
        self.own = pltpu.make_async_copy(sent.at[here], got.at[:, here], local_sem)
        self.copies = [
            remote(sent.at[peer], got.at[:, here], sems, first + at, wide, peer)
            for at, peer in enumerate(narrow_peers(here))
        ]

    def start(self):
        for copy in self.copies:
            copy.start()
        self.own.start()

    def wait(self):
        self.own.wait()
        for copy in self.copies:
            copy.wait()


class Return:
    def __init__(self, sent, got, sems, local_sem, first, wide, here):
        self.own = pltpu.make_async_copy(sent.at[:, here], got.at[here], local_sem)
        self.copies = [
            remote(sent.at[:, peer], got.at[here], sems, first + at, wide, peer)
            for at, peer in enumerate(narrow_peers(here))
        ]

    start = Exchange.start
    wait = Exchange.wait


HALVINGS = 3
EARLY = 32
SMALL = 16


class WideSum:
    def __init__(self, source, work, full, got, sems, first, wide, here, n_wide, done=0, order=None):
        self.source, self.work, self.full, self.got = source, work, full, got
        self.rows = work.shape[0]
        self.levels = min(HALVINGS, n_wide.bit_length() - 1)
        self.extra = n_wide.bit_length() - 1 - self.levels
        self.done = done
        self.wide, self.here, self.sems, self.first = wide, here, sems, first
        self.offsets = [0]
        self.masks = [1 << at for at in (order or range(HALVINGS)) if at < self.levels]
        for level in range(self.levels):
            bit = (wide // self.masks[level]) % 2
            self.offsets.append(self.offsets[-1] + bit * (self.rows >> (level + 1)))
        self.waiting = []

    def size(self, level):
        return self.rows >> level

    def at(self, ref, offset, size):
        return ref.at[ds(offset, size, 16)]

    def half_copy(self, level):
        size, base = self.size(level + 1), self.offsets[level]
        send = base + size - (self.offsets[level + 1] - base)
        source = self.source if level == self.done else self.work
        landing = self.rows - self.size(level)
        return remote(
            self.at(source, send, size), self.got.at[landing : landing + size],
            self.sems, self.first + level, self.wide ^ self.masks[level], self.here,
        )

    def start_half(self, level):
        self.half_copy(level).start()

    def finish_half(self, level):
        self.half_copy(level).wait_recv()
        size, landing = self.size(level + 1), self.rows - self.size(level)
        rows = ds(self.offsets[level + 1], size, 16)
        source = self.source if level == self.done else self.work
        self.work[rows, :] = (
            source[rows, :].astype(F32) + self.got[landing : landing + size, :].astype(F32)
        ).astype(BF16)

    def extras(self):
        size = self.size(self.levels)
        rows = ds(self.offsets[self.levels], size, 16)
        source = self.source if self.done == self.levels else self.work
        self.full[rows, :] = source[rows, :]
        for at in range(self.extra):
            landing = self.rows - size + at * size
            copy = remote(
                self.full.at[rows], self.got.at[landing : landing + size],
                self.sems, self.first + 2 * self.levels + at,
                self.wide ^ (1 << (self.levels + at)), self.here,
            )
            copy.start()
            copy.wait()
            self.full[rows, :] = (
                self.full[rows, :].astype(F32) + self.got[landing : landing + size, :].astype(F32)
            ).astype(BF16)

    def spread_copy(self, level):
        part = self.at(self.full, self.offsets[level + 1], self.size(level + 1))
        return remote(
            part, part, self.sems, self.first + self.levels + level, self.wide ^ self.masks[level], self.here
        )

    def actions(self):
        acts = []
        for level in range(self.done, self.levels):
            acts.append([partial(self.start_half, level)])
            if level > self.done:
                acts[-1].insert(0, partial(self.finish_half, level - 1))
        tail = [self.extras]
        if self.done < self.levels:
            tail.insert(0, partial(self.finish_half, self.levels - 1))
        for level in reversed(range(self.levels)):
            acts.append(tail + [lambda level=level: self.spread_copy(level).start()])
            tail = [lambda level=level: self.spread_copy(level).wait_recv()]
        acts.append(tail)
        return acts

    def wait_sends(self):
        for level in range(self.done, self.levels):
            self.half_copy(level).wait_send()
        for level in range(self.levels):
            self.spread_copy(level).wait_send()


def halvings_ahead(pieces, levels):
    return [min(levels, pieces - at) for at in range(pieces)]


def lane_rows(values_in, rows):
    cut = [
        one[:, at * LANES : (at + 1) * LANES] for one in values_in for at in range(one.shape[1] // LANES)
    ]
    return jnp.concatenate(cut + [jnp.zeros((rows - len(cut), LANES), F32)]).astype(BF16)


def greet(partners):
    barrier = pltpu.get_barrier_semaphore()
    for partner in partners:
        pl.semaphore_signal(
            barrier, inc=1, device_id=partner, device_id_type=pl.DeviceIdType.MESH
        )
    pl.semaphore_wait(barrier, len(partners))


def wide_partners(wide, here, n_wide):
    return [(wide ^ (1 << level), here) for level in range(n_wide.bit_length() - 1)]


def sum_semaphores(n_wide):
    levels = n_wide.bit_length() - 1
    return levels + min(levels, HALVINGS)


def sum_landing(rows, n_wide):
    levels = n_wide.bit_length() - 1
    last = rows >> min(levels, HALVINGS)
    return rows - last + max(levels - HALVINGS, 0) * last


def front_kernel(
    live_ref, silu_ref, taps_ref, tokens_hbm, cot_hbm, ada_hbm, wqkv_src, wout_src, wup_src, wdown_src, ktaps_src,
    x_hbm, cot_hbm_out, u_hbm, qkv_hbm, probs_hbm, ctx_hbm, wqkv_hbm, wout_hbm,
    mod_ref, att_ref, x1_ref, h2_ref, h2t_ref, db_ref, wup_ref, wdown_ref, ktaps_ref,
    x_ref, cot_ref, u_ref, qkv_ref, probs_ref, ctx_ref, wqkv_ref, wout_ref,
    base, shifted, shards, sent, sent_cot, got, ada, up_own, down_own, sems, local_sems, in_sems, out_sems,
):
    width = u_ref.shape[1]
    flushed = []

    def flush(src, dst):
        copy = pltpu.make_async_copy(src, dst, out_sems.at[len(flushed)])
        copy.start()
        flushed.append(copy)

    rows_all = u_ref.shape[0]
    latents, shard_rows = shards.shape[:2]
    wide, here = lax.axis_index("wide"), lax.axis_index("narrow")
    load_tokens = pltpu.make_async_copy(tokens_hbm, shards, in_sems.at[0])
    load_tokens.start()
    load_ada = pltpu.make_async_copy(ada_hbm, ada, in_sems.at[1])
    load_ada.start()
    load_up = pltpu.make_async_copy(wup_src, up_own, in_sems.at[2])
    load_up.start()
    load_down = pltpu.make_async_copy(wdown_src, down_own, in_sems.at[3])
    load_down.start()

    barrier = pltpu.get_barrier_semaphore()
    partners = [(wide, peer) for peer in narrow_peers(here)] + [(wide ^ 1, here), (wide ^ 2, here)]
    for partner in partners:
        pl.semaphore_signal(
            barrier, inc=1, device_id=partner, device_id_type=pl.DeviceIdType.MESH
        )
    permutation = group_permutation(shard_rows)
    load_tokens.wait()

    def permute(to):
        def one(at, carry):
            moved = mm(permutation, shards[at], NN).astype(BF16)
            for group in range(4):
                to[at, group] = moved[group * (shard_rows // 4) : (group + 1) * (shard_rows // 4)]
            return carry

        lax.fori_loop(0, latents, one, 0)

    permute(sent)
    pl.semaphore_wait(barrier, len(partners))
    exchange = Exchange(sent, got, sems, local_sems.at[0], 0, wide, here)
    exchange_cot = Exchange(sent_cot, cot_ref, sems, local_sems.at[1], 3, wide, here)
    gathers = [
        Gather(src, dst, sems, local_sems.at[2 + at], 9 + Gather.COPIES * at, wide, here)
        for at, (src, dst) in enumerate(
            (
                (wqkv_src, wqkv_ref),
                (wout_src, wout_ref),
                (up_own, wup_ref),
                (down_own, wdown_ref),
            )
        )
    ]
    g_qkv, g_out, g_up, g_down = gathers
    taps_own = pltpu.make_async_copy(ktaps_src, ktaps_ref.at[0], local_sems.at[6])
    taps_sends = [
        remote(ktaps_src, ktaps_ref.at[peer ^ here], sems, 6 + at, wide, peer)
        for at, peer in enumerate(narrow_peers(here))
    ]
    exchange.start()
    load_cot = pltpu.make_async_copy(cot_hbm, shards, in_sems.at[0])
    load_cot.start()
    load_up.wait()
    load_down.wait()
    for one in gathers:
        one.start_near()
    taps_own.start()
    for one in taps_sends:
        one.start()

    load_ada.wait()
    for part in range(6):
        mod_ref[part : part + 1, :] = mm(
            silu_ref[...], ada[:, part * width : (part + 1) * width], NN
        )[0:1, :]
    load_cot.wait()
    permute(sent_cot)
    shift_one, scale_one, gate_one = mod_ref[0:1, :], mod_ref[1:2, :], mod_ref[2:3, :]
    shift_two, scale_two, gate_two = mod_ref[3:4, :], mod_ref[4:5, :], mod_ref[5:6, :]
    clear_edges(base)
    clear_edges(shifted)
    exchange.wait()
    g_qkv.start_far()
    g_out.start_far()
    for group in range(4):
        for source in range(latents):
            start = group * PHASE + source * ROWS
            x_ref[start : start + ROWS, :] = got[group, source]
    flush(x_ref, x_hbm)

    def norm_step(step, carry):
        group, part = step // (PHASE // ROWS), step % (PHASE // ROWS)
        unit, _ = normed(x_ref[ds(step * ROWS, ROWS), :].astype(F32))
        h_one = (unit * (1.0 + scale_one) + shift_one).astype(BF16)
        base[group, ds(HALF + part * ROWS, ROWS, HALF), :] = h_one.astype(F32)
        return carry

    lax.fori_loop(0, rows_all // ROWS, norm_step, 0)
    g_qkv.swap()
    g_out.swap()
    g_up.start_far()

    def conv_step(block, carry):
        lanes = ds(block * LANES, LANES)
        shift_cols(base, shifted, lanes)
        taps = [taps_ref[t // 3, t % 3 : t % 3 + 1, lanes].astype(F32) for t in range(9)]

        def rows_step(step, carry):
            for group in range(4):
                total = jnp.zeros((ROWS, LANES), F32)
                for tap in range(9):
                    total += taps[tap] * tap_value(
                        base, shifted, group, tap // 3, tap % 3, step * ROWS, lanes
                    )
                u_ref[ds(group * PHASE + step * ROWS, ROWS), lanes] = total.astype(BF16)
            return carry

        return lax.fori_loop(0, PHASE // ROWS, rows_step, carry)

    blocks = width // LANES
    lax.fori_loop(0, 2 * blocks // 3, conv_step, 0)
    g_qkv.corner()
    g_out.corner()
    g_up.swap()
    g_down.start_far()
    lax.fori_loop(2 * blocks // 3, blocks, conv_step, 0)
    flush(u_ref, u_hbm)
    g_qkv.share_corner()
    g_qkv.finish()
    flush(wqkv_ref, wqkv_hbm)

    def project_step(step, carry):
        rows = ds(step * PHASE, PHASE)
        for part in range(3):
            cols = slice(part * width, (part + 1) * width)
            qkv_ref[rows, cols] = mm(u_ref[rows, :], wqkv_ref[:, cols], NT).astype(BF16)
        return carry

    lax.fori_loop(0, 4, project_step, 0)

    pairs = width // LANES
    first = lax.broadcasted_iota(jnp.int32, (PHASE, LANES), 1) < HEAD_DIM
    zero = jnp.zeros((PHASE, LANES), BF16)

    def attend_step(step, carry):
        group, pair = step // pairs, step % pairs
        rows = ds(group * PHASE, PHASE)
        query = qkv_ref[rows, ds(pair * LANES, LANES)]
        key = qkv_ref[rows, ds(width + pair * LANES, LANES)]
        value = qkv_ref[rows, ds(2 * width + pair * LANES, LANES)]
        found = []
        for head in range(2):
            own = jnp.where(first, query, zero) if head == 0 else jnp.where(first, zero, query)
            scores = mm(key, own, NT)
            top = jnp.max(scores, axis=0, keepdims=True)
            raised = jnp.exp2((scores - top) * (LOG2E * HEAD_DIM**-0.5))
            probs = (raised * (1.0 / jnp.sum(raised, axis=0, keepdims=True))).astype(BF16)
            probs_ref[step, :, head * PHASE : (head + 1) * PHASE] = probs
            found.append(mm(probs, value, TN))
        ctx_ref[rows, ds(pair * LANES, LANES)] = jnp.where(first, found[0], found[1]).astype(BF16)
        return carry

    flush(qkv_ref, qkv_hbm)
    g_up.corner()
    g_out.share_corner()
    g_down.swap()
    exchange_cot.start()

    def attend_group(group):
        lax.fori_loop(group * pairs, (group + 1) * pairs, attend_step, 0)
        done = slice(group * pairs, (group + 1) * pairs)
        flush(probs_ref.at[done], probs_hbm.at[done])

    attend_group(0)
    g_up.share_corner()
    attend_group(1)
    g_down.corner()
    attend_group(2)
    g_down.share_corner()
    attend_group(3)
    flush(ctx_ref, ctx_hbm)
    g_out.finish()
    flush(wout_ref, wout_hbm)

    def out_step(step, carry):
        rows = ds(step * PHASE, PHASE)
        total = mm(ctx_ref[rows, :], wout_ref[...], NN)
        att_ref[rows, :] = total.astype(BF16)
        x1_ref[rows, :] = x_ref[rows, :].astype(F32) + gate_one * total
        return carry

    lax.fori_loop(0, 4, out_step, 0)
    live = live_ref[0, 0]

    def second_step(step, carry):
        rows = ds(step * ROWS, ROWS)
        unit, _ = normed(x1_ref[rows, :])
        h2_ref[rows, :] = (unit * (1.0 + scale_two) + shift_two).astype(BF16)
        group, source = step // (PHASE // ROWS), step % (PHASE // ROWS)
        db_ref[rows, :] = (cot_ref[group, source].astype(F32) * live * gate_two).astype(BF16)
        return carry

    exchange_cot.wait()
    flush(cot_ref, cot_hbm_out)
    lax.fori_loop(0, rows_all // ROWS, second_step, 0)
    for part in range(4):
        h2t_ref[:, part * PHASE : (part + 1) * PHASE] = h2_ref[
            part * PHASE : (part + 1) * PHASE, :
        ].T
    g_up.finish()
    g_down.finish()
    for copy in flushed:
        copy.wait()
    taps_own.wait()
    for one in taps_sends:
        one.wait()


def whole(memory=pltpu.VMEM):
    return pl.BlockSpec(memory_space=memory)


def front(live, silu_row, taps, tokens, cot, w_ada, wqkv, wout, wup, wdown, ktaps):
    latents, shard_rows, width = tokens.shape
    rows = latents * shard_rows
    steps = 4 * (width // LANES)
    shape = jax.ShapeDtypeStruct
    full = lambda shard: shape((latents * shard.shape[0],) + shard.shape[1:], BF16)
    moved = (latents, 4, shard_rows // 4, width)
    streamed = (
        shape((rows, width), BF16),
        shape((4, latents, shard_rows // 4, width), BF16),
        shape((rows, width), BF16),
        shape((rows, 3 * width), BF16),
        shape((steps, PHASE, 2 * PHASE), BF16),
        shape((rows, width), BF16),
        full(wqkv),
        full(wout),
    )
    return pl.pallas_call(
        front_kernel,
        out_shape=streamed
        + (
            shape((6, width), F32),
            shape((rows, width), BF16),
            shape((rows, width), F32),
            shape((rows, width), BF16),
            shape((width, rows), BF16),
            shape((rows, width), BF16),
            full(wup),
            full(wdown),
            shape((latents,) + ktaps.shape, BF16),
        ),
        in_specs=[whole(pltpu.SMEM)] + [whole()] * 2 + [whole(pl.ANY)] * 3 + [whole()] * 2 + [whole(pl.ANY)] * 2 + [whole()],
        out_specs=(whole(pl.ANY),) * 8 + (whole(),) * 6 + (whole(pl.ANY),) * 2 + (whole(),),
        scratch_shapes=[pltpu.VMEM(one.shape, one.dtype) for one in streamed]
        + [
            pltpu.VMEM((4, PAD, width), F32),
            pltpu.VMEM((4, PAD, width), F32),
            pltpu.VMEM((latents, shard_rows, width), BF16),
            pltpu.VMEM(moved, BF16),
            pltpu.VMEM(moved, BF16),
            pltpu.VMEM((4, latents, shard_rows // 4, width), BF16),
            pltpu.VMEM(w_ada.shape, BF16),
            pltpu.VMEM(wup.shape, BF16),
            pltpu.VMEM(wdown.shape, BF16),
            pltpu.SemaphoreType.DMA((2, 9 + 4 * Gather.COPIES)),
            pltpu.SemaphoreType.DMA((7,)),
            pltpu.SemaphoreType.DMA((4,)),
            pltpu.SemaphoreType.DMA((len(streamed) + 3,)),
        ],
        compiler_params=pltpu.CompilerParams(
            vmem_limit_bytes=60 * MIB, collective_id=0, has_side_effects=True
        ),
        name="attn_forward",
    )(live, silu_row, taps, tokens, cot, w_ada, wqkv, wout, wup, wdown, ktaps)


def ffn_kernel(
    n_wide, live_ref, h2_ref, h2t_ref, db_ref, x1_hbm, cot_hbm, att_hbm, mod_ref,
    wup_before, wup_even, wup_odd, wup_after, wdown_even, wdown_odd, taps_even, taps_odd,
    block_ref, dx1_ref, datt_ref, dmod_ref, sums_ref,
    hid_even, hid_odd, hid_moved, grad, grad_moved, slope, act, act_t, dhid, branch, dtaps,
    work, chip_sum, got_near, got_far, got_sums, x1_ref, cot_ref, att_ref, sems, sum_sems, in_sems,
):
    rows_all, width = h2_ref.shape
    loads = [
        pltpu.make_async_copy(src, dst, in_sems.at[at])
        for at, (src, dst) in enumerate(((x1_hbm, x1_ref), (cot_hbm, cot_ref), (att_hbm, att_ref)))
    ]
    dh2 = dx1_ref
    wide, here = lax.axis_index("wide"), lax.axis_index("narrow")
    step, steps = pl.program_id(0), pl.num_programs(0)
    quarters = [slice(q * PHASE, (q + 1) * PHASE) for q in range(4)]
    inside = slice(HALF, HALF + PHASE)
    lane_blocks = [slice(at * LANES, (at + 1) * LANES) for at in range(CHUNK // LANES)]
    col = lax.broadcasted_iota(jnp.int32, (ROWS, LANES), 0) % HALF

    partners = [(wide, here ^ 1), (wide, here ^ 2)] + wide_partners(wide, here, n_wide)[:HALVINGS]
    pieces, sum_rows = got_sums.shape[0], got_sums.shape[1]
    sums = [
        WideSum(sums_ref.at[at, : 2 * width], sums_ref.at[at, : 2 * width], None, got_sums.at[at], sum_sems,
                at * HALVINGS, wide, here, n_wide)
        for at in range(pieces)
    ]
    schedule = halvings_ahead(pieces, sums[0].levels)

    def to_near(at):
        return remote(work.at[at % 2], got_near.at[at], sems, at, wide, here ^ 1)

    def to_far(at):
        return remote(chip_sum.at[at], got_far.at[at], sems, steps + at, wide, here ^ 2)

    @pl.when(step == 0)
    def _():
        for load in loads:
            load.start()
        barrier = pltpu.get_barrier_semaphore()
        for partner in partners:
            pl.semaphore_signal(
                barrier, inc=1, device_id=partner, device_id_type=pl.DeviceIdType.MESH
            )
        for ref in (hid_even, hid_odd, hid_moved, grad, grad_moved):
            clear_edges(ref)
        branch[...] = jnp.zeros_like(branch)
        dh2[...] = jnp.zeros_like(dh2)
        dtaps[...] = jnp.zeros_like(dtaps)
        dhid[...] = jnp.zeros_like(dhid)
        full = mm(h2_ref[...], wup_even[...], NN)
        for q in range(4):
            hid_even[q, inside, :] = full[quarters[q]]
        pl.semaphore_wait(barrier, len(partners))

    def moved_cols(group, value):
        if group % 2:
            return jnp.where(col == 0, 0.0, pltpu.roll(value, 1, 0))
        return jnp.where(col == HALF - 1, 0.0, pltpu.roll(value, ROWS - 1, 0))

    def static_tap(base, shifted, group, tap_row, tap_col, start, lanes):
        src_row, row_move = tap_source(group // 2, tap_row)
        src_col, col_move = tap_source(group % 2, tap_col)
        ref = base if col_move == 0 else shifted
        first = HALF + row_move * HALF + start
        return ref[2 * src_row + src_col, first : first + ROWS, lanes]

    def weights_back(q, wup_last, slot):
        dh2[quarters[q], :] += mm(dhid[quarters[q], :], wup_last[...], NT)
        if q < width // PHASE:
            slot[quarters[q], :] = mm(h2t_ref[quarters[q], :], dhid[...], NN).astype(BF16)

    def forward_products(part, wdown, wup_last, slot):
        grad[part, inside, :] = mm(db_ref[quarters[part], :], wdown[...], NT)
        yield
        for cols in quarters[: width // PHASE]:
            dh2[quarters[part], cols] += mm(dhid[quarters[part], :], wup_last[cols, :], NT)
            yield
        if part < width // PHASE:
            slot[quarters[part], :] = mm(h2t_ref[quarters[part], :], dhid[...], NN).astype(BF16)
        yield

    def backward_products(part, hid_next, wdown, wup_next, slot):
        hid_next[part, inside, :] = mm(h2_ref[quarters[part], :], wup_next[...], NN)
        yield
        for cols in quarters[: width // PHASE]:
            branch[quarters[part], cols] += mm(act[quarters[part], :], wdown[:, cols], NN)
            yield
        if part < width // CHUNK:
            block = slice(part * CHUNK, (part + 1) * CHUNK)
            slot[width + part * CHUNK : width + (part + 1) * CHUNK, :] = mm(
                act_t[...], db_ref[:, block], NN
            ).astype(BF16)
        yield

    def forward(hid, wdown, taps_ref, wup_last, slot):
        taps = [[taps_ref[0, t : t + 1, lanes].astype(F32) for t in range(9)] for lanes in lane_blocks]
        for part in range(PHASE // ROWS):
            rows = slice(HALF + part * ROWS, HALF + (part + 1) * ROWS)
            for group in range(4):
                for lanes in lane_blocks:
                    hid_moved[group, rows, lanes] = moved_cols(group, hid[group, rows, lanes])
        for part in range(PHASE // ROWS):
            products = forward_products(part, wdown, wup_last, slot)
            for group in range(4):
                for at, lanes in enumerate(lane_blocks):
                    next(products, None)
                    total = jnp.zeros((ROWS, LANES), F32)
                    for tap in range(9):
                        total += taps[at][tap] * static_tap(
                            hid, hid_moved, group, tap // 3, tap % 3, part * ROWS, lanes
                        )
                    square = total * total
                    turned = jnp.tanh(total * (square * (GELU_C * GELU_A) + GELU_C))
                    half = 0.5 * turned + 0.5
                    bend = total * (half - half * half)
                    start = group * PHASE + part * ROWS
                    act[start : start + ROWS, lanes] = (total * half).astype(BF16)
                    slope[start : start + ROWS, lanes] = half + bend * (
                        square * (6.0 * GELU_C * GELU_A) + 2.0 * GELU_C
                    )

    def backward(hid, hid_next, wdown, wup_next, taps_ref, slot):
        taps = [[taps_ref[0, t : t + 1, lanes].astype(F32) for t in range(9)] for lanes in lane_blocks]
        act_t[...] = act[...].T
        for part in range(PHASE // ROWS):
            rows = slice(HALF + part * ROWS, HALF + (part + 1) * ROWS)
            for group in range(4):
                start = group * PHASE + part * ROWS
                for lanes in lane_blocks:
                    value = grad[group, rows, lanes] * slope[start : start + ROWS, lanes]
                    grad[group, rows, lanes] = value
                    grad_moved[group, rows, lanes] = moved_cols(group, value)
        sums = [[jnp.zeros((8, LANES), F32) for _ in range(9)] for _ in lane_blocks]
        for part in range(PHASE // ROWS):
            products = backward_products(part, hid_next, wdown, wup_next, slot)
            for group in range(4):
                start = group * PHASE + part * ROWS
                for at, lanes in enumerate(lane_blocks):
                    next(products, None)
                    own = hid[group, HALF + part * ROWS : HALF + (part + 1) * ROWS, lanes]
                    total = jnp.zeros((ROWS, LANES), F32)
                    for tap in range(9):
                        moved = static_tap(
                            grad, grad_moved, group, 2 - tap // 3, 2 - tap % 3, part * ROWS, lanes
                        )
                        total += taps[at][tap] * moved
                        sums[at][tap] += (own * moved).reshape(ROWS // 8, 8, LANES).sum(axis=0)
                    dhid[start : start + ROWS, lanes] = total.astype(BF16)
        for at, lanes in enumerate(lane_blocks):
            for tap in range(9):
                dtaps[tap : tap + 1, lanes] = jnp.sum(sums[at][tap], axis=0, keepdims=True)
        slot[2 * width :, :] = dtaps[...].astype(BF16)

    def settle(pair):
        to_near(pair).wait_recv()

        @pl.when(pair < steps // 2)
        def _():
            chip_sum[pair] = (work[2].astype(F32) + got_near[pair].astype(F32)).astype(BF16)
            to_far(pair).start()

        @pl.when(pair >= steps // 2)
        def _():
            part = pair - steps // 2
            to_far(part).wait_recv()
            sums_ref[part] = (
                work[2].astype(F32) + got_near[pair].astype(F32) + got_far[part].astype(F32)
            ).astype(BF16)

        for part in range(pieces):

            @pl.when(pair == steps // 2 + part)
            def _():
                for at in range(part):
                    sums[at].finish_half(part - at - 1)
                for at in range(part + 1):
                    if part - at < schedule[at]:
                        sums[at].start_half(part - at)

    forward(hid_even, wdown_even, taps_even, wup_before, work.at[2])

    @pl.when(step >= 1)
    def _():
        settle(step - 1)

    @pl.when(step >= 2)
    def _():
        to_near(step - 2).wait_send()

    even_slot = work.at[step % 2]
    backward(hid_even, hid_odd, wdown_even, wup_odd, taps_even, even_slot)
    forward(hid_odd, wdown_odd, taps_odd, wup_even, even_slot)
    to_near(step).start()
    backward(hid_odd, hid_even, wdown_odd, wup_after, taps_odd, work.at[2])

    @pl.when(step == steps - 1)
    def _():
        for q in range(4):
            weights_back(q, wup_odd, work.at[2])
        settle(step)
        for load in loads:
            load.wait()
        gate_one, scale_two, gate_two = mod_ref[2:3, :], mod_ref[4:5, :], mod_ref[5:6, :]
        live = live_ref[0, 0]

        def fold(value):
            return value.reshape(ROWS // 8, 8, width).sum(axis=0)

        def rows_step(at, sums):
            rows = ds(at * ROWS, ROWS)
            after = x1_ref[rows, :]
            dout = cot_ref[rows, :].astype(F32) * live
            branch_rows = branch[rows, :]
            block_ref[rows, :] = ((after + gate_two * branch_rows) * live).astype(BF16)
            unit, inv = normed(after)
            dh2_rows = dh2[rows, :]
            dx1 = dout + norm_back(unit, inv, dh2_rows * (1.0 + scale_two))
            dx1_ref[rows, :] = dx1
            datt_ref[rows, :] = (dx1 * gate_one).astype(BF16)
            found = (dx1 * att_ref[rows, :].astype(F32), dh2_rows, dh2_rows * unit, dout * branch_rows)
            return tuple(total + fold(one) for total, one in zip(sums, found))

        start = tuple(jnp.zeros((8, width), F32) for _ in range(4))
        totals = lax.fori_loop(0, rows_all // ROWS, rows_step, start)
        for at in range(4):
            dmod_ref[at : at + 1, :] = jnp.sum(totals[at], axis=0, keepdims=True)
        for at in (steps - 2, steps - 1):
            to_near(at).wait_send()
        for at in range(steps // 2):
            to_far(at).wait_send()
        for at in range(pieces):
            sums[at].finish_half(schedule[at] - 1)
            for level in range(schedule[at]):
                sums[at].half_copy(level).wait_send()


def ffn(n_wide, live, h2, h2t, db, x1, cot, att, mod, wup, wdown, taps):
    rows, width = h2.shape
    shards, _, local = taps.shape
    per = local // CHUNK
    steps = shards * per // 2
    parcel = (2 * width + 16, CHUNK)
    shape = jax.ShapeDtypeStruct
    keep = lambda *block: pl.BlockSpec(
        block, lambda c: (0,) * len(block), pipeline_mode=pl.Buffered(1)
    )

    def slot_and_part(step, odd):
        return jnp.where(step < per, 3, 1) - odd, step % per

    def up_block(move, odd):
        def index(step):
            return slot_and_part(jnp.clip(step + move, 0, steps - 1), odd)

        return pl.BlockSpec((width, CHUNK), index)

    def down_block(odd):
        def index(step):
            slot, part = slot_and_part(step, odd)
            return slot * per + part, 0

        return pl.BlockSpec((CHUNK, width), index)

    def taps_block(odd):
        def index(step):
            slot, part = slot_and_part(step, odd)
            return slot, 0, part

        return pl.BlockSpec((1, taps.shape[1], CHUNK), index)

    return pl.pallas_call(
        partial(ffn_kernel, n_wide),
        grid=(steps,),
        out_shape=(
            shape((rows, width), BF16),
            shape((rows, width), F32),
            shape((rows, width), BF16),
            shape((4, width), F32),
            shape((per,) + parcel, BF16),
        ),
        in_specs=[
            whole(pltpu.SMEM),
            keep(rows, width),
            keep(width, rows),
            keep(rows, width),
            whole(pl.ANY),
            whole(pl.ANY),
            whole(pl.ANY),
            keep(6, width),
            up_block(-1, 1),
            up_block(0, 0),
            up_block(0, 1),
            up_block(1, 0),
            down_block(0),
            down_block(1),
            taps_block(0),
            taps_block(1),
        ],
        out_specs=(
            keep(rows, width),
            keep(rows, width),
            keep(rows, width),
            keep(4, width),
            keep(per, *parcel),
        ),
        scratch_shapes=[pltpu.VMEM((4, PAD, CHUNK), F32)] * 5
        + [
            pltpu.VMEM((rows, CHUNK), F32),
            pltpu.VMEM((rows, CHUNK), BF16),
            pltpu.VMEM((CHUNK, rows), BF16),
            pltpu.VMEM((rows, CHUNK), BF16),
            pltpu.VMEM((rows, width), F32),
            pltpu.VMEM((16, CHUNK), F32),
            pltpu.VMEM((3,) + parcel, BF16),
            pltpu.VMEM((per,) + parcel, BF16),
            pltpu.VMEM((steps,) + parcel, BF16),
            pltpu.VMEM((per,) + parcel, BF16),
            pltpu.VMEM((per, sum_landing(2 * width, n_wide), CHUNK), BF16),
            pltpu.VMEM((rows, width), F32),
            pltpu.VMEM((rows, width), BF16),
            pltpu.VMEM((rows, width), BF16),
            pltpu.SemaphoreType.DMA((2, steps + per)),
            pltpu.SemaphoreType.DMA((2, per * HALVINGS)),
            pltpu.SemaphoreType.DMA((3,)),
        ],
        compiler_params=pltpu.CompilerParams(
            vmem_limit_bytes=62 * MIB, collective_id=1, has_side_effects=True
        ),
        name="feed_forward",
    )(live, h2, h2t, db, x1, cot, att, mod, wup, wup, wup, wup, wdown, wdown, taps, taps)


def attn_backward_kernel(
    n_wide, datt_ref, ctx_ref, u_ref, wout_ref, parcels, silu_ref, dmod_ref, qkv_hbm, probs_hbm,
    dqkv_ref, own_ref, full, gtaps_ref, small,
    dctx, probs_buf, weights, got_near, chip_sum, got_far, work, got_sums, taps_sum, taps_got,
    sems, in_sems, sum_sems, small_sems,
):
    rows_all, width = u_ref.shape
    wide, here = lax.axis_index("wide"), lax.axis_index("narrow")
    pairs = width // LANES
    half_pairs = pairs // 2
    steps = 4 * pairs
    slots = weights.shape[0]
    load_qkv = pltpu.make_async_copy(qkv_hbm, dqkv_ref, in_sems.at[2])
    load_qkv.start()

    def pair_of(step):
        return (half_pairs + step // 4) % pairs

    def load_probs(step):
        return pltpu.make_async_copy(
            probs_hbm.at[(step % 4) * pairs + pair_of(step)], probs_buf.at[step % 2], in_sems.at[step % 2]
        )

    load_probs(0).start()
    greet([(wide, here ^ 2), (wide, here ^ 1)] + wide_partners(wide, here, n_wide))
    pieces = full.shape[0]
    rows = full.shape[1]
    per_sum = sum_semaphores(n_wide)
    ahead = halvings_ahead(pieces, min(HALVINGS, n_wide.bit_length() - 1))
    sums = [
        WideSum(parcels.at[at, :rows], work.at[at], full.at[at], got_sums.at[at], sum_sems, at * per_sum,
                wide, here, n_wide, done=ahead[at])
        for at in range(pieces)
    ]
    levels = n_wide.bit_length() - 1
    queues = [one.actions() for one in sums]

    def advance(*which):
        for at in which:
            if queues[at]:
                for act in queues[at].pop(0):
                    act()

    def taps_copy(level):
        return remote(taps_sum.at[level], taps_got.at[level], sems, 6 + level, wide ^ (1 << level), here)

    def taps_add(level):
        taps_copy(level).wait_recv()
        taps_sum[level + 1] = taps_sum[level] + taps_got[level]
        if level + 1 < levels:
            taps_copy(level + 1).start()

    for at in range(pieces):
        taps_sum[0, :, at * CHUNK : (at + 1) * CHUNK] = parcels[at, rows:, :].astype(F32)
    partners = wide_partners(wide, here, n_wide) + [(wide, here ^ 1), (wide, here ^ 2)]

    def small_copy(level):
        have = 1 << level
        return remote(small.at[:have], small.at[have : 2 * have], small_sems, level, *partners[level])

    def small_step(level):
        small_copy(level).wait_recv()
        if level + 1 < len(partners):
            small_copy(level + 1).start()

    early = [silu_ref[0:1, :].astype(F32)] + [dmod_ref[at : at + 1, :] for at in range(4)]
    small[0] = lane_rows(early, EARLY)
    small_copy(0).start()
    taps_copy(0).start()
    advance(2, 0, 1)

    def ctx_step(step, carry):
        span = ds(step * PHASE, PHASE)
        dctx[span, :] = mm(datt_ref[span, :], wout_ref[...], NT).astype(BF16)
        return carry

    lax.fori_loop(0, 4, ctx_step, 0)
    load_qkv.wait()

    first = lax.broadcasted_iota(jnp.int32, (PHASE, LANES), 1) < HEAD_DIM
    zero = jnp.zeros((PHASE, LANES), BF16)
    scale = HEAD_DIM**-0.5

    def attend(step):
        group, pair = step % 4, pair_of(step)
        load_probs(step).wait()

        @pl.when(step + 1 < steps)
        def _():
            load_probs(step + 1).start()

        span = ds(group * PHASE, PHASE)
        query = dqkv_ref[span, ds(pair * LANES, LANES)]
        key = dqkv_ref[span, ds(width + pair * LANES, LANES)]
        value = dqkv_ref[span, ds(2 * width + pair * LANES, LANES)]
        dctx_pair = dctx[span, ds(pair * LANES, LANES)]
        dq, dk, dv = [], None, None
        for head in range(2):
            own = lambda both: jnp.where(first, both, zero) if head == 0 else jnp.where(first, zero, both)
            probs = probs_buf[step % 2, :, head * PHASE : (head + 1) * PHASE]
            probs_f = probs.astype(F32)
            dctx_own, query_own = own(dctx_pair), own(query)
            dprobs = mm(value, dctx_own, NT)
            inner = jnp.sum(dprobs * probs_f, axis=0, keepdims=True)
            dscores = (probs_f * (dprobs - inner)).astype(BF16)
            dv_one = mm(probs, dctx_own, NN)
            dk_one = mm(dscores, query_own, NN)
            dv = dv_one if dv is None else dv + dv_one
            dk = dk_one if dk is None else dk + dk_one
            dq.append(mm(dscores, key, TN))
        dqkv_ref[span, ds(pair * LANES, LANES)] = (
            jnp.where(first, dq[0], dq[1]) * scale
        ).astype(BF16)
        dqkv_ref[span, ds(width + pair * LANES, LANES)] = (dk * scale).astype(BF16)
        dqkv_ref[span, ds(2 * width + pair * LANES, LANES)] = dv.astype(BF16)

    def attend_loop(begin, end, plan):
        def body(step, carry):
            for at, what in plan:
                pl.when(step == at)(what)
            attend(step)
            return carry

        lax.fori_loop(begin, end, body, 0)

    slab = width // slots

    def weight_grads(half):
        span = width // 2
        for part in range(3):
            left = dqkv_ref[:, part * width + half * span : part * width + (half + 1) * span]
            found = mm(left, u_ref[...], TN).astype(BF16)
            for one in range(2):
                weights[2 * half + one, part * slab : (part + 1) * slab, :] = found[
                    one * slab : (one + 1) * slab
                ]

    head, tail = slice(3 * slab), slice(3 * slab, 4 * slab)

    def near_copy(early, rows, at):
        return remote(
            weights.at[3 if early else 1, rows], got_near.at[0 if early else 1, rows], sems, at, wide, here ^ 1
        )

    def far_copy(rows, at):
        return remote(chip_sum.at[rows], got_far.at[rows], sems, at, wide, here ^ 2)

    def add_chip(rows):
        chip_sum[rows, :] = (weights[2, rows, :].astype(F32) + got_near[0, rows, :].astype(F32)).astype(BF16)

    near_out, near_early = near_copy(True, tail, 0), near_copy(True, head, 1)
    late_out, near_late = near_copy(False, tail, 2), near_copy(False, head, 3)
    far_out, far = far_copy(tail, 4), far_copy(head, 5)

    for part in range(width // PHASE):
        cols = slice(part * PHASE, (part + 1) * PHASE)
        found = mm(ctx_ref[:, cols], datt_ref[...], TN).astype(BF16)
        for slot in range(slots):
            low, high = max(part * PHASE, slot * slab), min((part + 1) * PHASE, (slot + 1) * slab)
            if low < high:
                weights[slot, 3 * slab + low - slot * slab : 3 * slab + high - slot * slab, :] = found[
                    low - part * PHASE : high - part * PHASE
                ]
    near_out.start()
    late_out.start()

    def send_out():
        near_out.wait_recv()
        add_chip(tail)
        far_out.start()

    later = lambda *which: partial(advance, *which)
    small_plan = [(2 * level + 3, partial(small_step, level)) for level in range(len(partners) - 1)]
    attend_loop(
        0, steps // 2,
        [one for one in small_plan if one[0] < steps // 2]
        + [(1, send_out), (2, later(2, 0)), (5, later(1)), (7, partial(taps_add, 0)), (8, later(2, 0)), (11, later(1))],
    )
    weight_grads(1)
    near_early.start()
    advance(2)
    near_early.wait_recv()
    add_chip(head)
    far.start()
    attend_loop(
        steps // 2, steps,
        [one for one in small_plan if one[0] >= steps // 2]
        + [(13, later(1, 0)), (14, partial(taps_add, 1)), (16, later(2))],
    )
    weight_grads(0)
    near_late.start()
    small_step(len(partners) - 1)
    for level in range(2, levels):
        taps_add(level)
    gtaps_ref[...] = taps_sum[levels]
    near_late.wait_recv()
    late_out.wait_recv()
    while any(queues):
        advance(0, 1, 2)
    far_out.wait_recv()
    far.wait_recv()
    own_ref[...] = (
        weights[0].astype(F32) + got_near[1].astype(F32) + got_far[...].astype(F32)
    ).astype(BF16)
    for one in sums:
        one.wait_sends()
    for level in range(levels):
        taps_copy(level).wait_send()
    for copy in (near_out, near_early, late_out, near_late, far_out, far):
        copy.wait_send()
    for level in range(len(partners)):
        small_copy(level).wait_send()


def attn_backward(n_wide, datt, ctx, u, wout, parcels, silu_row, dmod, qkv, probs):
    rows, width = u.shape
    slots = lax.axis_size("narrow")
    slab = wout.shape[0] // slots
    pieces, parcel_rows, _ = parcels.shape
    sum_rows = parcel_rows - 16
    shape = jax.ShapeDtypeStruct
    levels = n_wide.bit_length() - 1
    per_sum = sum_semaphores(n_wide)
    return pl.pallas_call(
        partial(attn_backward_kernel, n_wide),
        out_shape=(
            shape((rows, 3 * width), BF16),
            shape((4 * slab, width), BF16),
            shape((pieces, sum_rows, CHUNK), BF16),
            shape((16, pieces * CHUNK), F32),
            shape((n_wide * slots, EARLY, LANES), BF16),
        ),
        in_specs=[whole()] * 7 + [whole(pl.ANY)] * 2,
        out_specs=(whole(),) * 5,
        scratch_shapes=[
            pltpu.VMEM((rows, width), BF16),
            pltpu.VMEM((2, PHASE, 2 * PHASE), BF16),
            pltpu.VMEM((slots, 4 * slab, width), BF16),
            pltpu.VMEM((2, 4 * slab, width), BF16),
            pltpu.VMEM((4 * slab, width), BF16),
            pltpu.VMEM((4 * slab, width), BF16),
            pltpu.VMEM((pieces, sum_rows, CHUNK), BF16),
            pltpu.VMEM((pieces, sum_landing(sum_rows, n_wide), CHUNK), BF16),
            pltpu.VMEM((levels + 1, 16, pieces * CHUNK), F32),
            pltpu.VMEM((levels, 16, pieces * CHUNK), F32),
            pltpu.SemaphoreType.DMA((2, 6 + levels)),
            pltpu.SemaphoreType.DMA((3,)),
            pltpu.SemaphoreType.DMA((2, pieces * per_sum)),
            pltpu.SemaphoreType.DMA((2, levels + 2)),
        ],
        compiler_params=pltpu.CompilerParams(
            vmem_limit_bytes=56 * MIB, collective_id=2, has_side_effects=True
        ),
        name="attn_backward",
    )(datt, ctx, u, wout, parcels, silu_row, dmod, qkv, probs)


def one_hot(rows, columns, wanted):
    row = lax.broadcasted_iota(jnp.int32, (rows, columns), 0)
    column = lax.broadcasted_iota(jnp.int32, (rows, columns), 1)
    return jnp.where(column == wanted(row), 1.0, 0.0).astype(BF16)


def input_backward_kernel(
    n_wide, x_ref, mod_ref, taps_ref, own_ref, dx1_hbm, dqkv_hbm, wqkv_hbm, block_in,
    got_dx, got_block, full, late, dtaps_ref,
    base, shifted, first_in, dh1, dx1_ref, dqkv_ref, wqkv_ref, dx, work, got_sums, tap_parts, tap_sums, tap_got,
    sems, local_sems, sum_sems, taps_sems, late_sems,
):
    rows_all, width = x_ref.shape
    wide, here = lax.axis_index("wide"), lax.axis_index("narrow")
    loads = [
        pltpu.make_async_copy(src, dst, local_sems.at[2 + at])
        for at, (src, dst) in enumerate(
            ((dqkv_hbm, dqkv_ref), (wqkv_hbm, wqkv_ref), (dx1_hbm, dx1_ref))
        )
    ]
    for load in loads:
        load.start()
    shift_one, scale_one = mod_ref[0:1, :], mod_ref[1:2, :]
    greet([(wide, peer) for peer in narrow_peers(here)] + [(wide ^ away, here) for away in range(1, n_wide)])
    pieces = full.shape[0]
    rows = full.shape[1]
    per_sum = sum_semaphores(n_wide)
    sums = [
        WideSum(own_ref.at[at * rows : (at + 1) * rows], work.at[at], full.at[at], got_sums.at[at], sum_sems,
                at * per_sum, wide, here, n_wide, order=((0, 1, 2), (1, 2, 0))[at])
        for at in range(pieces)
    ]
    queues = [one.actions() for one in sums]

    def advance(*which):
        for at in which:
            if queues[at]:
                for act in queues[at].pop(0):
                    act()

    levels = n_wide.bit_length() - 1
    late_wide = [
        remote(late.at[0], late.at[away], late_sems, away - 1, wide ^ away, here) for away in range(1, n_wide)
    ]
    late_narrow = [
        remote(late.at[:n_wide], late.at[away * n_wide : (away + 1) * n_wide], late_sems, n_wide - 2 + away,
               wide, here ^ away)
        for away in (2, 3, 1)
    ]
    taps_narrow = [
        remote(tap_sums.at[levels], tap_got.at[levels + away - 1], taps_sems, levels + away - 1, wide, here ^ away)
        for away in (2, 3, 1)
    ]
    advance(0, 1)
    block_back = Return(block_in, got_block, sems, local_sems.at[1], 3, wide, here)
    block_back.start()
    clear_edges(base)
    clear_edges(shifted)

    def norm_step(step, carry):
        group, part = step // (PHASE // ROWS), step % (PHASE // ROWS)
        unit, _ = normed(x_ref[ds(step * ROWS, ROWS), :].astype(F32))
        h_one = (unit * (1.0 + scale_one) + shift_one).astype(BF16)
        first_in[group, ds(HALF + part * ROWS, ROWS, HALF), :] = h_one.astype(F32)
        return carry

    lax.fori_loop(0, rows_all // ROWS, norm_step, 0)

    def du_step(group, carry):
        span = ds(group * PHASE, PHASE)
        total = None
        for part in range(3):
            cols = slice(part * width, (part + 1) * width)
            one = mm(dqkv_ref[span, cols], wqkv_ref[:, cols], NN)
            total = one if total is None else total + one
        base[group, HALF : HALF + PHASE, :] = total
        return carry

    loads[0].wait()
    loads[1].wait()
    lax.fori_loop(0, 2, du_step, 0)
    advance(0, 1)
    lax.fori_loop(2, 4, du_step, 0)

    blocks = width // LANES

    def shift_step(block, carry):
        shift_cols(base, shifted, ds(block * LANES, LANES))
        return carry

    lax.fori_loop(0, blocks, shift_step, 0)
    tap_parts[...] = jnp.zeros_like(tap_parts)
    advance(0, 1)

    def taps_copy(level):
        return remote(tap_sums.at[level], tap_got.at[level], taps_sems, level, wide ^ (1 << level), here)

    def taps_step(level):
        taps_copy(level).wait_recv()
        tap_sums[level + 1] = tap_sums[level] + tap_got[level]
        if level + 1 < levels:
            taps_copy(level + 1).start()
        else:
            for copy in taps_narrow:
                copy.start()

    def fold(value):
        return value.reshape(ROWS // 8, 8, width).sum(axis=0)

    back = Return(dx, got_dx, sems, local_sems.at[0], 0, wide, here)
    found = tuple(jnp.zeros((8, width), F32) for _ in range(2))
    for at, away in enumerate((2, 3, 1, 0)):
        source = away ^ here

        def conv_step(block, carry, source=source):
            lanes = ds(block * LANES, LANES)
            taps = [taps_ref[t // 3, t % 3 : t % 3 + 1, lanes].astype(F32) for t in range(9)]
            sums = [jnp.zeros((8, LANES), F32) for _ in range(9)]
            for group in range(4):
                total = jnp.zeros((ROWS, LANES), F32)
                own = first_in[group, ds(HALF + source * ROWS, ROWS, HALF), lanes]
                for tap in range(9):
                    moved = tap_value(
                        base, shifted, group, 2 - tap // 3, 2 - tap % 3, source * ROWS, lanes
                    )
                    total += taps[tap] * moved
                    sums[tap] += (own * moved).reshape(ROWS // 8, 8, LANES).sum(axis=0)
                dh1[ds(group * PHASE + source * ROWS, ROWS), lanes] = total
            for tap in range(9):
                tap_parts[tap, :, lanes] += sums[tap]
            return carry

        def rows_step(group, sums, source=source):
            span = ds(group * PHASE + source * ROWS, ROWS)
            unit, inv = normed(x_ref[span, :].astype(F32))
            grad = dh1[span, :]
            dx[group, source] = (
                dx1_ref[span, :] + norm_back(unit, inv, grad * (1.0 + scale_one))
            ).astype(BF16)
            return tuple(total + fold(one) for total, one in zip(sums, (grad, grad * unit)))

        lax.fori_loop(0, blocks, conv_step, 0)
        if at == 0:
            loads[2].wait()
        if at == 3:
            for tap in range(9):
                tap_sums[0, tap : tap + 1, :] = jnp.sum(tap_parts[tap], axis=0, keepdims=True)
            tap_sums[0, 9:, :] = jnp.zeros((7, width), F32)
            taps_copy(0).start()
        advance(*((0, 1), (0, 1), (0,), (1,))[at])
        found = lax.fori_loop(0, 4, rows_step, found)
        if at < 3:
            back.copies[at].start()
    back.own.start()
    late[0] = lane_rows([jnp.sum(one, axis=0, keepdims=True) for one in found], SMALL)
    for copy in late_wide:
        copy.start()
    taps_step(0)
    for copy in late_wide:
        copy.wait_recv()
    for copy in late_narrow:
        copy.start()
    for level in range(1, levels):
        taps_step(level)
        advance(level % 2)
    for copy in late_narrow:
        copy.wait_recv()
    total = tap_sums[levels]
    for at, copy in enumerate(taps_narrow):
        copy.wait_recv()
        total += tap_got[levels + (1, 2, 0)[at]]
    dtaps_ref[...] = total
    while any(queues):
        advance(0, 1)
    block_back.wait()
    back.wait()
    for copy in late_wide + late_narrow + taps_narrow:
        copy.wait_send()
    for level in range(levels):
        taps_copy(level).wait_send()
    for one in sums:
        one.wait_sends()


def input_backward(n_wide, x, dx1, dqkv, mod, taps, wqkv, own, block):
    rows, width = x.shape
    slots = lax.axis_size("narrow")
    pieces = 2
    sum_rows = own.shape[0] // pieces
    shape = jax.ShapeDtypeStruct
    per_sum = sum_semaphores(n_wide)
    levels = n_wide.bit_length() - 1
    back = shape((slots, 4, rows // (4 * slots), width), BF16)
    return pl.pallas_call(
        partial(input_backward_kernel, n_wide),
        out_shape=(
            back,
            back,
            shape((pieces, sum_rows, width), BF16),
            shape((n_wide * slots, SMALL, LANES), BF16),
            shape((SMALL, width), F32),
        ),
        in_specs=[whole()] * 4 + [whole(pl.ANY)] * 4,
        out_specs=(whole(),) * 5,
        scratch_shapes=[pltpu.VMEM((4, PAD, width), F32)] * 3
        + [
            pltpu.VMEM((rows, width), F32),
            pltpu.VMEM((rows, width), F32),
            pltpu.VMEM((rows, 3 * width), BF16),
            pltpu.VMEM(wqkv.shape, BF16),
            pltpu.VMEM((4, slots, rows // (4 * slots), width), BF16),
            pltpu.VMEM((pieces, sum_rows, width), BF16),
            pltpu.VMEM((pieces, sum_landing(sum_rows, n_wide), width), BF16),
            pltpu.VMEM((9, 8, width), F32),
            pltpu.VMEM((levels + 1, SMALL, width), F32),
            pltpu.VMEM((levels + 3, SMALL, width), F32),
            pltpu.SemaphoreType.DMA((2, 6)),
            pltpu.SemaphoreType.DMA((5,)),
            pltpu.SemaphoreType.DMA((2, pieces * per_sum)),
            pltpu.SemaphoreType.DMA((2, levels + 3)),
            pltpu.SemaphoreType.DMA((2, n_wide + 2)),
        ],
        compiler_params=pltpu.CompilerParams(
            vmem_limit_bytes=56 * MIB, collective_id=3, has_side_effects=True
        ),
        name="input_backward",
    )(x, mod, taps, own, dx1, dqkv, wqkv, block)


def outputs_kernel(
    dx_in, block_in, attn_sum, ffn_sum, small, late, cond_ref, kattn_in, kffn_in, ada_hbm,
    gada_hbm, dx_hbm, block_hbm, gqkv_hbm, gout_hbm, gup_hbm, gdown_hbm, gcond_ref, kattn_ref, kffn_ref,
    ada, gada, dx, block, gqkv, gout, gup, gdown, early_rows, late_rows, sems, in_sem,
):
    width = gout.shape[-1]
    here = lax.axis_index("narrow")
    load_ada = pltpu.make_async_copy(ada_hbm, ada, in_sem.at[0])
    load_ada.start()
    started = []
    for row in range(3):
        kattn_ref[row] = kattn_in[3 * row : 3 * row + 3, :]
        kffn_ref[row] = kffn_in[3 * row : 3 * row + 3, :]

    def put(src, dst):
        copy = pltpu.make_async_copy(src, dst, sems.at[len(started)])
        copy.start()
        started.append(copy)

    devices = small.shape[0]
    blocks = width // LANES
    early_rows[...] = small[...].astype(F32).reshape(devices * EARLY, LANES)
    late_rows[...] = late[...].astype(F32).reshape(devices * SMALL, LANES)

    def pick(ref, share, number):
        cut = [ref[pl.ds(number * blocks + at, devices, share), :] for at in range(blocks)]
        return jnp.concatenate(cut, axis=1).astype(BF16)

    silu_all = pick(early_rows, EARLY, 0)
    dmods = [
        pick(late_rows, SMALL, part) if part < 2 else pick(early_rows, EARLY, part - 1) for part in range(6)
    ]
    for part in range(6):
        gada[part] = mm(silu_all, dmods[part], TN)
        put(gada.at[part], gada_hbm.at[:, part * width : (part + 1) * width])
    slab = attn_sum.shape[1] // 2
    for part in range(3):
        gqkv[part] = attn_sum[part // 2, (part % 2) * slab : (part % 2 + 1) * slab, :].astype(F32).T
        put(gqkv.at[part], gqkv_hbm.at[part])
    gout[...] = attn_sum[1, slab:, :].astype(F32)
    put(gout, gout_hbm)
    permutation = group_permutation(dx_in.shape[1] * dx_in.shape[2])
    for at in range(dx_in.shape[0]):
        for source, held, out in ((dx_in, dx, dx_hbm), (block_in, block, block_hbm)):
            groups = jnp.concatenate([source[at, group] for group in range(4)], axis=0)
            held[at] = mm(permutation, groups, TN).astype(held.dtype)
            put(held.at[at], out.at[at])
    for at in range(ffn_sum.shape[0]):
        cols = slice(at * CHUNK, (at + 1) * CHUNK)
        gup[:, cols] = ffn_sum[at, :width, :].astype(F32)
        for part in range(width // CHUNK):
            span = slice(width + part * CHUNK, width + (part + 1) * CHUNK)
            gdown[cols, part * CHUNK : (part + 1) * CHUNK] = ffn_sum[at, span, :].astype(F32)
        put(gdown.at[cols], gdown_hbm.at[cols])
    put(gup, gup_hbm)

    def own_place(row):
        away = row ^ here
        return jnp.where(row < cond_ref.shape[0], away * (devices // 4), -1)

    load_ada.wait()
    choose = one_hot(16, devices, own_place)
    grad_silu = jnp.zeros((16, width), F32)
    for part in range(6):
        own = mm(choose, dmods[part], NN).astype(BF16)
        grad_silu += mm(own, ada[:, part * width : (part + 1) * width], NT)
    cond = cond_ref[...].astype(F32)
    gate = 1.0 / (1.0 + jnp.exp(-cond))
    gcond_ref[...] = grad_silu[: cond_ref.shape[0]] * (gate * (1.0 + cond * (1.0 - gate)))
    for copy in started:
        copy.wait()


def outputs(dx, block, attn_sum, ffn_sum, small, late, cond, kattn, kffn, w_ada):
    slots, _, quarter, width = dx.shape
    slab = attn_sum.shape[1] // 2
    pieces = ffn_sum.shape[0]
    local = pieces * CHUNK
    shape = jax.ShapeDtypeStruct
    tokens = (slots, 4 * quarter, width)
    return pl.pallas_call(
        outputs_kernel,
        out_shape=(
            shape(w_ada.shape, F32),
            shape(tokens, F32),
            shape(tokens, BF16),
            shape((3, width, slab), F32),
            shape((slab, width), F32),
            shape((width, local), F32),
            shape((local, width), F32),
            shape(cond.shape, F32),
            shape((3, 3, width), F32),
            shape((3, 3, local), F32),
        ),
        in_specs=[whole()] * 9 + [whole(pl.ANY)],
        out_specs=(whole(pl.ANY),) * 7 + (whole(),) * 3,
        scratch_shapes=[
            pltpu.VMEM(w_ada.shape, BF16),
            pltpu.VMEM((6, width, width), F32),
            pltpu.VMEM(tokens, F32),
            pltpu.VMEM(tokens, BF16),
            pltpu.VMEM((3, width, slab), F32),
            pltpu.VMEM((slab, width), F32),
            pltpu.VMEM((width, local), F32),
            pltpu.VMEM((local, width), F32),
            pltpu.VMEM((small.shape[0] * EARLY, LANES), F32),
            pltpu.VMEM((small.shape[0] * SMALL, LANES), F32),
            pltpu.SemaphoreType.DMA((6 + 3 + 1 + 2 * slots + pieces + 1,)),
            pltpu.SemaphoreType.DMA((1,)),
        ],
        compiler_params=pltpu.CompilerParams(vmem_limit_bytes=56 * MIB),
        name="outputs",
    )(dx, block, attn_sum, ffn_sum, small, late, cond, kattn, kffn, w_ada)


def per_device(
    tokens, condition, cotangent, counts, w_ada, k_attn, w_qkv, w_out, w_up, k_ffn, w_down
):
    lat_dev, shard_rows, width = tokens.shape
    here = lax.axis_index("narrow")
    rows_all = shard_rows * lat_dev
    local = w_up.shape[1]

    n_wide = lax.axis_size("wide")
    qkv_t = w_qkv.transpose(2, 1, 0).reshape(w_qkv.shape[2], 3 * width)
    ktaps_own = jnp.pad(k_ffn.reshape(9, local), ((0, 7), (0, 0)))

    cond_f = condition.astype(F32)
    silu_low = jax.nn.silu(cond_f).astype(BF16)
    own_silu = jnp.broadcast_to(lax.dynamic_slice_in_dim(silu_low, here, 1, 0), (16, width))
    live = (here < counts[0]).astype(F32).reshape(1, 1)

    (x, cot, u, qkv, probs, ctx, wqkv, wout, mod, att, x1, h2, h2t, db, wup, wdown, ktaps) = front(
        live, own_silu, k_attn, tokens, cotangent, w_ada, qkv_t, w_out, w_up, w_down, ktaps_own
    )
    cot = cot.reshape(rows_all, width)
    block_g, dx1, datt, dmod_mid, parcels = ffn(
        n_wide, live, h2, h2t, db, x1, cot, att, mod, wup, wdown, ktaps
    )
    block_g = block_g.reshape(4, lat_dev, shard_rows // 4, width)
    dqkv, own, ffn_sum, gtaps, small = attn_backward(
        n_wide, datt, ctx, u, wout, parcels, own_silu, dmod_mid, qkv, probs
    )
    got_dx, got_block, attn_sum, late, dattn_taps = input_backward(
        n_wide, x, dx1, dqkv, mod, k_attn, wqkv, own, block_g
    )
    (
        grad_w_ada, grad_tokens, block, gqkv, grad_w_out, grad_w_up, grad_w_down, grad_condition,
        grad_k_attn, grad_k_ffn,
    ) = outputs(
        got_dx, got_block, attn_sum, ffn_sum, small, late, condition, dattn_taps, gtaps, w_ada
    )
    grad_w_qkv = gqkv.transpose(1, 0, 2)
    return (
        block,
        grad_tokens,
        grad_condition,
        grad_w_ada,
        grad_k_attn,
        grad_w_qkv,
        grad_w_out,
        grad_w_up,
        grad_k_ffn,
        grad_w_down,
    )


def solution(mesh):
    placed = (
        P("wide", "narrow", None),
        P("wide", None),
        P("wide", "narrow", None),
        P("wide"),
        P(),
        P(),
        P(None, None, "narrow"),
        P("narrow", None),
        P(None, "narrow"),
        P(None, None, "narrow"),
        P("narrow", None),
    )
    return jax.shard_map(
        per_device,
        mesh=mesh,
        in_specs=placed,
        out_specs=(
            P("wide", "narrow", None),
            P("wide", "narrow", None),
            P("wide", None),
            P(),
            P(),
            P(None, None, "narrow"),
            P("narrow", None),
            P(None, "narrow"),
            P(None, None, "narrow"),
            P("narrow", None),
        ),
        check_vma=False,
    )
```

```python
from functools import partial

import jax
import jax.numpy as jnp
from jax import lax
from jax.experimental import pallas as pl
from jax.experimental.pallas import tpu as pltpu
from jax.sharding import PartitionSpec as P

HEAD_DIM = 64
SIDE = 32
HALF = SIDE // 2
PHASE = HALF * HALF
PAD = PHASE + 2 * HALF
LANES = 128
ROWS = 64
CHUNK = 256
LOG2E = 1.4426950408889634
GELU_C = 0.7978845608028654
GELU_A = 0.044715
MIB = 1 << 20
F32 = jnp.float32
BF16 = jnp.bfloat16

NN = (((1,), (0,)), ((), ()))
NT = (((1,), (1,)), ((), ()))
TN = (((0,), (0,)), ((), ()))


def mm(left, right, dims):
    return lax.dot_general(left, right, dims, preferred_element_type=F32)


def ds(start, size, unit=None):
    return pl.ds(pl.multiple_of(start, unit or size), size)


def tap_source(parity, tap):
    return {-1: (1, -1), 0: (0, 0), 1: (1, 0), 2: (0, 1)}[parity + tap - 1]


def shift_cols(base, shifted, lanes):
    col = lax.broadcasted_iota(jnp.int32, (ROWS, LANES), 0) % HALF

    def rows_step(step, carry):
        for group in range(4):
            rows = ds(HALF + step * ROWS, ROWS, HALF)
            value = base[group, rows, lanes]
            if group % 2:
                moved = jnp.where(col == 0, 0.0, pltpu.roll(value, 1, 0))
            else:
                moved = jnp.where(col == HALF - 1, 0.0, pltpu.roll(value, ROWS - 1, 0))
            shifted[group, rows, lanes] = moved
        return carry

    lax.fori_loop(0, PHASE // ROWS, rows_step, 0)


def clear_edges(ref):
    edge = jnp.zeros((HALF, ref.shape[-1]), ref.dtype)
    for group in range(4):
        ref[group, :HALF, :] = edge
        ref[group, PAD - HALF :, :] = edge


def tap_value(base, shifted, group, tap_row, tap_col, start, lanes):
    src_row, row_move = tap_source(group // 2, tap_row)
    src_col, col_move = tap_source(group % 2, tap_col)
    ref = base if col_move == 0 else shifted
    return ref[2 * src_row + src_col, ds(HALF + row_move * HALF + start, ROWS, HALF), lanes]


def normed(values_in):
    mean_val = jnp.mean(values_in, axis=-1, keepdims=True)
    centred = values_in - mean_val
    inv = lax.rsqrt(jnp.mean(centred * centred, axis=-1, keepdims=True) + 1e-06)
    return centred * inv, inv


def norm_back(unit, inv, grad):
    mean_grad = jnp.mean(grad, axis=-1, keepdims=True)
    mean_dot = jnp.mean(grad * unit, axis=-1, keepdims=True)
    return (grad - mean_grad - unit * mean_dot) * inv


def narrow_peers(here):
    return [here ^ 2, here ^ 3, here ^ 1]


def remote(src, dst, sems, at, wide, narrow):
    return pltpu.make_async_remote_copy(
        src_ref=src,
        dst_ref=dst,
        send_sem=sems.at[0, at],
        recv_sem=sems.at[1, at],
        device_id=(wide, narrow),
        device_id_type=pl.DeviceIdType.MESH,
    )


class Gather:
    COPIES = 11

    def __init__(self, src, dst, sems, local_sem, first, wide, here):
        count = src.shape[0]
        quarter = count // 4
        front = -(-quarter // 32) * 16
        mine = wide % 4
        far, near = here ^ 2, here ^ 1

        def slot(k):
            return dst.at[k * count : (k + 1) * count]

        def at(k, which, start=0, size=quarter):
            return dst.at[ds(k * count + which * quarter + start, size, 16)]

        def send(number, source, target, wide_to, narrow_to):
            return remote(source, target, sems, first + number, wide_to, narrow_to)

        def same(number, which, wide_to, start=0, size=quarter):
            return send(number, at(2, which, start, size), at(2, which, start, size), wide_to, here)

        def share(number, which, start=0, size=quarter):
            return send(number, at(2, which, start, size), at(3, which, start, size), wide, near)

        own_part = src.at[ds(mine * quarter, quarter, 16)]
        rest = quarter - front
        self.own = pltpu.make_async_copy(src, slot(0), local_sem)
        self.near = send(0, src, slot(1), wide, near)
        self.far = send(1, own_part, at(2, mine), wide, far)
        self.swaps = [same(2, mine, wide ^ 1), same(3, mine, wide ^ 2)]
        self.corners = [same(4, mine ^ 1, wide ^ 2, 0, front), same(5, mine ^ 2, wide ^ 1, front, rest)]
        self.shares = [
            share(6, mine),
            share(7, mine ^ 1),
            share(8, mine ^ 2),
            share(9, mine ^ 3, 0, front),
            share(10, mine ^ 3, front, rest),
        ]

    def start_near(self):
        self.own.start()
        self.near.start()

    def start_far(self):
        self.far.start()

    def swap(self):
        self.far.wait_recv()
        self.swaps[0].start()
        self.swaps[1].start()
        self.shares[0].start()

    def corner(self):
        for which in range(2):
            self.swaps[which].wait_recv()
            self.corners[which].start()
            self.shares[1 + which].start()

    def share_corner(self):
        for which in range(2):
            self.corners[which].wait_recv()
            self.shares[3 + which].start()

    def finish(self):
        self.own.wait()
        self.near.wait()
        self.far.wait_send()
        for copy in self.swaps + self.corners:
            copy.wait_send()
        for copy in self.shares:
            copy.wait()


def group_permutation(rows):
    out = lax.broadcasted_iota(jnp.int32, (rows, rows), 0)
    source = lax.broadcasted_iota(jnp.int32, (rows, rows), 1)
    per_group = rows // 4
    group, rest = out // per_group, out % per_group
    line = 2 * (rest // HALF) + group // 2
    wanted = line * SIDE + 2 * (rest % HALF) + group % 2
    return jnp.where(source == wanted, 1.0, 0.0).astype(BF16)


class Exchange:
    def __init__(self, sent, got, sems, local_sem, first, wide, here):
        self.own = pltpu.make_async_copy(sent.at[here], got.at[:, here], local_sem)
        self.copies = [
            remote(sent.at[peer], got.at[:, here], sems, first + at, wide, peer)
            for at, peer in enumerate(narrow_peers(here))
        ]

    def start(self):
        for copy in self.copies:
            copy.start()
        self.own.start()

    def wait(self):
        self.own.wait()
        for copy in self.copies:
            copy.wait()


class Return:
    def __init__(self, sent, got, sems, local_sem, first, wide, here):
        self.own = pltpu.make_async_copy(sent.at[:, here], got.at[here], local_sem)
        self.copies = [
            remote(sent.at[:, peer], got.at[here], sems, first + at, wide, peer)
            for at, peer in enumerate(narrow_peers(here))
        ]

    start = Exchange.start
    wait = Exchange.wait


HALVINGS = 3
EARLY = 32
SMALL = 16


class WideSum:
    def __init__(self, source, work, full, got, sems, first, wide, here, n_wide, done=0, order=None):
        self.source, self.work, self.full, self.got = source, work, full, got
        self.rows = work.shape[0]
        self.levels = min(HALVINGS, n_wide.bit_length() - 1)
        self.extra = n_wide.bit_length() - 1 - self.levels
        self.done = done
        self.wide, self.here, self.sems, self.first = wide, here, sems, first
        self.offsets = [0]
        self.masks = [1 << at for at in (order or range(HALVINGS)) if at < self.levels]
        for level in range(self.levels):
            bit = (wide // self.masks[level]) % 2
            self.offsets.append(self.offsets[-1] + bit * (self.rows >> (level + 1)))
        self.waiting = []

    def size(self, level):
        return self.rows >> level

    def at(self, ref, offset, size):
        return ref.at[ds(offset, size, 16)]

    def half_copy(self, level):
        size, base = self.size(level + 1), self.offsets[level]
        send = base + size - (self.offsets[level + 1] - base)
        source = self.source if level == self.done else self.work
        landing = self.rows - self.size(level)
        return remote(
            self.at(source, send, size), self.got.at[landing : landing + size],
            self.sems, self.first + level, self.wide ^ self.masks[level], self.here,
        )

    def start_half(self, level):
        self.half_copy(level).start()

    def finish_half(self, level):
        self.half_copy(level).wait_recv()
        size, landing = self.size(level + 1), self.rows - self.size(level)
        rows = ds(self.offsets[level + 1], size, 16)
        source = self.source if level == self.done else self.work
        self.work[rows, :] = (
            source[rows, :].astype(F32) + self.got[landing : landing + size, :].astype(F32)
        ).astype(BF16)

    def extras(self):
        size = self.size(self.levels)
        rows = ds(self.offsets[self.levels], size, 16)
        source = self.source if self.done == self.levels else self.work
        self.full[rows, :] = source[rows, :]
        for at in range(self.extra):
            landing = self.rows - size + at * size
            copy = remote(
                self.full.at[rows], self.got.at[landing : landing + size],
                self.sems, self.first + 2 * self.levels + at,
                self.wide ^ (1 << (self.levels + at)), self.here,
            )
            copy.start()
            copy.wait()
            self.full[rows, :] = (
                self.full[rows, :].astype(F32) + self.got[landing : landing + size, :].astype(F32)
            ).astype(BF16)

    def spread_copy(self, level):
        part = self.at(self.full, self.offsets[level + 1], self.size(level + 1))
        return remote(
            part, part, self.sems, self.first + self.levels + level, self.wide ^ self.masks[level], self.here
        )

    def actions(self):
        acts = []
        for level in range(self.done, self.levels):
            acts.append([partial(self.start_half, level)])
            if level > self.done:
                acts[-1].insert(0, partial(self.finish_half, level - 1))
        tail = [self.extras]
        if self.done < self.levels:
            tail.insert(0, partial(self.finish_half, self.levels - 1))
        for level in reversed(range(self.levels)):
            acts.append(tail + [lambda level=level: self.spread_copy(level).start()])
            tail = [lambda level=level: self.spread_copy(level).wait_recv()]
        acts.append(tail)
        return acts

    def wait_sends(self):
        for level in range(self.done, self.levels):
            self.half_copy(level).wait_send()
        for level in range(self.levels):
            self.spread_copy(level).wait_send()


def halvings_ahead(pieces, levels):
    return [min(levels, pieces - at) for at in range(pieces)]


def lane_rows(values_in, rows):
    cut = [
        one[:, at * LANES : (at + 1) * LANES] for one in values_in for at in range(one.shape[1] // LANES)
    ]
    return jnp.concatenate(cut + [jnp.zeros((rows - len(cut), LANES), F32)]).astype(BF16)


def greet(partners):
    barrier = pltpu.get_barrier_semaphore()
    for partner in partners:
        pl.semaphore_signal(
            barrier, inc=1, device_id=partner, device_id_type=pl.DeviceIdType.MESH
        )
    pl.semaphore_wait(barrier, len(partners))


def wide_partners(wide, here, n_wide):
    return [(wide ^ (1 << level), here) for level in range(n_wide.bit_length() - 1)]


def sum_semaphores(n_wide):
    levels = n_wide.bit_length() - 1
    return levels + min(levels, HALVINGS)


def sum_landing(rows, n_wide):
    levels = n_wide.bit_length() - 1
    last = rows >> min(levels, HALVINGS)
    return rows - last + max(levels - HALVINGS, 0) * last


def front_kernel(
    live_ref, silu_ref, taps_ref, tokens_hbm, cot_hbm, ada_hbm, wqkv_src, wout_src, wup_src, wdown_src, ktaps_src,
    x_hbm, cot_hbm_out, u_hbm, qkv_hbm, probs_hbm, ctx_hbm, wqkv_hbm, wout_hbm,
    mod_ref, att_ref, x1_ref, h2_ref, h2t_ref, db_ref, wup_ref, wdown_ref, ktaps_ref,
    x_ref, cot_ref, u_ref, qkv_ref, probs_ref, ctx_ref, wqkv_ref, wout_ref,
    base, shifted, shards, sent, sent_cot, got, ada, up_own, down_own, sems, local_sems, in_sems, out_sems,
):
    width = u_ref.shape[1]
    flushed = []

    def flush(src, dst):
        copy = pltpu.make_async_copy(src, dst, out_sems.at[len(flushed)])
        copy.start()
        flushed.append(copy)

    rows_all = u_ref.shape[0]
    latents, shard_rows = shards.shape[:2]
    wide, here = lax.axis_index("wide"), lax.axis_index("narrow")
    load_tokens = pltpu.make_async_copy(tokens_hbm, shards, in_sems.at[0])
    load_tokens.start()
    load_ada = pltpu.make_async_copy(ada_hbm, ada, in_sems.at[1])
    load_ada.start()
    load_up = pltpu.make_async_copy(wup_src, up_own, in_sems.at[2])
    load_up.start()
    load_down = pltpu.make_async_copy(wdown_src, down_own, in_sems.at[3])
    load_down.start()

    barrier = pltpu.get_barrier_semaphore()
    partners = [(wide, peer) for peer in narrow_peers(here)] + [(wide ^ 1, here), (wide ^ 2, here)]
    for partner in partners:
        pl.semaphore_signal(
            barrier, inc=1, device_id=partner, device_id_type=pl.DeviceIdType.MESH
        )
    permutation = group_permutation(shard_rows)
    load_tokens.wait()

    def permute(to):
        def one(at, carry):
            moved = mm(permutation, shards[at], NN).astype(BF16)
            for group in range(4):
                to[at, group] = moved[group * (shard_rows // 4) : (group + 1) * (shard_rows // 4)]
            return carry

        lax.fori_loop(0, latents, one, 0)

    pl.semaphore_wait(barrier, len(partners))
    exchange = Exchange(sent, got, sems, local_sems.at[0], 0, wide, here)
    exchange_cot = Exchange(sent_cot, cot_ref, sems, local_sems.at[1], 3, wide, here)
    gathers = [
        Gather(src, dst, sems, local_sems.at[2 + at], 9 + Gather.COPIES * at, wide, here)
        for at, (src, dst) in enumerate(
            (
                (wqkv_src, wqkv_ref),
                (wout_src, wout_ref),
                (up_own, wup_ref),
                (down_own, wdown_ref),
            )
        )
    ]
    g_qkv, g_out, g_up, g_down = gathers
    taps_own = pltpu.make_async_copy(ktaps_src, ktaps_ref.at[0], local_sems.at[6])
    taps_sends = [
        remote(ktaps_src, ktaps_ref.at[peer ^ here], sems, 6 + at, wide, peer)
        for at, peer in enumerate(narrow_peers(here))
    ]
    g_qkv.start_far()
    permute(sent)
    exchange.start()
    load_cot = pltpu.make_async_copy(cot_hbm, shards, in_sems.at[0])
    load_cot.start()
    load_up.wait()
    load_down.wait()
    for one in gathers:
        one.start_near()
    taps_own.start()
    for one in taps_sends:
        one.start()

    load_ada.wait()
    for part in range(6):
        mod_ref[part : part + 1, :] = mm(
            silu_ref[...], ada[:, part * width : (part + 1) * width], NN
        )[0:1, :]
    load_cot.wait()
    permute(sent_cot)
    g_qkv.swap()
    shift_one, scale_one, gate_one = mod_ref[0:1, :], mod_ref[1:2, :], mod_ref[2:3, :]
    shift_two, scale_two, gate_two = mod_ref[3:4, :], mod_ref[4:5, :], mod_ref[5:6, :]
    clear_edges(base)
    clear_edges(shifted)
    exchange.wait()
    g_out.start_far()
    g_up.start_far()
    g_qkv.corner()
    for group in range(4):
        for source in range(latents):
            start = group * PHASE + source * ROWS
            x_ref[start : start + ROWS, :] = got[group, source]
    flush(x_ref, x_hbm)

    def norm_step(step, carry):
        group, part = step // (PHASE // ROWS), step % (PHASE // ROWS)
        unit, _ = normed(x_ref[ds(step * ROWS, ROWS), :].astype(F32))
        h_one = (unit * (1.0 + scale_one) + shift_one).astype(BF16)
        base[group, ds(HALF + part * ROWS, ROWS, HALF), :] = h_one.astype(F32)
        return carry

    lax.fori_loop(0, rows_all // ROWS, norm_step, 0)
    g_qkv.share_corner()
    g_out.swap()

    def conv_step(block, carry):
        lanes = ds(block * LANES, LANES)
        shift_cols(base, shifted, lanes)
        taps = [taps_ref[t // 3, t % 3 : t % 3 + 1, lanes].astype(F32) for t in range(9)]

        def rows_step(step, carry):
            for group in range(4):
                total = jnp.zeros((ROWS, LANES), F32)
                for tap in range(9):
                    total += taps[tap] * tap_value(
                        base, shifted, group, tap // 3, tap % 3, step * ROWS, lanes
                    )
                u_ref[ds(group * PHASE + step * ROWS, ROWS), lanes] = total.astype(BF16)
            return carry

        return lax.fori_loop(0, PHASE // ROWS, rows_step, carry)

    blocks = width // LANES
    lax.fori_loop(0, 2 * blocks // 3, conv_step, 0)
    g_out.corner()
    g_up.swap()
    g_down.start_far()
    lax.fori_loop(2 * blocks // 3, blocks, conv_step, 0)
    flush(u_ref, u_hbm)
    g_qkv.finish()
    flush(wqkv_ref, wqkv_hbm)

    def project_step(step, carry):
        rows = ds(step * PHASE, PHASE)
        for part in range(3):
            cols = slice(part * width, (part + 1) * width)
            qkv_ref[rows, cols] = mm(u_ref[rows, :], wqkv_ref[:, cols], NT).astype(BF16)
        return carry

    lax.fori_loop(0, 4, project_step, 0)

    pairs = width // LANES
    first = lax.broadcasted_iota(jnp.int32, (PHASE, LANES), 1) < HEAD_DIM
    zero = jnp.zeros((PHASE, LANES), BF16)

    def attend_step(step, carry):
        group, pair = step // pairs, step % pairs
        rows = ds(group * PHASE, PHASE)
        query = qkv_ref[rows, ds(pair * LANES, LANES)]
        key = qkv_ref[rows, ds(width + pair * LANES, LANES)]
        value = qkv_ref[rows, ds(2 * width + pair * LANES, LANES)]
        found = []
        for head in range(2):
            own = jnp.where(first, query, zero) if head == 0 else jnp.where(first, zero, query)
            scores = mm(key, own, NT)
            top = jnp.max(scores, axis=0, keepdims=True)
            raised = jnp.exp2((scores - top) * (LOG2E * HEAD_DIM**-0.5))
            probs = (raised * (1.0 / jnp.sum(raised, axis=0, keepdims=True))).astype(BF16)
            probs_ref[step, :, head * PHASE : (head + 1) * PHASE] = probs
            found.append(mm(probs, value, TN))
        ctx_ref[rows, ds(pair * LANES, LANES)] = jnp.where(first, found[0], found[1]).astype(BF16)
        return carry

    flush(qkv_ref, qkv_hbm)
    g_up.corner()
    g_out.share_corner()
    g_down.swap()
    exchange_cot.start()

    def attend_group(group):
        lax.fori_loop(group * pairs, (group + 1) * pairs, attend_step, 0)
        done = slice(group * pairs, (group + 1) * pairs)
        flush(probs_ref.at[done], probs_hbm.at[done])

    attend_group(0)
    g_up.share_corner()
    attend_group(1)
    g_down.corner()
    attend_group(2)
    g_down.share_corner()
    attend_group(3)
    flush(ctx_ref, ctx_hbm)
    g_out.finish()
    flush(wout_ref, wout_hbm)

    def out_step(step, carry):
        rows = ds(step * PHASE, PHASE)
        total = mm(ctx_ref[rows, :], wout_ref[...], NN)
        att_ref[rows, :] = total.astype(BF16)
        x1_ref[rows, :] = x_ref[rows, :].astype(F32) + gate_one * total
        return carry

    lax.fori_loop(0, 4, out_step, 0)
    live = live_ref[0, 0]

    def second_step(step, carry):
        rows = ds(step * ROWS, ROWS)
        unit, _ = normed(x1_ref[rows, :])
        h2_ref[rows, :] = (unit * (1.0 + scale_two) + shift_two).astype(BF16)
        group, source = step // (PHASE // ROWS), step % (PHASE // ROWS)
        db_ref[rows, :] = (cot_ref[group, source].astype(F32) * live * gate_two).astype(BF16)
        return carry

    exchange_cot.wait()
    flush(cot_ref, cot_hbm_out)
    lax.fori_loop(0, rows_all // ROWS, second_step, 0)
    for part in range(4):
        h2t_ref[:, part * PHASE : (part + 1) * PHASE] = h2_ref[
            part * PHASE : (part + 1) * PHASE, :
        ].T
    g_up.finish()
    g_down.finish()
    for copy in flushed:
        copy.wait()
    taps_own.wait()
    for one in taps_sends:
        one.wait()


def whole(memory=pltpu.VMEM):
    return pl.BlockSpec(memory_space=memory)


def front(live, silu_row, taps, tokens, cot, w_ada, wqkv, wout, wup, wdown, ktaps):
    latents, shard_rows, width = tokens.shape
    rows = latents * shard_rows
    steps = 4 * (width // LANES)
    shape = jax.ShapeDtypeStruct
    full = lambda shard: shape((latents * shard.shape[0],) + shard.shape[1:], BF16)
    moved = (latents, 4, shard_rows // 4, width)
    streamed = (
        shape((rows, width), BF16),
        shape((4, latents, shard_rows // 4, width), BF16),
        shape((rows, width), BF16),
        shape((rows, 3 * width), BF16),
        shape((steps, PHASE, 2 * PHASE), BF16),
        shape((rows, width), BF16),
        full(wqkv),
        full(wout),
    )
    return pl.pallas_call(
        front_kernel,
        out_shape=streamed
        + (
            shape((6, width), F32),
            shape((rows, width), BF16),
            shape((rows, width), F32),
            shape((rows, width), BF16),
            shape((width, rows), BF16),
            shape((rows, width), BF16),
            full(wup),
            full(wdown),
            shape((latents,) + ktaps.shape, BF16),
        ),
        in_specs=[whole(pltpu.SMEM)] + [whole()] * 2 + [whole(pl.ANY)] * 3 + [whole()] * 2 + [whole(pl.ANY)] * 2 + [whole()],
        out_specs=(whole(pl.ANY),) * 8 + (whole(),) * 6 + (whole(pl.ANY),) * 2 + (whole(),),
        scratch_shapes=[pltpu.VMEM(one.shape, one.dtype) for one in streamed]
        + [
            pltpu.VMEM((4, PAD, width), F32),
            pltpu.VMEM((4, PAD, width), F32),
            pltpu.VMEM((latents, shard_rows, width), BF16),
            pltpu.VMEM(moved, BF16),
            pltpu.VMEM(moved, BF16),
            pltpu.VMEM((4, latents, shard_rows // 4, width), BF16),
            pltpu.VMEM(w_ada.shape, BF16),
            pltpu.VMEM(wup.shape, BF16),
            pltpu.VMEM(wdown.shape, BF16),
            pltpu.SemaphoreType.DMA((2, 9 + 4 * Gather.COPIES)),
            pltpu.SemaphoreType.DMA((7,)),
            pltpu.SemaphoreType.DMA((4,)),
            pltpu.SemaphoreType.DMA((len(streamed) + 3,)),
        ],
        compiler_params=pltpu.CompilerParams(
            vmem_limit_bytes=60 * MIB, collective_id=0, has_side_effects=True
        ),
        name="attn_forward",
    )(live, silu_row, taps, tokens, cot, w_ada, wqkv, wout, wup, wdown, ktaps)


def ffn_kernel(
    n_wide, live_ref, h2_ref, h2t_ref, db_ref, x1_hbm, cot_hbm, att_hbm, mod_ref,
    wup_before, wup_even, wup_odd, wup_after, wdown_even, wdown_odd, taps_even, taps_odd,
    block_ref, dx1_ref, datt_ref, dmod_ref, sums_ref,
    hid_even, hid_odd, hid_moved, grad, grad_moved, slope, act, act_t, dhid, branch, dtaps,
    work, chip_sum, got_near, got_far, got_sums, x1_ref, cot_ref, att_ref, sems, sum_sems, in_sems,
):
    rows_all, width = h2_ref.shape
    loads = [
        pltpu.make_async_copy(src, dst, in_sems.at[at])
        for at, (src, dst) in enumerate(((x1_hbm, x1_ref), (cot_hbm, cot_ref), (att_hbm, att_ref)))
    ]
    dh2 = dx1_ref
    wide, here = lax.axis_index("wide"), lax.axis_index("narrow")
    step, steps = pl.program_id(0), pl.num_programs(0)
    quarters = [slice(q * PHASE, (q + 1) * PHASE) for q in range(4)]
    inside = slice(HALF, HALF + PHASE)
    lane_blocks = [slice(at * LANES, (at + 1) * LANES) for at in range(CHUNK // LANES)]
    col = lax.broadcasted_iota(jnp.int32, (ROWS, LANES), 0) % HALF

    partners = [(wide, here ^ 1), (wide, here ^ 2)] + wide_partners(wide, here, n_wide)[:HALVINGS]
    pieces, sum_rows = got_sums.shape[0], got_sums.shape[1]
    sums = [
        WideSum(sums_ref.at[at, : 2 * width], sums_ref.at[at, : 2 * width], None, got_sums.at[at], sum_sems,
                at * HALVINGS, wide, here, n_wide)
        for at in range(pieces)
    ]
    schedule = halvings_ahead(pieces, sums[0].levels)

    def to_near(at):
        return remote(work.at[at % 2], got_near.at[at], sems, at, wide, here ^ 1)

    def to_far(at):
        return remote(chip_sum.at[at], got_far.at[at], sems, steps + at, wide, here ^ 2)

    @pl.when(step == 0)
    def _():
        for load in loads:
            load.start()
        barrier = pltpu.get_barrier_semaphore()
        for partner in partners:
            pl.semaphore_signal(
                barrier, inc=1, device_id=partner, device_id_type=pl.DeviceIdType.MESH
            )
        for ref in (hid_even, hid_odd, hid_moved, grad, grad_moved):
            clear_edges(ref)
        branch[...] = jnp.zeros_like(branch)
        dh2[...] = jnp.zeros_like(dh2)
        dtaps[...] = jnp.zeros_like(dtaps)
        dhid[...] = jnp.zeros_like(dhid)
        full = mm(h2_ref[...], wup_even[...], NN)
        for q in range(4):
            hid_even[q, inside, :] = full[quarters[q]]
        pl.semaphore_wait(barrier, len(partners))

    def moved_cols(group, value):
        if group % 2:
            return jnp.where(col == 0, 0.0, pltpu.roll(value, 1, 0))
        return jnp.where(col == HALF - 1, 0.0, pltpu.roll(value, ROWS - 1, 0))

    def static_tap(base, shifted, group, tap_row, tap_col, start, lanes):
        src_row, row_move = tap_source(group // 2, tap_row)
        src_col, col_move = tap_source(group % 2, tap_col)
        ref = base if col_move == 0 else shifted
        first = HALF + row_move * HALF + start
        return ref[2 * src_row + src_col, first : first + ROWS, lanes]

    def weights_back(q, wup_last, slot):
        dh2[quarters[q], :] += mm(dhid[quarters[q], :], wup_last[...], NT)
        if q < width // PHASE:
            slot[quarters[q], :] = mm(h2t_ref[quarters[q], :], dhid[...], NN).astype(BF16)

    def forward_products(part, wdown, wup_last, slot):
        grad[part, inside, :] = mm(db_ref[quarters[part], :], wdown[...], NT)
        yield
        for cols in quarters[: width // PHASE]:
            dh2[quarters[part], cols] += mm(dhid[quarters[part], :], wup_last[cols, :], NT)
            yield
        if part < width // PHASE:
            slot[quarters[part], :] = mm(h2t_ref[quarters[part], :], dhid[...], NN).astype(BF16)
        yield

    def backward_products(part, hid_next, wdown, wup_next, slot):
        hid_next[part, inside, :] = mm(h2_ref[quarters[part], :], wup_next[...], NN)
        yield
        for cols in quarters[: width // PHASE]:
            branch[quarters[part], cols] += mm(act[quarters[part], :], wdown[:, cols], NN)
            yield
        if part < width // CHUNK:
            block = slice(part * CHUNK, (part + 1) * CHUNK)
            slot[width + part * CHUNK : width + (part + 1) * CHUNK, :] = mm(
                act_t[...], db_ref[:, block], NN
            ).astype(BF16)
        yield

    def forward(hid, wdown, taps_ref, wup_last, slot):
        taps = [[taps_ref[0, t : t + 1, lanes].astype(F32) for t in range(9)] for lanes in lane_blocks]
        for part in range(PHASE // ROWS):
            rows = slice(HALF + part * ROWS, HALF + (part + 1) * ROWS)
            for group in range(4):
                for lanes in lane_blocks:
                    hid_moved[group, rows, lanes] = moved_cols(group, hid[group, rows, lanes])
        for part in range(PHASE // ROWS):
            products = forward_products(part, wdown, wup_last, slot)
            for group in range(4):
                for at, lanes in enumerate(lane_blocks):
                    next(products, None)
                    total = jnp.zeros((ROWS, LANES), F32)
                    for tap in range(9):
                        total += taps[at][tap] * static_tap(
                            hid, hid_moved, group, tap // 3, tap % 3, part * ROWS, lanes
                        )
                    square = total * total
                    turned = jnp.tanh(total * (square * (GELU_C * GELU_A) + GELU_C))
                    half = 0.5 * turned + 0.5
                    bend = total * (half - half * half)
                    start = group * PHASE + part * ROWS
                    act[start : start + ROWS, lanes] = (total * half).astype(BF16)
                    slope[start : start + ROWS, lanes] = half + bend * (
                        square * (6.0 * GELU_C * GELU_A) + 2.0 * GELU_C
                    )

    def backward(hid, hid_next, wdown, wup_next, taps_ref, slot):
        taps = [[taps_ref[0, t : t + 1, lanes].astype(F32) for t in range(9)] for lanes in lane_blocks]
        act_t[...] = act[...].T
        for part in range(PHASE // ROWS):
            rows = slice(HALF + part * ROWS, HALF + (part + 1) * ROWS)
            for group in range(4):
                start = group * PHASE + part * ROWS
                for lanes in lane_blocks:
                    value = grad[group, rows, lanes] * slope[start : start + ROWS, lanes]
                    grad[group, rows, lanes] = value
                    grad_moved[group, rows, lanes] = moved_cols(group, value)
        sums = [[jnp.zeros((8, LANES), F32) for _ in range(9)] for _ in lane_blocks]
        for part in range(PHASE // ROWS):
            products = backward_products(part, hid_next, wdown, wup_next, slot)
            for group in range(4):
                start = group * PHASE + part * ROWS
                for at, lanes in enumerate(lane_blocks):
                    next(products, None)
                    own = hid[group, HALF + part * ROWS : HALF + (part + 1) * ROWS, lanes]
                    total = jnp.zeros((ROWS, LANES), F32)
                    for tap in range(9):
                        moved = static_tap(
                            grad, grad_moved, group, 2 - tap // 3, 2 - tap % 3, part * ROWS, lanes
                        )
                        total += taps[at][tap] * moved
                        sums[at][tap] += (own * moved).reshape(ROWS // 8, 8, LANES).sum(axis=0)
                    dhid[start : start + ROWS, lanes] = total.astype(BF16)
        for at, lanes in enumerate(lane_blocks):
            for tap in range(9):
                dtaps[tap : tap + 1, lanes] = jnp.sum(sums[at][tap], axis=0, keepdims=True)
        slot[2 * width :, :] = dtaps[...].astype(BF16)

    def settle(pair):
        to_near(pair).wait_recv()

        @pl.when(pair < steps // 2)
        def _():
            chip_sum[pair] = (work[2].astype(F32) + got_near[pair].astype(F32)).astype(BF16)
            to_far(pair).start()

        @pl.when(pair >= steps // 2)
        def _():
            part = pair - steps // 2
            to_far(part).wait_recv()
            sums_ref[part] = (
                work[2].astype(F32) + got_near[pair].astype(F32) + got_far[part].astype(F32)
            ).astype(BF16)

        for part in range(pieces):

            @pl.when(pair == steps // 2 + part)
            def _():
                for at in range(part):
                    sums[at].finish_half(part - at - 1)
                for at in range(part + 1):
                    if part - at < schedule[at]:
                        sums[at].start_half(part - at)

    forward(hid_even, wdown_even, taps_even, wup_before, work.at[2])

    @pl.when(step >= 1)
    def _():
        settle(step - 1)

    @pl.when(step >= 2)
    def _():
        to_near(step - 2).wait_send()

    even_slot = work.at[step % 2]
    backward(hid_even, hid_odd, wdown_even, wup_odd, taps_even, even_slot)
    forward(hid_odd, wdown_odd, taps_odd, wup_even, even_slot)
    to_near(step).start()
    backward(hid_odd, hid_even, wdown_odd, wup_after, taps_odd, work.at[2])

    @pl.when(step == steps - 1)
    def _():
        for q in range(4):
            weights_back(q, wup_odd, work.at[2])
        settle(step)
        for load in loads:
            load.wait()
        gate_one, scale_two, gate_two = mod_ref[2:3, :], mod_ref[4:5, :], mod_ref[5:6, :]
        live = live_ref[0, 0]

        def fold(value):
            return value.reshape(ROWS // 8, 8, width).sum(axis=0)

        def rows_step(at, sums):
            rows = ds(at * ROWS, ROWS)
            after = x1_ref[rows, :]
            dout = cot_ref[rows, :].astype(F32) * live
            branch_rows = branch[rows, :]
            block_ref[rows, :] = ((after + gate_two * branch_rows) * live).astype(BF16)
            unit, inv = normed(after)
            dh2_rows = dh2[rows, :]
            dx1 = dout + norm_back(unit, inv, dh2_rows * (1.0 + scale_two))
            dx1_ref[rows, :] = dx1
            datt_ref[rows, :] = (dx1 * gate_one).astype(BF16)
            found = (dx1 * att_ref[rows, :].astype(F32), dh2_rows, dh2_rows * unit, dout * branch_rows)
            return tuple(total + fold(one) for total, one in zip(sums, found))

        start = tuple(jnp.zeros((8, width), F32) for _ in range(4))
        totals = lax.fori_loop(0, rows_all // ROWS, rows_step, start)
        for at in range(4):
            dmod_ref[at : at + 1, :] = jnp.sum(totals[at], axis=0, keepdims=True)
        for at in (steps - 2, steps - 1):
            to_near(at).wait_send()
        for at in range(steps // 2):
            to_far(at).wait_send()
        for at in range(pieces):
            sums[at].finish_half(schedule[at] - 1)
            for level in range(schedule[at]):
                sums[at].half_copy(level).wait_send()


def ffn(n_wide, live, h2, h2t, db, x1, cot, att, mod, wup, wdown, taps):
    rows, width = h2.shape
    shards, _, local = taps.shape
    per = local // CHUNK
    steps = shards * per // 2
    parcel = (2 * width + 16, CHUNK)
    shape = jax.ShapeDtypeStruct
    keep = lambda *block: pl.BlockSpec(
        block, lambda c: (0,) * len(block), pipeline_mode=pl.Buffered(1)
    )

    def slot_and_part(step, odd):
        return jnp.where(step < per, 3, 1) - odd, step % per

    def up_block(move, odd):
        def index(step):
            return slot_and_part(jnp.clip(step + move, 0, steps - 1), odd)

        return pl.BlockSpec((width, CHUNK), index)

    def down_block(odd):
        def index(step):
            slot, part = slot_and_part(step, odd)
            return slot * per + part, 0

        return pl.BlockSpec((CHUNK, width), index)

    def taps_block(odd):
        def index(step):
            slot, part = slot_and_part(step, odd)
            return slot, 0, part

        return pl.BlockSpec((1, taps.shape[1], CHUNK), index)

    return pl.pallas_call(
        partial(ffn_kernel, n_wide),
        grid=(steps,),
        out_shape=(
            shape((rows, width), BF16),
            shape((rows, width), F32),
            shape((rows, width), BF16),
            shape((4, width), F32),
            shape((per,) + parcel, BF16),
        ),
        in_specs=[
            whole(pltpu.SMEM),
            keep(rows, width),
            keep(width, rows),
            keep(rows, width),
            whole(pl.ANY),
            whole(pl.ANY),
            whole(pl.ANY),
            keep(6, width),
            up_block(-1, 1),
            up_block(0, 0),
            up_block(0, 1),
            up_block(1, 0),
            down_block(0),
            down_block(1),
            taps_block(0),
            taps_block(1),
        ],
        out_specs=(
            keep(rows, width),
            keep(rows, width),
            keep(rows, width),
            keep(4, width),
            keep(per, *parcel),
        ),
        scratch_shapes=[pltpu.VMEM((4, PAD, CHUNK), F32)] * 5
        + [
            pltpu.VMEM((rows, CHUNK), F32),
            pltpu.VMEM((rows, CHUNK), BF16),
            pltpu.VMEM((CHUNK, rows), BF16),
            pltpu.VMEM((rows, CHUNK), BF16),
            pltpu.VMEM((rows, width), F32),
            pltpu.VMEM((16, CHUNK), F32),
            pltpu.VMEM((3,) + parcel, BF16),
            pltpu.VMEM((per,) + parcel, BF16),
            pltpu.VMEM((steps,) + parcel, BF16),
            pltpu.VMEM((per,) + parcel, BF16),
            pltpu.VMEM((per, sum_landing(2 * width, n_wide), CHUNK), BF16),
            pltpu.VMEM((rows, width), F32),
            pltpu.VMEM((rows, width), BF16),
            pltpu.VMEM((rows, width), BF16),
            pltpu.SemaphoreType.DMA((2, steps + per)),
            pltpu.SemaphoreType.DMA((2, per * HALVINGS)),
            pltpu.SemaphoreType.DMA((3,)),
        ],
        compiler_params=pltpu.CompilerParams(
            vmem_limit_bytes=62 * MIB, collective_id=1, has_side_effects=True
        ),
        name="feed_forward",
    )(live, h2, h2t, db, x1, cot, att, mod, wup, wup, wup, wup, wdown, wdown, taps, taps)


def attn_backward_kernel(
    n_wide, datt_ref, ctx_ref, u_ref, wout_ref, parcels, silu_ref, dmod_ref, qkv_hbm, probs_hbm,
    dqkv_ref, own_ref, full, gtaps_ref, small,
    dctx, probs_buf, weights, got_near, chip_sum, got_far, work, got_sums, taps_sum, taps_got,
    sems, in_sems, sum_sems, small_sems,
):
    rows_all, width = u_ref.shape
    wide, here = lax.axis_index("wide"), lax.axis_index("narrow")
    pairs = width // LANES
    half_pairs = pairs // 2
    steps = 4 * pairs
    slots = weights.shape[0]
    load_qkv = pltpu.make_async_copy(qkv_hbm, dqkv_ref, in_sems.at[2])
    load_qkv.start()

    def pair_of(step):
        return (half_pairs + step // 4) % pairs

    def load_probs(step):
        return pltpu.make_async_copy(
            probs_hbm.at[(step % 4) * pairs + pair_of(step)], probs_buf.at[step % 2], in_sems.at[step % 2]
        )

    load_probs(0).start()
    greet([(wide, here ^ 2), (wide, here ^ 1)] + wide_partners(wide, here, n_wide))
    pieces = full.shape[0]
    rows = full.shape[1]
    per_sum = sum_semaphores(n_wide)
    ahead = halvings_ahead(pieces, min(HALVINGS, n_wide.bit_length() - 1))
    sums = [
        WideSum(parcels.at[at, :rows], work.at[at], full.at[at], got_sums.at[at], sum_sems, at * per_sum,
                wide, here, n_wide, done=ahead[at])
        for at in range(pieces)
    ]
    levels = n_wide.bit_length() - 1
    queues = [one.actions() for one in sums]

    def advance(*which):
        for at in which:
            if queues[at]:
                for act in queues[at].pop(0):
                    act()

    def taps_copy(level):
        return remote(taps_sum.at[level], taps_got.at[level], sems, 6 + level, wide ^ (1 << level), here)

    def taps_add(level):
        taps_copy(level).wait_recv()
        taps_sum[level + 1] = taps_sum[level] + taps_got[level]
        if level + 1 < levels:
            taps_copy(level + 1).start()

    for at in range(pieces):
        taps_sum[0, :, at * CHUNK : (at + 1) * CHUNK] = parcels[at, rows:, :].astype(F32)
    partners = wide_partners(wide, here, n_wide) + [(wide, here ^ 1), (wide, here ^ 2)]

    def small_copy(level):
        have = 1 << level
        return remote(small.at[:have], small.at[have : 2 * have], small_sems, level, *partners[level])

    def small_step(level):
        small_copy(level).wait_recv()
        if level + 1 < len(partners):
            small_copy(level + 1).start()

    early = [silu_ref[0:1, :].astype(F32)] + [dmod_ref[at : at + 1, :] for at in range(4)]
    small[0] = lane_rows(early, EARLY)
    small_copy(0).start()
    taps_copy(0).start()
    advance(2, 0, 1)

    def ctx_step(step, carry):
        span = ds(step * PHASE, PHASE)
        dctx[span, :] = mm(datt_ref[span, :], wout_ref[...], NT).astype(BF16)
        return carry

    lax.fori_loop(0, 4, ctx_step, 0)
    load_qkv.wait()

    first = lax.broadcasted_iota(jnp.int32, (PHASE, LANES), 1) < HEAD_DIM
    zero = jnp.zeros((PHASE, LANES), BF16)
    scale = HEAD_DIM**-0.5

    def attend(step):
        group, pair = step % 4, pair_of(step)
        load_probs(step).wait()

        @pl.when(step + 1 < steps)
        def _():
            load_probs(step + 1).start()

        span = ds(group * PHASE, PHASE)
        query = dqkv_ref[span, ds(pair * LANES, LANES)]
        key = dqkv_ref[span, ds(width + pair * LANES, LANES)]
        value = dqkv_ref[span, ds(2 * width + pair * LANES, LANES)]
        dctx_pair = dctx[span, ds(pair * LANES, LANES)]
        dq, dk, dv = [], None, None
        for head in range(2):
            own = lambda both: jnp.where(first, both, zero) if head == 0 else jnp.where(first, zero, both)
            probs = probs_buf[step % 2, :, head * PHASE : (head + 1) * PHASE]
            probs_f = probs.astype(F32)
            dctx_own, query_own = own(dctx_pair), own(query)
            dprobs = mm(value, dctx_own, NT)
            inner = jnp.sum(dprobs * probs_f, axis=0, keepdims=True)
            dscores = (probs_f * (dprobs - inner)).astype(BF16)
            dv_one = mm(probs, dctx_own, NN)
            dk_one = mm(dscores, query_own, NN)
            dv = dv_one if dv is None else dv + dv_one
            dk = dk_one if dk is None else dk + dk_one
            dq.append(mm(dscores, key, TN))
        dqkv_ref[span, ds(pair * LANES, LANES)] = (
            jnp.where(first, dq[0], dq[1]) * scale
        ).astype(BF16)
        dqkv_ref[span, ds(width + pair * LANES, LANES)] = (dk * scale).astype(BF16)
        dqkv_ref[span, ds(2 * width + pair * LANES, LANES)] = dv.astype(BF16)

    def attend_loop(begin, end, plan):
        def body(step, carry):
            for at, what in plan:
                pl.when(step == at)(what)
            attend(step)
            return carry

        lax.fori_loop(begin, end, body, 0)

    slab = width // slots

    def weight_grads(half):
        span = width // 2
        for part in range(3):
            left = dqkv_ref[:, part * width + half * span : part * width + (half + 1) * span]
            found = mm(left, u_ref[...], TN).astype(BF16)
            for one in range(2):
                weights[2 * half + one, part * slab : (part + 1) * slab, :] = found[
                    one * slab : (one + 1) * slab
                ]

    head, tail = slice(3 * slab), slice(3 * slab, 4 * slab)

    def near_copy(early, rows, at):
        return remote(
            weights.at[3 if early else 1, rows], got_near.at[0 if early else 1, rows], sems, at, wide, here ^ 1
        )

    def far_copy(rows, at):
        return remote(chip_sum.at[rows], got_far.at[rows], sems, at, wide, here ^ 2)

    def add_chip(rows):
        chip_sum[rows, :] = (weights[2, rows, :].astype(F32) + got_near[0, rows, :].astype(F32)).astype(BF16)

    near_out, near_early = near_copy(True, tail, 0), near_copy(True, head, 1)
    late_out, near_late = near_copy(False, tail, 2), near_copy(False, head, 3)
    far_out, far = far_copy(tail, 4), far_copy(head, 5)

    for part in range(width // PHASE):
        cols = slice(part * PHASE, (part + 1) * PHASE)
        found = mm(ctx_ref[:, cols], datt_ref[...], TN).astype(BF16)
        for slot in range(slots):
            low, high = max(part * PHASE, slot * slab), min((part + 1) * PHASE, (slot + 1) * slab)
            if low < high:
                weights[slot, 3 * slab + low - slot * slab : 3 * slab + high - slot * slab, :] = found[
                    low - part * PHASE : high - part * PHASE
                ]
    near_out.start()
    late_out.start()

    def send_out():
        near_out.wait_recv()
        add_chip(tail)
        far_out.start()

    later = lambda *which: partial(advance, *which)
    hops = len(partners) - 1
    small_plan = [(4 + 18 * level // hops, partial(small_step, level)) for level in range(hops)]
    attend_loop(
        0, steps // 2,
        [one for one in small_plan if one[0] < steps // 2]
        + [(1, send_out), (2, later(2, 0)), (5, later(1)), (7, partial(taps_add, 0)), (8, later(2, 0)), (11, later(1))],
    )
    weight_grads(1)
    near_early.start()
    advance(2)
    near_early.wait_recv()
    add_chip(head)
    far.start()
    attend_loop(
        steps // 2, steps,
        [one for one in small_plan if one[0] >= steps // 2]
        + [(13, later(1, 0)), (14, partial(taps_add, 1)), (16, later(2))],
    )
    weight_grads(0)
    near_late.start()
    small_step(len(partners) - 1)
    for level in range(2, levels):
        taps_add(level)
    gtaps_ref[...] = taps_sum[levels]
    near_late.wait_recv()
    late_out.wait_recv()
    while any(queues):
        advance(0, 1, 2)
    far_out.wait_recv()
    far.wait_recv()
    own_ref[...] = (
        weights[0].astype(F32) + got_near[1].astype(F32) + got_far[...].astype(F32)
    ).astype(BF16)
    for one in sums:
        one.wait_sends()
    for level in range(levels):
        taps_copy(level).wait_send()
    for copy in (near_out, near_early, late_out, near_late, far_out, far):
        copy.wait_send()
    for level in range(len(partners)):
        small_copy(level).wait_send()


def attn_backward(n_wide, datt, ctx, u, wout, parcels, silu_row, dmod, qkv, probs):
    rows, width = u.shape
    slots = lax.axis_size("narrow")
    slab = wout.shape[0] // slots
    pieces, parcel_rows, _ = parcels.shape
    sum_rows = parcel_rows - 16
    shape = jax.ShapeDtypeStruct
    levels = n_wide.bit_length() - 1
    per_sum = sum_semaphores(n_wide)
    return pl.pallas_call(
        partial(attn_backward_kernel, n_wide),
        out_shape=(
            shape((rows, 3 * width), BF16),
            shape((4 * slab, width), BF16),
            shape((pieces, sum_rows, CHUNK), BF16),
            shape((16, pieces * CHUNK), F32),
            shape((n_wide * slots, EARLY, LANES), BF16),
        ),
        in_specs=[whole()] * 7 + [whole(pl.ANY)] * 2,
        out_specs=(whole(),) * 5,
        scratch_shapes=[
            pltpu.VMEM((rows, width), BF16),
            pltpu.VMEM((2, PHASE, 2 * PHASE), BF16),
            pltpu.VMEM((slots, 4 * slab, width), BF16),
            pltpu.VMEM((2, 4 * slab, width), BF16),
            pltpu.VMEM((4 * slab, width), BF16),
            pltpu.VMEM((4 * slab, width), BF16),
            pltpu.VMEM((pieces, sum_rows, CHUNK), BF16),
            pltpu.VMEM((pieces, sum_landing(sum_rows, n_wide), CHUNK), BF16),
            pltpu.VMEM((levels + 1, 16, pieces * CHUNK), F32),
            pltpu.VMEM((levels, 16, pieces * CHUNK), F32),
            pltpu.SemaphoreType.DMA((2, 6 + levels)),
            pltpu.SemaphoreType.DMA((3,)),
            pltpu.SemaphoreType.DMA((2, pieces * per_sum)),
            pltpu.SemaphoreType.DMA((2, levels + 2)),
        ],
        compiler_params=pltpu.CompilerParams(
            vmem_limit_bytes=56 * MIB, collective_id=2, has_side_effects=True
        ),
        name="attn_backward",
    )(datt, ctx, u, wout, parcels, silu_row, dmod, qkv, probs)


def one_hot(rows, columns, wanted):
    row = lax.broadcasted_iota(jnp.int32, (rows, columns), 0)
    column = lax.broadcasted_iota(jnp.int32, (rows, columns), 1)
    return jnp.where(column == wanted(row), 1.0, 0.0).astype(BF16)


def input_backward_kernel(
    n_wide, x_ref, mod_ref, taps_ref, own_ref, dx1_hbm, dqkv_hbm, wqkv_hbm, block_in,
    got_dx, got_block, full, late, dtaps_ref,
    base, shifted, first_in, dh1, dx1_ref, dqkv_ref, wqkv_ref, dx, work, got_sums, tap_parts, tap_sums, tap_got,
    sems, local_sems, sum_sems, taps_sems, late_sems,
):
    rows_all, width = x_ref.shape
    wide, here = lax.axis_index("wide"), lax.axis_index("narrow")
    loads = [
        pltpu.make_async_copy(src, dst, local_sems.at[2 + at])
        for at, (src, dst) in enumerate(
            ((dqkv_hbm, dqkv_ref), (wqkv_hbm, wqkv_ref), (dx1_hbm, dx1_ref))
        )
    ]
    for load in loads:
        load.start()
    shift_one, scale_one = mod_ref[0:1, :], mod_ref[1:2, :]
    greet([(wide, peer) for peer in narrow_peers(here)] + [(wide ^ away, here) for away in range(1, n_wide)])
    pieces = full.shape[0]
    rows = full.shape[1]
    per_sum = sum_semaphores(n_wide)
    sums = [
        WideSum(own_ref.at[at * rows : (at + 1) * rows], work.at[at], full.at[at], got_sums.at[at], sum_sems,
                at * per_sum, wide, here, n_wide, order=((0, 1, 2), (1, 2, 0))[at])
        for at in range(pieces)
    ]
    queues = [one.actions() for one in sums]

    def advance(*which):
        for at in which:
            if queues[at]:
                for act in queues[at].pop(0):
                    act()

    levels = n_wide.bit_length() - 1
    late_wide = [
        remote(late.at[0], late.at[away], late_sems, away - 1, wide ^ away, here) for away in range(1, n_wide)
    ]
    late_narrow = [
        remote(late.at[:n_wide], late.at[away * n_wide : (away + 1) * n_wide], late_sems, n_wide - 2 + away,
               wide, here ^ away)
        for away in (2, 3, 1)
    ]
    taps_narrow = [
        remote(tap_sums.at[levels], tap_got.at[levels + away - 1], taps_sems, levels + away - 1, wide, here ^ away)
        for away in (2, 3, 1)
    ]
    advance(0, 1)
    block_back = Return(block_in, got_block, sems, local_sems.at[1], 3, wide, here)
    block_back.start()
    clear_edges(base)
    clear_edges(shifted)

    def norm_step(step, carry):
        group, part = step // (PHASE // ROWS), step % (PHASE // ROWS)
        unit, _ = normed(x_ref[ds(step * ROWS, ROWS), :].astype(F32))
        h_one = (unit * (1.0 + scale_one) + shift_one).astype(BF16)
        first_in[group, ds(HALF + part * ROWS, ROWS, HALF), :] = h_one.astype(F32)
        return carry

    lax.fori_loop(0, rows_all // ROWS, norm_step, 0)

    def du_step(group, carry):
        span = ds(group * PHASE, PHASE)
        total = None
        for part in range(3):
            cols = slice(part * width, (part + 1) * width)
            one = mm(dqkv_ref[span, cols], wqkv_ref[:, cols], NN)
            total = one if total is None else total + one
        base[group, HALF : HALF + PHASE, :] = total
        return carry

    loads[0].wait()
    loads[1].wait()
    lax.fori_loop(0, 2, du_step, 0)
    advance(0, 1)
    lax.fori_loop(2, 4, du_step, 0)

    blocks = width // LANES

    def shift_step(block, carry):
        shift_cols(base, shifted, ds(block * LANES, LANES))
        return carry

    lax.fori_loop(0, blocks, shift_step, 0)
    tap_parts[...] = jnp.zeros_like(tap_parts)
    advance(0, 1)

    def taps_copy(level):
        return remote(tap_sums.at[level], tap_got.at[level], taps_sems, level, wide ^ (1 << level), here)

    def taps_step(level):
        taps_copy(level).wait_recv()
        tap_sums[level + 1] = tap_sums[level] + tap_got[level]
        if level + 1 < levels:
            taps_copy(level + 1).start()
        else:
            for copy in taps_narrow:
                copy.start()

    def fold(value):
        return value.reshape(ROWS // 8, 8, width).sum(axis=0)

    back = Return(dx, got_dx, sems, local_sems.at[0], 0, wide, here)
    found = tuple(jnp.zeros((8, width), F32) for _ in range(2))
    for at, away in enumerate((2, 3, 1, 0)):
        source = away ^ here

        def conv_step(block, carry, source=source):
            lanes = ds(block * LANES, LANES)
            taps = [taps_ref[t // 3, t % 3 : t % 3 + 1, lanes].astype(F32) for t in range(9)]
            sums = [jnp.zeros((8, LANES), F32) for _ in range(9)]
            for group in range(4):
                total = jnp.zeros((ROWS, LANES), F32)
                own = first_in[group, ds(HALF + source * ROWS, ROWS, HALF), lanes]
                for tap in range(9):
                    moved = tap_value(
                        base, shifted, group, 2 - tap // 3, 2 - tap % 3, source * ROWS, lanes
                    )
                    total += taps[tap] * moved
                    sums[tap] += (own * moved).reshape(ROWS // 8, 8, LANES).sum(axis=0)
                dh1[ds(group * PHASE + source * ROWS, ROWS), lanes] = total
            for tap in range(9):
                tap_parts[tap, :, lanes] += sums[tap]
            return carry

        def rows_step(group, sums, source=source):
            span = ds(group * PHASE + source * ROWS, ROWS)
            unit, inv = normed(x_ref[span, :].astype(F32))
            grad = dh1[span, :]
            dx[group, source] = (
                dx1_ref[span, :] + norm_back(unit, inv, grad * (1.0 + scale_one))
            ).astype(BF16)
            return tuple(total + fold(one) for total, one in zip(sums, (grad, grad * unit)))

        lax.fori_loop(0, blocks, conv_step, 0)
        if at == 0:
            loads[2].wait()
        if at == 3:
            for tap in range(9):
                tap_sums[0, tap : tap + 1, :] = jnp.sum(tap_parts[tap], axis=0, keepdims=True)
            tap_sums[0, 9:, :] = jnp.zeros((7, width), F32)
            taps_copy(0).start()
        advance(*((0, 1), (0, 1), (0,), (1,))[at])
        found = lax.fori_loop(0, 4, rows_step, found)
        if at < 3:
            back.copies[at].start()
    back.own.start()
    late[0] = lane_rows([jnp.sum(one, axis=0, keepdims=True) for one in found], SMALL)
    for copy in late_wide:
        copy.start()
    taps_step(0)
    for copy in late_wide:
        copy.wait_recv()
    for copy in late_narrow:
        copy.start()
    for level in range(1, levels):
        taps_step(level)
        advance(level % 2)
    for copy in late_narrow:
        copy.wait_recv()
    total = tap_sums[levels]
    for at, copy in enumerate(taps_narrow):
        copy.wait_recv()
        total += tap_got[levels + (1, 2, 0)[at]]
    dtaps_ref[...] = total
    while any(queues):
        advance(0, 1)
    block_back.wait()
    back.wait()
    for copy in late_wide + late_narrow + taps_narrow:
        copy.wait_send()
    for level in range(levels):
        taps_copy(level).wait_send()
    for one in sums:
        one.wait_sends()


def input_backward(n_wide, x, dx1, dqkv, mod, taps, wqkv, own, block):
    rows, width = x.shape
    slots = lax.axis_size("narrow")
    pieces = 2
    sum_rows = own.shape[0] // pieces
    shape = jax.ShapeDtypeStruct
    per_sum = sum_semaphores(n_wide)
    levels = n_wide.bit_length() - 1
    back = shape((slots, 4, rows // (4 * slots), width), BF16)
    return pl.pallas_call(
        partial(input_backward_kernel, n_wide),
        out_shape=(
            back,
            back,
            shape((pieces, sum_rows, width), BF16),
            shape((n_wide * slots, SMALL, LANES), BF16),
            shape((SMALL, width), F32),
        ),
        in_specs=[whole()] * 4 + [whole(pl.ANY)] * 4,
        out_specs=(whole(),) * 5,
        scratch_shapes=[pltpu.VMEM((4, PAD, width), F32)] * 3
        + [
            pltpu.VMEM((rows, width), F32),
            pltpu.VMEM((rows, width), F32),
            pltpu.VMEM((rows, 3 * width), BF16),
            pltpu.VMEM(wqkv.shape, BF16),
            pltpu.VMEM((4, slots, rows // (4 * slots), width), BF16),
            pltpu.VMEM((pieces, sum_rows, width), BF16),
            pltpu.VMEM((pieces, sum_landing(sum_rows, n_wide), width), BF16),
            pltpu.VMEM((9, 8, width), F32),
            pltpu.VMEM((levels + 1, SMALL, width), F32),
            pltpu.VMEM((levels + 3, SMALL, width), F32),
            pltpu.SemaphoreType.DMA((2, 6)),
            pltpu.SemaphoreType.DMA((5,)),
            pltpu.SemaphoreType.DMA((2, pieces * per_sum)),
            pltpu.SemaphoreType.DMA((2, levels + 3)),
            pltpu.SemaphoreType.DMA((2, n_wide + 2)),
        ],
        compiler_params=pltpu.CompilerParams(
            vmem_limit_bytes=56 * MIB, collective_id=3, has_side_effects=True
        ),
        name="input_backward",
    )(x, mod, taps, own, dx1, dqkv, wqkv, block)


def outputs_kernel(
    dx_in, block_in, attn_sum, ffn_sum, small, late, cond_ref, kattn_in, kffn_in, ada_hbm,
    gada_hbm, dx_hbm, block_hbm, gqkv_hbm, gout_hbm, gup_hbm, gdown_hbm, gcond_ref, kattn_ref, kffn_ref,
    ada, gada, dx, block, gqkv, gout, gup, gdown, early_rows, late_rows, sems, in_sem,
):
    width = gout.shape[-1]
    here = lax.axis_index("narrow")
    load_ada = pltpu.make_async_copy(ada_hbm, ada, in_sem.at[0])
    load_ada.start()
    started = []
    for row in range(3):
        kattn_ref[row] = kattn_in[3 * row : 3 * row + 3, :]
        kffn_ref[row] = kffn_in[3 * row : 3 * row + 3, :]

    def put(src, dst):
        copy = pltpu.make_async_copy(src, dst, sems.at[len(started)])
        copy.start()
        started.append(copy)

    devices = small.shape[0]
    blocks = width // LANES
    early_rows[...] = small[...].astype(F32).reshape(devices * EARLY, LANES)
    late_rows[...] = late[...].astype(F32).reshape(devices * SMALL, LANES)

    def pick(ref, share, number):
        cut = [ref[pl.ds(number * blocks + at, devices, share), :] for at in range(blocks)]
        return jnp.concatenate(cut, axis=1).astype(BF16)

    silu_all = pick(early_rows, EARLY, 0)
    dmods = [
        pick(late_rows, SMALL, part) if part < 2 else pick(early_rows, EARLY, part - 1) for part in range(6)
    ]
    for part in range(6):
        gada[part] = mm(silu_all, dmods[part], TN)
        put(gada.at[part], gada_hbm.at[:, part * width : (part + 1) * width])
    slab = attn_sum.shape[1] // 2
    for part in range(3):
        gqkv[part] = attn_sum[part // 2, (part % 2) * slab : (part % 2 + 1) * slab, :].astype(F32).T
        put(gqkv.at[part], gqkv_hbm.at[part])
    gout[...] = attn_sum[1, slab:, :].astype(F32)
    put(gout, gout_hbm)
    permutation = group_permutation(dx_in.shape[1] * dx_in.shape[2])
    for at in range(dx_in.shape[0]):
        for source, held, out in ((dx_in, dx, dx_hbm), (block_in, block, block_hbm)):
            groups = jnp.concatenate([source[at, group] for group in range(4)], axis=0)
            held[at] = mm(permutation, groups, TN).astype(held.dtype)
            put(held.at[at], out.at[at])
    for at in range(ffn_sum.shape[0]):
        cols = slice(at * CHUNK, (at + 1) * CHUNK)
        gup[:, cols] = ffn_sum[at, :width, :].astype(F32)
        for part in range(width // CHUNK):
            span = slice(width + part * CHUNK, width + (part + 1) * CHUNK)
            gdown[cols, part * CHUNK : (part + 1) * CHUNK] = ffn_sum[at, span, :].astype(F32)
        put(gdown.at[cols], gdown_hbm.at[cols])
    put(gup, gup_hbm)

    def own_place(row):
        away = row ^ here
        return jnp.where(row < cond_ref.shape[0], away * (devices // 4), -1)

    load_ada.wait()
    choose = one_hot(16, devices, own_place)
    grad_silu = jnp.zeros((16, width), F32)
    for part in range(6):
        own = mm(choose, dmods[part], NN).astype(BF16)
        grad_silu += mm(own, ada[:, part * width : (part + 1) * width], NT)
    cond = cond_ref[...].astype(F32)
    gate = 1.0 / (1.0 + jnp.exp(-cond))
    gcond_ref[...] = grad_silu[: cond_ref.shape[0]] * (gate * (1.0 + cond * (1.0 - gate)))
    for copy in started:
        copy.wait()


def outputs(dx, block, attn_sum, ffn_sum, small, late, cond, kattn, kffn, w_ada):
    slots, _, quarter, width = dx.shape
    slab = attn_sum.shape[1] // 2
    pieces = ffn_sum.shape[0]
    local = pieces * CHUNK
    shape = jax.ShapeDtypeStruct
    tokens = (slots, 4 * quarter, width)
    return pl.pallas_call(
        outputs_kernel,
        out_shape=(
            shape(w_ada.shape, F32),
            shape(tokens, F32),
            shape(tokens, BF16),
            shape((3, width, slab), F32),
            shape((slab, width), F32),
            shape((width, local), F32),
            shape((local, width), F32),
            shape(cond.shape, F32),
            shape((3, 3, width), F32),
            shape((3, 3, local), F32),
        ),
        in_specs=[whole()] * 9 + [whole(pl.ANY)],
        out_specs=(whole(pl.ANY),) * 7 + (whole(),) * 3,
        scratch_shapes=[
            pltpu.VMEM(w_ada.shape, BF16),
            pltpu.VMEM((6, width, width), F32),
            pltpu.VMEM(tokens, F32),
            pltpu.VMEM(tokens, BF16),
            pltpu.VMEM((3, width, slab), F32),
            pltpu.VMEM((slab, width), F32),
            pltpu.VMEM((width, local), F32),
            pltpu.VMEM((local, width), F32),
            pltpu.VMEM((small.shape[0] * EARLY, LANES), F32),
            pltpu.VMEM((small.shape[0] * SMALL, LANES), F32),
            pltpu.SemaphoreType.DMA((6 + 3 + 1 + 2 * slots + pieces + 1,)),
            pltpu.SemaphoreType.DMA((1,)),
        ],
        compiler_params=pltpu.CompilerParams(vmem_limit_bytes=56 * MIB),
        name="outputs",
    )(dx, block, attn_sum, ffn_sum, small, late, cond, kattn, kffn, w_ada)


def per_device(
    tokens, condition, cotangent, counts, w_ada, k_attn, w_qkv, w_out, w_up, k_ffn, w_down
):
    lat_dev, shard_rows, width = tokens.shape
    here = lax.axis_index("narrow")
    rows_all = shard_rows * lat_dev
    local = w_up.shape[1]

    n_wide = lax.axis_size("wide")
    qkv_t = w_qkv.transpose(2, 1, 0).reshape(w_qkv.shape[2], 3 * width)
    ktaps_own = jnp.pad(k_ffn.reshape(9, local), ((0, 7), (0, 0)))

    cond_f = condition.astype(F32)
    silu_low = jax.nn.silu(cond_f).astype(BF16)
    own_silu = jnp.broadcast_to(lax.dynamic_slice_in_dim(silu_low, here, 1, 0), (16, width))
    live = (here < counts[0]).astype(F32).reshape(1, 1)

    (x, cot, u, qkv, probs, ctx, wqkv, wout, mod, att, x1, h2, h2t, db, wup, wdown, ktaps) = front(
        live, own_silu, k_attn, tokens, cotangent, w_ada, qkv_t, w_out, w_up, w_down, ktaps_own
    )
    cot = cot.reshape(rows_all, width)
    block_g, dx1, datt, dmod_mid, parcels = ffn(
        n_wide, live, h2, h2t, db, x1, cot, att, mod, wup, wdown, ktaps
    )
    block_g = block_g.reshape(4, lat_dev, shard_rows // 4, width)
    dqkv, own, ffn_sum, gtaps, small = attn_backward(
        n_wide, datt, ctx, u, wout, parcels, own_silu, dmod_mid, qkv, probs
    )
    got_dx, got_block, attn_sum, late, dattn_taps = input_backward(
        n_wide, x, dx1, dqkv, mod, k_attn, wqkv, own, block_g
    )
    (
        grad_w_ada, grad_tokens, block, gqkv, grad_w_out, grad_w_up, grad_w_down, grad_condition,
        grad_k_attn, grad_k_ffn,
    ) = outputs(
        got_dx, got_block, attn_sum, ffn_sum, small, late, condition, dattn_taps, gtaps, w_ada
    )
    grad_w_qkv = gqkv.transpose(1, 0, 2)
    return (
        block,
        grad_tokens,
        grad_condition,
        grad_w_ada,
        grad_k_attn,
        grad_w_qkv,
        grad_w_out,
        grad_w_up,
        grad_k_ffn,
        grad_w_down,
    )


def solution(mesh):
    placed = (
        P("wide", "narrow", None),
        P("wide", None),
        P("wide", "narrow", None),
        P("wide"),
        P(),
        P(),
        P(None, None, "narrow"),
        P("narrow", None),
        P(None, "narrow"),
        P(None, None, "narrow"),
        P("narrow", None),
    )
    return jax.shard_map(
        per_device,
        mesh=mesh,
        in_specs=placed,
        out_specs=(
            P("wide", "narrow", None),
            P("wide", "narrow", None),
            P("wide", None),
            P(),
            P(),
            P(None, None, "narrow"),
            P("narrow", None),
            P(None, "narrow"),
            P(None, None, "narrow"),
            P("narrow", None),
        ),
        check_vma=False,
    )
```

```python
from functools import partial

import jax
import jax.numpy as jnp
from jax import lax
from jax.experimental import pallas as pl
from jax.experimental.pallas import tpu as pltpu
from jax.sharding import PartitionSpec as P

HEAD_DIM = 64
SIDE = 32
HALF = SIDE // 2
PHASE = HALF * HALF
PAD = PHASE + 2 * HALF
LANES = 128
ROWS = 64
CHUNK = 256
LOG2E = 1.4426950408889634
GELU_C = 0.7978845608028654
GELU_A = 0.044715
MIB = 1 << 20
F32 = jnp.float32
BF16 = jnp.bfloat16

NN = (((1,), (0,)), ((), ()))
NT = (((1,), (1,)), ((), ()))
TN = (((0,), (0,)), ((), ()))


def mm(left, right, dims):
    return lax.dot_general(left, right, dims, preferred_element_type=F32)


def ds(start, size, unit=None):
    return pl.ds(pl.multiple_of(start, unit or size), size)


def tap_source(parity, tap):
    return {-1: (1, -1), 0: (0, 0), 1: (1, 0), 2: (0, 1)}[parity + tap - 1]


def shift_cols(base, shifted, lanes):
    col = lax.broadcasted_iota(jnp.int32, (ROWS, LANES), 0) % HALF

    def rows_step(step, carry):
        for group in range(4):
            rows = ds(HALF + step * ROWS, ROWS, HALF)
            value = base[group, rows, lanes]
            if group % 2:
                moved = jnp.where(col == 0, 0.0, pltpu.roll(value, 1, 0))
            else:
                moved = jnp.where(col == HALF - 1, 0.0, pltpu.roll(value, ROWS - 1, 0))
            shifted[group, rows, lanes] = moved
        return carry

    lax.fori_loop(0, PHASE // ROWS, rows_step, 0)


def clear_edges(ref):
    edge = jnp.zeros((HALF, ref.shape[-1]), ref.dtype)
    for group in range(4):
        ref[group, :HALF, :] = edge
        ref[group, PAD - HALF :, :] = edge


def tap_value(base, shifted, group, tap_row, tap_col, start, lanes):
    src_row, row_move = tap_source(group // 2, tap_row)
    src_col, col_move = tap_source(group % 2, tap_col)
    ref = base if col_move == 0 else shifted
    return ref[2 * src_row + src_col, ds(HALF + row_move * HALF + start, ROWS, HALF), lanes]


def normed(values_in):
    mean_val = jnp.mean(values_in, axis=-1, keepdims=True)
    centred = values_in - mean_val
    inv = lax.rsqrt(jnp.mean(centred * centred, axis=-1, keepdims=True) + 1e-06)
    return centred * inv, inv


def norm_back(unit, inv, grad):
    mean_grad = jnp.mean(grad, axis=-1, keepdims=True)
    mean_dot = jnp.mean(grad * unit, axis=-1, keepdims=True)
    return (grad - mean_grad - unit * mean_dot) * inv


def narrow_peers(here):
    return [here ^ 2, here ^ 3, here ^ 1]


def remote(src, dst, sems, at, wide, narrow):
    return pltpu.make_async_remote_copy(
        src_ref=src,
        dst_ref=dst,
        send_sem=sems.at[0, at],
        recv_sem=sems.at[1, at],
        device_id=(wide, narrow),
        device_id_type=pl.DeviceIdType.MESH,
    )


class Gather:
    COPIES = 11

    def __init__(self, src, dst, sems, local_sem, first, wide, here):
        count = src.shape[0]
        quarter = count // 4
        front = -(-quarter // 32) * 16
        mine = wide % 4
        far, near = here ^ 2, here ^ 1

        def slot(k):
            return dst.at[k * count : (k + 1) * count]

        def at(k, which, start=0, size=quarter):
            return dst.at[ds(k * count + which * quarter + start, size, 16)]

        def send(number, source, target, wide_to, narrow_to):
            return remote(source, target, sems, first + number, wide_to, narrow_to)

        def same(number, which, wide_to, start=0, size=quarter):
            return send(number, at(2, which, start, size), at(2, which, start, size), wide_to, here)

        def share(number, which, start=0, size=quarter):
            return send(number, at(2, which, start, size), at(3, which, start, size), wide, near)

        own_part = src.at[ds(mine * quarter, quarter, 16)]
        rest = quarter - front
        self.own = pltpu.make_async_copy(src, slot(0), local_sem)
        self.near = send(0, src, slot(1), wide, near)
        self.far = send(1, own_part, at(2, mine), wide, far)
        self.swaps = [same(2, mine, wide ^ 1), same(3, mine, wide ^ 2)]
        self.corners = [same(4, mine ^ 1, wide ^ 2, 0, front), same(5, mine ^ 2, wide ^ 1, front, rest)]
        self.shares = [
            share(6, mine),
            share(7, mine ^ 1),
            share(8, mine ^ 2),
            share(9, mine ^ 3, 0, front),
            share(10, mine ^ 3, front, rest),
        ]

    def start_near(self):
        self.own.start()
        self.near.start()

    def start_far(self):
        self.far.start()

    def swap(self):
        self.far.wait_recv()
        self.swaps[0].start()
        self.swaps[1].start()
        self.shares[0].start()

    def corner(self):
        for which in range(2):
            self.swaps[which].wait_recv()
            self.corners[which].start()
            self.shares[1 + which].start()

    def share_corner(self):
        for which in range(2):
            self.corners[which].wait_recv()
            self.shares[3 + which].start()

    def finish(self):
        self.own.wait()
        self.near.wait()
        self.far.wait_send()
        for copy in self.swaps + self.corners:
            copy.wait_send()
        for copy in self.shares:
            copy.wait()


def group_permutation(rows):
    out = lax.broadcasted_iota(jnp.int32, (rows, rows), 0)
    source = lax.broadcasted_iota(jnp.int32, (rows, rows), 1)
    per_group = rows // 4
    group, rest = out // per_group, out % per_group
    line = 2 * (rest // HALF) + group // 2
    wanted = line * SIDE + 2 * (rest % HALF) + group % 2
    return jnp.where(source == wanted, 1.0, 0.0).astype(BF16)


class Exchange:
    def __init__(self, sent, got, sems, local_sem, first, wide, here):
        self.own = pltpu.make_async_copy(sent.at[here], got.at[:, here], local_sem)
        self.copies = [
            remote(sent.at[peer], got.at[:, here], sems, first + at, wide, peer)
            for at, peer in enumerate(narrow_peers(here))
        ]

    def start(self):
        for copy in self.copies:
            copy.start()
        self.own.start()

    def wait(self):
        self.own.wait()
        for copy in self.copies:
            copy.wait()


class Return:
    def __init__(self, sent, got, sems, local_sem, first, wide, here):
        self.own = pltpu.make_async_copy(sent.at[:, here], got.at[here], local_sem)
        self.copies = [
            remote(sent.at[:, peer], got.at[here], sems, first + at, wide, peer)
            for at, peer in enumerate(narrow_peers(here))
        ]

    start = Exchange.start
    wait = Exchange.wait


HALVINGS = 3
EARLY = 32
SMALL = 16


class WideSum:
    def __init__(self, source, work, full, got, sems, first, wide, here, n_wide, done=0, order=None):
        self.source, self.work, self.full, self.got = source, work, full, got
        self.rows = work.shape[0]
        self.levels = min(HALVINGS, n_wide.bit_length() - 1)
        self.extra = n_wide.bit_length() - 1 - self.levels
        self.done = done
        self.wide, self.here, self.sems, self.first = wide, here, sems, first
        self.offsets = [0]
        self.masks = [1 << at for at in (order or range(HALVINGS)) if at < self.levels]
        for level in range(self.levels):
            bit = (wide // self.masks[level]) % 2
            self.offsets.append(self.offsets[-1] + bit * (self.rows >> (level + 1)))
        self.waiting = []

    def size(self, level):
        return self.rows >> level

    def at(self, ref, offset, size):
        return ref.at[ds(offset, size, 16)]

    def half_copy(self, level):
        size, base = self.size(level + 1), self.offsets[level]
        send = base + size - (self.offsets[level + 1] - base)
        source = self.source if level == self.done else self.work
        landing = self.rows - self.size(level)
        return remote(
            self.at(source, send, size), self.got.at[landing : landing + size],
            self.sems, self.first + level, self.wide ^ self.masks[level], self.here,
        )

    def start_half(self, level):
        self.half_copy(level).start()

    def finish_half(self, level):
        self.half_copy(level).wait_recv()
        size, landing = self.size(level + 1), self.rows - self.size(level)
        rows = ds(self.offsets[level + 1], size, 16)
        source = self.source if level == self.done else self.work
        self.work[rows, :] = (
            source[rows, :].astype(F32) + self.got[landing : landing + size, :].astype(F32)
        ).astype(BF16)

    def extras(self):
        size = self.size(self.levels)
        rows = ds(self.offsets[self.levels], size, 16)
        source = self.source if self.done == self.levels else self.work
        self.full[rows, :] = source[rows, :]
        for at in range(self.extra):
            landing = self.rows - size + at * size
            copy = remote(
                self.full.at[rows], self.got.at[landing : landing + size],
                self.sems, self.first + 2 * self.levels + at,
                self.wide ^ (1 << (self.levels + at)), self.here,
            )
            copy.start()
            copy.wait()
            self.full[rows, :] = (
                self.full[rows, :].astype(F32) + self.got[landing : landing + size, :].astype(F32)
            ).astype(BF16)

    def spread_copy(self, level):
        part = self.at(self.full, self.offsets[level + 1], self.size(level + 1))
        return remote(
            part, part, self.sems, self.first + self.levels + level, self.wide ^ self.masks[level], self.here
        )

    def actions(self):
        acts = []
        for level in range(self.done, self.levels):
            acts.append([partial(self.start_half, level)])
            if level > self.done:
                acts[-1].insert(0, partial(self.finish_half, level - 1))
        tail = [self.extras]
        if self.done < self.levels:
            tail.insert(0, partial(self.finish_half, self.levels - 1))
        for level in reversed(range(self.levels)):
            acts.append(tail + [lambda level=level: self.spread_copy(level).start()])
            tail = [lambda level=level: self.spread_copy(level).wait_recv()]
        acts.append(tail)
        return acts

    def wait_sends(self):
        for level in range(self.done, self.levels):
            self.half_copy(level).wait_send()
        for level in range(self.levels):
            self.spread_copy(level).wait_send()


def halvings_ahead(pieces, levels):
    return [min(levels, pieces - at) for at in range(pieces)]


def lane_rows(values_in, rows):
    cut = [
        one[:, at * LANES : (at + 1) * LANES] for one in values_in for at in range(one.shape[1] // LANES)
    ]
    return jnp.concatenate(cut + [jnp.zeros((rows - len(cut), LANES), F32)]).astype(BF16)


def greet(partners):
    barrier = pltpu.get_barrier_semaphore()
    for partner in partners:
        pl.semaphore_signal(
            barrier, inc=1, device_id=partner, device_id_type=pl.DeviceIdType.MESH
        )
    pl.semaphore_wait(barrier, len(partners))


def wide_partners(wide, here, n_wide):
    return [(wide ^ (1 << level), here) for level in range(n_wide.bit_length() - 1)]


def sum_semaphores(n_wide):
    levels = n_wide.bit_length() - 1
    return levels + min(levels, HALVINGS)


def sum_landing(rows, n_wide):
    levels = n_wide.bit_length() - 1
    last = rows >> min(levels, HALVINGS)
    return rows - last + max(levels - HALVINGS, 0) * last


def front_kernel(
    live_ref, silu_ref, taps_ref, tokens_hbm, cot_hbm, ada_hbm, wqkv_src, wout_src, wup_src, wdown_src, ktaps_src,
    x_hbm, cot_hbm_out, u_hbm, qkv_hbm, probs_hbm, ctx_hbm, wqkv_hbm, wout_hbm,
    mod_ref, att_ref, x1_ref, h2_ref, h2t_ref, db_ref, wup_ref, wdown_ref, ktaps_ref,
    x_ref, cot_ref, u_ref, qkv_ref, probs_ref, ctx_ref, wqkv_ref, wout_ref,
    base, shifted, shards, sent, sent_cot, got, ada, up_own, down_own, sems, local_sems, in_sems, out_sems,
):
    width = u_ref.shape[1]
    flushed = []

    def flush(src, dst):
        copy = pltpu.make_async_copy(src, dst, out_sems.at[len(flushed)])
        copy.start()
        flushed.append(copy)

    rows_all = u_ref.shape[0]
    latents, shard_rows = shards.shape[:2]
    wide, here = lax.axis_index("wide"), lax.axis_index("narrow")
    load_tokens = pltpu.make_async_copy(tokens_hbm, shards, in_sems.at[0])
    load_tokens.start()
    load_ada = pltpu.make_async_copy(ada_hbm, ada, in_sems.at[1])
    load_ada.start()
    load_up = pltpu.make_async_copy(wup_src, up_own, in_sems.at[2])
    load_up.start()
    load_down = pltpu.make_async_copy(wdown_src, down_own, in_sems.at[3])
    load_down.start()

    barrier = pltpu.get_barrier_semaphore()
    partners = [(wide, peer) for peer in narrow_peers(here)] + [(wide ^ 1, here), (wide ^ 2, here)]
    for partner in partners:
        pl.semaphore_signal(
            barrier, inc=1, device_id=partner, device_id_type=pl.DeviceIdType.MESH
        )
    permutation = group_permutation(shard_rows)
    load_tokens.wait()

    def permute(to):
        def one(at, carry):
            moved = mm(permutation, shards[at], NN).astype(BF16)
            for group in range(4):
                to[at, group] = moved[group * (shard_rows // 4) : (group + 1) * (shard_rows // 4)]
            return carry

        lax.fori_loop(0, latents, one, 0)

    pl.semaphore_wait(barrier, len(partners))
    exchange = Exchange(sent, got, sems, local_sems.at[0], 0, wide, here)
    exchange_cot = Exchange(sent_cot, cot_ref, sems, local_sems.at[1], 3, wide, here)
    gathers = [
        Gather(src, dst, sems, local_sems.at[2 + at], 9 + Gather.COPIES * at, wide, here)
        for at, (src, dst) in enumerate(
            (
                (wqkv_src, wqkv_ref),
                (wout_src, wout_ref),
                (up_own, wup_ref),
                (down_own, wdown_ref),
            )
        )
    ]
    g_qkv, g_out, g_up, g_down = gathers
    taps_own = pltpu.make_async_copy(ktaps_src, ktaps_ref.at[0], local_sems.at[6])
    taps_sends = [
        remote(ktaps_src, ktaps_ref.at[peer ^ here], sems, 6 + at, wide, peer)
        for at, peer in enumerate(narrow_peers(here))
    ]
    g_qkv.start_far()
    permute(sent)
    exchange.start()
    load_cot = pltpu.make_async_copy(cot_hbm, shards, in_sems.at[0])
    load_cot.start()
    load_up.wait()
    load_down.wait()
    for one in gathers:
        one.start_near()
    taps_own.start()
    for one in taps_sends:
        one.start()

    load_ada.wait()
    for part in range(6):
        mod_ref[part : part + 1, :] = mm(
            silu_ref[...], ada[:, part * width : (part + 1) * width], NN
        )[0:1, :]
    load_cot.wait()
    permute(sent_cot)
    g_qkv.swap()
    shift_one, scale_one, gate_one = mod_ref[0:1, :], mod_ref[1:2, :], mod_ref[2:3, :]
    shift_two, scale_two, gate_two = mod_ref[3:4, :], mod_ref[4:5, :], mod_ref[5:6, :]
    clear_edges(base)
    clear_edges(shifted)
    exchange.wait()
    g_out.start_far()
    g_up.start_far()
    g_qkv.corner()
    for group in range(4):
        for source in range(latents):
            start = group * PHASE + source * ROWS
            x_ref[start : start + ROWS, :] = got[group, source]
    flush(x_ref, x_hbm)

    def norm_step(step, carry):
        group, part = step // (PHASE // ROWS), step % (PHASE // ROWS)
        unit, _ = normed(x_ref[ds(step * ROWS, ROWS), :].astype(F32))
        h_one = (unit * (1.0 + scale_one) + shift_one).astype(BF16)
        base[group, ds(HALF + part * ROWS, ROWS, HALF), :] = h_one.astype(F32)
        return carry

    lax.fori_loop(0, rows_all // ROWS, norm_step, 0)
    g_qkv.share_corner()
    g_out.swap()

    def conv_step(block, carry):
        lanes = ds(block * LANES, LANES)
        shift_cols(base, shifted, lanes)
        taps = [taps_ref[t // 3, t % 3 : t % 3 + 1, lanes].astype(F32) for t in range(9)]

        def rows_step(step, carry):
            for group in range(4):
                total = jnp.zeros((ROWS, LANES), F32)
                for tap in range(9):
                    total += taps[tap] * tap_value(
                        base, shifted, group, tap // 3, tap % 3, step * ROWS, lanes
                    )
                u_ref[ds(group * PHASE + step * ROWS, ROWS), lanes] = total.astype(BF16)
            return carry

        return lax.fori_loop(0, PHASE // ROWS, rows_step, carry)

    blocks = width // LANES
    lax.fori_loop(0, 2 * blocks // 3, conv_step, 0)
    g_out.corner()
    g_up.swap()
    g_down.start_far()
    lax.fori_loop(2 * blocks // 3, blocks, conv_step, 0)
    flush(u_ref, u_hbm)
    g_qkv.finish()
    flush(wqkv_ref, wqkv_hbm)

    def project_step(step, carry):
        rows = ds(step * PHASE, PHASE)
        for part in range(3):
            cols = slice(part * width, (part + 1) * width)
            qkv_ref[rows, cols] = mm(u_ref[rows, :], wqkv_ref[:, cols], NT).astype(BF16)
        return carry

    lax.fori_loop(0, 4, project_step, 0)

    pairs = width // LANES
    first = lax.broadcasted_iota(jnp.int32, (PHASE, LANES), 1) < HEAD_DIM
    zero = jnp.zeros((PHASE, LANES), BF16)

    def attend_step(step, carry):
        group, pair = step // pairs, step % pairs
        rows = ds(group * PHASE, PHASE)
        query = qkv_ref[rows, ds(pair * LANES, LANES)]
        key = qkv_ref[rows, ds(width + pair * LANES, LANES)]
        value = qkv_ref[rows, ds(2 * width + pair * LANES, LANES)]
        found = []
        for head in range(2):
            own = jnp.where(first, query, zero) if head == 0 else jnp.where(first, zero, query)
            scores = mm(key, own, NT)
            top = jnp.max(scores, axis=0, keepdims=True)
            raised = jnp.exp2((scores - top) * (LOG2E * HEAD_DIM**-0.5))
            probs = (raised * (1.0 / jnp.sum(raised, axis=0, keepdims=True))).astype(BF16)
            probs_ref[step, :, head * PHASE : (head + 1) * PHASE] = probs
            found.append(mm(probs, value, TN))
        ctx_ref[rows, ds(pair * LANES, LANES)] = jnp.where(first, found[0], found[1]).astype(BF16)
        return carry

    flush(qkv_ref, qkv_hbm)
    g_up.corner()
    g_out.share_corner()
    g_down.swap()
    exchange_cot.start()

    def attend_group(group):
        lax.fori_loop(group * pairs, (group + 1) * pairs, attend_step, 0)
        done = slice(group * pairs, (group + 1) * pairs)
        flush(probs_ref.at[done], probs_hbm.at[done])

    attend_group(0)
    g_up.share_corner()
    attend_group(1)
    g_down.corner()
    attend_group(2)
    g_down.share_corner()
    attend_group(3)
    flush(ctx_ref, ctx_hbm)
    g_out.finish()
    flush(wout_ref, wout_hbm)

    def out_step(step, carry):
        rows = ds(step * PHASE, PHASE)
        total = mm(ctx_ref[rows, :], wout_ref[...], NN)
        att_ref[rows, :] = total.astype(BF16)
        x1_ref[rows, :] = x_ref[rows, :].astype(F32) + gate_one * total
        return carry

    lax.fori_loop(0, 4, out_step, 0)
    live = live_ref[0, 0]

    def second_step(step, carry):
        rows = ds(step * ROWS, ROWS)
        unit, _ = normed(x1_ref[rows, :])
        h2_ref[rows, :] = (unit * (1.0 + scale_two) + shift_two).astype(BF16)
        group, source = step // (PHASE // ROWS), step % (PHASE // ROWS)
        db_ref[rows, :] = (cot_ref[group, source].astype(F32) * live * gate_two).astype(BF16)
        return carry

    exchange_cot.wait()
    flush(cot_ref, cot_hbm_out)
    lax.fori_loop(0, rows_all // ROWS, second_step, 0)
    for part in range(4):
        h2t_ref[:, part * PHASE : (part + 1) * PHASE] = h2_ref[
            part * PHASE : (part + 1) * PHASE, :
        ].T
    g_up.finish()
    g_down.finish()
    for copy in flushed:
        copy.wait()
    taps_own.wait()
    for one in taps_sends:
        one.wait()


def whole(memory=pltpu.VMEM):
    return pl.BlockSpec(memory_space=memory)


def front(live, silu_row, taps, tokens, cot, w_ada, wqkv, wout, wup, wdown, ktaps):
    latents, shard_rows, width = tokens.shape
    rows = latents * shard_rows
    steps = 4 * (width // LANES)
    shape = jax.ShapeDtypeStruct
    full = lambda shard: shape((latents * shard.shape[0],) + shard.shape[1:], BF16)
    moved = (latents, 4, shard_rows // 4, width)
    streamed = (
        shape((rows, width), BF16),
        shape((4, latents, shard_rows // 4, width), BF16),
        shape((rows, width), BF16),
        shape((rows, 3 * width), BF16),
        shape((steps, PHASE, 2 * PHASE), BF16),
        shape((rows, width), BF16),
        full(wqkv),
        full(wout),
    )
    return pl.pallas_call(
        front_kernel,
        out_shape=streamed
        + (
            shape((6, width), F32),
            shape((rows, width), BF16),
            shape((rows, width), F32),
            shape((rows, width), BF16),
            shape((width, rows), BF16),
            shape((rows, width), BF16),
            full(wup),
            full(wdown),
            shape((latents,) + ktaps.shape, BF16),
        ),
        in_specs=[whole(pltpu.SMEM)] + [whole()] * 2 + [whole(pl.ANY)] * 3 + [whole()] * 2 + [whole(pl.ANY)] * 2 + [whole()],
        out_specs=(whole(pl.ANY),) * 8 + (whole(),) * 6 + (whole(pl.ANY),) * 2 + (whole(),),
        scratch_shapes=[pltpu.VMEM(one.shape, one.dtype) for one in streamed]
        + [
            pltpu.VMEM((4, PAD, width), F32),
            pltpu.VMEM((4, PAD, width), F32),
            pltpu.VMEM((latents, shard_rows, width), BF16),
            pltpu.VMEM(moved, BF16),
            pltpu.VMEM(moved, BF16),
            pltpu.VMEM((4, latents, shard_rows // 4, width), BF16),
            pltpu.VMEM(w_ada.shape, BF16),
            pltpu.VMEM(wup.shape, BF16),
            pltpu.VMEM(wdown.shape, BF16),
            pltpu.SemaphoreType.DMA((2, 9 + 4 * Gather.COPIES)),
            pltpu.SemaphoreType.DMA((7,)),
            pltpu.SemaphoreType.DMA((4,)),
            pltpu.SemaphoreType.DMA((len(streamed) + 3,)),
        ],
        compiler_params=pltpu.CompilerParams(
            vmem_limit_bytes=60 * MIB, collective_id=0, has_side_effects=True
        ),
        name="attn_forward",
    )(live, silu_row, taps, tokens, cot, w_ada, wqkv, wout, wup, wdown, ktaps)


def ffn_kernel(
    n_wide, live_ref, h2_ref, h2t_ref, db_ref, x1_hbm, cot_hbm, att_hbm, mod_ref,
    wup_before, wup_even, wup_odd, wup_after, wdown_even, wdown_odd, taps_even, taps_odd,
    block_ref, dx1_ref, datt_ref, dmod_ref, sums_ref,
    hid_even, hid_odd, hid_moved, grad, grad_moved, slope, act, act_t, dhid, branch, dtaps,
    work, chip_sum, got_near, got_far, got_sums, x1_ref, cot_ref, att_ref, sems, sum_sems, in_sems,
):
    rows_all, width = h2_ref.shape
    loads = [
        pltpu.make_async_copy(src, dst, in_sems.at[at])
        for at, (src, dst) in enumerate(((x1_hbm, x1_ref), (cot_hbm, cot_ref), (att_hbm, att_ref)))
    ]
    dh2 = dx1_ref
    wide, here = lax.axis_index("wide"), lax.axis_index("narrow")
    step, steps = pl.program_id(0), pl.num_programs(0)
    quarters = [slice(q * PHASE, (q + 1) * PHASE) for q in range(4)]
    inside = slice(HALF, HALF + PHASE)
    lane_blocks = [slice(at * LANES, (at + 1) * LANES) for at in range(CHUNK // LANES)]
    col = lax.broadcasted_iota(jnp.int32, (ROWS, LANES), 0) % HALF

    partners = [(wide, here ^ 1), (wide, here ^ 2)] + wide_partners(wide, here, n_wide)[:HALVINGS]
    pieces, sum_rows = got_sums.shape[0], got_sums.shape[1]
    sums = [
        WideSum(sums_ref.at[at, : 2 * width], sums_ref.at[at, : 2 * width], None, got_sums.at[at], sum_sems,
                at * HALVINGS, wide, here, n_wide)
        for at in range(pieces)
    ]
    schedule = halvings_ahead(pieces, sums[0].levels)

    def to_near(at):
        return remote(work.at[at % 2], got_near.at[at], sems, at, wide, here ^ 1)

    def to_far(at):
        return remote(chip_sum.at[at], got_far.at[at], sems, steps + at, wide, here ^ 2)

    @pl.when(step == 0)
    def _():
        for load in loads:
            load.start()
        barrier = pltpu.get_barrier_semaphore()
        for partner in partners:
            pl.semaphore_signal(
                barrier, inc=1, device_id=partner, device_id_type=pl.DeviceIdType.MESH
            )
        for ref in (hid_even, hid_odd, hid_moved, grad, grad_moved):
            clear_edges(ref)
        branch[...] = jnp.zeros_like(branch)
        dh2[...] = jnp.zeros_like(dh2)
        dtaps[...] = jnp.zeros_like(dtaps)
        dhid[...] = jnp.zeros_like(dhid)
        full = mm(h2_ref[...], wup_even[...], NN)
        for q in range(4):
            hid_even[q, inside, :] = full[quarters[q]]
        pl.semaphore_wait(barrier, len(partners))

    def moved_cols(group, value):
        if group % 2:
            return jnp.where(col == 0, 0.0, pltpu.roll(value, 1, 0))
        return jnp.where(col == HALF - 1, 0.0, pltpu.roll(value, ROWS - 1, 0))

    def static_tap(base, shifted, group, tap_row, tap_col, start, lanes):
        src_row, row_move = tap_source(group // 2, tap_row)
        src_col, col_move = tap_source(group % 2, tap_col)
        ref = base if col_move == 0 else shifted
        first = HALF + row_move * HALF + start
        return ref[2 * src_row + src_col, first : first + ROWS, lanes]

    def weights_back(q, wup_last, slot):
        dh2[quarters[q], :] += mm(dhid[quarters[q], :], wup_last[...], NT)
        if q < width // PHASE:
            slot[quarters[q], :] = mm(h2t_ref[quarters[q], :], dhid[...], NN).astype(BF16)

    def forward_products(part, wdown, wup_last, slot):
        grad[part, inside, :] = mm(db_ref[quarters[part], :], wdown[...], NT)
        yield
        for cols in quarters[: width // PHASE]:
            dh2[quarters[part], cols] += mm(dhid[quarters[part], :], wup_last[cols, :], NT)
            yield
        if part < width // PHASE:
            slot[quarters[part], :] = mm(h2t_ref[quarters[part], :], dhid[...], NN).astype(BF16)
        yield

    def backward_products(part, hid_next, wdown, wup_next, slot):
        hid_next[part, inside, :] = mm(h2_ref[quarters[part], :], wup_next[...], NN)
        yield
        for cols in quarters[: width // PHASE]:
            branch[quarters[part], cols] += mm(act[quarters[part], :], wdown[:, cols], NN)
            yield
        if part < width // CHUNK:
            block = slice(part * CHUNK, (part + 1) * CHUNK)
            slot[width + part * CHUNK : width + (part + 1) * CHUNK, :] = mm(
                act_t[...], db_ref[:, block], NN
            ).astype(BF16)
        yield

    def forward(hid, wdown, taps_ref, wup_last, slot):
        taps = [[taps_ref[0, t : t + 1, lanes].astype(F32) for t in range(9)] for lanes in lane_blocks]
        for part in range(PHASE // ROWS):
            rows = slice(HALF + part * ROWS, HALF + (part + 1) * ROWS)
            for group in range(4):
                for lanes in lane_blocks:
                    hid_moved[group, rows, lanes] = moved_cols(group, hid[group, rows, lanes])
        for part in range(PHASE // ROWS):
            products = forward_products(part, wdown, wup_last, slot)
            for group in range(4):
                for at, lanes in enumerate(lane_blocks):
                    next(products, None)
                    total = jnp.zeros((ROWS, LANES), F32)
                    for tap in range(9):
                        total += taps[at][tap] * static_tap(
                            hid, hid_moved, group, tap // 3, tap % 3, part * ROWS, lanes
                        )
                    square = total * total
                    turned = jnp.tanh(total * (square * (GELU_C * GELU_A) + GELU_C))
                    half = 0.5 * turned + 0.5
                    bend = total * (half - half * half)
                    start = group * PHASE + part * ROWS
                    act[start : start + ROWS, lanes] = (total * half).astype(BF16)
                    slope[start : start + ROWS, lanes] = half + bend * (
                        square * (6.0 * GELU_C * GELU_A) + 2.0 * GELU_C
                    )

    def backward(hid, hid_next, wdown, wup_next, taps_ref, slot):
        taps = [[taps_ref[0, t : t + 1, lanes].astype(F32) for t in range(9)] for lanes in lane_blocks]
        act_t[...] = act[...].T
        for part in range(PHASE // ROWS):
            rows = slice(HALF + part * ROWS, HALF + (part + 1) * ROWS)
            for group in range(4):
                start = group * PHASE + part * ROWS
                for lanes in lane_blocks:
                    value = grad[group, rows, lanes] * slope[start : start + ROWS, lanes]
                    grad[group, rows, lanes] = value
                    grad_moved[group, rows, lanes] = moved_cols(group, value)
        sums = [[jnp.zeros((8, LANES), F32) for _ in range(9)] for _ in lane_blocks]
        for part in range(PHASE // ROWS):
            products = backward_products(part, hid_next, wdown, wup_next, slot)
            for group in range(4):
                start = group * PHASE + part * ROWS
                for at, lanes in enumerate(lane_blocks):
                    next(products, None)
                    own = hid[group, HALF + part * ROWS : HALF + (part + 1) * ROWS, lanes]
                    total = jnp.zeros((ROWS, LANES), F32)
                    for tap in range(9):
                        moved = static_tap(
                            grad, grad_moved, group, 2 - tap // 3, 2 - tap % 3, part * ROWS, lanes
                        )
                        total += taps[at][tap] * moved
                        sums[at][tap] += (own * moved).reshape(ROWS // 8, 8, LANES).sum(axis=0)
                    dhid[start : start + ROWS, lanes] = total.astype(BF16)
        for at, lanes in enumerate(lane_blocks):
            for tap in range(9):
                dtaps[tap : tap + 1, lanes] = jnp.sum(sums[at][tap], axis=0, keepdims=True)
        slot[2 * width :, :] = dtaps[...].astype(BF16)

    def settle(pair):
        to_near(pair).wait_recv()

        @pl.when(pair < steps // 2)
        def _():
            chip_sum[pair] = (work[2].astype(F32) + got_near[pair].astype(F32)).astype(BF16)
            to_far(pair).start()

        @pl.when(pair >= steps // 2)
        def _():
            part = pair - steps // 2
            to_far(part).wait_recv()
            sums_ref[part] = (
                work[2].astype(F32) + got_near[pair].astype(F32) + got_far[part].astype(F32)
            ).astype(BF16)

        for part in range(pieces):

            @pl.when(pair == steps // 2 + part)
            def _():
                for at in range(part):
                    sums[at].finish_half(part - at - 1)
                for at in range(part + 1):
                    if part - at < schedule[at]:
                        sums[at].start_half(part - at)

    forward(hid_even, wdown_even, taps_even, wup_before, work.at[2])

    @pl.when(step >= 1)
    def _():
        settle(step - 1)

    @pl.when(step >= 2)
    def _():
        to_near(step - 2).wait_send()

    even_slot = work.at[step % 2]
    backward(hid_even, hid_odd, wdown_even, wup_odd, taps_even, even_slot)
    forward(hid_odd, wdown_odd, taps_odd, wup_even, even_slot)
    to_near(step).start()
    backward(hid_odd, hid_even, wdown_odd, wup_after, taps_odd, work.at[2])

    @pl.when(step == steps - 1)
    def _():
        for q in range(4):
            weights_back(q, wup_odd, work.at[2])
        settle(step)
        for load in loads:
            load.wait()
        gate_one, scale_two, gate_two = mod_ref[2:3, :], mod_ref[4:5, :], mod_ref[5:6, :]
        live = live_ref[0, 0]

        def fold(value):
            return value.reshape(ROWS // 8, 8, width).sum(axis=0)

        def rows_step(at, sums):
            rows = ds(at * ROWS, ROWS)
            after = x1_ref[rows, :]
            dout = cot_ref[rows, :].astype(F32) * live
            branch_rows = branch[rows, :]
            block_ref[rows, :] = ((after + gate_two * branch_rows) * live).astype(BF16)
            unit, inv = normed(after)
            dh2_rows = dh2[rows, :]
            dx1 = dout + norm_back(unit, inv, dh2_rows * (1.0 + scale_two))
            dx1_ref[rows, :] = dx1
            datt_ref[rows, :] = (dx1 * gate_one).astype(BF16)
            found = (dx1 * att_ref[rows, :].astype(F32), dh2_rows, dh2_rows * unit, dout * branch_rows)
            return tuple(total + fold(one) for total, one in zip(sums, found))

        start = tuple(jnp.zeros((8, width), F32) for _ in range(4))
        totals = lax.fori_loop(0, rows_all // ROWS, rows_step, start)
        for at in range(4):
            dmod_ref[at : at + 1, :] = jnp.sum(totals[at], axis=0, keepdims=True)
        for at in (steps - 2, steps - 1):
            to_near(at).wait_send()
        for at in range(steps // 2):
            to_far(at).wait_send()
        for at in range(pieces):
            sums[at].finish_half(schedule[at] - 1)
            for level in range(schedule[at]):
                sums[at].half_copy(level).wait_send()


def ffn(n_wide, live, h2, h2t, db, x1, cot, att, mod, wup, wdown, taps):
    rows, width = h2.shape
    shards, _, local = taps.shape
    per = local // CHUNK
    steps = shards * per // 2
    parcel = (2 * width + 16, CHUNK)
    shape = jax.ShapeDtypeStruct
    keep = lambda *block: pl.BlockSpec(
        block, lambda c: (0,) * len(block), pipeline_mode=pl.Buffered(1)
    )

    def slot_and_part(step, odd):
        return jnp.where(step < per, 3, 1) - odd, step % per

    def up_block(move, odd):
        def index(step):
            return slot_and_part(jnp.clip(step + move, 0, steps - 1), odd)

        return pl.BlockSpec((width, CHUNK), index)

    def down_block(odd):
        def index(step):
            slot, part = slot_and_part(step, odd)
            return slot * per + part, 0

        return pl.BlockSpec((CHUNK, width), index)

    def taps_block(odd):
        def index(step):
            slot, part = slot_and_part(step, odd)
            return slot, 0, part

        return pl.BlockSpec((1, taps.shape[1], CHUNK), index)

    return pl.pallas_call(
        partial(ffn_kernel, n_wide),
        grid=(steps,),
        out_shape=(
            shape((rows, width), BF16),
            shape((rows, width), F32),
            shape((rows, width), BF16),
            shape((4, width), F32),
            shape((per,) + parcel, BF16),
        ),
        in_specs=[
            whole(pltpu.SMEM),
            keep(rows, width),
            keep(width, rows),
            keep(rows, width),
            whole(pl.ANY),
            whole(pl.ANY),
            whole(pl.ANY),
            keep(6, width),
            up_block(-1, 1),
            up_block(0, 0),
            up_block(0, 1),
            up_block(1, 0),
            down_block(0),
            down_block(1),
            taps_block(0),
            taps_block(1),
        ],
        out_specs=(
            keep(rows, width),
            keep(rows, width),
            keep(rows, width),
            keep(4, width),
            keep(per, *parcel),
        ),
        scratch_shapes=[pltpu.VMEM((4, PAD, CHUNK), F32)] * 5
        + [
            pltpu.VMEM((rows, CHUNK), F32),
            pltpu.VMEM((rows, CHUNK), BF16),
            pltpu.VMEM((CHUNK, rows), BF16),
            pltpu.VMEM((rows, CHUNK), BF16),
            pltpu.VMEM((rows, width), F32),
            pltpu.VMEM((16, CHUNK), F32),
            pltpu.VMEM((3,) + parcel, BF16),
            pltpu.VMEM((per,) + parcel, BF16),
            pltpu.VMEM((steps,) + parcel, BF16),
            pltpu.VMEM((per,) + parcel, BF16),
            pltpu.VMEM((per, sum_landing(2 * width, n_wide), CHUNK), BF16),
            pltpu.VMEM((rows, width), F32),
            pltpu.VMEM((rows, width), BF16),
            pltpu.VMEM((rows, width), BF16),
            pltpu.SemaphoreType.DMA((2, steps + per)),
            pltpu.SemaphoreType.DMA((2, per * HALVINGS)),
            pltpu.SemaphoreType.DMA((3,)),
        ],
        compiler_params=pltpu.CompilerParams(
            vmem_limit_bytes=62 * MIB, collective_id=1, has_side_effects=True
        ),
        name="feed_forward",
    )(live, h2, h2t, db, x1, cot, att, mod, wup, wup, wup, wup, wdown, wdown, taps, taps)


def attn_backward_kernel(
    n_wide, datt_ref, ctx_ref, u_ref, wout_ref, parcels, silu_ref, dmod_ref, qkv_hbm, probs_hbm,
    dqkv_ref, own_ref, full, gtaps_ref, small,
    dctx, probs_buf, weights, got_near, chip_sum, got_far, work, got_sums, taps_sum, taps_got,
    sems, in_sems, sum_sems, small_sems,
):
    rows_all, width = u_ref.shape
    wide, here = lax.axis_index("wide"), lax.axis_index("narrow")
    pairs = width // LANES
    half_pairs = pairs // 2
    steps = 4 * pairs
    slots = weights.shape[0]
    load_qkv = pltpu.make_async_copy(qkv_hbm, dqkv_ref, in_sems.at[2])
    load_qkv.start()

    def pair_of(step):
        return (half_pairs + step // 4) % pairs

    def load_probs(step):
        return pltpu.make_async_copy(
            probs_hbm.at[(step % 4) * pairs + pair_of(step)], probs_buf.at[step % 2], in_sems.at[step % 2]
        )

    load_probs(0).start()
    greet([(wide, here ^ 2), (wide, here ^ 1)] + wide_partners(wide, here, n_wide))
    pieces = full.shape[0]
    rows = full.shape[1]
    per_sum = sum_semaphores(n_wide)
    ahead = halvings_ahead(pieces, min(HALVINGS, n_wide.bit_length() - 1))
    sums = [
        WideSum(parcels.at[at, :rows], work.at[at], full.at[at], got_sums.at[at], sum_sems, at * per_sum,
                wide, here, n_wide, done=ahead[at])
        for at in range(pieces)
    ]
    levels = n_wide.bit_length() - 1
    queues = [one.actions() for one in sums]

    def advance(*which):
        for at in which:
            if queues[at]:
                for act in queues[at].pop(0):
                    act()

    def taps_copy(level):
        return remote(taps_sum.at[level], taps_got.at[level], sems, 6 + level, wide ^ (1 << level), here)

    def taps_add(level):
        taps_copy(level).wait_recv()
        taps_sum[level + 1] = taps_sum[level] + taps_got[level]
        if level + 1 < levels:
            taps_copy(level + 1).start()

    for at in range(pieces):
        taps_sum[0, :, at * CHUNK : (at + 1) * CHUNK] = parcels[at, rows:, :].astype(F32)
    partners = wide_partners(wide, here, n_wide) + [(wide, here ^ 1), (wide, here ^ 2)]

    def small_copy(level):
        have = 1 << level
        return remote(small.at[:have], small.at[have : 2 * have], small_sems, level, *partners[level])

    def small_step(level):
        small_copy(level).wait_recv()
        if level + 1 < len(partners):
            small_copy(level + 1).start()

    early = [silu_ref[0:1, :].astype(F32)] + [dmod_ref[at : at + 1, :] for at in range(4)]
    small[0] = lane_rows(early, EARLY)
    small_copy(0).start()
    taps_copy(0).start()
    advance(2, 0, 1)

    def ctx_step(step, carry):
        span = ds(step * PHASE, PHASE)
        dctx[span, :] = mm(datt_ref[span, :], wout_ref[...], NT).astype(BF16)
        return carry

    lax.fori_loop(0, 4, ctx_step, 0)
    load_qkv.wait()

    first = lax.broadcasted_iota(jnp.int32, (PHASE, LANES), 1) < HEAD_DIM
    zero = jnp.zeros((PHASE, LANES), BF16)
    scale = HEAD_DIM**-0.5

    def attend(step):
        group, pair = step % 4, pair_of(step)
        load_probs(step).wait()

        @pl.when(step + 1 < steps)
        def _():
            load_probs(step + 1).start()

        span = ds(group * PHASE, PHASE)
        query = dqkv_ref[span, ds(pair * LANES, LANES)]
        key = dqkv_ref[span, ds(width + pair * LANES, LANES)]
        value = dqkv_ref[span, ds(2 * width + pair * LANES, LANES)]
        dctx_pair = dctx[span, ds(pair * LANES, LANES)]
        dq, dk, dv = [], None, None
        for head in range(2):
            own = lambda both: jnp.where(first, both, zero) if head == 0 else jnp.where(first, zero, both)
            probs = probs_buf[step % 2, :, head * PHASE : (head + 1) * PHASE]
            probs_f = probs.astype(F32)
            dctx_own, query_own = own(dctx_pair), own(query)
            dprobs = mm(value, dctx_own, NT)
            inner = jnp.sum(dprobs * probs_f, axis=0, keepdims=True)
            dscores = (probs_f * (dprobs - inner)).astype(BF16)
            dv_one = mm(probs, dctx_own, NN)
            dk_one = mm(dscores, query_own, NN)
            dv = dv_one if dv is None else dv + dv_one
            dk = dk_one if dk is None else dk + dk_one
            dq.append(mm(dscores, key, TN))
        dqkv_ref[span, ds(pair * LANES, LANES)] = (
            jnp.where(first, dq[0], dq[1]) * scale
        ).astype(BF16)
        dqkv_ref[span, ds(width + pair * LANES, LANES)] = (dk * scale).astype(BF16)
        dqkv_ref[span, ds(2 * width + pair * LANES, LANES)] = dv.astype(BF16)

    def attend_loop(begin, end, plan):
        def body(step, carry):
            for at, what in plan:
                pl.when(step == at)(what)
            attend(step)
            return carry

        lax.fori_loop(begin, end, body, 0)

    slab = width // slots

    def weight_grads(half):
        span = width // 2
        for part in range(3):
            left = dqkv_ref[:, part * width + half * span : part * width + (half + 1) * span]
            found = mm(left, u_ref[...], TN).astype(BF16)
            for one in range(2):
                weights[2 * half + one, part * slab : (part + 1) * slab, :] = found[
                    one * slab : (one + 1) * slab
                ]

    head, tail = slice(3 * slab), slice(3 * slab, 4 * slab)

    def near_copy(early, rows, at):
        return remote(
            weights.at[3 if early else 1, rows], got_near.at[0 if early else 1, rows], sems, at, wide, here ^ 1
        )

    def far_copy(rows, at):
        return remote(chip_sum.at[rows], got_far.at[rows], sems, at, wide, here ^ 2)

    def add_chip(rows):
        chip_sum[rows, :] = (weights[2, rows, :].astype(F32) + got_near[0, rows, :].astype(F32)).astype(BF16)

    near_out, near_early = near_copy(True, tail, 0), near_copy(True, head, 1)
    late_out, near_late = near_copy(False, tail, 2), near_copy(False, head, 3)
    far_out, far = far_copy(tail, 4), far_copy(head, 5)

    for part in range(width // PHASE):
        cols = slice(part * PHASE, (part + 1) * PHASE)
        found = mm(ctx_ref[:, cols], datt_ref[...], TN).astype(BF16)
        for slot in range(slots):
            low, high = max(part * PHASE, slot * slab), min((part + 1) * PHASE, (slot + 1) * slab)
            if low < high:
                weights[slot, 3 * slab + low - slot * slab : 3 * slab + high - slot * slab, :] = found[
                    low - part * PHASE : high - part * PHASE
                ]
    near_out.start()
    late_out.start()

    def send_out():
        near_out.wait_recv()
        add_chip(tail)
        far_out.start()

    later = lambda *which: partial(advance, *which)
    hops = len(partners) - 1
    small_plan = [(4 + 18 * level // hops, partial(small_step, level)) for level in range(hops)]
    attend_loop(
        0, steps // 2,
        [one for one in small_plan if one[0] < steps // 2]
        + [(1, send_out), (2, later(2, 0)), (5, later(1)), (7, partial(taps_add, 0)), (8, later(2, 0)), (11, later(1))],
    )
    weight_grads(1)
    near_early.start()
    advance(2)
    near_early.wait_recv()
    add_chip(head)
    far.start()
    attend_loop(
        steps // 2, steps,
        [one for one in small_plan if one[0] >= steps // 2]
        + [(13, later(1, 0)), (14, partial(taps_add, 1)), (16, later(2))],
    )
    weight_grads(0)
    near_late.start()
    small_step(len(partners) - 1)
    for level in range(2, levels):
        taps_add(level)
    gtaps_ref[...] = taps_sum[levels]
    near_late.wait_recv()
    late_out.wait_recv()
    while any(queues):
        advance(0, 1, 2)
    far_out.wait_recv()
    far.wait_recv()
    own_ref[...] = (
        weights[0].astype(F32) + got_near[1].astype(F32) + got_far[...].astype(F32)
    ).astype(BF16)
    for one in sums:
        one.wait_sends()
    for level in range(levels):
        taps_copy(level).wait_send()
    for copy in (near_out, near_early, late_out, near_late, far_out, far):
        copy.wait_send()
    for level in range(len(partners)):
        small_copy(level).wait_send()


def attn_backward(n_wide, datt, ctx, u, wout, parcels, silu_row, dmod, qkv, probs):
    rows, width = u.shape
    slots = lax.axis_size("narrow")
    slab = wout.shape[0] // slots
    pieces, parcel_rows, _ = parcels.shape
    sum_rows = parcel_rows - 16
    shape = jax.ShapeDtypeStruct
    levels = n_wide.bit_length() - 1
    per_sum = sum_semaphores(n_wide)
    return pl.pallas_call(
        partial(attn_backward_kernel, n_wide),
        out_shape=(
            shape((rows, 3 * width), BF16),
            shape((4 * slab, width), BF16),
            shape((pieces, sum_rows, CHUNK), BF16),
            shape((16, pieces * CHUNK), F32),
            shape((n_wide * slots, EARLY, LANES), BF16),
        ),
        in_specs=[whole()] * 7 + [whole(pl.ANY)] * 2,
        out_specs=(whole(),) * 5,
        scratch_shapes=[
            pltpu.VMEM((rows, width), BF16),
            pltpu.VMEM((2, PHASE, 2 * PHASE), BF16),
            pltpu.VMEM((slots, 4 * slab, width), BF16),
            pltpu.VMEM((2, 4 * slab, width), BF16),
            pltpu.VMEM((4 * slab, width), BF16),
            pltpu.VMEM((4 * slab, width), BF16),
            pltpu.VMEM((pieces, sum_rows, CHUNK), BF16),
            pltpu.VMEM((pieces, sum_landing(sum_rows, n_wide), CHUNK), BF16),
            pltpu.VMEM((levels + 1, 16, pieces * CHUNK), F32),
            pltpu.VMEM((levels, 16, pieces * CHUNK), F32),
            pltpu.SemaphoreType.DMA((2, 6 + levels)),
            pltpu.SemaphoreType.DMA((3,)),
            pltpu.SemaphoreType.DMA((2, pieces * per_sum)),
            pltpu.SemaphoreType.DMA((2, levels + 2)),
        ],
        compiler_params=pltpu.CompilerParams(
            vmem_limit_bytes=56 * MIB, collective_id=2, has_side_effects=True
        ),
        name="attn_backward",
    )(datt, ctx, u, wout, parcels, silu_row, dmod, qkv, probs)


def one_hot(rows, columns, wanted):
    row = lax.broadcasted_iota(jnp.int32, (rows, columns), 0)
    column = lax.broadcasted_iota(jnp.int32, (rows, columns), 1)
    return jnp.where(column == wanted(row), 1.0, 0.0).astype(BF16)


def input_backward_kernel(
    n_wide, x_ref, mod_ref, taps_ref, own_ref, dx1_hbm, dqkv_hbm, wqkv_hbm, block_in,
    got_dx, got_block, full, late, dtaps_ref,
    base, shifted, first_in, dh1, dx1_ref, dqkv_ref, wqkv_ref, dx, work, got_sums, tap_parts, tap_sums, tap_got,
    sems, local_sems, sum_sems, taps_sems, late_sems,
):
    rows_all, width = x_ref.shape
    wide, here = lax.axis_index("wide"), lax.axis_index("narrow")
    loads = [
        pltpu.make_async_copy(src, dst, local_sems.at[2 + at])
        for at, (src, dst) in enumerate(
            ((dqkv_hbm, dqkv_ref), (wqkv_hbm, wqkv_ref), (dx1_hbm, dx1_ref))
        )
    ]
    for load in loads:
        load.start()
    shift_one, scale_one = mod_ref[0:1, :], mod_ref[1:2, :]
    greet([(wide, peer) for peer in narrow_peers(here)] + [(wide ^ away, here) for away in range(1, n_wide)])
    pieces = full.shape[0]
    rows = full.shape[1]
    per_sum = sum_semaphores(n_wide)
    sums = [
        WideSum(own_ref.at[at * rows : (at + 1) * rows], work.at[at], full.at[at], got_sums.at[at], sum_sems,
                at * per_sum, wide, here, n_wide, order=((0, 1, 2), (1, 2, 0))[at])
        for at in range(pieces)
    ]
    queues = [one.actions() for one in sums]

    def advance(*which):
        for at in which:
            if queues[at]:
                for act in queues[at].pop(0):
                    act()

    levels = n_wide.bit_length() - 1
    late_wide = [
        remote(late.at[0], late.at[away], late_sems, away - 1, wide ^ away, here) for away in range(1, n_wide)
    ]
    late_narrow = [
        remote(late.at[:n_wide], late.at[away * n_wide : (away + 1) * n_wide], late_sems, n_wide - 2 + away,
               wide, here ^ away)
        for away in (2, 3, 1)
    ]
    taps_narrow = [
        remote(tap_sums.at[levels], tap_got.at[levels + away - 1], taps_sems, levels + away - 1, wide, here ^ away)
        for away in (2, 3, 1)
    ]
    advance(0, 1)
    block_back = Return(block_in, got_block, sems, local_sems.at[1], 3, wide, here)
    block_back.start()
    clear_edges(base)
    clear_edges(shifted)

    def norm_step(step, carry):
        group, part = step // (PHASE // ROWS), step % (PHASE // ROWS)
        unit, _ = normed(x_ref[ds(step * ROWS, ROWS), :].astype(F32))
        h_one = (unit * (1.0 + scale_one) + shift_one).astype(BF16)
        first_in[group, ds(HALF + part * ROWS, ROWS, HALF), :] = h_one.astype(F32)
        return carry

    lax.fori_loop(0, rows_all // ROWS, norm_step, 0)

    def du_step(group, carry):
        span = ds(group * PHASE, PHASE)
        total = None
        for part in range(3):
            cols = slice(part * width, (part + 1) * width)
            one = mm(dqkv_ref[span, cols], wqkv_ref[:, cols], NN)
            total = one if total is None else total + one
        base[group, HALF : HALF + PHASE, :] = total
        return carry

    loads[0].wait()
    loads[1].wait()
    lax.fori_loop(0, 2, du_step, 0)
    advance(0, 1)
    lax.fori_loop(2, 4, du_step, 0)

    blocks = width // LANES

    def shift_step(block, carry):
        shift_cols(base, shifted, ds(block * LANES, LANES))
        return carry

    lax.fori_loop(0, blocks, shift_step, 0)
    tap_parts[...] = jnp.zeros_like(tap_parts)
    advance(0, 1)

    def taps_copy(level):
        return remote(tap_sums.at[level], tap_got.at[level], taps_sems, level, wide ^ (1 << level), here)

    def taps_step(level):
        taps_copy(level).wait_recv()
        tap_sums[level + 1] = tap_sums[level] + tap_got[level]
        if level + 1 < levels:
            taps_copy(level + 1).start()
        else:
            for copy in taps_narrow:
                copy.start()

    def fold(value):
        return value.reshape(ROWS // 8, 8, width).sum(axis=0)

    back = Return(dx, got_dx, sems, local_sems.at[0], 0, wide, here)
    found = tuple(jnp.zeros((8, width), F32) for _ in range(2))
    for at, away in enumerate((2, 3, 1, 0)):
        source = away ^ here

        def conv_step(block, carry, source=source):
            lanes = ds(block * LANES, LANES)
            taps = [taps_ref[t // 3, t % 3 : t % 3 + 1, lanes].astype(F32) for t in range(9)]
            sums = [jnp.zeros((8, LANES), F32) for _ in range(9)]
            for group in range(4):
                total = jnp.zeros((ROWS, LANES), F32)
                own = first_in[group, ds(HALF + source * ROWS, ROWS, HALF), lanes]
                for tap in range(9):
                    moved = tap_value(
                        base, shifted, group, 2 - tap // 3, 2 - tap % 3, source * ROWS, lanes
                    )
                    total += taps[tap] * moved
                    sums[tap] += (own * moved).reshape(ROWS // 8, 8, LANES).sum(axis=0)
                dh1[ds(group * PHASE + source * ROWS, ROWS), lanes] = total
            for tap in range(9):
                tap_parts[tap, :, lanes] += sums[tap]
            return carry

        def rows_step(group, sums, source=source):
            span = ds(group * PHASE + source * ROWS, ROWS)
            unit, inv = normed(x_ref[span, :].astype(F32))
            grad = dh1[span, :]
            dx[group, source] = (
                dx1_ref[span, :] + norm_back(unit, inv, grad * (1.0 + scale_one))
            ).astype(BF16)
            return tuple(total + fold(one) for total, one in zip(sums, (grad, grad * unit)))

        lax.fori_loop(0, blocks, conv_step, 0)
        if at == 0:
            loads[2].wait()
        if at == 3:
            for tap in range(9):
                tap_sums[0, tap : tap + 1, :] = jnp.sum(tap_parts[tap], axis=0, keepdims=True)
            tap_sums[0, 9:, :] = jnp.zeros((7, width), F32)
            taps_copy(0).start()
        advance(*((0, 1), (1,), (0,), (0, 1))[at])
        found = lax.fori_loop(0, 4, rows_step, found)
        if at < 3:
            back.copies[at].start()
    back.own.start()
    late[0] = lane_rows([jnp.sum(one, axis=0, keepdims=True) for one in found], SMALL)
    for copy in late_wide:
        copy.start()
    taps_step(0)
    for copy in late_wide:
        copy.wait_recv()
    for copy in late_narrow:
        copy.start()
    for level in range(1, levels):
        taps_step(level)
        advance(level % 2)
    for copy in late_narrow:
        copy.wait_recv()
    total = tap_sums[levels]
    for at, copy in enumerate(taps_narrow):
        copy.wait_recv()
        total += tap_got[levels + (1, 2, 0)[at]]
    dtaps_ref[...] = total
    while any(queues):
        advance(0, 1)
    block_back.wait()
    back.wait()
    for copy in late_wide + late_narrow + taps_narrow:
        copy.wait_send()
    for level in range(levels):
        taps_copy(level).wait_send()
    for one in sums:
        one.wait_sends()


def input_backward(n_wide, x, dx1, dqkv, mod, taps, wqkv, own, block):
    rows, width = x.shape
    slots = lax.axis_size("narrow")
    pieces = 2
    sum_rows = own.shape[0] // pieces
    shape = jax.ShapeDtypeStruct
    per_sum = sum_semaphores(n_wide)
    levels = n_wide.bit_length() - 1
    back = shape((slots, 4, rows // (4 * slots), width), BF16)
    return pl.pallas_call(
        partial(input_backward_kernel, n_wide),
        out_shape=(
            back,
            back,
            shape((pieces, sum_rows, width), BF16),
            shape((n_wide * slots, SMALL, LANES), BF16),
            shape((SMALL, width), F32),
        ),
        in_specs=[whole()] * 4 + [whole(pl.ANY)] * 4,
        out_specs=(whole(),) * 5,
        scratch_shapes=[pltpu.VMEM((4, PAD, width), F32)] * 3
        + [
            pltpu.VMEM((rows, width), F32),
            pltpu.VMEM((rows, width), F32),
            pltpu.VMEM((rows, 3 * width), BF16),
            pltpu.VMEM(wqkv.shape, BF16),
            pltpu.VMEM((4, slots, rows // (4 * slots), width), BF16),
            pltpu.VMEM((pieces, sum_rows, width), BF16),
            pltpu.VMEM((pieces, sum_landing(sum_rows, n_wide), width), BF16),
            pltpu.VMEM((9, 8, width), F32),
            pltpu.VMEM((levels + 1, SMALL, width), F32),
            pltpu.VMEM((levels + 3, SMALL, width), F32),
            pltpu.SemaphoreType.DMA((2, 6)),
            pltpu.SemaphoreType.DMA((5,)),
            pltpu.SemaphoreType.DMA((2, pieces * per_sum)),
            pltpu.SemaphoreType.DMA((2, levels + 3)),
            pltpu.SemaphoreType.DMA((2, n_wide + 2)),
        ],
        compiler_params=pltpu.CompilerParams(
            vmem_limit_bytes=56 * MIB, collective_id=3, has_side_effects=True
        ),
        name="input_backward",
    )(x, mod, taps, own, dx1, dqkv, wqkv, block)


def outputs_kernel(
    dx_in, block_in, attn_sum, ffn_sum, small, late, cond_ref, kattn_in, kffn_in, ada_hbm,
    gada_hbm, dx_hbm, block_hbm, gqkv_hbm, gout_hbm, gup_hbm, gdown_hbm, gcond_ref, kattn_ref, kffn_ref,
    ada, gada, dx, block, gqkv, gout, gup, gdown, early_rows, late_rows, sems, in_sem,
):
    width = gout.shape[-1]
    here = lax.axis_index("narrow")
    load_ada = pltpu.make_async_copy(ada_hbm, ada, in_sem.at[0])
    load_ada.start()
    started = []
    for row in range(3):
        kattn_ref[row] = kattn_in[3 * row : 3 * row + 3, :]
        kffn_ref[row] = kffn_in[3 * row : 3 * row + 3, :]

    def put(src, dst):
        copy = pltpu.make_async_copy(src, dst, sems.at[len(started)])
        copy.start()
        started.append(copy)

    devices = small.shape[0]
    blocks = width // LANES
    early_rows[...] = small[...].astype(F32).reshape(devices * EARLY, LANES)
    late_rows[...] = late[...].astype(F32).reshape(devices * SMALL, LANES)

    def pick(ref, share, number):
        cut = [ref[pl.ds(number * blocks + at, devices, share), :] for at in range(blocks)]
        return jnp.concatenate(cut, axis=1).astype(BF16)

    silu_all = pick(early_rows, EARLY, 0)
    dmods = [
        pick(late_rows, SMALL, part) if part < 2 else pick(early_rows, EARLY, part - 1) for part in range(6)
    ]
    for part in range(6):
        gada[part] = mm(silu_all, dmods[part], TN)
        put(gada.at[part], gada_hbm.at[:, part * width : (part + 1) * width])
    slab = attn_sum.shape[1] // 2
    for part in range(3):
        gqkv[part] = attn_sum[part // 2, (part % 2) * slab : (part % 2 + 1) * slab, :].astype(F32).T
        put(gqkv.at[part], gqkv_hbm.at[part])
    gout[...] = attn_sum[1, slab:, :].astype(F32)
    put(gout, gout_hbm)
    permutation = group_permutation(dx_in.shape[1] * dx_in.shape[2])
    for at in range(dx_in.shape[0]):
        for source, held, out in ((dx_in, dx, dx_hbm), (block_in, block, block_hbm)):
            groups = jnp.concatenate([source[at, group] for group in range(4)], axis=0)
            held[at] = mm(permutation, groups, TN).astype(held.dtype)
            put(held.at[at], out.at[at])
    for at in range(ffn_sum.shape[0]):
        cols = slice(at * CHUNK, (at + 1) * CHUNK)
        gup[:, cols] = ffn_sum[at, :width, :].astype(F32)
        for part in range(width // CHUNK):
            span = slice(width + part * CHUNK, width + (part + 1) * CHUNK)
            gdown[cols, part * CHUNK : (part + 1) * CHUNK] = ffn_sum[at, span, :].astype(F32)
        put(gdown.at[cols], gdown_hbm.at[cols])
    put(gup, gup_hbm)

    def own_place(row):
        away = row ^ here
        return jnp.where(row < cond_ref.shape[0], away * (devices // 4), -1)

    load_ada.wait()
    choose = one_hot(16, devices, own_place)
    grad_silu = jnp.zeros((16, width), F32)
    for part in range(6):
        own = mm(choose, dmods[part], NN).astype(BF16)
        grad_silu += mm(own, ada[:, part * width : (part + 1) * width], NT)
    cond = cond_ref[...].astype(F32)
    gate = 1.0 / (1.0 + jnp.exp(-cond))
    gcond_ref[...] = grad_silu[: cond_ref.shape[0]] * (gate * (1.0 + cond * (1.0 - gate)))
    for copy in started:
        copy.wait()


def outputs(dx, block, attn_sum, ffn_sum, small, late, cond, kattn, kffn, w_ada):
    slots, _, quarter, width = dx.shape
    slab = attn_sum.shape[1] // 2
    pieces = ffn_sum.shape[0]
    local = pieces * CHUNK
    shape = jax.ShapeDtypeStruct
    tokens = (slots, 4 * quarter, width)
    return pl.pallas_call(
        outputs_kernel,
        out_shape=(
            shape(w_ada.shape, F32),
            shape(tokens, F32),
            shape(tokens, BF16),
            shape((3, width, slab), F32),
            shape((slab, width), F32),
            shape((width, local), F32),
            shape((local, width), F32),
            shape(cond.shape, F32),
            shape((3, 3, width), F32),
            shape((3, 3, local), F32),
        ),
        in_specs=[whole()] * 9 + [whole(pl.ANY)],
        out_specs=(whole(pl.ANY),) * 7 + (whole(),) * 3,
        scratch_shapes=[
            pltpu.VMEM(w_ada.shape, BF16),
            pltpu.VMEM((6, width, width), F32),
            pltpu.VMEM(tokens, F32),
            pltpu.VMEM(tokens, BF16),
            pltpu.VMEM((3, width, slab), F32),
            pltpu.VMEM((slab, width), F32),
            pltpu.VMEM((width, local), F32),
            pltpu.VMEM((local, width), F32),
            pltpu.VMEM((small.shape[0] * EARLY, LANES), F32),
            pltpu.VMEM((small.shape[0] * SMALL, LANES), F32),
            pltpu.SemaphoreType.DMA((6 + 3 + 1 + 2 * slots + pieces + 1,)),
            pltpu.SemaphoreType.DMA((1,)),
        ],
        compiler_params=pltpu.CompilerParams(vmem_limit_bytes=56 * MIB),
        name="outputs",
    )(dx, block, attn_sum, ffn_sum, small, late, cond, kattn, kffn, w_ada)


def per_device(
    tokens, condition, cotangent, counts, w_ada, k_attn, w_qkv, w_out, w_up, k_ffn, w_down
):
    lat_dev, shard_rows, width = tokens.shape
    here = lax.axis_index("narrow")
    rows_all = shard_rows * lat_dev
    local = w_up.shape[1]

    n_wide = lax.axis_size("wide")
    qkv_t = w_qkv.transpose(2, 1, 0).reshape(w_qkv.shape[2], 3 * width)
    ktaps_own = jnp.pad(k_ffn.reshape(9, local), ((0, 7), (0, 0)))

    cond_f = condition.astype(F32)
    silu_low = jax.nn.silu(cond_f).astype(BF16)
    own_silu = jnp.broadcast_to(lax.dynamic_slice_in_dim(silu_low, here, 1, 0), (16, width))
    live = (here < counts[0]).astype(F32).reshape(1, 1)

    (x, cot, u, qkv, probs, ctx, wqkv, wout, mod, att, x1, h2, h2t, db, wup, wdown, ktaps) = front(
        live, own_silu, k_attn, tokens, cotangent, w_ada, qkv_t, w_out, w_up, w_down, ktaps_own
    )
    cot = cot.reshape(rows_all, width)
    block_g, dx1, datt, dmod_mid, parcels = ffn(
        n_wide, live, h2, h2t, db, x1, cot, att, mod, wup, wdown, ktaps
    )
    block_g = block_g.reshape(4, lat_dev, shard_rows // 4, width)
    dqkv, own, ffn_sum, gtaps, small = attn_backward(
        n_wide, datt, ctx, u, wout, parcels, own_silu, dmod_mid, qkv, probs
    )
    got_dx, got_block, attn_sum, late, dattn_taps = input_backward(
        n_wide, x, dx1, dqkv, mod, k_attn, wqkv, own, block_g
    )
    (
        grad_w_ada, grad_tokens, block, gqkv, grad_w_out, grad_w_up, grad_w_down, grad_condition,
        grad_k_attn, grad_k_ffn,
    ) = outputs(
        got_dx, got_block, attn_sum, ffn_sum, small, late, condition, dattn_taps, gtaps, w_ada
    )
    grad_w_qkv = gqkv.transpose(1, 0, 2)
    return (
        block,
        grad_tokens,
        grad_condition,
        grad_w_ada,
        grad_k_attn,
        grad_w_qkv,
        grad_w_out,
        grad_w_up,
        grad_k_ffn,
        grad_w_down,
    )


def solution(mesh):
    placed = (
        P("wide", "narrow", None),
        P("wide", None),
        P("wide", "narrow", None),
        P("wide"),
        P(),
        P(),
        P(None, None, "narrow"),
        P("narrow", None),
        P(None, "narrow"),
        P(None, None, "narrow"),
        P("narrow", None),
    )
    return jax.shard_map(
        per_device,
        mesh=mesh,
        in_specs=placed,
        out_specs=(
            P("wide", "narrow", None),
            P("wide", "narrow", None),
            P("wide", None),
            P(),
            P(),
            P(None, None, "narrow"),
            P("narrow", None),
            P(None, "narrow"),
            P(None, None, "narrow"),
            P("narrow", None),
        ),
        check_vma=False,
    )
```
